32 devices in a mesh: dp: 8 (over y, x, core), tensor: 4 (over z).
Axes of the slice: x: 2, y: 2, z: 4, core: 2. Of those that a mesh axis runs over, the one named last changes fastest.
Arguments:
- tokens: bfloat16 [8192, 1536], P('dp'), may hold values from -6 to 6
- cotangent: bfloat16 [8192, 1536], P('dp'), may hold values from -6 to 6
- segment_ids: int32 [8, 1024], P('dp'), may hold values from 0 to 2, never falling along the last dimension, each value on 1 to 512 neighbouring positions
- routes: int32 [8192, 8], P('dp'), may hold values from 0 to 39, all different within a row; in each aligned block of 1024 rows (0 to 1023, 1024 to 2047, ...) at most 384 rows name the same one
- attn_gain: float32 [1536], replicated, may hold values from 0.5 to 1.5
- query_weight: bfloat16 [1536, 1536], P(None, 'tensor'), may hold values from -0.15625 to 0.15625
- key_weight: bfloat16 [1536, 512], P(None, 'tensor'), may hold values from -0.15625 to 0.15625
- value_weight: bfloat16 [1536, 512], P(None, 'tensor'), may hold values from -0.15625 to 0.15625
- out_weight: bfloat16 [1536, 1536], P('tensor'), may hold values from -3 to 3
- ffn_gain: float32 [1536], replicated, may hold values from 0.5 to 1.5
- router_weight: bfloat16 [1536, 40], replicated, may hold values from -0.15625 to 0.15625
- gate_weight: bfloat16 [40, 1536, 512], P('tensor'), may hold values from -0.15625 to 0.15625
- up_weight: bfloat16 [40, 1536, 512], P('tensor'), may hold values from -0.15625 to 0.15625
- down_weight: bfloat16 [40, 512, 1536], P('tensor'), may hold values from -2 to 2
Outputs:
- output: bfloat16 [8192, 1536], P('dp')
- grad_tokens: float32 [8192, 1536], P('dp')
- grad_attn_gain: float32 [1536], P('dp')
- grad_query: float32 [1536, 1536], P('dp', 'tensor')
- grad_key: float32 [1536, 512], P('dp', 'tensor')
- grad_value: float32 [1536, 512], P('dp', 'tensor')
- grad_out: float32 [1536, 1536], P('tensor', 'dp')
- grad_ffn_gain: float32 [1536], P('dp')
- grad_router: float32 [1536, 40], P('dp')
- grad_gate: float32 [40, 1536, 512], P('tensor', 'dp')
- grad_up: float32 [40, 1536, 512], P('tensor', 'dp')
- grad_down: float32 [40, 512, 1536], P('tensor', 'dp')
The draws below stay inside these ranges and needn't reach their ends.
Inputs may be any that keep to these rules, and one draw needn't show every extreme that they name: `routes`: each token names 8 different experts, and every expert is named by some token; among the tokens of one packed sequence no expert is named more than 384 times, and in every draw some expert is named exactly 384 times within some sequence. `segment_ids`: ids never fall along a sequence; a document has 1 to 512 tokens, and one has exactly 512.
All inputs are finite; a program needn't handle non-finite values.
Results may differ from the reference program's by a relative error of at most 0.014.
Values sent between devices are 32-bit elements; how exact they have to be, the bound alone decides.
A program may use at most 448 MiB of HBM per device.

```python
import math
import jax
import jax.numpy as jnp
import numpy as np
from jax import lax

D = 1536
HQ = 24
KV = 8
HEAD = 64
E = 40
FF = 512
TOP = 8
SEQ = 1024
CAP = 384
SEQS = 8
TOKENS = 8192


def shard_levels(own_key, extent, cuts, low, top_value):
    loudness = 1.0
    for dim, blocks in cuts:
        draws = jax.random.uniform(jax.random.fold_in(jax.random.fold_in(own_key, 6), dim), (blocks,), jnp.float32, low / len(cuts), top_value / len(cuts))
        loudness = loudness * jnp.repeat(jnp.exp(draws), extent[dim] // blocks).reshape((-1,) + (1,) * (len(extent) - 1 - dim))
    return loudness


def split_up(count, total, reach, lean):
    weights = [(1 << 20) // math.isqrt(rank ** lean) + 1 for rank in range(2, count + 1)]
    rest, holding = total - reach - (count - 1), [1] * (count - 1)
    while rest > 0:
        movable = [i for i in range(count - 1) if holding[i] < reach]
        pool, left = sum([weights[i] for i in movable]), rest
        for i in movable:
            extra = min(reach - holding[i], max(1, left * weights[i] // pool), rest)
            holding[i] = holding[i] + extra
            rest = rest - extra
    return np.array([reach] + holding)


def ragged(rng, number_of, total, limit, skew):
    if number_of == 2:
        one = jax.random.randint(rng, (), max(1, total - limit), min(limit, total - 1) + 1)
        return jnp.stack([one, total - one])
    tallies = jnp.asarray(split_up(number_of, total, limit, skew), jnp.int32)
    twos = (number_of - 1) // 2
    donor, taker = tallies[1:1 + 2 * twos:2], tallies[2:2 + 2 * twos:2]
    room = jnp.minimum(donor - 1, limit - taker)
    moved = jax.random.randint(jax.random.fold_in(rng, 1), (twos,), 0, 1 << 20) % (room + 1)
    tallies = tallies.at[1:1 + 2 * twos:2].set(donor - moved).at[2:2 + 2 * twos:2].set(taker + moved)
    return tallies[jax.random.permutation(jax.random.fold_in(rng, 2), number_of)]


def deal_out(key, own, number, rows, number_of, top, bound, lean):
    ranking = jax.random.permutation(key, number_of)
    heavy_load, usual = load_shares(number_of, rows * top, bound, lean, True), load_shares(number_of, rows * top, bound, lean, False)
    places = jnp.arange(number_of)

    def named(tallies, rotation):
        used = int((tallies > 0).sum())
        fixed = max(1, used // 4)
        moved = fixed + (places - fixed + rotation * (used - fixed)) % max(1, number_of - fixed)
        return jnp.zeros((number_of,), jnp.int32).at[ranking[jnp.where(places < fixed, places, moved)]].set(jnp.asarray(tallies, jnp.int32))

    tallies = jnp.where(number % 4 == 0, named(heavy_load, number // 4), named(usual, number - number // 4 - 1))
    mixed = jax.random.permutation(jax.random.fold_in(own, 3), number_of)
    giver, sink = mixed[0:number_of // 2 * 2:2], mixed[1:number_of // 2 * 2:2]
    slack = jnp.minimum(tallies[giver] - 1, bound - tallies[sink]) // 2
    slack = jnp.where((giver == ranking[0]) | (sink == ranking[0]) | (tallies[sink] == 0), 0, jnp.maximum(slack, 0))
    moved = jax.random.randint(jax.random.fold_in(own, 4), (number_of // 2,), 0, 1 << 20) % (slack + 1)
    tallies = tallies.at[giver].add(-moved).at[sink].add(moved)
    members = jnp.searchsorted(jnp.cumsum(tallies), jnp.arange(rows * top), side="right").astype(jnp.int32)
    table = members.reshape(top, rows).T
    table = table[jax.random.permutation(jax.random.fold_in(own, 1), rows)]
    rotation = jax.random.randint(jax.random.fold_in(own, 2), (rows, 1), 0, top)
    return jnp.take_along_axis(table, (jnp.arange(top)[None, :] + rotation) % top, axis=1)


def load_shares(count, total, bound, lean, full):
    weights = [(1 << 20) // math.isqrt(grade ** lean) + 1 for grade in range(1, count + 1)]
    largest = bound if full else min(bound, max(-(-total // count), total * weights[0] // sum(weights)))
    least = 1 if total - largest >= count - 1 else 0
    counts, surplus = [largest] + [least] * (count - 1), total - largest - least * (count - 1)
    while surplus > 0:
        movable = [i for i in range(1, count) if counts[i] < largest] or [i for i in range(1, count) if counts[i] < bound]
        mass, budget = sum([weights[i] for i in movable]), surplus
        for i in movable:
            more = min(bound - counts[i], max(1, budget * weights[i] // mass), surplus)
            counts[i] = counts[i] + more
            surplus = surplus - more
    return np.array(counts)


def centred(stream_key, extent, width, most, cuts=(), kind=jnp.bfloat16):
    entries = jax.random.normal(stream_key, extent, jnp.float32) * width
    if len(cuts) > 0:
        entries = shard_levels(stream_key, extent, cuts, -0.22, 0.18) * entries
    return jnp.clip(entries, min=-most, max=most).astype(kind)


def setup_inputs(seed: int = 0) -> dict:
    key_list = jax.random.split(jax.random.key(seed), 15)
    tokens = centred(key_list[0], (TOKENS, D), 1.0, 6.0, ((0, 8),))
    cotangent = centred(key_list[1], (TOKENS, D), 1.0, 6.0, ((0, 8),))
    segment_ids = jax.vmap(lambda own: jnp.searchsorted(jnp.cumsum(ragged(own, 3, SEQ, SEQ // 2, 0)), jnp.arange(SEQ), side="right"))(jax.random.split(key_list[2], SEQS)).reshape((SEQS, SEQ)).astype(jnp.int32)
    routes_keys = jax.random.split(jax.random.fold_in(key_list[3], 1), TOKENS // SEQ)
    routes_turns = jax.random.permutation(jax.random.fold_in(key_list[3], 3), TOKENS // SEQ)
    routes = jax.vmap(lambda own, number: deal_out(jax.random.fold_in(key_list[3], 2), own, number, SEQ, E, TOP, CAP, 1))(routes_keys, routes_turns).reshape((TOKENS, TOP))
    attn_gain = jnp.clip(1.0 + 0.1 * jax.random.normal(key_list[4], (D,), jnp.float32), 0.5, 1.5)
    query_weight = centred(key_list[5], (D, HQ * HEAD), D ** -0.5, 0.15625, ((1, 4),))
    key_weight = centred(key_list[6], (D, KV * HEAD), D ** -0.5, 0.15625, ((1, 4),))
    value_weight = centred(key_list[7], (D, KV * HEAD), D ** -0.5, 0.15625, ((1, 4),))
    out_weight = centred(key_list[8], (HQ * HEAD, D), (max(1, D // 384)) ** -0.5, 3.0, ((0, 4),))
    ffn_gain = jnp.clip(1.0 + 0.1 * jax.random.normal(key_list[9], (D,), jnp.float32), 0.5, 1.5)
    router_weight = centred(key_list[10], (D, E), D ** -0.5, 0.15625)
    gate_weight = centred(key_list[11], (E, D, FF), D ** -0.5, 0.15625, ((0, 4),))
    up_weight = centred(key_list[12], (E, D, FF), D ** -0.5, 0.15625, ((0, 4),))
    down_weight = centred(key_list[13], (E, FF, D), (max(1, FF // 64)) ** -0.5, 2.0, ((0, 4),))
    return dict(tokens=tokens, cotangent=cotangent, segment_ids=segment_ids, routes=routes, attn_gain=attn_gain, query_weight=query_weight, key_weight=key_weight, value_weight=value_weight, out_weight=out_weight, ffn_gain=ffn_gain, router_weight=router_weight, gate_weight=gate_weight, up_weight=up_weight, down_weight=down_weight)


EPSILON = 1e-06
RESIDUAL = 0.22
ATTN_SCALE = 0.015625
ROPE_BASE = 10000.0
MASKED = -1e+30

def doc_positions(segment):
    places = jnp.arange(segment.shape[0], dtype=jnp.int32)
    starts_here = jnp.concatenate([jnp.ones((1,), dtype=jnp.bool_), segment[1:] != segment[:-1]])
    opening = lax.cummax(jnp.where(starts_here, places, jnp.zeros_like(places)), axis=0)
    return places - opening

def rope_tables(segment, head_size):
    halfway = head_size // 2
    spread = jnp.arange(halfway, dtype=jnp.float32) * (2.0 / head_size)
    inverse = jnp.power(ROPE_BASE, -spread)
    angles = doc_positions(segment).astype(jnp.float32)[:, None] * inverse[None, :]
    cosine = jnp.cos(angles)
    sine_table = jnp.sin(angles)
    return (jnp.concatenate([cosine, cosine], 1)[:, None, :], jnp.concatenate([sine_table, sine_table], 1)[:, None, :])

def rotate_half(vector):
    halfway = vector.shape[-1] // 2
    return jnp.concatenate([-vector[..., halfway:], vector[..., :halfway]], -1)

def rotate_back(vector):
    halfway = vector.shape[-1] // 2
    return jnp.concatenate([vector[..., halfway:], -vector[..., :halfway]], -1)

def rope_apply(vector, cosine, sine_table):
    return vector * cosine + rotate_half(vector) * sine_table

def rope_undo(gradient, cosine, sine_table):
    return gradient * cosine + rotate_back(gradient * sine_table)

def rms_forward(hidden, gain):
    recip = lax.rsqrt(lax.optimization_barrier(jnp.mean(hidden * hidden, axis=-1, keepdims=True)) + EPSILON)
    unit = hidden * recip
    return (unit * gain, unit, recip)

def rms_backward(gradient, unit, recip, gain):
    gain_grad = lax.optimization_barrier(jnp.sum(gradient * unit, axis=0))
    scaled = gradient * gain
    return (recip * (scaled - unit * lax.optimization_barrier(jnp.mean(scaled * unit, axis=-1, keepdims=True))), gain_grad)

def attend_scores(queries, keys_wide, allowed):
    scores = ATTN_SCALE * jnp.einsum('qhe,khe->hqk', queries.astype(jnp.float32), keys_wide.astype(jnp.float32))
    return jnp.where(allowed[None], scores, MASKED)

def route_slots(route_rows, expert_ids, capacity):
    length = route_rows.shape[0]
    count_experts = expert_ids.shape[0]
    picked = lax.optimization_barrier(jnp.sum((route_rows[:, :, None] == expert_ids[None, None, :]).astype(jnp.int32), axis=1)).astype(jnp.int32)
    before = (jnp.cumsum(picked, axis=0).astype(jnp.int32) - picked).astype(jnp.int32)
    columns = jnp.arange(count_experts, dtype=jnp.int32)[None, :]
    target = jnp.where(picked > 0, columns * capacity + before, count_experts * capacity).astype(jnp.int32)
    places = jnp.broadcast_to(jnp.arange(length, dtype=jnp.int32)[:, None], target.shape)
    slots = jnp.zeros((count_experts * capacity,), jnp.int32).at[target.reshape(-1)].set(places.reshape(-1), mode='drop')
    filled = lax.optimization_barrier(jnp.sum(picked, axis=0)).astype(jnp.int32)
    valid = (jnp.arange(capacity, dtype=jnp.int32)[None, :] < filled[:, None]).astype(jnp.float32)
    return (slots.reshape(count_experts, capacity), valid, picked > 0)

def one_sequence(token_rows, cot_rows, segment, route_rows, weights):
    attn_gain, query_weight, key_weight, value_weight, out_weight, ffn_gain, router_weight, gate_weight, up_weight, down_weight = weights
    length = token_rows.shape[0]
    group_size = HQ // KV
    cosine, sine_table = rope_tables(segment, HEAD)
    places = jnp.arange(length, dtype=jnp.int32)
    allowed = (segment[:, None] == segment[None, :]) & (places[:, None] >= places[None, :])
    hidden_in = token_rows.astype(jnp.float32)
    normed, unit_one, recip_one = rms_forward(hidden_in, attn_gain)
    normed_b = normed.astype(jnp.bfloat16)
    queries = rope_apply(jnp.dot(normed_b, query_weight, preferred_element_type=jnp.float32).reshape(length, HQ, HEAD), cosine, sine_table).astype(jnp.bfloat16)
    keys_rot = rope_apply(jnp.dot(normed_b, key_weight, preferred_element_type=jnp.float32).reshape(length, KV, HEAD), cosine, sine_table).astype(jnp.bfloat16)
    values = jnp.dot(normed_b, value_weight, preferred_element_type=jnp.float32).astype(jnp.bfloat16).reshape(length, KV, HEAD)
    keys_wide = jnp.repeat(keys_rot, group_size, axis=1)
    values_wide = jnp.repeat(values, group_size, axis=1)
    scores = attend_scores(queries, keys_wide, allowed)
    logsum = jnp.log(lax.optimization_barrier(jnp.sum(jnp.exp(scores), axis=-1, keepdims=True)))
    prob_b = jnp.exp(scores - logsum).astype(jnp.bfloat16)
    attended = jnp.einsum('hqk,khe->qhe', prob_b.astype(jnp.float32), values_wide.astype(jnp.float32)).astype(jnp.bfloat16)
    attended_flat = attended.reshape(length, HQ * HEAD)
    attn_out = jnp.dot(attended_flat, out_weight, preferred_element_type=jnp.float32)
    middle = hidden_in + RESIDUAL * attn_out
    normed_two, unit_two, recip_two = rms_forward(middle, ffn_gain)
    normed_two_b = normed_two.astype(jnp.bfloat16)
    logits = jnp.dot(normed_two_b, router_weight, preferred_element_type=jnp.float32)
    expert_ids = jnp.arange(E, dtype=jnp.int32)
    slot_token, valid, chosen = route_slots(route_rows, expert_ids, CAP)
    raised = jnp.where(chosen, jnp.exp(logits), 0.0)
    gate_probs = raised / lax.optimization_barrier(jnp.sum(raised, axis=-1, keepdims=True))
    gate_slots = jnp.take_along_axis(jnp.transpose(gate_probs), slot_token, axis=1) * valid

    def expert_forward(running, pieces):
        gate_slice, up_slice, down_slice, slot_row, gate_slot = pieces
        rows_in = normed_two_b[slot_row]
        gate_input = jnp.dot(rows_in, gate_slice, preferred_element_type=jnp.float32)
        up_input = jnp.dot(rows_in, up_slice, preferred_element_type=jnp.float32)
        activation = (gate_input * jax.nn.sigmoid(gate_input) * up_input * gate_slot[:, None]).astype(jnp.bfloat16)
        return (running.at[slot_row].add(jnp.dot(activation, down_slice, preferred_element_type=jnp.float32)), None)
    moe_out, unused = lax.scan(expert_forward, jnp.zeros((length, D), jnp.float32), (gate_weight, up_weight, down_weight, slot_token, gate_slots))
    output = (middle + RESIDUAL * moe_out).astype(jnp.bfloat16)
    grad_moe_b = (RESIDUAL * cot_rows.astype(jnp.float32)).astype(jnp.bfloat16)

    def expert_backward(running, pieces):
        gate_slice, up_slice, down_slice, slot_row, gate_slot, valid_row = pieces
        rows_in = normed_two_b[slot_row]
        grad_rows = grad_moe_b[slot_row]
        gate_input = jnp.dot(rows_in, gate_slice, preferred_element_type=jnp.float32)
        up_input = jnp.dot(rows_in, up_slice, preferred_element_type=jnp.float32)
        sigmoid_val = jax.nn.sigmoid(gate_input)
        silu_out = gate_input * sigmoid_val
        hidden = silu_out * up_input
        activation = (hidden * gate_slot[:, None]).astype(jnp.bfloat16)
        grad_down = jnp.dot(activation.T, grad_rows, preferred_element_type=jnp.float32)
        grad_act = jnp.dot(grad_rows, down_slice.T, preferred_element_type=jnp.float32)
        grad_column = lax.optimization_barrier(jnp.sum(grad_act * hidden, axis=-1)) * valid_row
        grad_hidden = grad_act * gate_slot[:, None]
        grad_gate_in = (grad_hidden * up_input * sigmoid_val * (1.0 + gate_input * (1.0 - sigmoid_val))).astype(jnp.bfloat16)
        grad_up_in = (grad_hidden * silu_out).astype(jnp.bfloat16)
        grad_gate = jnp.dot(rows_in.T, grad_gate_in, preferred_element_type=jnp.float32)
        grad_up = jnp.dot(rows_in.T, grad_up_in, preferred_element_type=jnp.float32)
        grad_rows_in = jnp.dot(grad_gate_in, gate_slice.T, preferred_element_type=jnp.float32) + jnp.dot(grad_up_in, up_slice.T, preferred_element_type=jnp.float32)
        return (running.at[slot_row].add(grad_rows_in), (grad_gate, grad_up, grad_down, grad_column))
    grad_normed_sum, (grad_gate, grad_up, grad_down, grad_columns) = lax.scan(expert_backward, jnp.zeros((length, D), jnp.float32), (gate_weight, up_weight, down_weight, slot_token, gate_slots, valid))
    grad_gates = jnp.zeros((length, E), jnp.float32).at[slot_token, expert_ids[:, None]].add(grad_columns)
    weighted = lax.optimization_barrier(jnp.sum(gate_probs * grad_gates, axis=-1, keepdims=True))
    grad_logits_b = (gate_probs * (grad_gates - weighted)).astype(jnp.bfloat16)
    grad_router = jnp.dot(normed_two_b.T, grad_logits_b, preferred_element_type=jnp.float32)
    grad_normed_two = grad_normed_sum + jnp.dot(grad_logits_b, router_weight.T, preferred_element_type=jnp.float32)
    grad_from_norm, grad_ffn_gain = rms_backward(grad_normed_two, unit_two, recip_two, ffn_gain)
    grad_middle = cot_rows.astype(jnp.float32) + grad_from_norm
    grad_branch_b = (RESIDUAL * grad_middle).astype(jnp.bfloat16)
    grad_out = jnp.dot(attended_flat.T, grad_branch_b, preferred_element_type=jnp.float32)
    grad_attended = jnp.dot(grad_branch_b, out_weight.T, preferred_element_type=jnp.float32).astype(jnp.bfloat16).reshape(length, HQ, HEAD)
    probs = jnp.exp(scores - logsum)
    row_dot = jnp.transpose(lax.optimization_barrier(jnp.sum(grad_attended.astype(jnp.float32) * attended.astype(jnp.float32), axis=-1)))[:, :, None]
    grad_values_wide = jnp.einsum('hqk,qhe->khe', prob_b.astype(jnp.float32), grad_attended.astype(jnp.float32))
    grad_probs = jnp.einsum('qhe,khe->hqk', grad_attended.astype(jnp.float32), values_wide.astype(jnp.float32))
    grad_scores = (ATTN_SCALE * probs * (grad_probs - row_dot)).astype(jnp.bfloat16)
    grad_queries_wide = jnp.einsum('hqk,khe->qhe', grad_scores.astype(jnp.float32), keys_wide.astype(jnp.float32))
    grad_keys_wide = jnp.einsum('hqk,qhe->khe', grad_scores.astype(jnp.float32), queries.astype(jnp.float32))
    grad_queries_b = rope_undo(grad_queries_wide, cosine, sine_table).astype(jnp.bfloat16).reshape(length, HQ * HEAD)
    grad_keys_b = rope_undo(lax.optimization_barrier(jnp.sum(grad_keys_wide.reshape(length, KV, group_size, HEAD), axis=2)), cosine, sine_table).astype(jnp.bfloat16).reshape(length, KV * HEAD)
    grad_values_b = lax.optimization_barrier(jnp.sum(grad_values_wide.reshape(length, KV, group_size, HEAD), axis=2)).astype(jnp.bfloat16).reshape(length, KV * HEAD)
    grad_query = jnp.dot(normed_b.T, grad_queries_b, preferred_element_type=jnp.float32)
    grad_key = jnp.dot(normed_b.T, grad_keys_b, preferred_element_type=jnp.float32)
    grad_value = jnp.dot(normed_b.T, grad_values_b, preferred_element_type=jnp.float32)
    grad_normed = jnp.dot(grad_queries_b, query_weight.T, preferred_element_type=jnp.float32) + jnp.dot(grad_keys_b, key_weight.T, preferred_element_type=jnp.float32) + jnp.dot(grad_values_b, value_weight.T, preferred_element_type=jnp.float32)
    grad_from_first, grad_attn_gain = rms_backward(grad_normed, unit_one, recip_one, attn_gain)
    grad_tokens = grad_middle + grad_from_first
    grads = (grad_attn_gain, grad_query, grad_key, grad_value, grad_out, grad_ffn_gain, grad_router, grad_gate, grad_up, grad_down)
    return (output, grad_tokens, grads)

def reference(tokens, cotangent, segment_ids, routes, attn_gain, query_weight, key_weight, value_weight, out_weight, ffn_gain, router_weight, gate_weight, up_weight, down_weight):
    sequences = segment_ids.shape[0]
    length = segment_ids.shape[1]
    weights = (attn_gain, query_weight, key_weight, value_weight, out_weight, ffn_gain, router_weight, gate_weight, up_weight, down_weight)

    def per_sequence(totals, pieces):
        token_rows, cot_rows, segment, route_rows = pieces
        output, grad_tokens, grads = one_sequence(token_rows, cot_rows, segment, route_rows, weights)
        totals = tuple((running + update for running, update in zip(totals, grads)))
        return (totals, (output, grad_tokens))
    zero_grads = tuple((jnp.zeros(weight.shape, jnp.float32) for weight in weights))
    totals, (outputs, grad_rows) = lax.scan(per_sequence, zero_grads, (tokens.reshape(sequences, length, D), cotangent.reshape(sequences, length, D), segment_ids, routes.reshape(sequences, length, TOP)))
    return (outputs.reshape(sequences * length, D), grad_rows.reshape(sequences * length, D), totals[0], totals[1], totals[2], totals[3], totals[4], totals[5], totals[6], totals[7], totals[8], totals[9])
```

```python
import functools

import jax
import jax.numpy as jnp
from jax import lax
from jax.experimental import pallas as pl
from jax.experimental.pallas import tpu as pltpu
from jax.sharding import PartitionSpec as P

MESH = pl.DeviceIdType.MESH

HEAD = 64
CAP = 384


EPSILON = 1e-06
RESIDUAL = 0.22
ATTN_SCALE = 0.015625
ROPE_BASE = 10000.0
MASKED = -1e30


def left_inner(first, second):
    return lax.dot_general(
        first, second, (((0,), (0,)), ((), ())), preferred_element_type=jnp.float32
    )


def right_inner(first, second):
    return lax.dot_general(
        first, second, (((1,), (1,)), ((), ())), preferred_element_type=jnp.float32
    )


def doc_positions(segment):
    places = jnp.arange(segment.shape[0], dtype=jnp.int32)
    opening = jnp.sum((segment[None, :] < segment[:, None]).astype(jnp.int32), axis=1)
    return places - opening


def rope_tables(segment, head_size):
    halfway = head_size // 2
    spread = jnp.arange(halfway, dtype=jnp.float32) * (2.0 / head_size)
    inverse = jnp.power(ROPE_BASE, -spread)
    angles = doc_positions(segment).astype(jnp.float32)[:, None] * inverse[None, :]
    cosine = jnp.cos(angles)
    sine_table = jnp.sin(angles)
    return (
        jnp.concatenate([cosine, cosine], 1)[:, None, :],
        jnp.concatenate([sine_table, sine_table], 1)[:, None, :],
    )


def rotate_half(vector):
    halfway = vector.shape[-1] // 2
    return jnp.concatenate([-vector[..., halfway:], vector[..., :halfway]], -1)


def rotate_back(vector):
    halfway = vector.shape[-1] // 2
    return jnp.concatenate([vector[..., halfway:], -vector[..., :halfway]], -1)


def rope_apply(vector, cosine, sine_table):
    return vector * cosine + rotate_half(vector) * sine_table


def rope_undo(gradient, cosine, sine_table):
    return gradient * cosine + rotate_back(gradient * sine_table)


def rms_forward(hidden, gain):
    recip = lax.rsqrt(jnp.mean(hidden * hidden, axis=-1, keepdims=True) + EPSILON)
    unit = hidden * recip
    return (unit * gain, unit, recip)


def rms_backward(gradient, unit, recip, gain):
    gain_grad = jnp.sum(gradient * unit, axis=0)
    scaled = gradient * gain
    return (recip * (scaled - unit * jnp.mean(scaled * unit, axis=-1, keepdims=True)), gain_grad)


def slot_places(picked):
    length = picked.shape[1]
    tokens = jnp.arange(length, dtype=jnp.int32)
    earlier = (tokens[:, None] < tokens[None, :]).astype(jnp.bfloat16)
    before = jnp.dot(picked.astype(jnp.bfloat16), earlier, preferred_element_type=jnp.float32)
    return jnp.where(picked > 0, before.astype(jnp.int32), -1)


def block_mask(segment, first_row, block_rows):
    rows = first_row + jnp.arange(block_rows, dtype=jnp.int32)
    row_segment = lax.dynamic_slice_in_dim(segment, first_row, block_rows)
    columns = jnp.arange(segment.shape[0], dtype=jnp.int32)
    return (row_segment[:, None] == segment[None, :]) & (rows[:, None] >= columns[None, :])


def attend_scores(queries, keys_wide, allowed):
    scores = ATTN_SCALE * jnp.einsum(
        "qhe,khe->hqk", queries, keys_wide, preferred_element_type=jnp.float32
    )
    return jnp.where(allowed[None], scores, MASKED)


def attend_forward(queries, keys_wide, values_wide, allowed):
    scores = attend_scores(queries, keys_wide, allowed)
    logsum = jnp.log(jnp.sum(jnp.exp(scores), axis=-1, keepdims=True))
    prob_b = jnp.exp(scores - logsum).astype(jnp.bfloat16)
    attended = jnp.einsum(
        "hqk,khe->qhe", prob_b, values_wide, preferred_element_type=jnp.float32
    ).astype(jnp.bfloat16)
    return (attended, logsum)


def attend_backward(queries, keys_wide, values_wide, allowed, logsum, attended, grad_attended):
    scores = attend_scores(queries, keys_wide, allowed)
    probs = jnp.exp(scores - logsum)
    prob_b = probs.astype(jnp.bfloat16)
    row_dot = jnp.transpose(
        jnp.sum(grad_attended.astype(jnp.float32) * attended.astype(jnp.float32), axis=-1)
    )[:, :, None]
    grad_values = jnp.einsum(
        "hqk,qhe->khe", prob_b, grad_attended, preferred_element_type=jnp.float32
    )
    grad_probs = jnp.einsum(
        "qhe,khe->hqk", grad_attended, values_wide, preferred_element_type=jnp.float32
    )
    grad_scores = (ATTN_SCALE * probs * (grad_probs - row_dot)).astype(jnp.bfloat16)
    grad_queries = jnp.einsum(
        "hqk,khe->qhe", grad_scores, keys_wide, preferred_element_type=jnp.float32
    )
    grad_keys = jnp.einsum("hqk,qhe->khe", grad_scores, queries, preferred_element_type=jnp.float32)
    return (grad_queries, grad_keys, grad_values)


STEPS = 32
LAG = 2
GATE_ROWS = 512


def line_sum_kernel(n, count, *refs):
    xs, outs = refs[:count], refs[count : 2 * count]
    lows, highs = refs[2 * count : 3 * count], refs[3 * count : 4 * count]
    low_recv, high_recv, total_recv, up_send, low_send, high_send = refs[4 * count :]
    me = lax.axis_index("tensor")
    root = n // 2
    has_low, has_high = me > 0, me < n - 1
    barrier = pltpu.get_barrier_semaphore()

    @pl.when(has_low)
    def _():
        pl.semaphore_signal(barrier, inc=1, device_id={"tensor": me - 1}, device_id_type=MESH)

    @pl.when(has_high)
    def _():
        pl.semaphore_signal(barrier, inc=1, device_id={"tensor": me + 1}, device_id_type=MESH)

    pl.semaphore_wait(barrier, has_low.astype(jnp.int32) + has_high.astype(jnp.int32))

    def piece(ref, c):
        rows = ref.shape[0] // STEPS
        return ref.at[pl.ds(pl.multiple_of(c * rows, rows), rows), :]

    def copies(sources, targets, c, send, recv, to):
        return [
            pltpu.make_async_remote_copy(
                src_ref=piece(source, c),
                dst_ref=piece(target, c),
                send_sem=send.at[i, c],
                recv_sem=recv.at[i, c],
                device_id={"tensor": to},
                device_id_type=MESH,
            )
            for i, (source, target) in enumerate(zip(sources, targets))
        ]

    def start(sources, targets, c, send, recv, to):
        for copy in copies(sources, targets, c, send, recv, to):
            copy.start()

    def arrived(targets, c, send, recv):
        for copy in copies(targets, targets, c, send, recv, me):
            copy.wait_recv()

    def reduce_step(c):
        for side, inner, held, recv, to in (
            (me < root, has_low, lows, low_recv, me + 1),
            (me > root, has_high, highs, high_recv, me - 1),
        ):

            @pl.when(side & inner)
            def _():
                arrived(held, c, up_send, recv)
                for x, h in zip(xs, held):
                    piece(h, c)[...] += piece(x, c)[...]
                start(held, held, c, up_send, recv, to)

            @pl.when(side & jnp.logical_not(inner))
            def _():
                start(xs, held, c, up_send, recv, to)

        @pl.when(me == root)
        def _():
            arrived(lows, c, up_send, low_recv)
            if root < n - 1:
                arrived(highs, c, up_send, high_recv)
            for x, low, high, out in zip(xs, lows, highs, outs):
                total = piece(x, c)[...] + piece(low, c)[...]
                if root < n - 1:
                    total += piece(high, c)[...]
                piece(out, c)[...] = total
            start(outs, outs, c, low_send, total_recv, me - 1)
            if root < n - 1:
                start(outs, outs, c, high_send, total_recv, me + 1)

    def total_step(c):
        @pl.when(me != root)
        def _():
            arrived(outs, c, low_send, total_recv)

        @pl.when((me < root) & has_low)
        def _():
            start(outs, outs, c, low_send, total_recv, me - 1)

        @pl.when((me > root) & has_high)
        def _():
            start(outs, outs, c, high_send, total_recv, me + 1)

    lag = jnp.where(has_low & has_high, LAG, STEPS)

    def step(t, carry):
        @pl.when(t < STEPS)
        def _():
            reduce_step(t)

        @pl.when((t >= lag) & (t - lag < STEPS))
        def _():
            total_step(t - lag)

        return carry

    lax.fori_loop(0, 2 * STEPS, step, 0)

    def drain(c, carry):
        for condition, send in (
            (me != root, up_send),
            ((me <= root) & has_low, low_send),
            ((me >= root) & has_high, high_send),
        ):

            @pl.when(condition)
            def _():
                for copy in copies(xs, lows, c, send, low_recv, me):
                    copy.wait_send()

        return carry

    lax.fori_loop(0, STEPS, drain, 0)


def line_sum(x, extra, n, name):
    arrays = [x] if extra is None else [x, extra]
    count = len(arrays)
    shapes = [jax.ShapeDtypeStruct(array.shape, jnp.float32) for array in arrays]
    size = sum(array.size for array in arrays)
    results = pl.pallas_call(
        functools.partial(line_sum_kernel, n, count),
        out_shape=shapes,
        in_specs=[pl.BlockSpec(memory_space=pltpu.VMEM)] * count,
        out_specs=[pl.BlockSpec(memory_space=pltpu.VMEM)] * count,
        scratch_shapes=[pltpu.VMEM(array.shape, jnp.float32) for array in arrays * 2]
        + [pltpu.SemaphoreType.DMA((count, STEPS))] * 6,
        compiler_params=pltpu.CompilerParams(
            collective_id=name, has_side_effects=True, vmem_limit_bytes=40 << 20
        ),
        cost_estimate=pl.CostEstimate(
            flops=3 * size, bytes_accessed=8 * size, transcendentals=0
        ),
    )(*arrays)
    return (results[0], None) if extra is None else tuple(results)


def expert_kernel(
    first,
    chained,
    count_ref,
    place_ref,
    gate_ref,
    normed_ref,
    grad_ref,
    gate_w,
    up_w,
    down_w,
    *refs,
):
    if chained:
        moe_in, back_in = refs[:2]
        refs = refs[2:]
    both_out, down_out, moe_out, back_out, gates_out = refs[:5]
    rows_ref, grads_ref, moe_rows, back_rows, slot_gate, slot_grad, sems = refs[5:]
    expert, half = pl.program_id(0), pl.program_id(1)
    halves = pl.num_programs(1)
    filled = count_ref[first + expert]
    length = normed_ref.shape[0]
    block = gate_w.shape[2]
    started = (expert == 0) & (half == 0)

    if chained:
        copy_moe = pltpu.make_async_copy(moe_in, moe_out, sems.at[0])
        copy_back = pltpu.make_async_copy(back_in, back_out, sems.at[1])

        @pl.when(started)
        def _():
            copy_moe.start()
            copy_back.start()

        @pl.when((expert == 0) & (half == halves - 1))
        def _():
            copy_moe.wait()
            copy_back.wait()

    else:

        @pl.when(started)
        def _():
            moe_out[...] = jnp.zeros_like(moe_out)
            back_out[...] = jnp.zeros_like(back_out)

    def run(rows):
        mask = lax.broadcasted_iota(jnp.int32, (rows, length), 0) == place_ref[0]

        @pl.when(half == 0)
        def _():
            picks = jnp.where(mask, 1.0, 0.0).astype(jnp.bfloat16)
            rows_ref[:rows] = jnp.dot(
                picks, normed_ref[...], preferred_element_type=jnp.float32
            ).astype(jnp.bfloat16)
            grads_ref[:rows] = jnp.dot(
                picks, grad_ref[...], preferred_element_type=jnp.float32
            ).astype(jnp.bfloat16)
            slot_gate[:rows] = jnp.broadcast_to(
                jnp.sum(jnp.where(mask, gate_ref[0], 0.0), axis=1, keepdims=True), (rows, 128)
            )

        rows_in = rows_ref[:rows]
        grad_rows = grads_ref[:rows]
        gate = slot_gate[:rows, :1]
        gate_input = jnp.dot(rows_in, gate_w[0], preferred_element_type=jnp.float32)
        up_input = jnp.dot(rows_in, up_w[0], preferred_element_type=jnp.float32)
        grad_act = right_inner(grad_rows, down_w[0])
        sigmoid_val = jax.nn.sigmoid(gate_input)
        silu_out = gate_input * sigmoid_val
        hidden = silu_out * up_input
        activation = (hidden * gate).astype(jnp.bfloat16)
        column = jnp.sum(grad_act * hidden, axis=1, keepdims=True)
        grad_hidden = grad_act * gate
        grad_gate_in = (
            grad_hidden * up_input * sigmoid_val * (1.0 + gate_input * (1.0 - sigmoid_val))
        ).astype(jnp.bfloat16)
        grad_up_in = (grad_hidden * silu_out).astype(jnp.bfloat16)
        down_out[0] = left_inner(activation, grad_rows)
        grads = left_inner(rows_in, jnp.concatenate([grad_gate_in, grad_up_in], 1))
        both_out[0, 0] = grads[:, :block]
        both_out[0, 1] = grads[:, block:]
        moe = jnp.dot(activation, down_w[0], preferred_element_type=jnp.float32)
        back = right_inner(grad_gate_in, gate_w[0]) + right_inner(grad_up_in, up_w[0])

        @pl.when(half == 0)
        def _():
            moe_rows[:rows] = moe
            back_rows[:rows] = back
            slot_grad[:rows] = jnp.broadcast_to(column, (rows, 128))

        @pl.when((half > 0) & (half < halves - 1))
        def _():
            moe_rows[:rows] += moe
            back_rows[:rows] += back
            slot_grad[:rows] += jnp.broadcast_to(column, (rows, 128))

        @pl.when(half == halves - 1)
        def _():
            picks = jnp.where(mask, 1.0, 0.0).astype(jnp.bfloat16)
            moe_out[...] += left_inner(picks, (moe_rows[:rows] + moe).astype(jnp.bfloat16))
            back_out[...] += left_inner(picks, (back_rows[:rows] + back).astype(jnp.bfloat16))
            total = slot_grad[:rows, :1] + column
            gates_out[0] = jnp.sum(jnp.where(mask, total, 0.0), axis=0, keepdims=True)

    sizes = (128, 256, CAP)
    for low, rows in zip((-1,) + sizes[:-1], sizes):
        pl.when((filled > low) & (filled <= rows))(functools.partial(run, rows))


def expert_stage(first, last, counts, places, gate_rows, normed_b, grad_b, gate_w, up_w, down_w, sums):
    number = last - first
    length, width = normed_b.shape
    hidden = gate_w.shape[2]
    block = 256
    halves = hidden // block
    experts = places.shape[0]
    chained = sums is not None
    whole = lambda e, h, c: (0, 0)
    row_spec = pl.BlockSpec((1, 1, length), lambda e, h, c: (first + e, 0, 0))
    once = pl.Buffered(1)
    in_specs = [
        row_spec,
        row_spec,
        pl.BlockSpec((length, width), whole, pipeline_mode=once),
        pl.BlockSpec((length, width), whole, pipeline_mode=once),
        pl.BlockSpec((1, width, block), lambda e, h, c: (first + e, 0, h)),
        pl.BlockSpec((1, width, block), lambda e, h, c: (first + e, 0, h)),
        pl.BlockSpec((1, block, width), lambda e, h, c: (first + e, h, 0)),
    ]
    args = [
        counts,
        places.reshape(experts, 1, length),
        gate_rows.reshape(experts, 1, length),
        normed_b,
        grad_b,
        gate_w,
        up_w,
        down_w,
    ]
    if chained:
        in_specs += [pl.BlockSpec(memory_space=pl.ANY)] * 2
        args += [sums[0], sums[1]]
    both, down, moe, back, gates = pl.pallas_call(
        functools.partial(expert_kernel, first, chained),
        out_shape=[
            jax.ShapeDtypeStruct((number, 2, width, hidden), jnp.float32),
            jax.ShapeDtypeStruct((number, hidden, width), jnp.float32),
            jax.ShapeDtypeStruct((length, width), jnp.float32),
            jax.ShapeDtypeStruct((length, width), jnp.float32),
            jax.ShapeDtypeStruct((number, 1, length), jnp.float32),
        ],
        grid_spec=pltpu.PrefetchScalarGridSpec(
            num_scalar_prefetch=1,
            grid=(number, halves),
            in_specs=in_specs,
            out_specs=[
                pl.BlockSpec((1, 2, width, block), lambda e, h, c: (e, 0, 0, h)),
                pl.BlockSpec((1, block, width), lambda e, h, c: (e, h, 0)),
                pl.BlockSpec((length, width), whole, pipeline_mode=once),
                pl.BlockSpec((length, width), whole, pipeline_mode=once),
                pl.BlockSpec((1, 1, length), lambda e, h, c: (e, 0, 0)),
            ],
            scratch_shapes=[
                pltpu.VMEM((CAP, width), jnp.bfloat16),
                pltpu.VMEM((CAP, width), jnp.bfloat16),
                pltpu.VMEM((CAP, width), jnp.float32),
                pltpu.VMEM((CAP, width), jnp.float32),
                pltpu.VMEM((CAP, 128), jnp.float32),
                pltpu.VMEM((CAP, 128), jnp.float32),
                pltpu.SemaphoreType.DMA((2,)),
            ],
        ),
        compiler_params=pltpu.CompilerParams(
            dimension_semantics=("arbitrary", "arbitrary"), vmem_limit_bytes=60 << 20
        ),
        cost_estimate=pl.CostEstimate(
            flops=number * 8 * 10**9, bytes_accessed=number * 14 * 10**6, transcendentals=0
        ),
    )(*args)
    return ((both, down), (moe, back, gates))


def on_device(
    ring,
    tokens,
    cotangent,
    segment_ids,
    routes,
    attn_gain,
    query_weight,
    key_weight,
    value_weight,
    out_weight,
    ffn_gain,
    router_weight,
    gate_weight,
    up_weight,
    down_weight,
):
    length = tokens.shape[0]
    width = tokens.shape[1]
    segment = segment_ids[0]
    heads_local = query_weight.shape[1] // HEAD
    kv_local = key_weight.shape[1] // HEAD
    group_size = heads_local // kv_local
    experts_all = router_weight.shape[1]
    experts_local = gate_weight.shape[0]
    cosine, sine_table = rope_tables(segment, HEAD)
    hidden_in = tokens.astype(jnp.float32)
    normed, unit_one, recip_one = rms_forward(hidden_in, attn_gain)
    normed_b = normed.astype(jnp.bfloat16)
    queries = rope_apply(
        jnp.dot(normed_b, query_weight, preferred_element_type=jnp.float32).reshape(
            length, heads_local, HEAD
        ),
        cosine,
        sine_table,
    ).astype(jnp.bfloat16)
    keys_rot = rope_apply(
        jnp.dot(normed_b, key_weight, preferred_element_type=jnp.float32).reshape(
            length, kv_local, HEAD
        ),
        cosine,
        sine_table,
    ).astype(jnp.bfloat16)
    values = (
        jnp.dot(normed_b, value_weight, preferred_element_type=jnp.float32)
        .astype(jnp.bfloat16)
        .reshape(length, kv_local, HEAD)
    )
    keys_wide = jnp.repeat(keys_rot, group_size, axis=1)
    values_wide = jnp.repeat(values, group_size, axis=1)
    block_rows = min(512, length)
    count_blocks = length // block_rows
    first_rows = jnp.arange(count_blocks, dtype=jnp.int32) * block_rows
    query_blocks = queries.reshape(count_blocks, block_rows, heads_local, HEAD)

    def forward_block(pieces):
        query_part, first_row = pieces
        return attend_forward(
            query_part, keys_wide, values_wide, block_mask(segment, first_row, block_rows)
        )

    attended, logsum = lax.map(forward_block, (query_blocks, first_rows))
    attended_flat = attended.reshape(length, heads_local * HEAD)
    attn_out, unused = line_sum(
        jnp.dot(attended_flat, out_weight, preferred_element_type=jnp.float32), None, ring, 1
    )
    middle = hidden_in + RESIDUAL * attn_out
    normed_two, unit_two, recip_two = rms_forward(middle, ffn_gain)
    normed_two_b = normed_two.astype(jnp.bfloat16)
    logits = jnp.dot(normed_two_b, router_weight, preferred_element_type=jnp.float32)
    all_ids = jnp.arange(experts_all, dtype=jnp.int32)
    chosen = jnp.sum((routes[:, :, None] == all_ids[None, None, :]).astype(jnp.int32), axis=1) > 0
    raised = jnp.where(chosen, jnp.exp(logits), 0.0)
    gate_probs = raised / jnp.sum(raised, axis=-1, keepdims=True)
    first_expert = lax.axis_index("tensor") * experts_local
    local_ids = first_expert + jnp.arange(experts_local, dtype=jnp.int32)
    picked = jnp.sum((routes[None, :, :] == local_ids[:, None, None]).astype(jnp.int32), axis=2)
    places = slot_places(picked)
    counts = jnp.sum(picked, axis=1)
    gate_rows = jnp.transpose(lax.dynamic_slice_in_dim(gate_probs, first_expert, experts_local, 1))
    grad_moe_b = (RESIDUAL * cotangent.astype(jnp.float32)).astype(jnp.bfloat16)
    middle_expert = experts_local // 2
    grads_first, sums = expert_stage(
        0, middle_expert, counts, places, gate_rows, normed_two_b, grad_moe_b,
        gate_weight, up_weight, down_weight, None,
    )
    grads_last, sums_last = expert_stage(
        middle_expert, experts_local, counts, places, gate_rows, normed_two_b, grad_moe_b,
        gate_weight, up_weight, down_weight, sums,
    )
    moe_part, grad_normed_part, unused = sums_last
    grad_gates_local = jnp.concatenate([sums[2], sums_last[2]], 0)
    shard_up_down = [
        (
            lax.psum_scatter(both, "dp", scatter_dimension=2, tiled=True),
            lax.psum_scatter(down, "dp", scatter_dimension=1, tiled=True),
        )
        for both, down in (grads_first, grads_last)
    ]
    grad_gates_part = lax.dynamic_update_slice_in_dim(
        jnp.zeros((experts_all, length), jnp.float32),
        grad_gates_local.reshape(experts_local, length),
        first_expert,
        0,
    ).reshape(-1, 128)
    grad_gates_part = jnp.pad(grad_gates_part, ((0, GATE_ROWS - grad_gates_part.shape[0]), (0, 0)))
    grad_normed_sum, gates_sum = line_sum(grad_normed_part, grad_gates_part, ring, 2)
    grad_gates = jnp.transpose(
        gates_sum[: experts_all * length // 128].reshape(experts_all, length)
    )
    weighted = jnp.sum(gate_probs * grad_gates, axis=-1, keepdims=True)
    grad_logits_b = (gate_probs * (grad_gates - weighted)).astype(jnp.bfloat16)
    grad_router = left_inner(normed_two_b, grad_logits_b)
    grad_normed_two = grad_normed_sum + right_inner(grad_logits_b, router_weight)
    grad_from_norm, grad_ffn_gain = rms_backward(grad_normed_two, unit_two, recip_two, ffn_gain)
    grad_middle = cotangent.astype(jnp.float32) + grad_from_norm
    grad_branch_b = (RESIDUAL * grad_middle).astype(jnp.bfloat16)
    grad_out = left_inner(attended_flat, grad_branch_b)
    grad_attended = (
        right_inner(grad_branch_b, out_weight)
        .astype(jnp.bfloat16)
        .reshape(count_blocks, block_rows, heads_local, HEAD)
    )

    def backward_block(running, pieces):
        query_part, first_row, logsum_part, attended_part, grad_part = pieces
        grad_queries, grad_keys, grad_values = attend_backward(
            query_part,
            keys_wide,
            values_wide,
            block_mask(segment, first_row, block_rows),
            logsum_part,
            attended_part,
            grad_part,
        )
        return ((running[0] + grad_keys, running[1] + grad_values), grad_queries)

    wide_zero = jnp.zeros((length, heads_local, HEAD), jnp.float32)
    (grad_keys_wide, grad_values_wide), grad_query_blocks = lax.scan(
        backward_block,
        (wide_zero, wide_zero),
        (query_blocks, first_rows, logsum, attended, grad_attended),
    )
    grad_queries_b = (
        rope_undo(grad_query_blocks.reshape(length, heads_local, HEAD), cosine, sine_table)
        .astype(jnp.bfloat16)
        .reshape(length, heads_local * HEAD)
    )
    grad_keys_b = (
        rope_undo(
            jnp.sum(grad_keys_wide.reshape(length, kv_local, group_size, HEAD), axis=2),
            cosine,
            sine_table,
        )
        .astype(jnp.bfloat16)
        .reshape(length, kv_local * HEAD)
    )
    grad_values_b = (
        jnp.sum(grad_values_wide.reshape(length, kv_local, group_size, HEAD), axis=2)
        .astype(jnp.bfloat16)
        .reshape(length, kv_local * HEAD)
    )
    grads_wide = jnp.concatenate([grad_queries_b, grad_keys_b, grad_values_b], 1)
    grad_projections = left_inner(normed_b, grads_wide)
    grad_normed_local = (
        right_inner(grad_queries_b, query_weight)
        + right_inner(grad_keys_b, key_weight)
        + right_inner(grad_values_b, value_weight)
    )
    grad_normed, unused = line_sum(grad_normed_local, None, ring, 3)
    grad_from_first, grad_attn_gain = rms_backward(grad_normed, unit_one, recip_one, attn_gain)
    grad_tokens = grad_middle + grad_from_first
    moe_out, unused = line_sum(moe_part, None, ring, 4)
    output = (middle + RESIDUAL * moe_out).astype(jnp.bfloat16)
    small = jnp.concatenate(
        [
            grad_projections,
            left_inner(grad_branch_b, attended_flat),
            grad_router,
            grad_ffn_gain[:, None],
            grad_attn_gain[:, None],
        ],
        1,
    )
    small = lax.psum_scatter(small, "dp", scatter_dimension=0, tiled=True)
    wide_q, wide_k = heads_local * HEAD, kv_local * HEAD
    at = [0, wide_q, wide_q + wide_k, wide_q + 2 * wide_k]
    at += [at[3] + wide_q, at[3] + wide_q + experts_all]
    return (
        output,
        grad_tokens,
        small[:, at[5] + 1],
        small[:, at[0] : at[1]],
        small[:, at[1] : at[2]],
        small[:, at[2] : at[3]],
        jnp.transpose(small[:, at[3] : at[4]]),
        small[:, at[5]],
        small[:, at[4] : at[5]],
        jnp.concatenate([both[:, 0] for both, down in shard_up_down], 0),
        jnp.concatenate([both[:, 1] for both, down in shard_up_down], 0),
        jnp.concatenate([down for both, down in shard_up_down], 0),
    )


def solution(mesh):
    return jax.shard_map(
        functools.partial(on_device, mesh.shape["tensor"]),
        mesh=mesh,
        in_specs=(
            P("dp", None),
            P("dp", None),
            P("dp", None),
            P("dp", None),
            P(),
            P(None, "tensor"),
            P(None, "tensor"),
            P(None, "tensor"),
            P("tensor", None),
            P(),
            P(),
            P("tensor", None, None),
            P("tensor", None, None),
            P("tensor", None, None),
        ),
        out_specs=(
            P("dp", None),
            P("dp", None),
            P("dp"),
            P("dp", "tensor"),
            P("dp", "tensor"),
            P("dp", "tensor"),
            P("tensor", "dp"),
            P("dp"),
            P("dp", None),
            P("tensor", "dp", None),
            P("tensor", "dp", None),
            P("tensor", "dp", None),
        ),
        check_vma=False,
    )
```

```python
import functools

import jax
import jax.numpy as jnp
from jax import lax
from jax.experimental import pallas as pl
from jax.experimental.pallas import tpu as pltpu
from jax.sharding import PartitionSpec as P

MESH = pl.DeviceIdType.MESH

HEAD = 64
CAP = 384


EPSILON = 1e-06
RESIDUAL = 0.22
ATTN_SCALE = 0.015625
ROPE_BASE = 10000.0


def left_inner(first, second):
    return lax.dot_general(
        first, second, (((0,), (0,)), ((), ())), preferred_element_type=jnp.float32
    )


def right_inner(first, second):
    return lax.dot_general(
        first, second, (((1,), (1,)), ((), ())), preferred_element_type=jnp.float32
    )


def doc_openings(segment):
    return jnp.sum((segment[None, :] < segment[:, None]).astype(jnp.int32), axis=1)


def rope_tables(opening, head_size):
    halfway = head_size // 2
    spread = jnp.arange(halfway, dtype=jnp.float32) * (2.0 / head_size)
    inverse = jnp.power(ROPE_BASE, -spread)
    places = jnp.arange(opening.shape[0], dtype=jnp.int32)
    angles = (places - opening).astype(jnp.float32)[:, None] * inverse[None, :]
    cosine, sine = jnp.cos(angles), jnp.sin(angles)
    none = jnp.zeros_like(sine)
    return (
        jnp.concatenate([cosine] * 4, 1),
        jnp.concatenate([-sine, none] * 2, 1),
        jnp.concatenate([none, sine] * 2, 1),
    )


def pad_columns(weight):
    missing = -weight.shape[1] % 128
    return weight if missing == 0 else jnp.pad(weight, ((0, 0), (0, missing)))


def rms_forward(hidden, gain):
    recip = lax.rsqrt(jnp.mean(hidden * hidden, axis=-1, keepdims=True) + EPSILON)
    unit = hidden * recip
    return (unit * gain, unit, recip)


def rms_backward(gradient, unit, recip, gain):
    gain_grad = jnp.sum(gradient * unit, axis=0)
    scaled = gradient * gain
    return (recip * (scaled - unit * jnp.mean(scaled * unit, axis=-1, keepdims=True)), gain_grad)


def slot_places(picked):
    length = picked.shape[1]
    tokens = jnp.arange(length, dtype=jnp.int32)
    earlier = (tokens[:, None] < tokens[None, :]).astype(jnp.bfloat16)
    before = jnp.dot(picked.astype(jnp.bfloat16), earlier, preferred_element_type=jnp.float32)
    return jnp.where(picked > 0, before.astype(jnp.int32), -1)


STEPS = 32
LAG = 2
GATE_ROWS = 512


def line_stages(n, xs, outs, scratch):
    count = len(xs)
    lows, highs = scratch[:count], scratch[count : 2 * count]
    low_recv, high_recv, total_recv, up_send, low_send, high_send = scratch[2 * count :]
    me = lax.axis_index("tensor")
    root = n // 2
    has_low, has_high = me > 0, me < n - 1

    def begin(others=()):
        barrier = pltpu.get_barrier_semaphore()
        for other in others:
            pl.semaphore_signal(barrier, inc=1, device_id=other, device_id_type=MESH)

        @pl.when(has_low)
        def _():
            pl.semaphore_signal(barrier, inc=1, device_id={"tensor": me - 1}, device_id_type=MESH)

        @pl.when(has_high)
        def _():
            pl.semaphore_signal(barrier, inc=1, device_id={"tensor": me + 1}, device_id_type=MESH)

        pl.semaphore_wait(
            barrier, len(others) + has_low.astype(jnp.int32) + has_high.astype(jnp.int32)
        )

    def piece(ref, c):
        rows = ref.shape[0] // STEPS
        return ref.at[pl.ds(pl.multiple_of(c * rows, rows), rows), :]

    def copies(sources, targets, c, send, recv, to):
        return [
            pltpu.make_async_remote_copy(
                src_ref=piece(source, c),
                dst_ref=piece(target, c),
                send_sem=send.at[i, c],
                recv_sem=recv.at[i, c],
                device_id={"tensor": to},
                device_id_type=MESH,
            )
            for i, (source, target) in enumerate(zip(sources, targets))
        ]

    def start(sources, targets, c, send, recv, to):
        for copy in copies(sources, targets, c, send, recv, to):
            copy.start()

    def arrived(targets, c, send, recv):
        for copy in copies(targets, targets, c, send, recv, me):
            copy.wait_recv()

    def reduce_step(c):
        for side, inner, held, recv, to in (
            (me < root, has_low, lows, low_recv, me + 1),
            (me > root, has_high, highs, high_recv, me - 1),
        ):

            @pl.when(side & inner)
            def _():
                arrived(held, c, up_send, recv)
                for x, h in zip(xs, held):
                    piece(h, c)[...] += piece(x, c)[...]
                start(held, held, c, up_send, recv, to)

            @pl.when(side & jnp.logical_not(inner))
            def _():
                start(xs, held, c, up_send, recv, to)

        @pl.when(me == root)
        def _():
            arrived(lows, c, up_send, low_recv)
            if root < n - 1:
                arrived(highs, c, up_send, high_recv)
            for x, low, high, out in zip(xs, lows, highs, outs):
                total = piece(x, c)[...] + piece(low, c)[...]
                if root < n - 1:
                    total += piece(high, c)[...]
                piece(out, c)[...] = total
            start(outs, outs, c, low_send, total_recv, me - 1)
            if root < n - 1:
                start(outs, outs, c, high_send, total_recv, me + 1)

    def total_step(c):
        @pl.when(me != root)
        def _():
            arrived(outs, c, low_send, total_recv)

        @pl.when((me < root) & has_low)
        def _():
            start(outs, outs, c, low_send, total_recv, me - 1)

        @pl.when((me > root) & has_high)
        def _():
            start(outs, outs, c, high_send, total_recv, me + 1)

    lag = jnp.where(has_low & has_high, LAG, STEPS)

    def step(t, carry):
        @pl.when(t < STEPS)
        def _():
            reduce_step(t)

        @pl.when((t >= lag) & (t - lag < STEPS))
        def _():
            total_step(t - lag)

        return carry

    def finish():
        def drain(c, carry):
            for condition, send in (
                (me != root, up_send),
                ((me <= root) & has_low, low_send),
                ((me >= root) & has_high, high_send),
            ):

                @pl.when(condition)
                def _():
                    for copy in copies(xs, lows, c, send, low_recv, me):
                        copy.wait_send()

            return carry

        lax.fori_loop(0, STEPS, drain, 0)

    return begin, step, finish


def line_scratch(arrays):
    return [pltpu.VMEM(array.shape, jnp.float32) for array in arrays * 2] + [
        pltpu.SemaphoreType.DMA((len(arrays), STEPS))
    ] * 6


def line_sum_kernel(n, count, *refs):
    begin, step, finish = line_stages(n, refs[:count], refs[count : 2 * count], refs[2 * count :])
    begin()
    lax.fori_loop(0, 2 * STEPS, step, 0)
    finish()


def line_sum(x, extra, n, name):
    arrays = [x] if extra is None else [x, extra]
    count = len(arrays)
    shapes = [jax.ShapeDtypeStruct(array.shape, jnp.float32) for array in arrays]
    size = sum(array.size for array in arrays)
    results = pl.pallas_call(
        functools.partial(line_sum_kernel, n, count),
        out_shape=shapes,
        in_specs=[pl.BlockSpec(memory_space=pltpu.VMEM)] * count,
        out_specs=[pl.BlockSpec(memory_space=pltpu.VMEM)] * count,
        scratch_shapes=line_scratch(arrays),
        compiler_params=pltpu.CompilerParams(
            collective_id=name, has_side_effects=True, vmem_limit_bytes=40 << 20
        ),
        cost_estimate=pl.CostEstimate(
            flops=3 * size, bytes_accessed=8 * size, transcendentals=0
        ),
    )(*arrays)
    return (results[0], None) if extra is None else tuple(results)


def expert_kernel(
    parts,
    first,
    chained,
    count_ref,
    place_ref,
    gate_ref,
    normed_ref,
    grad_ref,
    gate_w,
    up_w,
    down_w,
    *refs,
):
    if chained:
        moe_in, back_in = refs[:2]
        refs = refs[2:]
    grads_out, moe_out, back_out, gates_out = refs[:4]
    rows_ref, grads_ref, moe_rows, back_rows, slot_gate, slot_grad, sems = refs[4:]
    expert, half = pl.program_id(0), pl.program_id(1)
    halves = pl.num_programs(1)
    filled = count_ref[first + expert]
    length = normed_ref.shape[0]
    block = gate_w.shape[2]
    started = (expert == 0) & (half == 0)

    if chained:
        copy_moe = pltpu.make_async_copy(moe_in, moe_out, sems.at[0])
        copy_back = pltpu.make_async_copy(back_in, back_out, sems.at[1])

        @pl.when(started)
        def _():
            copy_moe.start()
            copy_back.start()

        @pl.when((expert == 0) & (half == halves - 1))
        def _():
            copy_moe.wait()
            copy_back.wait()

    else:

        @pl.when(started)
        def _():
            moe_out[...] = jnp.zeros_like(moe_out)
            back_out[...] = jnp.zeros_like(back_out)

    def run(rows):
        mask = lax.broadcasted_iota(jnp.int32, (rows, length), 0) == place_ref[0]

        @pl.when(half == 0)
        def _():
            picks = jnp.where(mask, 1.0, 0.0).astype(jnp.bfloat16)
            rows_ref[:rows] = jnp.dot(
                picks, normed_ref[...], preferred_element_type=jnp.float32
            ).astype(jnp.bfloat16)
            grads_ref[:rows] = jnp.dot(
                picks, grad_ref[...], preferred_element_type=jnp.float32
            ).astype(jnp.bfloat16)
            slot_gate[:rows] = jnp.broadcast_to(
                jnp.sum(jnp.where(mask, gate_ref[0], 0.0), axis=1, keepdims=True), (rows, 128)
            )

        rows_in = rows_ref[:rows]
        grad_rows = grads_ref[:rows]
        gate = slot_gate[:rows, :1]
        gate_input = jnp.dot(rows_in, gate_w[0], preferred_element_type=jnp.float32)
        up_input = jnp.dot(rows_in, up_w[0], preferred_element_type=jnp.float32)
        grad_act = right_inner(grad_rows, down_w[0])
        sigmoid_val = jax.nn.sigmoid(gate_input)
        silu_out = gate_input * sigmoid_val
        hidden = silu_out * up_input
        activation = (hidden * gate).astype(jnp.bfloat16)
        column = jnp.sum(grad_act * hidden, axis=1, keepdims=True)
        grad_hidden = grad_act * gate
        grad_gate_in = (
            grad_hidden * up_input * sigmoid_val * (1.0 + gate_input * (1.0 - sigmoid_val))
        ).astype(jnp.bfloat16)
        grad_up_in = (grad_hidden * silu_out).astype(jnp.bfloat16)
        lanes = pl.ds(pl.multiple_of(half * block, block), block)
        grads = left_inner(rows_in, jnp.concatenate([grad_gate_in, grad_up_in], 1))
        grads_out[0, 0, :, lanes] = grads[:, :block]
        grads_out[0, 1, :, lanes] = grads[:, block:]
        grad_down = left_inner(activation, grad_rows)
        hidden_all, width = grads_out.shape[3], grads_out.shape[2]
        own = hidden_all // parts
        blocks = width // hidden_all
        for part in range(block // own):
            for piece in range(blocks):
                at = half * (block // own) * blocks * own + (part * blocks + piece) * own
                grads_out[0, 2, pl.ds(pl.multiple_of(at, own), own), :] = grad_down[
                    part * own : (part + 1) * own, piece * hidden_all : (piece + 1) * hidden_all
                ]
        moe = jnp.dot(activation, down_w[0], preferred_element_type=jnp.float32)
        back = right_inner(grad_gate_in, gate_w[0]) + right_inner(grad_up_in, up_w[0])

        @pl.when(half == 0)
        def _():
            moe_rows[:rows] = moe
            back_rows[:rows] = back
            slot_grad[:rows] = jnp.broadcast_to(column, (rows, 128))

        @pl.when((half > 0) & (half < halves - 1))
        def _():
            moe_rows[:rows] += moe
            back_rows[:rows] += back
            slot_grad[:rows] += jnp.broadcast_to(column, (rows, 128))

        @pl.when(half == halves - 1)
        def _():
            picks = jnp.where(mask, 1.0, 0.0).astype(jnp.bfloat16)
            moe_out[...] += left_inner(picks, (moe_rows[:rows] + moe).astype(jnp.bfloat16))
            back_out[...] += left_inner(picks, (back_rows[:rows] + back).astype(jnp.bfloat16))
            total = slot_grad[:rows, :1] + column
            gates_out[0] = jnp.sum(jnp.where(mask, total, 0.0), axis=0, keepdims=True)

    sizes = (128, 256, CAP)
    for low, rows in zip((-1,) + sizes[:-1], sizes):
        pl.when((filled > low) & (filled <= rows))(functools.partial(run, rows))


def expert_stage(parts, first, last, counts, places, gate_rows, normed_b, grad_b, gate_w, up_w, down_w, sums):
    number = last - first
    length, width = normed_b.shape
    hidden = gate_w.shape[2]
    block = 256
    halves = hidden // block
    experts = places.shape[0]
    chained = sums is not None
    whole = lambda e, h, c: (0, 0)
    row_spec = pl.BlockSpec((1, 1, length), lambda e, h, c: (first + e, 0, 0))
    once = pl.Buffered(1)
    in_specs = [
        row_spec,
        row_spec,
        pl.BlockSpec((length, width), whole, pipeline_mode=once),
        pl.BlockSpec((length, width), whole, pipeline_mode=once),
        pl.BlockSpec((1, width, block), lambda e, h, c: (first + e, 0, h)),
        pl.BlockSpec((1, width, block), lambda e, h, c: (first + e, 0, h)),
        pl.BlockSpec((1, block, width), lambda e, h, c: (first + e, h, 0)),
    ]
    args = [
        counts,
        places.reshape(experts, 1, length),
        gate_rows.reshape(experts, 1, length),
        normed_b,
        grad_b,
        gate_w,
        up_w,
        down_w,
    ]
    if chained:
        in_specs += [pl.BlockSpec(memory_space=pl.ANY)] * 2
        args += [sums[0], sums[1]]
    grads, moe, back, gates = pl.pallas_call(
        functools.partial(expert_kernel, parts, first, chained),
        out_shape=[
            jax.ShapeDtypeStruct((number, 3, width, hidden), jnp.float32),
            jax.ShapeDtypeStruct((length, width), jnp.float32),
            jax.ShapeDtypeStruct((length, width), jnp.float32),
            jax.ShapeDtypeStruct((number, 1, length), jnp.float32),
        ],
        grid_spec=pltpu.PrefetchScalarGridSpec(
            num_scalar_prefetch=1,
            grid=(number, halves),
            in_specs=in_specs,
            out_specs=[
                pl.BlockSpec((1, 3, width, hidden), lambda e, h, c: (e, 0, 0, 0)),
                pl.BlockSpec((length, width), whole, pipeline_mode=once),
                pl.BlockSpec((length, width), whole, pipeline_mode=once),
                pl.BlockSpec((1, 1, length), lambda e, h, c: (e, 0, 0)),
            ],
            scratch_shapes=[
                pltpu.VMEM((CAP, width), jnp.bfloat16),
                pltpu.VMEM((CAP, width), jnp.bfloat16),
                pltpu.VMEM((CAP, width), jnp.float32),
                pltpu.VMEM((CAP, width), jnp.float32),
                pltpu.VMEM((CAP, 128), jnp.float32),
                pltpu.VMEM((CAP, 128), jnp.float32),
                pltpu.SemaphoreType.DMA((2,)),
            ],
        ),
        compiler_params=pltpu.CompilerParams(
            dimension_semantics=("arbitrary", "arbitrary"), vmem_limit_bytes=63 << 20
        ),
        cost_estimate=pl.CostEstimate(
            flops=number * 8 * 10**9, bytes_accessed=number * 14 * 10**6, transcendentals=0
        ),
    )(*args)
    return (grads, (moe, back, gates))


SPAN = 768
ROWS = 256


def lane_halves(shape):
    return lax.broadcasted_iota(jnp.int32, shape, len(shape) - 1) // HEAD


def select_halves(tile, source, half):
    kept = jnp.where(lane_halves(tile.shape) == source, tile, 0.0)
    return kept if source == half else pltpu.roll(kept, HEAD, 1)


def spread_pairs(tile, target):
    for source in range(2):
        for half in range(2):
            target[2 * source + half] = select_halves(tile, source, half).astype(jnp.bfloat16)


def rope_tile(tile, cosine, sine_low, sine_high):
    return tile * cosine + pltpu.roll(tile, 128 - HEAD // 2, 1) * sine_low + pltpu.roll(
        tile, HEAD // 2, 1
    ) * sine_high


def rope_back_tile(tile, cosine, sine_low, sine_high):
    return (
        tile * cosine
        + pltpu.roll(tile * sine_low, HEAD // 2, 1)
        + pltpu.roll(tile * sine_high, 128 - HEAD // 2, 1)
    )


def window(block):
    first = block * ROWS
    return first, jnp.maximum(first + ROWS - SPAN, 0)


def attend_forward_kernel(
    heads,
    group,
    tokens_ref,
    gain_ref,
    query_w,
    key_w,
    value_w,
    cosine_ref,
    sine_low_ref,
    sine_high_ref,
    opening_ref,
    normed_out,
    query_out,
    key_out,
    value_out,
    attended_out,
    logsum_out,
    key_pairs,
    value_pairs,
    tiles_ref,
):
    tiles, length, unused = query_out.shape
    hidden = tokens_ref[...].astype(jnp.float32)
    recip = lax.rsqrt(jnp.mean(hidden * hidden, axis=1, keepdims=True) + EPSILON)
    normed_out[...] = (hidden * recip * gain_ref[...]).astype(jnp.bfloat16)
    cosine, sine_low, sine_high = cosine_ref[...], sine_low_ref[...], sine_high_ref[...]
    for tile in range(tiles):
        query = jnp.dot(
            normed_out[...],
            query_w[:, tile * 128 : (tile + 1) * 128],
            preferred_element_type=jnp.float32,
        )
        query_out[tile] = rope_tile(query, cosine, sine_low, sine_high).astype(jnp.bfloat16)
    key = rope_tile(
        jnp.dot(normed_out[...], key_w[...], preferred_element_type=jnp.float32),
        cosine,
        sine_low,
        sine_high,
    )
    value = jnp.dot(normed_out[...], value_w[...], preferred_element_type=jnp.float32)
    key_out[...] = key.astype(jnp.bfloat16)
    value_out[...] = value.astype(jnp.bfloat16)
    spread_pairs(key, key_pairs)
    spread_pairs(value, value_pairs)
    blocks = length // ROWS
    tiles_ref[...] = jnp.zeros_like(tiles_ref)

    def unit(step, carry):
        head, block = step // blocks, step % blocks
        tile, half = head // 2, head % 2
        pair = 2 * (head // group) + half
        first, low = window(block)
        rows = pl.ds(pl.multiple_of(first, ROWS), ROWS)
        span = pl.ds(pl.multiple_of(low, ROWS), SPAN)
        scores = right_inner(query_out[tile, rows, :], key_pairs[pair, span, :])
        columns = low + lax.broadcasted_iota(jnp.int32, (ROWS, SPAN), 1)
        own = first + lax.broadcasted_iota(jnp.int32, (ROWS, SPAN), 0)
        allowed = (columns >= opening_ref[rows, :]) & (columns <= own)
        raised = jnp.where(allowed, jnp.exp(ATTN_SCALE * scores), 0.0)
        total = jnp.sum(raised, axis=1, keepdims=True)
        product = jnp.dot(
            raised.astype(jnp.bfloat16), value_pairs[pair, span, :], preferred_element_type=jnp.float32
        )
        tiles_ref[tile, rows, :] += product / total
        wide = jnp.broadcast_to(jnp.log(total), (ROWS, 128))
        logsum_out[head, :, rows] = jnp.transpose(wide)[:1]
        return carry

    lax.fori_loop(0, heads * blocks, unit, 0)
    for tile in range(tiles):
        attended_out[:, tile * 128 : (tile + 1) * 128] = tiles_ref[tile].astype(jnp.bfloat16)


def attend_forward(tokens, gain, query_w, key_w, value_w, tables, opening, heads, group):
    length, width = tokens.shape
    wide = query_w.shape[1]
    tiles = wide // 128
    bf16, f32 = jnp.bfloat16, jnp.float32
    full = pl.BlockSpec(memory_space=pltpu.VMEM)
    return pl.pallas_call(
        functools.partial(attend_forward_kernel, heads, group),
        out_shape=[
            jax.ShapeDtypeStruct((length, width), bf16),
            jax.ShapeDtypeStruct((tiles, length, 128), bf16),
            jax.ShapeDtypeStruct((length, 128), bf16),
            jax.ShapeDtypeStruct((length, 128), bf16),
            jax.ShapeDtypeStruct((length, wide), bf16),
            jax.ShapeDtypeStruct((heads, 1, length), f32),
        ],
        in_specs=[full] * 9,
        out_specs=[full] * 6,
        scratch_shapes=[
            pltpu.VMEM((4, length, 128), bf16),
            pltpu.VMEM((4, length, 128), bf16),
            pltpu.VMEM((tiles, length, 128), f32),
        ],
        compiler_params=pltpu.CompilerParams(vmem_limit_bytes=48 << 20),
        cost_estimate=pl.CostEstimate(
            flops=8 * 10**9, bytes_accessed=12 * 10**6, transcendentals=5 * 10**6
        ),
    )(tokens, gain.reshape(1, width), query_w, key_w, value_w, *tables, opening.reshape(length, 1))


def attend_backward_kernel(
    n,
    heads,
    group,
    branch_ref,
    out_w,
    query_ref,
    key_ref,
    value_ref,
    attended_ref,
    logsum_ref,
    query_w,
    key_w,
    value_w,
    cosine_ref,
    sine_low_ref,
    sine_high_ref,
    opening_ref,
    moe_ref,
    grads_out,
    normed_out,
    moe_out,
    key_pairs,
    value_pairs,
    attend_grads,
    query_grads,
    key_grads,
    value_grads,
    delta_ref,
    *line,
):
    tiles, length, unused = query_ref.shape
    line_start, line_step, line_end = line_stages(n, [moe_ref], [moe_out], line)
    line_start()
    spread_pairs(key_ref[...].astype(jnp.float32), key_pairs)
    spread_pairs(value_ref[...].astype(jnp.float32), value_pairs)
    halves = (
        lax.broadcasted_iota(jnp.int32, (8, 128), 0) == lane_halves((8, 128))
    ).astype(jnp.float32)
    for tile in range(tiles):
        lanes = slice(tile * 128, (tile + 1) * 128)
        grad = right_inner(branch_ref[...], out_w[lanes, :]).astype(jnp.bfloat16)
        attend_grads[tile] = grad
        products = grad.astype(jnp.float32) * attended_ref[:, lanes].astype(jnp.float32)
        sums = lax.dot_general(
            halves,
            products,
            (((1,), (1,)), ((), ())),
            precision=lax.Precision.HIGHEST,
            preferred_element_type=jnp.float32,
        )
        delta_ref[2 * tile] = sums[0:1]
        delta_ref[2 * tile + 1] = sums[1:2]
    query_grads[...] = jnp.zeros_like(query_grads)
    key_grads[...] = jnp.zeros_like(key_grads)
    value_grads[...] = jnp.zeros_like(value_grads)
    blocks = length // ROWS
    units = heads * blocks
    each = -(-2 * STEPS // units)

    def unit(step, carry):
        lax.fori_loop(step * each, step * each + each, line_step, 0)
        head, block = step // blocks, step % blocks
        tile, half = head // 2, head % 2
        pair = 2 * (head // group) + half
        first, low = window(block)
        rows = pl.ds(pl.multiple_of(first, ROWS), ROWS)
        span = pl.ds(pl.multiple_of(low, ROWS), SPAN)
        keys = key_pairs[pair, span, :]
        query = query_ref[tile, rows, :]
        grad = attend_grads[tile, rows, :]
        scores = right_inner(keys, query)
        columns = low + lax.broadcasted_iota(jnp.int32, (SPAN, ROWS), 0)
        own = first + lax.broadcasted_iota(jnp.int32, (SPAN, ROWS), 1)
        allowed = (columns >= opening_ref[:, rows]) & (columns <= own)
        probs = jnp.where(
            allowed, jnp.exp(ATTN_SCALE * scores - logsum_ref[head, :, rows]), 0.0
        )
        grad_probs = right_inner(value_pairs[pair, span, :], grad)
        grad_scores = (probs * (grad_probs - delta_ref[head, :, rows])).astype(jnp.bfloat16)
        value_grads[pair, span, :] += jnp.dot(
            probs.astype(jnp.bfloat16), grad, preferred_element_type=jnp.float32
        )
        key_grads[pair, span, :] += jnp.dot(
            grad_scores, query, preferred_element_type=jnp.float32
        )
        query_grads[tile, rows, :] += left_inner(grad_scores, keys)
        return carry

    lax.fori_loop(0, units, unit, 0)
    cosine, sine_low, sine_high = cosine_ref[...], sine_low_ref[...], sine_high_ref[...]
    wide = tiles * 128
    for tile in range(tiles):
        grads_out[:, tile * 128 : (tile + 1) * 128] = rope_back_tile(
            ATTN_SCALE * query_grads[tile], cosine, sine_low, sine_high
        ).astype(jnp.bfloat16)
    totals = []
    for grads in (key_grads, value_grads):
        totals.append(
            sum(
                select_halves(grads[2 * source + half], half, source)
                for source in range(2)
                for half in range(2)
            )
        )
    grads_out[:, wide : wide + 128] = rope_back_tile(
        ATTN_SCALE * totals[0], cosine, sine_low, sine_high
    ).astype(jnp.bfloat16)
    grads_out[:, wide + 128 : wide + 256] = totals[1].astype(jnp.bfloat16)
    normed_out[...] = (
        right_inner(grads_out[:, :wide], query_w[...])
        + right_inner(grads_out[:, wide : wide + 128], key_w[...])
        + right_inner(grads_out[:, wide + 128 :], value_w[...])
    )
    line_end()


def attend_backward(
    n, branch, out_w, query, key, value, attended, logsum, query_w, key_w, value_w, tables, opening, moe,
    heads, group, name,
):
    length, width = branch.shape
    tiles = query.shape[0]
    wide = tiles * 128
    bf16, f32 = jnp.bfloat16, jnp.float32
    full = pl.BlockSpec(memory_space=pltpu.VMEM)
    return pl.pallas_call(
        functools.partial(attend_backward_kernel, n, heads, group),
        out_shape=[
            jax.ShapeDtypeStruct((length, wide + 256), bf16),
            jax.ShapeDtypeStruct((length, width), f32),
            jax.ShapeDtypeStruct((length, width), f32),
        ],
        in_specs=[full] * 15,
        out_specs=[full] * 3,
        scratch_shapes=[
            pltpu.VMEM((4, length, 128), bf16),
            pltpu.VMEM((4, length, 128), bf16),
            pltpu.VMEM((tiles, length, 128), bf16),
            pltpu.VMEM((tiles, length, 128), f32),
            pltpu.VMEM((4, length, 128), f32),
            pltpu.VMEM((4, length, 128), f32),
            pltpu.VMEM((2 * tiles, 1, length), f32),
        ]
        + line_scratch([moe]),
        compiler_params=pltpu.CompilerParams(
            collective_id=name, has_side_effects=True, vmem_limit_bytes=60 << 20
        ),
        cost_estimate=pl.CostEstimate(
            flops=12 * 10**9, bytes_accessed=30 * 10**6, transcendentals=5 * 10**6
        ),
    )(
        branch, out_w, query, key, value, attended, logsum, query_w, key_w, value_w, *tables,
        opening.reshape(1, length), moe,
    )


def finish_kernel(
    n,
    parts,
    local_ref,
    normed_ref,
    grads_ref,
    branch_ref,
    attended_ref,
    normed_two_ref,
    logits_ref,
    gain_ref,
    normed_out,
    shard_out,
    weights_ref,
    *scratch,
):
    levels = parts.bit_length() - 1
    held = scratch[:levels]
    sends, recvs = scratch[levels : levels + 2]
    line_start, line_step, line_end = line_stages(n, [local_ref], [normed_out], scratch[levels + 2 :])
    me = lax.axis_index("dp")
    width = normed_ref.shape[1]
    own = width // parts
    wide, attended_wide = grads_ref.shape[1], attended_ref.shape[1]
    line_start([{"dp": jnp.bitwise_xor(me, 1 << level)} for level in range(levels)])

    def run_line(first, last):
        lax.fori_loop(first, last, line_step, 0)

    run_line(0, 2)
    pieces = 4
    block = width // pieces
    for piece in range(pieces):
        rows = slice(piece * block, (piece + 1) * block)
        weights_ref[rows, :wide] = left_inner(normed_ref[:, rows], grads_ref[...])
        weights_ref[rows, wide : wide + attended_wide] = left_inner(
            branch_ref[:, rows], attended_ref[...]
        )
        gain = jnp.transpose(jnp.broadcast_to(gain_ref[:, rows], (128, block)))
        lanes = lax.broadcasted_iota(jnp.int32, (block, 128), 1)
        weights_ref[rows, wide + attended_wide :] = jnp.where(
            lanes == 127, gain, left_inner(normed_two_ref[:, rows], logits_ref[...])
        )
        run_line(2 + 2 * piece, 4 + 2 * piece)
    done = 2 + 2 * pieces

    def shard(number):
        return weights_ref.at[pl.ds(pl.multiple_of(number * own, own), own), :]

    def copies(level):
        peer = jnp.bitwise_xor(me, 1 << level)
        low = jnp.bitwise_and(peer, (2 << level) - 1)
        return [
            pltpu.make_async_remote_copy(
                src_ref=shard(low + (i << (level + 1))),
                dst_ref=held[level].at[i],
                send_sem=sends.at[level, i],
                recv_sem=recvs.at[level, i],
                device_id={"dp": peer},
                device_id_type=MESH,
            )
            for i in range(parts >> (level + 1))
        ]

    stops = [10, 12, 14, 10]
    for level in range(levels):
        for copy in copies(level):
            copy.start()
        until = done + stops[level]
        run_line(done, until)
        done = until
        kept = jnp.bitwise_and(me, (2 << level) - 1)
        for i, copy in enumerate(copies(level)):
            copy.wait_recv()
            target = shard(kept + (i << (level + 1)))
            target[...] += held[level][i]
    run_line(done, 2 * STEPS)
    shard_out[...] = shard(me)[...]
    for level in range(levels):
        for copy in copies(level):
            copy.wait_send()
    line_end()


def finish(n, parts, grad_local, normed_b, grads_wide, branch_b, attended, normed_two_b, grad_logits_b, ffn_gain_grad, name):
    length, width = normed_b.shape
    columns = grads_wide.shape[1] + attended.shape[1] + 128
    logits = jnp.pad(grad_logits_b, ((0, 0), (0, 128 - grad_logits_b.shape[1])))
    full = pl.BlockSpec(memory_space=pltpu.VMEM)
    levels = parts.bit_length() - 1
    own = width // parts
    f32 = jnp.float32
    return pl.pallas_call(
        functools.partial(finish_kernel, n, parts),
        out_shape=[
            jax.ShapeDtypeStruct((length, width), f32),
            jax.ShapeDtypeStruct((own, columns), f32),
        ],
        in_specs=[full] * 8,
        out_specs=[full] * 2,
        scratch_shapes=[pltpu.VMEM((width, columns), f32)]
        + [pltpu.VMEM((parts >> (level + 1), own, columns), f32) for level in range(levels)]
        + [pltpu.SemaphoreType.DMA((levels, parts // 2))] * 2
        + line_scratch([grad_local]),
        compiler_params=pltpu.CompilerParams(
            collective_id=name, has_side_effects=True, vmem_limit_bytes=60 << 20
        ),
        cost_estimate=pl.CostEstimate(
            flops=2 * length * width * columns, bytes_accessed=50 * 10**6, transcendentals=0
        ),
    )(
        grad_local, normed_b, grads_wide, branch_b, attended, normed_two_b, logits,
        ffn_gain_grad.reshape(1, width),
    )


def place_kernel(shards_ref, *refs):
    gate_out, up_out, down_out = refs[-3:]
    gate_out[0] = shards_ref[0, 0]
    up_out[0] = shards_ref[0, 1]
    rows, hidden = down_out.shape[1], shards_ref.shape[3]
    for piece in range(down_out.shape[2] // hidden):
        down_out[0, :, piece * hidden : (piece + 1) * hidden] = shards_ref[
            0, 2, piece * rows : (piece + 1) * rows, :
        ]


def place_shards(parts, shards, first, experts, before):
    number, unused, rows, hidden = shards.shape
    down_rows = hidden // parts
    width = rows * parts
    shapes = [(experts, rows, hidden), (experts, rows, hidden), (experts, down_rows, width)]
    spec = lambda shape: pl.BlockSpec((1,) + shape[1:], lambda e: (first + e, 0, 0))
    args, extra, aliases = [shards], [], {}
    if before is not None:
        args += list(before)
        extra = [pl.BlockSpec(memory_space=pl.ANY)] * 3
        aliases = {1: 0, 2: 1, 3: 2}
    return pl.pallas_call(
        place_kernel,
        out_shape=[jax.ShapeDtypeStruct(shape, jnp.float32) for shape in shapes],
        grid=(number,),
        in_specs=[pl.BlockSpec((1, 3, rows, hidden), lambda e: (e, 0, 0, 0))] + extra,
        out_specs=[spec(shape) for shape in shapes],
        input_output_aliases=aliases,
        cost_estimate=pl.CostEstimate(
            flops=0, bytes_accessed=8 * shards.size, transcendentals=0
        ),
    )(*args)


def on_device(
    ring,
    tokens,
    cotangent,
    segment_ids,
    routes,
    attn_gain,
    query_weight,
    key_weight,
    value_weight,
    out_weight,
    ffn_gain,
    router_weight,
    gate_weight,
    up_weight,
    down_weight,
):
    length = tokens.shape[0]
    width = tokens.shape[1]
    segment = segment_ids[0]
    heads_local = query_weight.shape[1] // HEAD
    kv_local = key_weight.shape[1] // HEAD
    group_size = heads_local // kv_local
    experts_all = router_weight.shape[1]
    experts_local = gate_weight.shape[0]
    parts = lax.axis_size("dp")
    opening = doc_openings(segment)
    tables = rope_tables(opening, HEAD)
    query_w, key_w, value_w = (pad_columns(w) for w in (query_weight, key_weight, value_weight))
    out_w = jnp.transpose(pad_columns(jnp.transpose(out_weight)))
    hidden_in = tokens.astype(jnp.float32)
    normed_b, queries, keys, values, attended, logsum = attend_forward(
        tokens, attn_gain, query_w, key_w, value_w, tables, opening, heads_local, group_size
    )
    all_ids = jnp.arange(experts_all, dtype=jnp.int32)
    chosen = jnp.sum((routes[:, :, None] == all_ids[None, None, :]).astype(jnp.int32), axis=1) > 0
    first_expert = lax.axis_index("tensor") * experts_local
    local_ids = first_expert + jnp.arange(experts_local, dtype=jnp.int32)
    picked = jnp.sum((routes[None, :, :] == local_ids[:, None, None]).astype(jnp.int32), axis=2)
    places_in = slot_places(picked)
    counts = jnp.sum(picked, axis=1)
    grad_moe_b = (RESIDUAL * cotangent.astype(jnp.float32)).astype(jnp.bfloat16)
    attn_out, unused = line_sum(
        jnp.dot(attended, out_w, preferred_element_type=jnp.float32), None, ring, 1
    )
    middle = hidden_in + RESIDUAL * attn_out
    normed_two, unit_two, recip_two = rms_forward(middle, ffn_gain)
    normed_two_b = normed_two.astype(jnp.bfloat16)
    logits = jnp.dot(normed_two_b, router_weight, preferred_element_type=jnp.float32)
    raised = jnp.where(chosen, jnp.exp(logits), 0.0)
    gate_probs = raised / jnp.sum(raised, axis=-1, keepdims=True)
    gate_rows = jnp.transpose(lax.dynamic_slice_in_dim(gate_probs, first_expert, experts_local, 1))
    early = 2 * experts_local // 5
    grads_first, sums = expert_stage(
        parts, 0, early, counts, places_in, gate_rows, normed_two_b, grad_moe_b,
        gate_weight, up_weight, down_weight, None,
    )
    shards_first = lax.psum_scatter(grads_first, "dp", scatter_dimension=2, tiled=True)
    grads_last, sums_last = expert_stage(
        parts, early, experts_local, counts, places_in, gate_rows, normed_two_b, grad_moe_b,
        gate_weight, up_weight, down_weight, sums,
    )
    moe_part, grad_normed_part, unused = sums_last
    grad_gates_local = jnp.concatenate([sums[2], sums_last[2]], 0)
    grad_gates_part = lax.dynamic_update_slice_in_dim(
        jnp.zeros((experts_all, length), jnp.float32),
        grad_gates_local.reshape(experts_local, length),
        first_expert,
        0,
    ).reshape(-1, 128)
    grad_gates_part = jnp.pad(grad_gates_part, ((0, GATE_ROWS - grad_gates_part.shape[0]), (0, 0)))
    grad_normed_sum, gates_sum = line_sum(grad_normed_part, grad_gates_part, ring, 2)
    grad_gates = jnp.transpose(
        gates_sum[: experts_all * length // 128].reshape(experts_all, length)
    )
    weighted = jnp.sum(gate_probs * grad_gates, axis=-1, keepdims=True)
    grad_logits_b = (gate_probs * (grad_gates - weighted)).astype(jnp.bfloat16)
    grad_normed_two = grad_normed_sum + right_inner(grad_logits_b, router_weight)
    grad_from_norm, grad_ffn_gain = rms_backward(grad_normed_two, unit_two, recip_two, ffn_gain)
    grad_middle = cotangent.astype(jnp.float32) + grad_from_norm
    grad_branch_b = (RESIDUAL * grad_middle).astype(jnp.bfloat16)
    shards_first, grads_last, grad_branch_b = lax.optimization_barrier(
        (shards_first, grads_last, grad_branch_b)
    )
    shards_last = lax.psum_scatter(grads_last, "dp", scatter_dimension=2, tiled=True)
    grads_wide, grad_normed_local, moe_out = attend_backward(
        ring, grad_branch_b, out_w, queries, keys, values, attended, logsum,
        query_w, key_w, value_w, tables, opening, moe_part, heads_local, group_size, 3,
    )
    output = (middle + RESIDUAL * moe_out).astype(jnp.bfloat16)
    grad_normed, small = finish(
        ring, parts, grad_normed_local, normed_b, grads_wide, grad_branch_b, attended, normed_two_b,
        grad_logits_b, grad_ffn_gain, 4,
    )
    recip_one = lax.rsqrt(jnp.mean(hidden_in * hidden_in, axis=-1, keepdims=True) + EPSILON)
    unit_one = hidden_in * recip_one
    grad_from_first, grad_attn_gain = rms_backward(grad_normed, unit_one, recip_one, attn_gain)
    grad_tokens = grad_middle + grad_from_first
    grad_attn_gain = lax.psum_scatter(grad_attn_gain, "dp", scatter_dimension=0, tiled=True)
    shards_last, grad_attn_gain = lax.optimization_barrier((shards_last, grad_attn_gain))
    tiled_q = query_w.shape[1]
    wide_q, wide_k = heads_local * HEAD, kv_local * HEAD
    at_out = tiled_q + 256
    at_router = at_out + tiled_q
    grads_placed = place_shards(parts, shards_first, 0, experts_local, None)
    grad_gate, grad_up, grad_down = place_shards(parts, shards_last, early, experts_local, grads_placed)
    return (
        output,
        grad_tokens,
        grad_attn_gain,
        small[:, :wide_q],
        small[:, tiled_q : tiled_q + wide_k],
        small[:, tiled_q + 128 : tiled_q + 128 + wide_k],
        jnp.transpose(small[:, at_out : at_out + wide_q]),
        small[:, at_router + 127],
        small[:, at_router : at_router + experts_all],
        grad_gate,
        grad_up,
        grad_down,
    )


def solution(mesh):
    return jax.shard_map(
        functools.partial(on_device, mesh.shape["tensor"]),
        mesh=mesh,
        in_specs=(
            P("dp", None),
            P("dp", None),
            P("dp", None),
            P("dp", None),
            P(),
            P(None, "tensor"),
            P(None, "tensor"),
            P(None, "tensor"),
            P("tensor", None),
            P(),
            P(),
            P("tensor", None, None),
            P("tensor", None, None),
            P("tensor", None, None),
        ),
        out_specs=(
            P("dp", None),
            P("dp", None),
            P("dp"),
            P("dp", "tensor"),
            P("dp", "tensor"),
            P("dp", "tensor"),
            P("tensor", "dp"),
            P("dp"),
            P("dp", None),
            P("tensor", "dp", None),
            P("tensor", "dp", None),
            P("tensor", "dp", None),
        ),
        check_vma=False,
    )
```

```python
import functools

import jax
import jax.numpy as jnp
from jax import lax
from jax.experimental import pallas as pl
from jax.experimental.pallas import tpu as pltpu
from jax.sharding import PartitionSpec as P

MESH = pl.DeviceIdType.MESH

HEAD = 64
CAP = 384


EPSILON = 1e-06
RESIDUAL = 0.22
ATTN_SCALE = 0.015625
ROPE_BASE = 10000.0


def left_inner(first, second):
    return lax.dot_general(
        first, second, (((0,), (0,)), ((), ())), preferred_element_type=jnp.float32
    )


def right_inner(first, second):
    return lax.dot_general(
        first, second, (((1,), (1,)), ((), ())), preferred_element_type=jnp.float32
    )


def doc_openings(segment):
    return jnp.sum((segment[None, :] < segment[:, None]).astype(jnp.int32), axis=1)


def rope_tables(opening, head_size):
    halfway = head_size // 2
    spread = jnp.arange(halfway, dtype=jnp.float32) * (2.0 / head_size)
    inverse = jnp.power(ROPE_BASE, -spread)
    places = jnp.arange(opening.shape[0], dtype=jnp.int32)
    angles = (places - opening).astype(jnp.float32)[:, None] * inverse[None, :]
    cosine, sine = jnp.cos(angles), jnp.sin(angles)
    none = jnp.zeros_like(sine)
    return (
        jnp.concatenate([cosine] * 4, 1),
        jnp.concatenate([-sine, none] * 2, 1),
        jnp.concatenate([none, sine] * 2, 1),
    )


def pad_columns(weight):
    missing = -weight.shape[1] % 128
    return weight if missing == 0 else jnp.pad(weight, ((0, 0), (0, missing)))


def rms_forward(hidden, gain):
    recip = lax.rsqrt(jnp.mean(hidden * hidden, axis=-1, keepdims=True) + EPSILON)
    unit = hidden * recip
    return (unit * gain, unit, recip)


def rms_backward(gradient, unit, recip, gain):
    gain_grad = jnp.sum(gradient * unit, axis=0)
    scaled = gradient * gain
    return (recip * (scaled - unit * jnp.mean(scaled * unit, axis=-1, keepdims=True)), gain_grad)


def slot_places(picked):
    length = picked.shape[1]
    tokens = jnp.arange(length, dtype=jnp.int32)
    earlier = (tokens[:, None] < tokens[None, :]).astype(jnp.bfloat16)
    before = jnp.dot(picked.astype(jnp.bfloat16), earlier, preferred_element_type=jnp.float32)
    return jnp.where(picked > 0, before.astype(jnp.int32), -1)


STEPS = 32
LAG = 2
GATE_ROWS = 512


def line_stages(n, xs, outs, scratch):
    count = len(xs)
    lows, highs = scratch[:count], scratch[count : 2 * count]
    low_recv, high_recv, total_recv, up_send, low_send, high_send = scratch[2 * count :]
    me = lax.axis_index("tensor")
    root = n // 2
    has_low, has_high = me > 0, me < n - 1

    def begin(others=()):
        barrier = pltpu.get_barrier_semaphore()
        for other in others:
            pl.semaphore_signal(barrier, inc=1, device_id=other, device_id_type=MESH)

        @pl.when(has_low)
        def _():
            pl.semaphore_signal(barrier, inc=1, device_id={"tensor": me - 1}, device_id_type=MESH)

        @pl.when(has_high)
        def _():
            pl.semaphore_signal(barrier, inc=1, device_id={"tensor": me + 1}, device_id_type=MESH)

        pl.semaphore_wait(
            barrier, len(others) + has_low.astype(jnp.int32) + has_high.astype(jnp.int32)
        )

    def piece(ref, c):
        rows = ref.shape[0] // STEPS
        return ref.at[pl.ds(pl.multiple_of(c * rows, rows), rows), :]

    def copies(sources, targets, c, send, recv, to):
        return [
            pltpu.make_async_remote_copy(
                src_ref=piece(source, c),
                dst_ref=piece(target, c),
                send_sem=send.at[i, c],
                recv_sem=recv.at[i, c],
                device_id={"tensor": to},
                device_id_type=MESH,
            )
            for i, (source, target) in enumerate(zip(sources, targets))
        ]

    def start(sources, targets, c, send, recv, to):
        for copy in copies(sources, targets, c, send, recv, to):
            copy.start()

    def arrived(targets, c, send, recv):
        for copy in copies(targets, targets, c, send, recv, me):
            copy.wait_recv()

    def reduce_step(c):
        for side, inner, held, recv, to in (
            (me < root, has_low, lows, low_recv, me + 1),
            (me > root, has_high, highs, high_recv, me - 1),
        ):

            @pl.when(side & inner)
            def _():
                arrived(held, c, up_send, recv)
                for x, h in zip(xs, held):
                    piece(h, c)[...] += piece(x, c)[...]
                start(held, held, c, up_send, recv, to)

            @pl.when(side & jnp.logical_not(inner))
            def _():
                start(xs, held, c, up_send, recv, to)

        @pl.when(me == root)
        def _():
            arrived(lows, c, up_send, low_recv)
            if root < n - 1:
                arrived(highs, c, up_send, high_recv)
            for x, low, high, out in zip(xs, lows, highs, outs):
                total = piece(x, c)[...] + piece(low, c)[...]
                if root < n - 1:
                    total += piece(high, c)[...]
                piece(out, c)[...] = total
            start(outs, outs, c, low_send, total_recv, me - 1)
            if root < n - 1:
                start(outs, outs, c, high_send, total_recv, me + 1)

    def total_step(c):
        @pl.when(me != root)
        def _():
            arrived(outs, c, low_send, total_recv)

        @pl.when((me < root) & has_low)
        def _():
            start(outs, outs, c, low_send, total_recv, me - 1)

        @pl.when((me > root) & has_high)
        def _():
            start(outs, outs, c, high_send, total_recv, me + 1)

    lag = jnp.where(has_low & has_high, LAG, STEPS)

    def step(t, carry):
        @pl.when(t < STEPS)
        def _():
            reduce_step(t)

        @pl.when((t >= lag) & (t - lag < STEPS))
        def _():
            total_step(t - lag)

        return carry

    def finish():
        def drain(c, carry):
            for condition, send in (
                (me != root, up_send),
                ((me <= root) & has_low, low_send),
                ((me >= root) & has_high, high_send),
            ):

                @pl.when(condition)
                def _():
                    for copy in copies(xs, lows, c, send, low_recv, me):
                        copy.wait_send()

            return carry

        lax.fori_loop(0, STEPS, drain, 0)

    return begin, step, finish


def line_scratch(arrays):
    return [pltpu.VMEM(array.shape, jnp.float32) for array in arrays * 2] + [
        pltpu.SemaphoreType.DMA((len(arrays), STEPS))
    ] * 6


def line_sum_kernel(n, count, *refs):
    begin, step, finish = line_stages(n, refs[:count], refs[count : 2 * count], refs[2 * count :])
    begin()
    lax.fori_loop(0, 2 * STEPS, step, 0)
    finish()


def line_sum(x, extra, n, name):
    arrays = [x] if extra is None else [x, extra]
    count = len(arrays)
    shapes = [jax.ShapeDtypeStruct(array.shape, jnp.float32) for array in arrays]
    size = sum(array.size for array in arrays)
    results = pl.pallas_call(
        functools.partial(line_sum_kernel, n, count),
        out_shape=shapes,
        in_specs=[pl.BlockSpec(memory_space=pltpu.VMEM)] * count,
        out_specs=[pl.BlockSpec(memory_space=pltpu.VMEM)] * count,
        scratch_shapes=line_scratch(arrays),
        compiler_params=pltpu.CompilerParams(
            collective_id=name, has_side_effects=True, vmem_limit_bytes=40 << 20
        ),
        cost_estimate=pl.CostEstimate(
            flops=3 * size, bytes_accessed=8 * size, transcendentals=0
        ),
    )(*arrays)
    return (results[0], None) if extra is None else tuple(results)


def expert_kernel(
    parts,
    first,
    numbers,
    chained,
    count_ref,
    place_ref,
    gate_ref,
    normed_ref,
    grad_ref,
    gate_w,
    up_w,
    down_w,
    *refs,
):
    if chained:
        moe_in, back_in = refs[:2]
        refs = refs[2:]
    grads_out, refs = refs[: len(numbers)], refs[len(numbers) :]
    moe_out, back_out, gates_out = refs[:3]
    rows_ref, grads_ref, active_ref, gate_in_ref, up_in_ref, weights_ref, sems, out_sems = refs[3:]
    expert = pl.program_id(0)
    filled = count_ref[first + expert]
    length, width = normed_ref.shape
    hidden_size = gate_w.shape[2]
    sizes = (128, 256, CAP)

    def by_size(run):
        low = None
        for rows in sizes:
            fits = filled <= rows if low is None else filled > low
            if low is not None and rows != sizes[-1]:
                fits = fits & (filled <= rows)
            pl.when(fits)(functools.partial(run, rows))
            low = rows

    if chained:
        copy_moe = pltpu.make_async_copy(moe_in, moe_out, sems.at[0])
        copy_back = pltpu.make_async_copy(back_in, back_out, sems.at[1])

        @pl.when(expert == 0)
        def _():
            copy_moe.start()
            copy_back.start()

    else:

        @pl.when(expert == 0)
        def _():
            moe_out[...] = jnp.zeros_like(moe_out)
            back_out[...] = jnp.zeros_like(back_out)

    def slots(rows):
        mask = lax.broadcasted_iota(jnp.int32, (rows, length), 0) == place_ref[0]
        return mask, jnp.where(mask, 1.0, 0.0).astype(jnp.bfloat16)

    def enter(rows):
        mask, picks = slots(rows)
        rows_in = jnp.dot(picks, normed_ref[...], preferred_element_type=jnp.float32).astype(jnp.bfloat16)
        grad_rows = jnp.dot(picks, grad_ref[...], preferred_element_type=jnp.float32).astype(jnp.bfloat16)
        rows_ref[:rows] = rows_in
        grads_ref[:rows] = grad_rows
        gate = jnp.sum(jnp.where(mask, gate_ref[0], 0.0), axis=1, keepdims=True)
        gate_input = jnp.dot(rows_in, gate_w[0], preferred_element_type=jnp.float32)
        up_input = jnp.dot(rows_in, up_w[0], preferred_element_type=jnp.float32)
        grad_act = right_inner(grad_rows, down_w[0])
        sigmoid_val = jax.nn.sigmoid(gate_input)
        silu_out = gate_input * sigmoid_val
        hidden = silu_out * up_input
        active_ref[:rows] = (hidden * gate).astype(jnp.bfloat16)
        column = jnp.sum(grad_act * hidden, axis=1, keepdims=True)
        gates_out[0] = jnp.sum(jnp.where(mask, column, 0.0), axis=0, keepdims=True)
        grad_hidden = grad_act * gate
        gate_in_ref[:rows] = (
            grad_hidden * up_input * sigmoid_val * (1.0 + gate_input * (1.0 - sigmoid_val))
        ).astype(jnp.bfloat16)
        up_in_ref[:rows] = (grad_hidden * silu_out).astype(jnp.bfloat16)

    by_size(enter)
    if chained:

        @pl.when(expert == 0)
        def _():
            copy_moe.wait()
            copy_back.wait()

    def leave(rows):
        mask, picks = slots(rows)
        moe = jnp.dot(active_ref[:rows], down_w[0], preferred_element_type=jnp.float32)
        moe_out[...] += left_inner(picks, moe.astype(jnp.bfloat16))
        back = right_inner(gate_in_ref[:rows], gate_w[0]) + right_inner(up_in_ref[:rows], up_w[0])
        back_out[...] += left_inner(picks, back.astype(jnp.bfloat16))

    by_size(leave)

    def copies(target, number):
        return [
            pltpu.make_async_copy(weights_ref.at[kind], target.at[number, kind], out_sems.at[kind])
            for kind in range(3)
        ]

    @pl.when(expert > 0)
    def _():
        for copy in copies(grads_out[0], 0):
            copy.wait()

    def weigh(rows):
        grads = left_inner(
            rows_ref[:rows], jnp.concatenate([gate_in_ref[:rows], up_in_ref[:rows]], 1)
        )
        weights_ref[0] = grads[:, :hidden_size]
        weights_ref[1] = grads[:, hidden_size:]
        grad_down = left_inner(active_ref[:rows], grads_ref[:rows])
        own = hidden_size // parts
        blocks = width // hidden_size
        for part in range(parts):
            for piece in range(blocks):
                at = (part * blocks + piece) * own
                weights_ref[2, at : at + own, :] = grad_down[
                    part * own : (part + 1) * own, piece * hidden_size : (piece + 1) * hidden_size
                ]

    by_size(weigh)
    start = 0
    for target, number in zip(grads_out, numbers):

        @pl.when((expert >= start) & (expert < start + number))
        def _():
            for copy in copies(target, expert - start):
                copy.start()

        start += number

    @pl.when(expert == pl.num_programs(0) - 1)
    def _():
        for copy in copies(grads_out[0], 0):
            copy.wait()


def expert_stage(parts, first, numbers, counts, places, gate_rows, normed_b, grad_b, gate_w, up_w, down_w, sums):
    number = sum(numbers)
    length, width = normed_b.shape
    hidden = gate_w.shape[2]
    experts = places.shape[0]
    chained = sums is not None
    whole = lambda e, c: (0, 0)
    row_spec = pl.BlockSpec((1, 1, length), lambda e, c: (first + e, 0, 0))
    once = pl.Buffered(1)
    f32, bf16 = jnp.float32, jnp.bfloat16
    in_specs = [
        row_spec,
        row_spec,
        pl.BlockSpec((length, width), whole, pipeline_mode=once),
        pl.BlockSpec((length, width), whole, pipeline_mode=once),
        pl.BlockSpec((1, width, hidden), lambda e, c: (first + e, 0, 0)),
        pl.BlockSpec((1, width, hidden), lambda e, c: (first + e, 0, 0)),
        pl.BlockSpec((1, hidden, width), lambda e, c: (first + e, 0, 0)),
    ]
    args = [
        counts,
        places.reshape(experts, 1, length),
        gate_rows.reshape(experts, 1, length),
        normed_b,
        grad_b,
        gate_w,
        up_w,
        down_w,
    ]
    if chained:
        in_specs += [pl.BlockSpec(memory_space=pl.ANY)] * 2
        args += [sums[0], sums[1]]
    results = pl.pallas_call(
        functools.partial(expert_kernel, parts, first, numbers, chained),
        out_shape=[jax.ShapeDtypeStruct((some, 3, width, hidden), f32) for some in numbers]
        + [
            jax.ShapeDtypeStruct((length, width), f32),
            jax.ShapeDtypeStruct((length, width), f32),
            jax.ShapeDtypeStruct((number, 1, length), f32),
        ],
        grid_spec=pltpu.PrefetchScalarGridSpec(
            num_scalar_prefetch=1,
            grid=(number,),
            in_specs=in_specs,
            out_specs=[pl.BlockSpec(memory_space=pl.ANY)] * len(numbers)
            + [
                pl.BlockSpec((length, width), whole, pipeline_mode=once),
                pl.BlockSpec((length, width), whole, pipeline_mode=once),
                pl.BlockSpec((1, 1, length), lambda e, c: (e, 0, 0)),
            ],
            scratch_shapes=[
                pltpu.VMEM((CAP, width), bf16),
                pltpu.VMEM((CAP, width), bf16),
                pltpu.VMEM((CAP, hidden), bf16),
                pltpu.VMEM((CAP, hidden), bf16),
                pltpu.VMEM((CAP, hidden), bf16),
                pltpu.VMEM((3, width, hidden), f32),
                pltpu.SemaphoreType.DMA((2,)),
                pltpu.SemaphoreType.DMA((3,)),
            ],
        ),
        compiler_params=pltpu.CompilerParams(
            dimension_semantics=("arbitrary",), vmem_limit_bytes=63 << 20
        ),
        cost_estimate=pl.CostEstimate(
            flops=number * 8 * 10**9, bytes_accessed=number * 14 * 10**6, transcendentals=0
        ),
    )(*args)
    return results[: len(numbers)], results[len(numbers) :]


PIECES = 16


def line_gather_kernel(n, x_ref, out_ref, blocks_ref, recv, up_send, down_send):
    me = lax.axis_index("tensor")
    has_low, has_high = me > 0, me < n - 1
    barrier = pltpu.get_barrier_semaphore()

    @pl.when(has_low)
    def _():
        pl.semaphore_signal(barrier, inc=1, device_id={"tensor": me - 1}, device_id_type=MESH)

    @pl.when(has_high)
    def _():
        pl.semaphore_signal(barrier, inc=1, device_id={"tensor": me + 1}, device_id_type=MESH)

    blocks_ref[me] = x_ref[...].astype(jnp.float32)
    pl.semaphore_wait(barrier, has_low.astype(jnp.int32) + has_high.astype(jnp.int32))
    rows = x_ref.shape[0] // PIECES

    def copy(block, c, send, to):
        piece = blocks_ref.at[block, pl.ds(pl.multiple_of(c * rows, rows), rows), :]
        return pltpu.make_async_remote_copy(
            src_ref=piece,
            dst_ref=piece,
            send_sem=send.at[block, c],
            recv_sem=recv.at[block, c],
            device_id={"tensor": to},
            device_id_type=MESH,
        )

    for hop in range(n):
        low, high = me - hop, me + hop

        def step(c, carry):
            @pl.when(low >= 0)
            def _():
                if hop > 0:
                    copy(low, c, up_send, me).wait_recv()

                @pl.when(has_high)
                def _():
                    copy(low, c, up_send, me + 1).start()

            @pl.when(high < n)
            def _():
                if hop > 0:
                    copy(high, c, down_send, me).wait_recv()

                @pl.when(has_low)
                def _():
                    copy(high, c, down_send, me - 1).start()

            return carry

        lax.fori_loop(0, PIECES, step, 0)
    wide = x_ref.shape[1]
    for block in range(n):
        out_ref[:, block * wide : (block + 1) * wide] = blocks_ref[block].astype(jnp.bfloat16)
    for hop in range(n):
        low, high = me - hop, me + hop

        def drain(c, carry):
            @pl.when((low >= 0) & has_high)
            def _():
                copy(low, c, up_send, me).wait_send()

            @pl.when((high < n) & has_low)
            def _():
                copy(high, c, down_send, me).wait_send()

            return carry

        lax.fori_loop(0, PIECES, drain, 0)


def line_gather(x, n, name):
    length, wide = x.shape
    full = pl.BlockSpec(memory_space=pltpu.VMEM)
    return pl.pallas_call(
        functools.partial(line_gather_kernel, n),
        out_shape=jax.ShapeDtypeStruct((length, n * wide), jnp.bfloat16),
        in_specs=[full],
        out_specs=full,
        scratch_shapes=[pltpu.VMEM((n, length, wide), jnp.float32)]
        + [pltpu.SemaphoreType.DMA((n, PIECES))] * 3,
        compiler_params=pltpu.CompilerParams(
            collective_id=name, has_side_effects=True, vmem_limit_bytes=32 << 20
        ),
        cost_estimate=pl.CostEstimate(
            flops=0, bytes_accessed=16 * n * x.size, transcendentals=0
        ),
    )(x)


BLOCK = 256


def own_rows_kernel(parts, weight_ref, out_ref):
    rows = out_ref.shape[0]
    first = lax.axis_index("dp") * rows if parts > 1 else 0
    out_ref[...] = weight_ref[pl.ds(pl.multiple_of(first, 16), rows), :].astype(jnp.float32)


def gather_out_weight(out_weight, parts):
    rows, width = out_weight.shape
    ways = parts if rows % (16 * parts) == 0 else 1
    full = pl.BlockSpec(memory_space=pltpu.VMEM)
    own = pl.pallas_call(
        functools.partial(own_rows_kernel, ways),
        out_shape=jax.ShapeDtypeStruct((rows // ways, width), jnp.float32),
        in_specs=[full],
        out_specs=full,
    )(out_weight)
    gathered = lax.all_gather(own, "tensor")
    return lax.all_gather(gathered, "dp") if ways > 1 else gathered[None]


def middle_kernel(
    attended_ref, weight_all_ref, tokens_ref, gain_ref, router_ref, chosen_ref, middle_out, normed_out, gates_out, weight_ref
):
    ways, n, rows, unused = weight_all_ref.shape
    for way in range(ways):
        for block in range(n):
            at = (block * ways + way) * rows
            weight_ref[at : at + rows, :] = weight_all_ref[way, block].astype(jnp.bfloat16)
    for first in range(0, tokens_ref.shape[0], BLOCK):
        own = slice(first, first + BLOCK)
        branch = jnp.dot(attended_ref[own, :], weight_ref[...], preferred_element_type=jnp.float32)
        middle = tokens_ref[own, :].astype(jnp.float32) + RESIDUAL * branch
        middle_out[own, :] = middle
        recip = lax.rsqrt(jnp.mean(middle * middle, axis=1, keepdims=True) + EPSILON)
        normed = (middle * recip * gain_ref[...]).astype(jnp.bfloat16)
        normed_out[own, :] = normed
        logits = jnp.dot(normed, router_ref[...], preferred_element_type=jnp.float32)
        raised = jnp.where(chosen_ref[own, :] > 0.0, jnp.exp(logits), 0.0)
        gates_out[own, :] = raised / jnp.sum(raised, axis=1, keepdims=True)


def enter_middle(attended, weight_all, tokens, gain, router, chosen):
    length, width = tokens.shape
    full = pl.BlockSpec(memory_space=pltpu.VMEM)
    return pl.pallas_call(
        middle_kernel,
        out_shape=[
            jax.ShapeDtypeStruct((length, width), jnp.float32),
            jax.ShapeDtypeStruct((length, width), jnp.bfloat16),
            jax.ShapeDtypeStruct((length, router.shape[1]), jnp.float32),
        ],
        in_specs=[full] * 6,
        out_specs=[full] * 3,
        scratch_shapes=[pltpu.VMEM((attended.shape[1], width), jnp.bfloat16)],
        compiler_params=pltpu.CompilerParams(vmem_limit_bytes=56 << 20),
        cost_estimate=pl.CostEstimate(
            flops=2 * length * width * width, bytes_accessed=25 * 10**6, transcendentals=0
        ),
    )(attended, weight_all, tokens, gain.reshape(1, width), router, chosen)


def turn_kernel(
    summed_ref, grad_gates_ref, gates_ref, middle_ref, cotangent_ref, gain_ref, router_ref, grad_out, branch_out, logits_out, gain_out
):
    length, width = summed_ref.shape
    experts = grad_gates_ref.shape[0]
    gates_rows = jnp.concatenate(
        [grad_gates_ref[...], jnp.zeros((128 - experts, length), jnp.float32)], 0
    )
    gain_sum = jnp.zeros((1, width), jnp.float32)
    for first in range(0, length, BLOCK):
        own = slice(first, first + BLOCK)
        grad_gates = jnp.transpose(gates_rows[:, own])
        gates = gates_ref[own, :]
        weighted = jnp.sum(gates * grad_gates, axis=1, keepdims=True)
        grad_logits = (gates * (grad_gates - weighted)).astype(jnp.bfloat16)
        logits_out[own, :] = grad_logits
        grad = summed_ref[own, :] + right_inner(grad_logits, router_ref[...])
        middle = middle_ref[own, :]
        recip = lax.rsqrt(jnp.mean(middle * middle, axis=1, keepdims=True) + EPSILON)
        unit = middle * recip
        gain_sum += jnp.sum(grad * unit, axis=0, keepdims=True)
        scaled = grad * gain_ref[...]
        back = recip * (scaled - unit * jnp.mean(scaled * unit, axis=1, keepdims=True))
        total = cotangent_ref[own, :].astype(jnp.float32) + back
        grad_out[own, :] = total
        branch_out[own, :] = (RESIDUAL * total).astype(jnp.bfloat16)
    gain_out[...] = gain_sum


def turn_middle(summed, grad_gates, gates, middle, cotangent, gain, router):
    length, width = summed.shape
    full = pl.BlockSpec(memory_space=pltpu.VMEM)
    return pl.pallas_call(
        turn_kernel,
        out_shape=[
            jax.ShapeDtypeStruct((length, width), jnp.float32),
            jax.ShapeDtypeStruct((length, width), jnp.bfloat16),
            jax.ShapeDtypeStruct((length, gates.shape[1]), jnp.bfloat16),
            jax.ShapeDtypeStruct((1, width), jnp.float32),
        ],
        in_specs=[full] * 7,
        out_specs=[full] * 4,
        compiler_params=pltpu.CompilerParams(vmem_limit_bytes=48 << 20),
        cost_estimate=pl.CostEstimate(
            flops=40 * length * width, bytes_accessed=25 * 10**6, transcendentals=0
        ),
    )(summed, grad_gates, gates, middle, cotangent, gain.reshape(1, width), router)


SPAN = 768
ROWS = 256


def lane_halves(shape):
    return lax.broadcasted_iota(jnp.int32, shape, len(shape) - 1) // HEAD


def select_halves(tile, source, half):
    kept = jnp.where(lane_halves(tile.shape) == source, tile, 0.0)
    return kept if source == half else pltpu.roll(kept, HEAD, 1)


def spread_pairs(tile, target):
    for source in range(2):
        for half in range(2):
            target[2 * source + half] = select_halves(tile, source, half).astype(jnp.bfloat16)


def rope_tile(tile, cosine, sine_low, sine_high):
    return tile * cosine + pltpu.roll(tile, 128 - HEAD // 2, 1) * sine_low + pltpu.roll(
        tile, HEAD // 2, 1
    ) * sine_high


def rope_back_tile(tile, cosine, sine_low, sine_high):
    return (
        tile * cosine
        + pltpu.roll(tile * sine_low, HEAD // 2, 1)
        + pltpu.roll(tile * sine_high, 128 - HEAD // 2, 1)
    )


def window(block):
    first = block * ROWS
    return first, jnp.maximum(first + ROWS - SPAN, 0)


def attend_forward_kernel(
    heads,
    group,
    tokens_ref,
    gain_ref,
    query_w,
    key_w,
    value_w,
    cosine_ref,
    sine_low_ref,
    sine_high_ref,
    opening_ref,
    normed_out,
    query_out,
    key_out,
    value_out,
    attended_out,
    logsum_out,
    key_pairs,
    value_pairs,
    tiles_ref,
):
    tiles, length, unused = query_out.shape
    hidden = tokens_ref[...].astype(jnp.float32)
    recip = lax.rsqrt(jnp.mean(hidden * hidden, axis=1, keepdims=True) + EPSILON)
    normed_out[...] = (hidden * recip * gain_ref[...]).astype(jnp.bfloat16)
    cosine, sine_low, sine_high = cosine_ref[...], sine_low_ref[...], sine_high_ref[...]
    for tile in range(tiles):
        query = jnp.dot(
            normed_out[...],
            query_w[:, tile * 128 : (tile + 1) * 128],
            preferred_element_type=jnp.float32,
        )
        query_out[tile] = rope_tile(query, cosine, sine_low, sine_high).astype(jnp.bfloat16)
    key = rope_tile(
        jnp.dot(normed_out[...], key_w[...], preferred_element_type=jnp.float32),
        cosine,
        sine_low,
        sine_high,
    )
    value = jnp.dot(normed_out[...], value_w[...], preferred_element_type=jnp.float32)
    key_out[...] = key.astype(jnp.bfloat16)
    value_out[...] = value.astype(jnp.bfloat16)
    spread_pairs(key, key_pairs)
    spread_pairs(value, value_pairs)
    blocks = length // ROWS
    tiles_ref[...] = jnp.zeros_like(tiles_ref)

    def unit(step, carry):
        head, block = step // blocks, step % blocks
        tile, half = head // 2, head % 2
        pair = 2 * (head // group) + half
        first, low = window(block)
        rows = pl.ds(pl.multiple_of(first, ROWS), ROWS)
        span = pl.ds(pl.multiple_of(low, ROWS), SPAN)
        scores = right_inner(query_out[tile, rows, :], key_pairs[pair, span, :])
        columns = low + lax.broadcasted_iota(jnp.int32, (ROWS, SPAN), 1)
        own = first + lax.broadcasted_iota(jnp.int32, (ROWS, SPAN), 0)
        allowed = (columns >= opening_ref[rows, :]) & (columns <= own)
        raised = jnp.where(allowed, jnp.exp(ATTN_SCALE * scores), 0.0)
        total = jnp.sum(raised, axis=1, keepdims=True)
        product = jnp.dot(
            raised.astype(jnp.bfloat16), value_pairs[pair, span, :], preferred_element_type=jnp.float32
        )
        tiles_ref[tile, rows, :] += product / total
        wide = jnp.broadcast_to(jnp.log(total), (ROWS, 128))
        logsum_out[head, :, rows] = jnp.transpose(wide)[:1]
        return carry

    lax.fori_loop(0, heads * blocks, unit, 0)
    for tile in range(tiles):
        attended_out[:, tile * 128 : (tile + 1) * 128] = tiles_ref[tile].astype(jnp.bfloat16)


def attend_forward(tokens, gain, query_w, key_w, value_w, tables, opening, heads, group):
    length, width = tokens.shape
    wide = query_w.shape[1]
    tiles = wide // 128
    bf16, f32 = jnp.bfloat16, jnp.float32
    full = pl.BlockSpec(memory_space=pltpu.VMEM)
    return pl.pallas_call(
        functools.partial(attend_forward_kernel, heads, group),
        out_shape=[
            jax.ShapeDtypeStruct((length, width), bf16),
            jax.ShapeDtypeStruct((tiles, length, 128), bf16),
            jax.ShapeDtypeStruct((length, 128), bf16),
            jax.ShapeDtypeStruct((length, 128), bf16),
            jax.ShapeDtypeStruct((length, wide), bf16),
            jax.ShapeDtypeStruct((heads, 1, length), f32),
        ],
        in_specs=[full] * 9,
        out_specs=[full] * 6,
        scratch_shapes=[
            pltpu.VMEM((4, length, 128), bf16),
            pltpu.VMEM((4, length, 128), bf16),
            pltpu.VMEM((tiles, length, 128), f32),
        ],
        compiler_params=pltpu.CompilerParams(vmem_limit_bytes=48 << 20),
        cost_estimate=pl.CostEstimate(
            flops=8 * 10**9, bytes_accessed=12 * 10**6, transcendentals=5 * 10**6
        ),
    )(tokens, gain.reshape(1, width), query_w, key_w, value_w, *tables, opening.reshape(length, 1))


def attend_backward_kernel(
    n,
    heads,
    group,
    branch_ref,
    out_w,
    query_ref,
    key_ref,
    value_ref,
    attended_ref,
    logsum_ref,
    query_w,
    key_w,
    value_w,
    cosine_ref,
    sine_low_ref,
    sine_high_ref,
    opening_ref,
    moe_ref,
    grads_out,
    normed_out,
    moe_out,
    key_pairs,
    value_pairs,
    attend_grads,
    query_grads,
    key_grads,
    value_grads,
    delta_ref,
    *line,
):
    tiles, length, unused = query_ref.shape
    line_start, line_step, line_end = line_stages(n, [moe_ref], [moe_out], line)
    line_start()
    spread_pairs(key_ref[...].astype(jnp.float32), key_pairs)
    spread_pairs(value_ref[...].astype(jnp.float32), value_pairs)
    halves = (
        lax.broadcasted_iota(jnp.int32, (8, 128), 0) == lane_halves((8, 128))
    ).astype(jnp.float32)
    for tile in range(tiles):
        lanes = slice(tile * 128, (tile + 1) * 128)
        grad = right_inner(branch_ref[...], out_w[lanes, :]).astype(jnp.bfloat16)
        attend_grads[tile] = grad
        products = grad.astype(jnp.float32) * attended_ref[:, lanes].astype(jnp.float32)
        sums = lax.dot_general(
            halves,
            products,
            (((1,), (1,)), ((), ())),
            precision=lax.Precision.HIGHEST,
            preferred_element_type=jnp.float32,
        )
        delta_ref[2 * tile] = sums[0:1]
        delta_ref[2 * tile + 1] = sums[1:2]
    query_grads[...] = jnp.zeros_like(query_grads)
    key_grads[...] = jnp.zeros_like(key_grads)
    value_grads[...] = jnp.zeros_like(value_grads)
    blocks = length // ROWS
    units = heads * blocks
    each = -(-2 * STEPS // units)

    def unit(step, carry):
        lax.fori_loop(step * each, step * each + each, line_step, 0)
        head, block = step // blocks, step % blocks
        tile, half = head // 2, head % 2
        pair = 2 * (head // group) + half
        first, low = window(block)
        rows = pl.ds(pl.multiple_of(first, ROWS), ROWS)
        span = pl.ds(pl.multiple_of(low, ROWS), SPAN)
        keys = key_pairs[pair, span, :]
        query = query_ref[tile, rows, :]
        grad = attend_grads[tile, rows, :]
        scores = right_inner(keys, query)
        columns = low + lax.broadcasted_iota(jnp.int32, (SPAN, ROWS), 0)
        own = first + lax.broadcasted_iota(jnp.int32, (SPAN, ROWS), 1)
        allowed = (columns >= opening_ref[:, rows]) & (columns <= own)
        probs = jnp.where(
            allowed, jnp.exp(ATTN_SCALE * scores - logsum_ref[head, :, rows]), 0.0
        )
        grad_probs = right_inner(value_pairs[pair, span, :], grad)
        grad_scores = (probs * (grad_probs - delta_ref[head, :, rows])).astype(jnp.bfloat16)
        value_grads[pair, span, :] += jnp.dot(
            probs.astype(jnp.bfloat16), grad, preferred_element_type=jnp.float32
        )
        key_grads[pair, span, :] += jnp.dot(
            grad_scores, query, preferred_element_type=jnp.float32
        )
        query_grads[tile, rows, :] += left_inner(grad_scores, keys)
        return carry

    lax.fori_loop(0, units, unit, 0)
    cosine, sine_low, sine_high = cosine_ref[...], sine_low_ref[...], sine_high_ref[...]
    wide = tiles * 128
    for tile in range(tiles):
        grads_out[:, tile * 128 : (tile + 1) * 128] = rope_back_tile(
            ATTN_SCALE * query_grads[tile], cosine, sine_low, sine_high
        ).astype(jnp.bfloat16)
    totals = []
    for grads in (key_grads, value_grads):
        totals.append(
            sum(
                select_halves(grads[2 * source + half], half, source)
                for source in range(2)
                for half in range(2)
            )
        )
    grads_out[:, wide : wide + 128] = rope_back_tile(
        ATTN_SCALE * totals[0], cosine, sine_low, sine_high
    ).astype(jnp.bfloat16)
    grads_out[:, wide + 128 : wide + 256] = totals[1].astype(jnp.bfloat16)
    normed_out[...] = (
        right_inner(grads_out[:, :wide], query_w[...])
        + right_inner(grads_out[:, wide : wide + 128], key_w[...])
        + right_inner(grads_out[:, wide + 128 :], value_w[...])
    )
    line_end()


def attend_backward(
    n, branch, out_w, query, key, value, attended, logsum, query_w, key_w, value_w, tables, opening, moe,
    heads, group, name,
):
    length, width = branch.shape
    tiles = query.shape[0]
    wide = tiles * 128
    bf16, f32 = jnp.bfloat16, jnp.float32
    full = pl.BlockSpec(memory_space=pltpu.VMEM)
    return pl.pallas_call(
        functools.partial(attend_backward_kernel, n, heads, group),
        out_shape=[
            jax.ShapeDtypeStruct((length, wide + 256), bf16),
            jax.ShapeDtypeStruct((length, width), f32),
            jax.ShapeDtypeStruct((length, width), f32),
        ],
        in_specs=[full] * 15,
        out_specs=[full] * 3,
        scratch_shapes=[
            pltpu.VMEM((4, length, 128), bf16),
            pltpu.VMEM((4, length, 128), bf16),
            pltpu.VMEM((tiles, length, 128), bf16),
            pltpu.VMEM((tiles, length, 128), f32),
            pltpu.VMEM((4, length, 128), f32),
            pltpu.VMEM((4, length, 128), f32),
            pltpu.VMEM((2 * tiles, 1, length), f32),
        ]
        + line_scratch([moe]),
        compiler_params=pltpu.CompilerParams(
            collective_id=name, has_side_effects=True, vmem_limit_bytes=60 << 20
        ),
        cost_estimate=pl.CostEstimate(
            flops=12 * 10**9, bytes_accessed=30 * 10**6, transcendentals=5 * 10**6
        ),
    )(
        branch, out_w, query, key, value, attended, logsum, query_w, key_w, value_w, *tables,
        opening.reshape(1, length), moe,
    )


def finish_kernel(
    n,
    parts,
    local_ref,
    normed_ref,
    grads_ref,
    branch_ref,
    attended_ref,
    normed_two_ref,
    logits_ref,
    gain_ref,
    normed_out,
    shard_out,
    weights_ref,
    *scratch,
):
    levels = parts.bit_length() - 1
    held = scratch[:levels]
    sends, recvs = scratch[levels : levels + 2]
    line_start, line_step, line_end = line_stages(n, [local_ref], [normed_out], scratch[levels + 2 :])
    me = lax.axis_index("dp")
    width = normed_ref.shape[1]
    own = width // parts
    wide, attended_wide = grads_ref.shape[1], attended_ref.shape[1]
    line_start([{"dp": jnp.bitwise_xor(me, 1 << level)} for level in range(levels)])

    def run_line(first, last):
        lax.fori_loop(first, last, line_step, 0)

    run_line(0, 2)
    pieces = 4
    block = width // pieces
    for piece in range(pieces):
        rows = slice(piece * block, (piece + 1) * block)
        weights_ref[rows, :wide] = left_inner(normed_ref[:, rows], grads_ref[...])
        weights_ref[rows, wide : wide + attended_wide] = left_inner(
            branch_ref[:, rows], attended_ref[...]
        )
        gain = jnp.transpose(jnp.broadcast_to(gain_ref[:, rows], (128, block)))
        lanes = lax.broadcasted_iota(jnp.int32, (block, 128), 1)
        weights_ref[rows, wide + attended_wide :] = jnp.where(
            lanes == 127, gain, left_inner(normed_two_ref[:, rows], logits_ref[...])
        )
        run_line(2 + 2 * piece, 4 + 2 * piece)
    done = 2 + 2 * pieces

    def shard(number):
        return weights_ref.at[pl.ds(pl.multiple_of(number * own, own), own), :]

    def copies(level):
        peer = jnp.bitwise_xor(me, 1 << level)
        low = jnp.bitwise_and(peer, (2 << level) - 1)
        return [
            pltpu.make_async_remote_copy(
                src_ref=shard(low + (i << (level + 1))),
                dst_ref=held[level].at[i],
                send_sem=sends.at[level, i],
                recv_sem=recvs.at[level, i],
                device_id={"dp": peer},
                device_id_type=MESH,
            )
            for i in range(parts >> (level + 1))
        ]

    stops = [6, 26, 16, 4]
    for level in range(levels):
        for copy in copies(level):
            copy.start()
        until = done + stops[level]
        run_line(done, until)
        done = until
        kept = jnp.bitwise_and(me, (2 << level) - 1)
        for i, copy in enumerate(copies(level)):
            copy.wait_recv()
            target = shard(kept + (i << (level + 1)))
            target[...] += held[level][i]
    run_line(done, 2 * STEPS)
    shard_out[...] = shard(me)[...]
    for level in range(levels):
        for copy in copies(level):
            copy.wait_send()
    line_end()


def finish(n, parts, grad_local, normed_b, grads_wide, branch_b, attended, normed_two_b, grad_logits_b, ffn_gain_grad, name):
    length, width = normed_b.shape
    columns = grads_wide.shape[1] + attended.shape[1] + 128
    full = pl.BlockSpec(memory_space=pltpu.VMEM)
    levels = parts.bit_length() - 1
    own = width // parts
    f32 = jnp.float32
    return pl.pallas_call(
        functools.partial(finish_kernel, n, parts),
        out_shape=[
            jax.ShapeDtypeStruct((length, width), f32),
            jax.ShapeDtypeStruct((own, columns), f32),
        ],
        in_specs=[full] * 8,
        out_specs=[full] * 2,
        scratch_shapes=[pltpu.VMEM((width, columns), f32)]
        + [pltpu.VMEM((parts >> (level + 1), own, columns), f32) for level in range(levels)]
        + [pltpu.SemaphoreType.DMA((levels, parts // 2))] * 2
        + line_scratch([grad_local]),
        compiler_params=pltpu.CompilerParams(
            collective_id=name, has_side_effects=True, vmem_limit_bytes=60 << 20
        ),
        cost_estimate=pl.CostEstimate(
            flops=2 * length * width * columns, bytes_accessed=50 * 10**6, transcendentals=0
        ),
    )(
        grad_local, normed_b, grads_wide, branch_b, attended, normed_two_b, grad_logits_b,
        ffn_gain_grad,
    )


def place_kernel(shards_ref, *refs):
    gate_out, up_out, down_out = refs[-3:]
    gate_out[0] = shards_ref[0, 0]
    up_out[0] = shards_ref[0, 1]
    rows, hidden = down_out.shape[1], shards_ref.shape[3]
    for piece in range(down_out.shape[2] // hidden):
        down_out[0, :, piece * hidden : (piece + 1) * hidden] = shards_ref[
            0, 2, piece * rows : (piece + 1) * rows, :
        ]


def place_shards(parts, shards, first, experts, before):
    number, unused, rows, hidden = shards.shape
    down_rows = hidden // parts
    width = rows * parts
    shapes = [(experts, rows, hidden), (experts, rows, hidden), (experts, down_rows, width)]
    spec = lambda shape: pl.BlockSpec((1,) + shape[1:], lambda e: (first + e, 0, 0))
    args, extra, aliases = [shards], [], {}
    if before is not None:
        args += list(before)
        extra = [pl.BlockSpec(memory_space=pl.ANY)] * 3
        aliases = {1: 0, 2: 1, 3: 2}
    return pl.pallas_call(
        place_kernel,
        out_shape=[jax.ShapeDtypeStruct(shape, jnp.float32) for shape in shapes],
        grid=(number,),
        in_specs=[pl.BlockSpec((1, 3, rows, hidden), lambda e: (e, 0, 0, 0))] + extra,
        out_specs=[spec(shape) for shape in shapes],
        input_output_aliases=aliases,
        cost_estimate=pl.CostEstimate(
            flops=0, bytes_accessed=8 * shards.size, transcendentals=0
        ),
    )(*args)


def on_device(
    ring,
    tokens,
    cotangent,
    segment_ids,
    routes,
    attn_gain,
    query_weight,
    key_weight,
    value_weight,
    out_weight,
    ffn_gain,
    router_weight,
    gate_weight,
    up_weight,
    down_weight,
):
    length = tokens.shape[0]
    width = tokens.shape[1]
    segment = segment_ids[0]
    heads_local = query_weight.shape[1] // HEAD
    kv_local = key_weight.shape[1] // HEAD
    group_size = heads_local // kv_local
    experts_all = router_weight.shape[1]
    experts_local = gate_weight.shape[0]
    parts = lax.axis_size("dp")
    opening = doc_openings(segment)
    tables = rope_tables(opening, HEAD)
    query_w, key_w, value_w = (pad_columns(w) for w in (query_weight, key_weight, value_weight))
    out_w = jnp.transpose(pad_columns(jnp.transpose(out_weight)))
    hidden_in = tokens.astype(jnp.float32)
    out_all = gather_out_weight(out_weight, parts)
    normed_b, queries, keys, values, attended, logsum = attend_forward(
        tokens, attn_gain, query_w, key_w, value_w, tables, opening, heads_local, group_size
    )
    all_ids = jnp.arange(experts_all, dtype=jnp.int32)
    chosen = jnp.sum((routes[:, :, None] == all_ids[None, None, :]).astype(jnp.int32), axis=1) > 0
    first_expert = lax.axis_index("tensor") * experts_local
    local_ids = first_expert + jnp.arange(experts_local, dtype=jnp.int32)
    picked = jnp.sum((routes[None, :, :] == local_ids[:, None, None]).astype(jnp.int32), axis=2)
    places_in = slot_places(picked)
    counts = jnp.sum(picked, axis=1)
    grad_moe_b = (RESIDUAL * cotangent.astype(jnp.float32)).astype(jnp.bfloat16)
    attended_all = line_gather(attended, ring, 1)
    attended_all = attended_all.reshape(length, ring, attended.shape[1])
    attended_all = attended_all[:, :, : heads_local * HEAD].reshape(length, -1)
    router_w = pad_columns(router_weight)
    middle, normed_two_b, gate_probs = enter_middle(
        attended_all, out_all, tokens, ffn_gain, router_w, pad_columns(chosen.astype(jnp.float32))
    )
    gate_rows = jnp.transpose(lax.dynamic_slice_in_dim(gate_probs, first_expert, experts_local, 1))
    numbers = (max(1, experts_local // 5), max(1, 3 * experts_local // 10))
    numbers += (experts_local - sum(numbers),)
    (grads_first,), sums = expert_stage(
        parts, 0, numbers[:1], counts, places_in, gate_rows, normed_two_b, grad_moe_b,
        gate_weight, up_weight, down_weight, None,
    )
    shards_first = lax.psum_scatter(grads_first, "dp", scatter_dimension=2, tiled=True)
    (grads_middle, grads_last), sums_last = expert_stage(
        parts, numbers[0], numbers[1:], counts, places_in, gate_rows, normed_two_b, grad_moe_b,
        gate_weight, up_weight, down_weight, sums,
    )
    shards_first, grads_middle = lax.optimization_barrier((shards_first, grads_middle))
    shards_middle = lax.psum_scatter(grads_middle, "dp", scatter_dimension=2, tiled=True)
    moe_part, grad_normed_part, unused = sums_last
    grad_gates_local = jnp.concatenate([sums[2], sums_last[2]], 0)
    grad_gates_part = lax.dynamic_update_slice_in_dim(
        jnp.zeros((experts_all, length), jnp.float32),
        grad_gates_local.reshape(experts_local, length),
        first_expert,
        0,
    ).reshape(-1, 128)
    grad_gates_part = jnp.pad(grad_gates_part, ((0, GATE_ROWS - grad_gates_part.shape[0]), (0, 0)))
    shards_first, grad_normed_part = lax.optimization_barrier((shards_first, grad_normed_part))
    grad_normed_sum, gates_sum = line_sum(grad_normed_part, grad_gates_part, ring, 2)
    grad_gates = gates_sum[: experts_all * length // 128].reshape(experts_all, length)
    grad_middle, grad_branch_b, grad_logits_b, grad_ffn_gain = turn_middle(
        grad_normed_sum, grad_gates, gate_probs, middle, cotangent, ffn_gain, router_w
    )
    shards_middle, grads_last, grad_branch_b = lax.optimization_barrier(
        (shards_middle, grads_last, grad_branch_b)
    )
    shards_last = lax.psum_scatter(grads_last, "dp", scatter_dimension=2, tiled=True)
    grads_wide, grad_normed_local, moe_out = attend_backward(
        ring, grad_branch_b, out_w, queries, keys, values, attended, logsum,
        query_w, key_w, value_w, tables, opening, moe_part, heads_local, group_size, 3,
    )
    output = (middle + RESIDUAL * moe_out).astype(jnp.bfloat16)
    grad_normed, small = finish(
        ring, parts, grad_normed_local, normed_b, grads_wide, grad_branch_b, attended, normed_two_b,
        grad_logits_b, grad_ffn_gain, 4,
    )
    recip_one = lax.rsqrt(jnp.mean(hidden_in * hidden_in, axis=-1, keepdims=True) + EPSILON)
    unit_one = hidden_in * recip_one
    grad_from_first, grad_attn_gain = rms_backward(grad_normed, unit_one, recip_one, attn_gain)
    grad_tokens = grad_middle + grad_from_first
    grad_attn_gain = lax.psum_scatter(grad_attn_gain, "dp", scatter_dimension=0, tiled=True)
    shards_last, grad_attn_gain = lax.optimization_barrier((shards_last, grad_attn_gain))
    tiled_q = query_w.shape[1]
    wide_q, wide_k = heads_local * HEAD, kv_local * HEAD
    at_out = tiled_q + 256
    at_router = at_out + tiled_q
    grads_placed = place_shards(parts, shards_first, 0, experts_local, None)
    grads_placed = place_shards(parts, shards_middle, numbers[0], experts_local, grads_placed)
    grad_gate, grad_up, grad_down = place_shards(
        parts, shards_last, numbers[0] + numbers[1], experts_local, grads_placed
    )
    return (
        output,
        grad_tokens,
        grad_attn_gain,
        small[:, :wide_q],
        small[:, tiled_q : tiled_q + wide_k],
        small[:, tiled_q + 128 : tiled_q + 128 + wide_k],
        jnp.transpose(small[:, at_out : at_out + wide_q]),
        small[:, at_router + 127],
        small[:, at_router : at_router + experts_all],
        grad_gate,
        grad_up,
        grad_down,
    )


def solution(mesh):
    return jax.shard_map(
        functools.partial(on_device, mesh.shape["tensor"]),
        mesh=mesh,
        in_specs=(
            P("dp", None),
            P("dp", None),
            P("dp", None),
            P("dp", None),
            P(),
            P(None, "tensor"),
            P(None, "tensor"),
            P(None, "tensor"),
            P("tensor", None),
            P(),
            P(),
            P("tensor", None, None),
            P("tensor", None, None),
            P("tensor", None, None),
        ),
        out_specs=(
            P("dp", None),
            P("dp", None),
            P("dp"),
            P("dp", "tensor"),
            P("dp", "tensor"),
            P("dp", "tensor"),
            P("tensor", "dp"),
            P("dp"),
            P("dp", None),
            P("tensor", "dp", None),
            P("tensor", "dp", None),
            P("tensor", "dp", None),
        ),
        check_vma=False,
    )
```

```python
import functools

import jax
import jax.numpy as jnp
from jax import lax
from jax.experimental import pallas as pl
from jax.experimental.pallas import tpu as pltpu
from jax.sharding import PartitionSpec as P

MESH = pl.DeviceIdType.MESH

HEAD = 64
CAP = 384


EPSILON = 1e-06
RESIDUAL = 0.22
ATTN_SCALE = 0.015625
ROPE_BASE = 10000.0


def left_inner(first, second):
    return lax.dot_general(
        first, second, (((0,), (0,)), ((), ())), preferred_element_type=jnp.float32
    )


def right_inner(first, second):
    return lax.dot_general(
        first, second, (((1,), (1,)), ((), ())), preferred_element_type=jnp.float32
    )


def doc_openings(segment):
    return jnp.sum((segment[None, :] < segment[:, None]).astype(jnp.int32), axis=1)


def rope_tables(opening, head_size):
    halfway = head_size // 2
    spread = jnp.arange(halfway, dtype=jnp.float32) * (2.0 / head_size)
    inverse = jnp.power(ROPE_BASE, -spread)
    places = jnp.arange(opening.shape[0], dtype=jnp.int32)
    angles = (places - opening).astype(jnp.float32)[:, None] * inverse[None, :]
    cosine, sine = jnp.cos(angles), jnp.sin(angles)
    none = jnp.zeros_like(sine)
    return (
        jnp.concatenate([cosine] * 4, 1),
        jnp.concatenate([-sine, none] * 2, 1),
        jnp.concatenate([none, sine] * 2, 1),
    )


def pad_columns(weight):
    missing = -weight.shape[1] % 128
    return weight if missing == 0 else jnp.pad(weight, ((0, 0), (0, missing)))


def rms_forward(hidden, gain):
    recip = lax.rsqrt(jnp.mean(hidden * hidden, axis=-1, keepdims=True) + EPSILON)
    unit = hidden * recip
    return (unit * gain, unit, recip)


def rms_backward(gradient, unit, recip, gain):
    gain_grad = jnp.sum(gradient * unit, axis=0)
    scaled = gradient * gain
    return (recip * (scaled - unit * jnp.mean(scaled * unit, axis=-1, keepdims=True)), gain_grad)


def slot_places(picked):
    length = picked.shape[1]
    tokens = jnp.arange(length, dtype=jnp.int32)
    earlier = (tokens[:, None] < tokens[None, :]).astype(jnp.bfloat16)
    before = jnp.dot(picked.astype(jnp.bfloat16), earlier, preferred_element_type=jnp.float32)
    return jnp.where(picked > 0, before.astype(jnp.int32), -1)


STEPS = 32
LAG = 2
GATE_ROWS = 512


def line_stages(n, xs, outs, scratch):
    count = len(xs)
    lows, highs = scratch[:count], scratch[count : 2 * count]
    low_recv, high_recv, total_recv, up_send, low_send, high_send = scratch[2 * count :]
    me = lax.axis_index("tensor")
    root = n // 2
    has_low, has_high = me > 0, me < n - 1

    def begin(others=()):
        barrier = pltpu.get_barrier_semaphore()
        for other in others:
            pl.semaphore_signal(barrier, inc=1, device_id=other, device_id_type=MESH)

        @pl.when(has_low)
        def _():
            pl.semaphore_signal(barrier, inc=1, device_id={"tensor": me - 1}, device_id_type=MESH)

        @pl.when(has_high)
        def _():
            pl.semaphore_signal(barrier, inc=1, device_id={"tensor": me + 1}, device_id_type=MESH)

        pl.semaphore_wait(
            barrier, len(others) + has_low.astype(jnp.int32) + has_high.astype(jnp.int32)
        )

    def piece(ref, c):
        rows = ref.shape[0] // STEPS
        return ref.at[pl.ds(pl.multiple_of(c * rows, rows), rows), :]

    def copies(sources, targets, c, send, recv, to):
        return [
            pltpu.make_async_remote_copy(
                src_ref=piece(source, c),
                dst_ref=piece(target, c),
                send_sem=send.at[i, c],
                recv_sem=recv.at[i, c],
                device_id={"tensor": to},
                device_id_type=MESH,
            )
            for i, (source, target) in enumerate(zip(sources, targets))
        ]

    def start(sources, targets, c, send, recv, to):
        for copy in copies(sources, targets, c, send, recv, to):
            copy.start()

    def arrived(targets, c, send, recv):
        for copy in copies(targets, targets, c, send, recv, me):
            copy.wait_recv()

    def reduce_step(c):
        for side, inner, held, recv, to in (
            (me < root, has_low, lows, low_recv, me + 1),
            (me > root, has_high, highs, high_recv, me - 1),
        ):

            @pl.when(side & inner)
            def _():
                arrived(held, c, up_send, recv)
                for x, h in zip(xs, held):
                    piece(h, c)[...] += piece(x, c)[...]
                start(held, held, c, up_send, recv, to)

            @pl.when(side & jnp.logical_not(inner))
            def _():
                start(xs, held, c, up_send, recv, to)

        @pl.when(me == root)
        def _():
            arrived(lows, c, up_send, low_recv)
            if root < n - 1:
                arrived(highs, c, up_send, high_recv)
            for x, low, high, out in zip(xs, lows, highs, outs):
                total = piece(x, c)[...] + piece(low, c)[...]
                if root < n - 1:
                    total += piece(high, c)[...]
                piece(out, c)[...] = total
            start(outs, outs, c, low_send, total_recv, me - 1)
            if root < n - 1:
                start(outs, outs, c, high_send, total_recv, me + 1)

    def total_step(c):
        @pl.when(me != root)
        def _():
            arrived(outs, c, low_send, total_recv)

        @pl.when((me < root) & has_low)
        def _():
            start(outs, outs, c, low_send, total_recv, me - 1)

        @pl.when((me > root) & has_high)
        def _():
            start(outs, outs, c, high_send, total_recv, me + 1)

    lag = jnp.where(has_low & has_high, LAG, STEPS)

    def step(t, carry):
        @pl.when(t < STEPS)
        def _():
            reduce_step(t)

        @pl.when((t >= lag) & (t - lag < STEPS))
        def _():
            total_step(t - lag)

        return carry

    def finish():
        def drain(c, carry):
            for condition, send in (
                (me != root, up_send),
                ((me <= root) & has_low, low_send),
                ((me >= root) & has_high, high_send),
            ):

                @pl.when(condition)
                def _():
                    for copy in copies(xs, lows, c, send, low_recv, me):
                        copy.wait_send()

            return carry

        lax.fori_loop(0, STEPS, drain, 0)

    return begin, step, finish


def line_scratch(arrays):
    return [pltpu.VMEM(array.shape, jnp.float32) for array in arrays * 2] + [
        pltpu.SemaphoreType.DMA((len(arrays), STEPS))
    ] * 6


def line_sum_kernel(n, count, *refs):
    begin, step, finish = line_stages(n, refs[:count], refs[count : 2 * count], refs[2 * count :])
    begin()
    lax.fori_loop(0, 2 * STEPS, step, 0)
    finish()


def line_sum(x, extra, n, name):
    arrays = [x] if extra is None else [x, extra]
    count = len(arrays)
    shapes = [jax.ShapeDtypeStruct(array.shape, jnp.float32) for array in arrays]
    size = sum(array.size for array in arrays)
    results = pl.pallas_call(
        functools.partial(line_sum_kernel, n, count),
        out_shape=shapes,
        in_specs=[pl.BlockSpec(memory_space=pltpu.VMEM)] * count,
        out_specs=[pl.BlockSpec(memory_space=pltpu.VMEM)] * count,
        scratch_shapes=line_scratch(arrays),
        compiler_params=pltpu.CompilerParams(
            collective_id=name, has_side_effects=True, vmem_limit_bytes=40 << 20
        ),
        cost_estimate=pl.CostEstimate(
            flops=3 * size, bytes_accessed=8 * size, transcendentals=0
        ),
    )(*arrays)
    return (results[0], None) if extra is None else tuple(results)


def expert_kernel(
    parts,
    first,
    numbers,
    chained,
    count_ref,
    place_ref,
    gate_ref,
    normed_ref,
    grad_ref,
    gate_w,
    up_w,
    down_w,
    *refs,
):
    if chained:
        moe_in, back_in = refs[:2]
        refs = refs[2:]
    grads_out, refs = refs[: len(numbers)], refs[len(numbers) :]
    moe_out, back_out, gates_out = refs[:3]
    rows_ref, grads_ref, active_ref, gate_in_ref, up_in_ref, weights_ref, sems, out_sems = refs[3:]
    expert = pl.program_id(0)
    filled = count_ref[first + expert]
    length, width = normed_ref.shape
    hidden_size = gate_w.shape[2]
    sizes = (128, 192, 256, 320, CAP)

    def by_size(run):
        low = None
        for rows in sizes:
            fits = filled <= rows if low is None else filled > low
            if low is not None and rows != sizes[-1]:
                fits = fits & (filled <= rows)
            pl.when(fits)(functools.partial(run, rows))
            low = rows

    if chained:
        copy_moe = pltpu.make_async_copy(moe_in, moe_out, sems.at[0])
        copy_back = pltpu.make_async_copy(back_in, back_out, sems.at[1])

        @pl.when(expert == 0)
        def _():
            copy_moe.start()
            copy_back.start()

    else:

        @pl.when(expert == 0)
        def _():
            moe_out[...] = jnp.zeros_like(moe_out)
            back_out[...] = jnp.zeros_like(back_out)

    def slots(rows):
        mask = lax.broadcasted_iota(jnp.int32, (rows, length), 0) == place_ref[0]
        return mask, jnp.where(mask, 1.0, 0.0).astype(jnp.bfloat16)

    def enter(rows):
        mask, picks = slots(rows)
        rows_in = jnp.dot(picks, normed_ref[...], preferred_element_type=jnp.float32).astype(jnp.bfloat16)
        grad_rows = (
            RESIDUAL * jnp.dot(picks, grad_ref[...], preferred_element_type=jnp.float32)
        ).astype(jnp.bfloat16)
        rows_ref[:rows] = rows_in
        grads_ref[:rows] = grad_rows
        gate = jnp.sum(jnp.where(mask, gate_ref[0], 0.0), axis=1, keepdims=True)
        gate_input = jnp.dot(rows_in, gate_w[0], preferred_element_type=jnp.float32)
        up_input = jnp.dot(rows_in, up_w[0], preferred_element_type=jnp.float32)
        grad_act = right_inner(grad_rows, down_w[0])
        sigmoid_val = jax.nn.sigmoid(gate_input)
        silu_out = gate_input * sigmoid_val
        hidden = silu_out * up_input
        active_ref[:rows] = (hidden * gate).astype(jnp.bfloat16)
        column = jnp.sum(grad_act * hidden, axis=1, keepdims=True)
        gates_out[0] = jnp.sum(jnp.where(mask, column, 0.0), axis=0, keepdims=True)
        grad_hidden = grad_act * gate
        gate_in_ref[:rows] = (
            grad_hidden * up_input * sigmoid_val * (1.0 + gate_input * (1.0 - sigmoid_val))
        ).astype(jnp.bfloat16)
        up_in_ref[:rows] = (grad_hidden * silu_out).astype(jnp.bfloat16)

    by_size(enter)
    if chained:

        @pl.when(expert == 0)
        def _():
            copy_moe.wait()
            copy_back.wait()

    def leave(rows):
        mask, picks = slots(rows)
        moe = jnp.dot(active_ref[:rows], down_w[0], preferred_element_type=jnp.float32)
        moe_out[...] += left_inner(picks, moe.astype(jnp.bfloat16))
        back = right_inner(gate_in_ref[:rows], gate_w[0]) + right_inner(up_in_ref[:rows], up_w[0])
        back_out[...] += left_inner(picks, back.astype(jnp.bfloat16))

    by_size(leave)

    def copies(target, number):
        return [
            pltpu.make_async_copy(weights_ref.at[kind], target.at[number, kind], out_sems.at[kind])
            for kind in range(3)
        ]

    @pl.when(expert > 0)
    def _():
        for copy in copies(grads_out[0], 0):
            copy.wait()

    def weigh(rows):
        grads = left_inner(
            rows_ref[:rows], jnp.concatenate([gate_in_ref[:rows], up_in_ref[:rows]], 1)
        )
        weights_ref[0] = grads[:, :hidden_size]
        weights_ref[1] = grads[:, hidden_size:]
        grad_down = left_inner(active_ref[:rows], grads_ref[:rows])
        own = hidden_size // parts
        blocks = width // hidden_size
        for part in range(parts):
            for piece in range(blocks):
                at = (part * blocks + piece) * own
                weights_ref[2, at : at + own, :] = grad_down[
                    part * own : (part + 1) * own, piece * hidden_size : (piece + 1) * hidden_size
                ]

    by_size(weigh)
    start = 0
    for target, number in zip(grads_out, numbers):

        @pl.when((expert >= start) & (expert < start + number))
        def _():
            for copy in copies(target, expert - start):
                copy.start()

        start += number

    @pl.when(expert == pl.num_programs(0) - 1)
    def _():
        for copy in copies(grads_out[0], 0):
            copy.wait()


def expert_stage(parts, first, numbers, counts, places, gate_rows, normed_b, grad_b, gate_w, up_w, down_w, sums):
    number = sum(numbers)
    length, width = normed_b.shape
    hidden = gate_w.shape[2]
    experts = places.shape[0]
    chained = sums is not None
    whole = lambda e, c: (0, 0)
    row_spec = pl.BlockSpec((1, 1, length), lambda e, c: (first + e, 0, 0))
    once = pl.Buffered(1)
    f32, bf16 = jnp.float32, jnp.bfloat16
    in_specs = [
        row_spec,
        row_spec,
        pl.BlockSpec((length, width), whole, pipeline_mode=once),
        pl.BlockSpec((length, width), whole, pipeline_mode=once),
        pl.BlockSpec((1, width, hidden), lambda e, c: (first + e, 0, 0)),
        pl.BlockSpec((1, width, hidden), lambda e, c: (first + e, 0, 0)),
        pl.BlockSpec((1, hidden, width), lambda e, c: (first + e, 0, 0)),
    ]
    args = [
        counts,
        places.reshape(experts, 1, length),
        gate_rows.reshape(experts, 1, length),
        normed_b,
        grad_b,
        gate_w,
        up_w,
        down_w,
    ]
    if chained:
        in_specs += [pl.BlockSpec(memory_space=pl.ANY)] * 2
        args += [sums[0], sums[1]]
    results = pl.pallas_call(
        functools.partial(expert_kernel, parts, first, numbers, chained),
        out_shape=[jax.ShapeDtypeStruct((some, 3, width, hidden), f32) for some in numbers]
        + [
            jax.ShapeDtypeStruct((length, width), f32),
            jax.ShapeDtypeStruct((length, width), f32),
            jax.ShapeDtypeStruct((number, 1, length), f32),
        ],
        grid_spec=pltpu.PrefetchScalarGridSpec(
            num_scalar_prefetch=1,
            grid=(number,),
            in_specs=in_specs,
            out_specs=[pl.BlockSpec(memory_space=pl.ANY)] * len(numbers)
            + [
                pl.BlockSpec((length, width), whole, pipeline_mode=once),
                pl.BlockSpec((length, width), whole, pipeline_mode=once),
                pl.BlockSpec((1, 1, length), lambda e, c: (e, 0, 0)),
            ],
            scratch_shapes=[
                pltpu.VMEM((CAP, width), bf16),
                pltpu.VMEM((CAP, width), bf16),
                pltpu.VMEM((CAP, hidden), bf16),
                pltpu.VMEM((CAP, hidden), bf16),
                pltpu.VMEM((CAP, hidden), bf16),
                pltpu.VMEM((3, width, hidden), f32),
                pltpu.SemaphoreType.DMA((2,)),
                pltpu.SemaphoreType.DMA((3,)),
            ],
        ),
        compiler_params=pltpu.CompilerParams(
            dimension_semantics=("arbitrary",), vmem_limit_bytes=63 << 20
        ),
        cost_estimate=pl.CostEstimate(
            flops=number * 8 * 10**9, bytes_accessed=number * 14 * 10**6, transcendentals=0
        ),
    )(*args)
    return results[: len(numbers)], results[len(numbers) :]


PIECES = 16


def line_gather_kernel(n, x_ref, out_ref, blocks_ref, recv, up_send, down_send):
    me = lax.axis_index("tensor")
    has_low, has_high = me > 0, me < n - 1
    barrier = pltpu.get_barrier_semaphore()

    @pl.when(has_low)
    def _():
        pl.semaphore_signal(barrier, inc=1, device_id={"tensor": me - 1}, device_id_type=MESH)

    @pl.when(has_high)
    def _():
        pl.semaphore_signal(barrier, inc=1, device_id={"tensor": me + 1}, device_id_type=MESH)

    blocks_ref[me] = x_ref[...].astype(jnp.float32)
    pl.semaphore_wait(barrier, has_low.astype(jnp.int32) + has_high.astype(jnp.int32))
    rows = x_ref.shape[0] // PIECES

    def copy(block, c, send, to):
        piece = blocks_ref.at[block, pl.ds(pl.multiple_of(c * rows, rows), rows), :]
        return pltpu.make_async_remote_copy(
            src_ref=piece,
            dst_ref=piece,
            send_sem=send.at[block, c],
            recv_sem=recv.at[block, c],
            device_id={"tensor": to},
            device_id_type=MESH,
        )

    for hop in range(n):
        low, high = me - hop, me + hop

        def step(c, carry):
            @pl.when(low >= 0)
            def _():
                if hop > 0:
                    copy(low, c, up_send, me).wait_recv()

                @pl.when(has_high)
                def _():
                    copy(low, c, up_send, me + 1).start()

            @pl.when(high < n)
            def _():
                if hop > 0:
                    copy(high, c, down_send, me).wait_recv()

                @pl.when(has_low)
                def _():
                    copy(high, c, down_send, me - 1).start()

            return carry

        lax.fori_loop(0, PIECES, step, 0)
    wide = x_ref.shape[1]
    for block in range(n):
        out_ref[:, block * wide : (block + 1) * wide] = blocks_ref[block].astype(jnp.bfloat16)
    for hop in range(n):
        low, high = me - hop, me + hop

        def drain(c, carry):
            @pl.when((low >= 0) & has_high)
            def _():
                copy(low, c, up_send, me).wait_send()

            @pl.when((high < n) & has_low)
            def _():
                copy(high, c, down_send, me).wait_send()

            return carry

        lax.fori_loop(0, PIECES, drain, 0)


def line_gather(x, n, name):
    length, wide = x.shape
    full = pl.BlockSpec(memory_space=pltpu.VMEM)
    return pl.pallas_call(
        functools.partial(line_gather_kernel, n),
        out_shape=jax.ShapeDtypeStruct((length, n * wide), jnp.bfloat16),
        in_specs=[full],
        out_specs=full,
        scratch_shapes=[pltpu.VMEM((n, length, wide), jnp.float32)]
        + [pltpu.SemaphoreType.DMA((n, PIECES))] * 3,
        compiler_params=pltpu.CompilerParams(
            collective_id=name, has_side_effects=True, vmem_limit_bytes=32 << 20
        ),
        cost_estimate=pl.CostEstimate(
            flops=0, bytes_accessed=16 * n * x.size, transcendentals=0
        ),
    )(x)


BLOCK = 256


def own_rows_kernel(parts, weight_ref, out_ref):
    rows = out_ref.shape[0]
    first = lax.axis_index("dp") * rows if parts > 1 else 0
    out_ref[...] = weight_ref[pl.ds(pl.multiple_of(first, 16), rows), :].astype(jnp.float32)


def gather_out_weight(out_weight, parts):
    rows, width = out_weight.shape
    ways = parts if rows % (16 * parts) == 0 else 1
    full = pl.BlockSpec(memory_space=pltpu.VMEM)
    own = pl.pallas_call(
        functools.partial(own_rows_kernel, ways),
        out_shape=jax.ShapeDtypeStruct((rows // ways, width), jnp.float32),
        in_specs=[full],
        out_specs=full,
    )(out_weight)
    return ways, lax.all_gather(own, "tensor")


def middle_kernel(
    attended_ref, weight_all_ref, tokens_ref, gain_ref, router_ref, chosen_ref, middle_out, normed_out, gates_out, weight_ref
):
    ways, n, rows, unused = weight_all_ref.shape
    for way in range(ways):
        for block in range(n):
            at = (block * ways + way) * rows
            weight_ref[at : at + rows, :] = weight_all_ref[way, block].astype(jnp.bfloat16)
    for first in range(0, tokens_ref.shape[0], BLOCK):
        own = slice(first, first + BLOCK)
        branch = jnp.dot(attended_ref[own, :], weight_ref[...], preferred_element_type=jnp.float32)
        middle = tokens_ref[own, :].astype(jnp.float32) + RESIDUAL * branch
        middle_out[own, :] = middle
        recip = lax.rsqrt(jnp.mean(middle * middle, axis=1, keepdims=True) + EPSILON)
        normed = (middle * recip * gain_ref[...]).astype(jnp.bfloat16)
        normed_out[own, :] = normed
        logits = jnp.dot(normed, router_ref[...], preferred_element_type=jnp.float32)
        raised = jnp.where(chosen_ref[own, :] > 0.0, jnp.exp(logits), 0.0)
        gates_out[own, :] = raised / jnp.sum(raised, axis=1, keepdims=True)


def enter_middle(attended, weight_all, tokens, gain, router, chosen):
    length, width = tokens.shape
    full = pl.BlockSpec(memory_space=pltpu.VMEM)
    return pl.pallas_call(
        middle_kernel,
        out_shape=[
            jax.ShapeDtypeStruct((length, width), jnp.float32),
            jax.ShapeDtypeStruct((length, width), jnp.bfloat16),
            jax.ShapeDtypeStruct((length, router.shape[1]), jnp.float32),
        ],
        in_specs=[full] * 6,
        out_specs=[full] * 3,
        scratch_shapes=[pltpu.VMEM((attended.shape[1], width), jnp.bfloat16)],
        compiler_params=pltpu.CompilerParams(vmem_limit_bytes=56 << 20),
        cost_estimate=pl.CostEstimate(
            flops=2 * length * width * width, bytes_accessed=25 * 10**6, transcendentals=0
        ),
    )(attended, weight_all, tokens, gain.reshape(1, width), router, chosen)


def turn_kernel(
    summed_ref, grad_gates_ref, gates_ref, middle_ref, cotangent_ref, gain_ref, router_ref, grad_out, branch_out, logits_out, gain_out
):
    length, width = summed_ref.shape
    experts = grad_gates_ref.shape[0]
    gates_rows = jnp.concatenate(
        [grad_gates_ref[...], jnp.zeros((128 - experts, length), jnp.float32)], 0
    )
    gain_sum = jnp.zeros((1, width), jnp.float32)
    for first in range(0, length, BLOCK):
        own = slice(first, first + BLOCK)
        grad_gates = jnp.transpose(gates_rows[:, own])
        gates = gates_ref[own, :]
        weighted = jnp.sum(gates * grad_gates, axis=1, keepdims=True)
        grad_logits = (gates * (grad_gates - weighted)).astype(jnp.bfloat16)
        logits_out[own, :] = grad_logits
        grad = summed_ref[own, :] + right_inner(grad_logits, router_ref[...])
        middle = middle_ref[own, :]
        recip = lax.rsqrt(jnp.mean(middle * middle, axis=1, keepdims=True) + EPSILON)
        unit = middle * recip
        gain_sum += jnp.sum(grad * unit, axis=0, keepdims=True)
        scaled = grad * gain_ref[...]
        back = recip * (scaled - unit * jnp.mean(scaled * unit, axis=1, keepdims=True))
        total = cotangent_ref[own, :].astype(jnp.float32) + back
        grad_out[own, :] = total
        branch_out[own, :] = (RESIDUAL * total).astype(jnp.bfloat16)
    gain_out[...] = gain_sum


def turn_middle(summed, grad_gates, gates, middle, cotangent, gain, router):
    length, width = summed.shape
    full = pl.BlockSpec(memory_space=pltpu.VMEM)
    return pl.pallas_call(
        turn_kernel,
        out_shape=[
            jax.ShapeDtypeStruct((length, width), jnp.float32),
            jax.ShapeDtypeStruct((length, width), jnp.bfloat16),
            jax.ShapeDtypeStruct((length, gates.shape[1]), jnp.bfloat16),
            jax.ShapeDtypeStruct((1, width), jnp.float32),
        ],
        in_specs=[full] * 7,
        out_specs=[full] * 4,
        compiler_params=pltpu.CompilerParams(vmem_limit_bytes=48 << 20),
        cost_estimate=pl.CostEstimate(
            flops=40 * length * width, bytes_accessed=25 * 10**6, transcendentals=0
        ),
    )(summed, grad_gates, gates, middle, cotangent, gain.reshape(1, width), router)


SPAN = 768
ROWS = 256


def lane_halves(shape):
    return lax.broadcasted_iota(jnp.int32, shape, len(shape) - 1) // HEAD


def select_halves(tile, source, half):
    kept = jnp.where(lane_halves(tile.shape) == source, tile, 0.0)
    return kept if source == half else pltpu.roll(kept, HEAD, 1)


def spread_pairs(tile, target):
    for source in range(2):
        for half in range(2):
            target[2 * source + half] = select_halves(tile, source, half).astype(jnp.bfloat16)


def rope_tile(tile, cosine, sine_low, sine_high):
    return tile * cosine + pltpu.roll(tile, 128 - HEAD // 2, 1) * sine_low + pltpu.roll(
        tile, HEAD // 2, 1
    ) * sine_high


def rope_back_tile(tile, cosine, sine_low, sine_high):
    return (
        tile * cosine
        + pltpu.roll(tile * sine_low, HEAD // 2, 1)
        + pltpu.roll(tile * sine_high, 128 - HEAD // 2, 1)
    )


def window(block):
    first = block * ROWS
    return first, jnp.maximum(first + ROWS - SPAN, 0)


def attend_forward_kernel(
    heads,
    group,
    tokens_ref,
    gain_ref,
    query_w,
    key_w,
    value_w,
    cosine_ref,
    sine_low_ref,
    sine_high_ref,
    opening_ref,
    normed_out,
    query_out,
    key_out,
    value_out,
    attended_out,
    logsum_out,
    key_pairs,
    value_pairs,
    tiles_ref,
):
    tiles, length, unused = query_out.shape
    hidden = tokens_ref[...].astype(jnp.float32)
    recip = lax.rsqrt(jnp.mean(hidden * hidden, axis=1, keepdims=True) + EPSILON)
    normed_out[...] = (hidden * recip * gain_ref[...]).astype(jnp.bfloat16)
    cosine, sine_low, sine_high = cosine_ref[...], sine_low_ref[...], sine_high_ref[...]
    for tile in range(tiles):
        query = jnp.dot(
            normed_out[...],
            query_w[:, tile * 128 : (tile + 1) * 128],
            preferred_element_type=jnp.float32,
        )
        query_out[tile] = rope_tile(query, cosine, sine_low, sine_high).astype(jnp.bfloat16)
    key = rope_tile(
        jnp.dot(normed_out[...], key_w[...], preferred_element_type=jnp.float32),
        cosine,
        sine_low,
        sine_high,
    )
    value = jnp.dot(normed_out[...], value_w[...], preferred_element_type=jnp.float32)
    key_out[...] = key.astype(jnp.bfloat16)
    value_out[...] = value.astype(jnp.bfloat16)
    spread_pairs(key, key_pairs)
    spread_pairs(value, value_pairs)
    blocks = length // ROWS
    tiles_ref[...] = jnp.zeros_like(tiles_ref)

    def unit(step, carry):
        head, block = step // blocks, step % blocks
        tile, half = head // 2, head % 2
        pair = 2 * (head // group) + half
        first, low = window(block)
        rows = pl.ds(pl.multiple_of(first, ROWS), ROWS)
        span = pl.ds(pl.multiple_of(low, ROWS), SPAN)
        scores = right_inner(query_out[tile, rows, :], key_pairs[pair, span, :])
        columns = low + lax.broadcasted_iota(jnp.int32, (ROWS, SPAN), 1)
        own = first + lax.broadcasted_iota(jnp.int32, (ROWS, SPAN), 0)
        allowed = (columns >= opening_ref[rows, :]) & (columns <= own)
        raised = jnp.where(allowed, jnp.exp(ATTN_SCALE * scores), 0.0)
        total = jnp.sum(raised, axis=1, keepdims=True)
        product = jnp.dot(
            raised.astype(jnp.bfloat16), value_pairs[pair, span, :], preferred_element_type=jnp.float32
        )
        tiles_ref[tile, rows, :] += product / total
        wide = jnp.broadcast_to(jnp.log(total), (ROWS, 128))
        logsum_out[head, :, rows] = jnp.transpose(wide)[:1]
        return carry

    lax.fori_loop(0, heads * blocks, unit, 0)
    for tile in range(tiles):
        attended_out[:, tile * 128 : (tile + 1) * 128] = tiles_ref[tile].astype(jnp.bfloat16)


def attend_forward(tokens, gain, query_w, key_w, value_w, tables, opening, heads, group):
    length, width = tokens.shape
    wide = query_w.shape[1]
    tiles = wide // 128
    bf16, f32 = jnp.bfloat16, jnp.float32
    full = pl.BlockSpec(memory_space=pltpu.VMEM)
    return pl.pallas_call(
        functools.partial(attend_forward_kernel, heads, group),
        out_shape=[
            jax.ShapeDtypeStruct((length, width), bf16),
            jax.ShapeDtypeStruct((tiles, length, 128), bf16),
            jax.ShapeDtypeStruct((length, 128), bf16),
            jax.ShapeDtypeStruct((length, 128), bf16),
            jax.ShapeDtypeStruct((length, wide), bf16),
            jax.ShapeDtypeStruct((heads, 1, length), f32),
        ],
        in_specs=[full] * 9,
        out_specs=[full] * 6,
        scratch_shapes=[
            pltpu.VMEM((4, length, 128), bf16),
            pltpu.VMEM((4, length, 128), bf16),
            pltpu.VMEM((tiles, length, 128), f32),
        ],
        compiler_params=pltpu.CompilerParams(vmem_limit_bytes=48 << 20),
        cost_estimate=pl.CostEstimate(
            flops=8 * 10**9, bytes_accessed=12 * 10**6, transcendentals=5 * 10**6
        ),
    )(tokens, gain.reshape(1, width), query_w, key_w, value_w, *tables, opening.reshape(length, 1))


def attend_backward_kernel(
    n,
    heads,
    group,
    branch_ref,
    out_w,
    query_ref,
    key_ref,
    value_ref,
    attended_ref,
    logsum_ref,
    query_w,
    key_w,
    value_w,
    cosine_ref,
    sine_low_ref,
    sine_high_ref,
    opening_ref,
    tokens_ref,
    moe_ref,
    grads_out,
    normed_out,
    gain_out,
    moe_out,
    key_pairs,
    value_pairs,
    attend_grads,
    query_grads,
    key_grads,
    value_grads,
    delta_ref,
    *line,
):
    tiles, length, unused = query_ref.shape
    line_start, line_step, line_end = line_stages(n, [moe_ref], [moe_out], line)
    line_start()
    blocks = length // ROWS
    units = heads * blocks
    taken = 0

    def run_line(steps):
        nonlocal taken
        until = min(taken + steps, 2 * STEPS)
        lax.fori_loop(taken, until, line_step, 0)
        taken = until

    run_line(2)
    spread_pairs(key_ref[...].astype(jnp.float32), key_pairs)
    spread_pairs(value_ref[...].astype(jnp.float32), value_pairs)
    halves = (
        lax.broadcasted_iota(jnp.int32, (8, 128), 0) == lane_halves((8, 128))
    ).astype(jnp.float32)
    for tile in range(tiles):
        lanes = slice(tile * 128, (tile + 1) * 128)
        grad = right_inner(branch_ref[...], out_w[lanes, :]).astype(jnp.bfloat16)
        attend_grads[tile] = grad
        products = grad.astype(jnp.float32) * attended_ref[:, lanes].astype(jnp.float32)
        sums = lax.dot_general(
            halves,
            products,
            (((1,), (1,)), ((), ())),
            precision=lax.Precision.HIGHEST,
            preferred_element_type=jnp.float32,
        )
        delta_ref[2 * tile] = sums[0:1]
        delta_ref[2 * tile + 1] = sums[1:2]
        run_line(2)
    query_grads[...] = jnp.zeros_like(query_grads)
    key_grads[...] = jnp.zeros_like(key_grads)
    value_grads[...] = jnp.zeros_like(value_grads)
    before, each = taken, (2 * STEPS - 8 - taken) // units
    taken += units * each

    def unit(step, carry):
        lax.fori_loop(before + step * each, before + step * each + each, line_step, 0)
        head, block = step // blocks, step % blocks
        tile, half = head // 2, head % 2
        pair = 2 * (head // group) + half
        first, low = window(block)
        rows = pl.ds(pl.multiple_of(first, ROWS), ROWS)
        span = pl.ds(pl.multiple_of(low, ROWS), SPAN)
        keys = key_pairs[pair, span, :]
        query = query_ref[tile, rows, :]
        grad = attend_grads[tile, rows, :]
        scores = right_inner(keys, query)
        columns = low + lax.broadcasted_iota(jnp.int32, (SPAN, ROWS), 0)
        own = first + lax.broadcasted_iota(jnp.int32, (SPAN, ROWS), 1)
        allowed = (columns >= opening_ref[:, rows]) & (columns <= own)
        probs = jnp.where(
            allowed, jnp.exp(ATTN_SCALE * scores - logsum_ref[head, :, rows]), 0.0
        )
        grad_probs = right_inner(value_pairs[pair, span, :], grad)
        grad_scores = (probs * (grad_probs - delta_ref[head, :, rows])).astype(jnp.bfloat16)
        value_grads[pair, span, :] += jnp.dot(
            probs.astype(jnp.bfloat16), grad, preferred_element_type=jnp.float32
        )
        key_grads[pair, span, :] += jnp.dot(
            grad_scores, query, preferred_element_type=jnp.float32
        )
        query_grads[tile, rows, :] += left_inner(grad_scores, keys)
        return carry

    lax.fori_loop(0, units, unit, 0)
    cosine, sine_low, sine_high = cosine_ref[...], sine_low_ref[...], sine_high_ref[...]
    wide = tiles * 128
    for tile in range(tiles):
        grads_out[:, tile * 128 : (tile + 1) * 128] = rope_back_tile(
            ATTN_SCALE * query_grads[tile], cosine, sine_low, sine_high
        ).astype(jnp.bfloat16)
    totals = []
    for grads in (key_grads, value_grads):
        totals.append(
            sum(
                select_halves(grads[2 * source + half], half, source)
                for source in range(2)
                for half in range(2)
            )
        )
    grads_out[:, wide : wide + 128] = rope_back_tile(
        ATTN_SCALE * totals[0], cosine, sine_low, sine_high
    ).astype(jnp.bfloat16)
    grads_out[:, wide + 128 : wide + 256] = totals[1].astype(jnp.bfloat16)
    gain_sum = jnp.zeros((1, normed_out.shape[1]), jnp.float32)
    for block in range(blocks):
        rows = slice(block * ROWS, (block + 1) * ROWS)
        normed = (
            right_inner(grads_out[rows, :wide], query_w[...])
            + right_inner(grads_out[rows, wide : wide + 128], key_w[...])
            + right_inner(grads_out[rows, wide + 128 :], value_w[...])
        )
        normed_out[rows, :] = normed
        hidden = tokens_ref[rows, :].astype(jnp.float32)
        recip = lax.rsqrt(jnp.mean(hidden * hidden, axis=1, keepdims=True) + EPSILON)
        gain_sum += jnp.sum(normed * (hidden * recip), axis=0, keepdims=True)
        run_line(2)
    gain_out[...] = gain_sum
    run_line(2 * STEPS)
    line_end()


def attend_backward(
    n, branch, out_w, query, key, value, attended, logsum, query_w, key_w, value_w, tables, opening, tokens, moe,
    heads, group, name,
):
    length, width = branch.shape
    tiles = query.shape[0]
    wide = tiles * 128
    bf16, f32 = jnp.bfloat16, jnp.float32
    full = pl.BlockSpec(memory_space=pltpu.VMEM)
    return pl.pallas_call(
        functools.partial(attend_backward_kernel, n, heads, group),
        out_shape=[
            jax.ShapeDtypeStruct((length, wide + 256), bf16),
            jax.ShapeDtypeStruct((length, width), f32),
            jax.ShapeDtypeStruct((1, width), f32),
            jax.ShapeDtypeStruct((length, width), f32),
        ],
        in_specs=[full] * 16,
        out_specs=[full] * 4,
        scratch_shapes=[
            pltpu.VMEM((4, length, 128), bf16),
            pltpu.VMEM((4, length, 128), bf16),
            pltpu.VMEM((tiles, length, 128), bf16),
            pltpu.VMEM((tiles, length, 128), f32),
            pltpu.VMEM((4, length, 128), f32),
            pltpu.VMEM((4, length, 128), f32),
            pltpu.VMEM((2 * tiles, 1, length), f32),
        ]
        + line_scratch([moe]),
        compiler_params=pltpu.CompilerParams(
            collective_id=name, has_side_effects=True, vmem_limit_bytes=62 << 20
        ),
        cost_estimate=pl.CostEstimate(
            flops=12 * 10**9, bytes_accessed=30 * 10**6, transcendentals=5 * 10**6
        ),
    )(
        branch, out_w, query, key, value, attended, logsum, query_w, key_w, value_w, *tables,
        opening.reshape(1, length), tokens, moe,
    )


def finish_kernel(
    n,
    parts,
    local_ref,
    normed_ref,
    grads_ref,
    branch_ref,
    attended_ref,
    normed_two_ref,
    logits_ref,
    gain_ref,
    first_gain_ref,
    normed_out,
    query_out,
    key_out,
    value_out,
    branch_out,
    router_out,
    gain_out,
    first_gain_out,
    weights_ref,
    gains_ref,
    gain_send,
    gain_recv,
    *scratch,
):
    levels = parts.bit_length() - 1
    held = scratch[:levels]
    sends, recvs = scratch[levels : levels + 2]
    line_start, line_step, line_end = line_stages(n, [local_ref], [normed_out], scratch[levels + 2 :])
    me = lax.axis_index("dp")
    width = normed_ref.shape[1]
    own = width // parts
    wide, attended_wide = grads_ref.shape[1], attended_ref.shape[1]
    mine = lax.axis_index("tensor")
    line_start(
        [{"dp": jnp.bitwise_xor(me, 1 << level)} for level in range(levels)]
        + [{"tensor": lax.rem(mine + ahead, n)} for ahead in range(1, n)]
    )

    def run_line(first, last):
        lax.fori_loop(first, last, line_step, 0)

    run_line(0, 2)
    pieces = 4
    block = width // pieces
    for piece in range(pieces):
        rows = slice(piece * block, (piece + 1) * block)
        weights_ref[rows, :wide] = left_inner(normed_ref[:, rows], grads_ref[...])
        weights_ref[rows, wide : wide + attended_wide] = left_inner(
            branch_ref[:, rows], attended_ref[...]
        )
        gain = jnp.transpose(jnp.broadcast_to(gain_ref[:, rows], (128, block)))
        first_gain = jnp.transpose(jnp.broadcast_to(first_gain_ref[:, rows], (128, block)))
        lanes = lax.broadcasted_iota(jnp.int32, (block, 128), 1)
        weights_ref[rows, wide + attended_wide :] = jnp.where(
            lanes == 127,
            gain,
            jnp.where(
                lanes == 126, first_gain, left_inner(normed_two_ref[:, rows], logits_ref[...])
            ),
        )
        run_line(2 + 2 * piece, 4 + 2 * piece)
    done = 2 + 2 * pieces

    def shard(number):
        return weights_ref.at[pl.ds(pl.multiple_of(number * own, own), own), :]

    def copies(level):
        peer = jnp.bitwise_xor(me, 1 << level)
        low = jnp.bitwise_and(peer, (2 << level) - 1)
        return [
            pltpu.make_async_remote_copy(
                src_ref=shard(low + (i << (level + 1))),
                dst_ref=held[level].at[i],
                send_sem=sends.at[level, i],
                recv_sem=recvs.at[level, i],
                device_id={"dp": peer},
                device_id_type=MESH,
            )
            for i in range(parts >> (level + 1))
        ]

    stops = [6, 24, 16, 2]
    for level in range(levels):
        for copy in copies(level):
            copy.start()
        until = done + stops[level]
        run_line(done, until)
        done = until
        kept = jnp.bitwise_and(me, (2 << level) - 1)
        for i, copy in enumerate(copies(level)):
            copy.wait_recv()
            target = shard(kept + (i << (level + 1)))
            target[...] += held[level][i]
    gains_ref[0] = shard(me)[:, wide + attended_wide :]
    gain_copies = [
        pltpu.make_async_remote_copy(
            src_ref=gains_ref.at[0],
            dst_ref=gains_ref.at[ahead],
            send_sem=gain_send.at[ahead],
            recv_sem=gain_recv.at[ahead],
            device_id={"tensor": lax.rem(mine + ahead, n)},
            device_id_type=MESH,
        )
        for ahead in range(1, n)
    ]
    for copy in gain_copies:
        copy.start()
    kept = shard(me)
    query_out[...] = kept[:, : query_out.shape[1]]
    key_out[...] = kept[:, wide - 256 : wide - 256 + key_out.shape[1]]
    value_out[...] = kept[:, wide - 128 : wide - 128 + value_out.shape[1]]
    branch_out[...] = jnp.transpose(kept[:, wide : wide + attended_wide])[: branch_out.shape[0]]
    router_out[...] = gains_ref[0][:, : router_out.shape[1]]
    run_line(done, 2 * STEPS)
    total = gains_ref[0]
    for ahead, copy in enumerate(gain_copies, 1):
        copy.wait_recv()
        total = total + gains_ref[ahead]
    gain_out[...] = jnp.transpose(gains_ref[0])[127:]
    first_gain_out[...] = jnp.transpose(total)[126:127]
    for level in range(levels):
        for copy in copies(level):
            copy.wait_send()
    for copy in gain_copies:
        copy.wait_send()
    line_end()


def finish(
    n, parts, grad_local, normed_b, grads_wide, branch_b, attended, normed_two_b, grad_logits_b, gain_grad, first_gain_grad,
    wide_q, wide_k, experts, name,
):
    length, width = normed_b.shape
    columns = grads_wide.shape[1] + attended.shape[1] + 128
    full = pl.BlockSpec(memory_space=pltpu.VMEM)
    levels = parts.bit_length() - 1
    own = width // parts
    f32 = jnp.float32
    shapes = [(length, width), (own, wide_q), (own, wide_k), (own, wide_k), (wide_q, own)]
    shapes += [(own, experts), (1, own), (1, own)]
    return pl.pallas_call(
        functools.partial(finish_kernel, n, parts),
        out_shape=[jax.ShapeDtypeStruct(shape, f32) for shape in shapes],
        in_specs=[full] * 9,
        out_specs=[full] * 8,
        scratch_shapes=[
            pltpu.VMEM((width, columns), f32),
            pltpu.VMEM((n, own, 128), f32),
            pltpu.SemaphoreType.DMA((n,)),
            pltpu.SemaphoreType.DMA((n,)),
        ]
        + [pltpu.VMEM((parts >> (level + 1), own, columns), f32) for level in range(levels)]
        + [pltpu.SemaphoreType.DMA((levels, parts // 2))] * 2
        + line_scratch([grad_local]),
        compiler_params=pltpu.CompilerParams(
            collective_id=name, has_side_effects=True, vmem_limit_bytes=62 << 20
        ),
        cost_estimate=pl.CostEstimate(
            flops=2 * length * width * columns, bytes_accessed=50 * 10**6, transcendentals=0
        ),
    )(
        grad_local, normed_b, grads_wide, branch_b, attended, normed_two_b, grad_logits_b, gain_grad,
        first_gain_grad,
    )


def place_kernel(shards_ref, *refs):
    gate_out, up_out, down_out = refs[-3:]
    gate_out[0] = shards_ref[0, 0]
    up_out[0] = shards_ref[0, 1]
    rows, hidden = down_out.shape[1], shards_ref.shape[3]
    for piece in range(down_out.shape[2] // hidden):
        down_out[0, :, piece * hidden : (piece + 1) * hidden] = shards_ref[
            0, 2, piece * rows : (piece + 1) * rows, :
        ]


def place_shards(parts, shards, first, experts, before):
    number, unused, rows, hidden = shards.shape
    down_rows = hidden // parts
    width = rows * parts
    shapes = [(experts, rows, hidden), (experts, rows, hidden), (experts, down_rows, width)]
    spec = lambda shape: pl.BlockSpec((1,) + shape[1:], lambda e: (first + e, 0, 0))
    args, extra, aliases = [shards], [], {}
    if before is not None:
        args += list(before)
        extra = [pl.BlockSpec(memory_space=pl.ANY)] * 3
        aliases = {1: 0, 2: 1, 3: 2}
    return pl.pallas_call(
        place_kernel,
        out_shape=[jax.ShapeDtypeStruct(shape, jnp.float32) for shape in shapes],
        grid=(number,),
        in_specs=[pl.BlockSpec((1, 3, rows, hidden), lambda e: (e, 0, 0, 0))] + extra,
        out_specs=[spec(shape) for shape in shapes],
        input_output_aliases=aliases,
        cost_estimate=pl.CostEstimate(
            flops=0, bytes_accessed=8 * shards.size, transcendentals=0
        ),
    )(*args)


def on_device(
    ring,
    tokens,
    cotangent,
    segment_ids,
    routes,
    attn_gain,
    query_weight,
    key_weight,
    value_weight,
    out_weight,
    ffn_gain,
    router_weight,
    gate_weight,
    up_weight,
    down_weight,
):
    length = tokens.shape[0]
    width = tokens.shape[1]
    segment = segment_ids[0]
    heads_local = query_weight.shape[1] // HEAD
    kv_local = key_weight.shape[1] // HEAD
    group_size = heads_local // kv_local
    experts_all = router_weight.shape[1]
    experts_local = gate_weight.shape[0]
    parts = lax.axis_size("dp")
    opening = doc_openings(segment)
    tables = rope_tables(opening, HEAD)
    query_w, key_w, value_w = (pad_columns(w) for w in (query_weight, key_weight, value_weight))
    out_w = jnp.transpose(pad_columns(jnp.transpose(out_weight)))
    hidden_in = tokens.astype(jnp.float32)
    ways, out_rows = gather_out_weight(out_weight, parts)
    normed_b, queries, keys, values, attended, logsum = attend_forward(
        tokens, attn_gain, query_w, key_w, value_w, tables, opening, heads_local, group_size
    )
    all_ids = jnp.arange(experts_all, dtype=jnp.int32)
    chosen = jnp.sum((routes[:, :, None] == all_ids[None, None, :]).astype(jnp.int32), axis=1) > 0
    first_expert = lax.axis_index("tensor") * experts_local
    local_ids = first_expert + jnp.arange(experts_local, dtype=jnp.int32)
    picked = jnp.sum((routes[None, :, :] == local_ids[:, None, None]).astype(jnp.int32), axis=2)
    places_in = slot_places(picked)
    counts = jnp.sum(picked, axis=1)
    out_rows, attended = lax.optimization_barrier((out_rows, attended))
    out_all = lax.all_gather(out_rows, "dp") if ways > 1 else out_rows[None]
    attended_all = line_gather(attended, ring, 1)
    attended_all = attended_all.reshape(length, ring, attended.shape[1])
    attended_all = attended_all[:, :, : heads_local * HEAD].reshape(length, -1)
    router_w = pad_columns(router_weight)
    middle, normed_two_b, gate_probs = enter_middle(
        attended_all, out_all, tokens, ffn_gain, router_w, pad_columns(chosen.astype(jnp.float32))
    )
    gate_rows = jnp.transpose(lax.dynamic_slice_in_dim(gate_probs, first_expert, experts_local, 1))
    numbers = (max(1, experts_local // 10), max(1, 3 * experts_local // 10))
    numbers += (experts_local - sum(numbers),)
    (grads_first,), sums = expert_stage(
        parts, 0, numbers[:1], counts, places_in, gate_rows, normed_two_b, cotangent,
        gate_weight, up_weight, down_weight, None,
    )
    shards_first = lax.psum_scatter(grads_first, "dp", scatter_dimension=2, tiled=True)
    (grads_middle, grads_last), sums_last = expert_stage(
        parts, numbers[0], numbers[1:], counts, places_in, gate_rows, normed_two_b, cotangent,
        gate_weight, up_weight, down_weight, sums,
    )
    shards_first, grads_middle = lax.optimization_barrier((shards_first, grads_middle))
    shards_middle = lax.psum_scatter(grads_middle, "dp", scatter_dimension=2, tiled=True)
    moe_part, grad_normed_part, unused = sums_last
    grad_gates_local = jnp.concatenate([sums[2], sums_last[2]], 0)
    grad_gates_part = lax.dynamic_update_slice_in_dim(
        jnp.zeros((experts_all, length), jnp.float32),
        grad_gates_local.reshape(experts_local, length),
        first_expert,
        0,
    ).reshape(-1, 128)
    grad_gates_part = jnp.pad(grad_gates_part, ((0, GATE_ROWS - grad_gates_part.shape[0]), (0, 0)))
    shards_first, grad_normed_part = lax.optimization_barrier((shards_first, grad_normed_part))
    grad_normed_sum, gates_sum = line_sum(grad_normed_part, grad_gates_part, ring, 2)
    grad_gates = gates_sum[: experts_all * length // 128].reshape(experts_all, length)
    grad_middle, grad_branch_b, grad_logits_b, grad_ffn_gain = turn_middle(
        grad_normed_sum, grad_gates, gate_probs, middle, cotangent, ffn_gain, router_w
    )
    shards_middle, grads_last, grad_branch_b = lax.optimization_barrier(
        (shards_middle, grads_last, grad_branch_b)
    )
    shards_last = lax.psum_scatter(grads_last, "dp", scatter_dimension=2, tiled=True)
    grads_wide, grad_normed_local, first_gain, moe_out = attend_backward(
        ring, grad_branch_b, out_w, queries, keys, values, attended, logsum,
        query_w, key_w, value_w, tables, opening, tokens, moe_part, heads_local, group_size, 3,
    )
    output = (middle + RESIDUAL * moe_out).astype(jnp.bfloat16)
    wide_q, wide_k = heads_local * HEAD, kv_local * HEAD
    grad_normed, *small = finish(
        ring, parts, grad_normed_local, normed_b, grads_wide, grad_branch_b, attended, normed_two_b,
        grad_logits_b, grad_ffn_gain, first_gain, wide_q, wide_k, experts_all, 4,
    )
    grad_query, grad_key, grad_value, grad_out, grad_router, grad_ffn_gain, grad_attn_gain = small
    recip_one = lax.rsqrt(jnp.mean(hidden_in * hidden_in, axis=-1, keepdims=True) + EPSILON)
    unit_one = hidden_in * recip_one
    scaled = grad_normed * attn_gain
    inner = jnp.mean(scaled * unit_one, axis=-1, keepdims=True)
    grad_tokens = grad_middle + recip_one * (scaled - unit_one * inner)
    shards_last, grad_tokens = lax.optimization_barrier((shards_last, grad_tokens))
    grads_placed = place_shards(parts, shards_first, 0, experts_local, None)
    grads_placed = place_shards(parts, shards_middle, numbers[0], experts_local, grads_placed)
    grad_gate, grad_up, grad_down = place_shards(
        parts, shards_last, numbers[0] + numbers[1], experts_local, grads_placed
    )
    return (
        output,
        grad_tokens,
        grad_attn_gain.reshape(-1),
        grad_query,
        grad_key,
        grad_value,
        grad_out,
        grad_ffn_gain.reshape(-1),
        grad_router,
        grad_gate,
        grad_up,
        grad_down,
    )


def solution(mesh):
    return jax.shard_map(
        functools.partial(on_device, mesh.shape["tensor"]),
        mesh=mesh,
        in_specs=(
            P("dp", None),
            P("dp", None),
            P("dp", None),
            P("dp", None),
            P(),
            P(None, "tensor"),
            P(None, "tensor"),
            P(None, "tensor"),
            P("tensor", None),
            P(),
            P(),
            P("tensor", None, None),
            P("tensor", None, None),
            P("tensor", None, None),
        ),
        out_specs=(
            P("dp", None),
            P("dp", None),
            P("dp"),
            P("dp", "tensor"),
            P("dp", "tensor"),
            P("dp", "tensor"),
            P("tensor", "dp"),
            P("dp"),
            P("dp", None),
            P("tensor", "dp", None),
            P("tensor", "dp", None),
            P("tensor", "dp", None),
        ),
        check_vma=False,
    )
```

```python
import functools

import jax
import jax.numpy as jnp
from jax import lax
from jax.experimental import pallas as pl
from jax.experimental.pallas import tpu as pltpu
from jax.sharding import PartitionSpec as P

MESH = pl.DeviceIdType.MESH

HEAD = 64
CAP = 384


EPSILON = 1e-06
RESIDUAL = 0.22
ATTN_SCALE = 0.015625
ROPE_BASE = 10000.0


def left_inner(first, second):
    return lax.dot_general(
        first, second, (((0,), (0,)), ((), ())), preferred_element_type=jnp.float32
    )


def right_inner(first, second):
    return lax.dot_general(
        first, second, (((1,), (1,)), ((), ())), preferred_element_type=jnp.float32
    )


def doc_openings(segment):
    return jnp.sum((segment[None, :] < segment[:, None]).astype(jnp.int32), axis=1)


def rope_tables(opening, head_size):
    halfway = head_size // 2
    spread = jnp.arange(halfway, dtype=jnp.float32) * (2.0 / head_size)
    inverse = jnp.power(ROPE_BASE, -spread)
    places = jnp.arange(opening.shape[0], dtype=jnp.int32)
    angles = (places - opening).astype(jnp.float32)[:, None] * inverse[None, :]
    cosine, sine = jnp.cos(angles), jnp.sin(angles)
    none = jnp.zeros_like(sine)
    return (
        jnp.concatenate([cosine] * 4, 1),
        jnp.concatenate([-sine, none] * 2, 1),
        jnp.concatenate([none, sine] * 2, 1),
    )


def pad_columns(weight):
    missing = -weight.shape[1] % 128
    return weight if missing == 0 else jnp.pad(weight, ((0, 0), (0, missing)))


def rms_forward(hidden, gain):
    recip = lax.rsqrt(jnp.mean(hidden * hidden, axis=-1, keepdims=True) + EPSILON)
    unit = hidden * recip
    return (unit * gain, unit, recip)


def rms_backward(gradient, unit, recip, gain):
    gain_grad = jnp.sum(gradient * unit, axis=0)
    scaled = gradient * gain
    return (recip * (scaled - unit * jnp.mean(scaled * unit, axis=-1, keepdims=True)), gain_grad)


def slot_places(picked):
    length = picked.shape[1]
    tokens = jnp.arange(length, dtype=jnp.int32)
    earlier = (tokens[:, None] < tokens[None, :]).astype(jnp.bfloat16)
    before = jnp.dot(picked.astype(jnp.bfloat16), earlier, preferred_element_type=jnp.float32)
    return jnp.where(picked > 0, before.astype(jnp.int32), -1)


STEPS = 32
LAG = 2
GATE_ROWS = 512


def line_stages(n, xs, outs, scratch):
    count = len(xs)
    lows, highs = scratch[:count], scratch[count : 2 * count]
    low_recv, high_recv, total_recv, up_send, low_send, high_send = scratch[2 * count :]
    me = lax.axis_index("tensor")
    root = n // 2
    has_low, has_high = me > 0, me < n - 1

    def begin(others=()):
        barrier = pltpu.get_barrier_semaphore()
        for other in others:
            pl.semaphore_signal(barrier, inc=1, device_id=other, device_id_type=MESH)

        @pl.when(has_low)
        def _():
            pl.semaphore_signal(barrier, inc=1, device_id={"tensor": me - 1}, device_id_type=MESH)

        @pl.when(has_high)
        def _():
            pl.semaphore_signal(barrier, inc=1, device_id={"tensor": me + 1}, device_id_type=MESH)

        pl.semaphore_wait(
            barrier, len(others) + has_low.astype(jnp.int32) + has_high.astype(jnp.int32)
        )

    def piece(ref, c):
        rows = ref.shape[0] // STEPS
        return ref.at[pl.ds(pl.multiple_of(c * rows, rows), rows), :]

    def copies(sources, targets, c, send, recv, to):
        return [
            pltpu.make_async_remote_copy(
                src_ref=piece(source, c),
                dst_ref=piece(target, c),
                send_sem=send.at[i, c],
                recv_sem=recv.at[i, c],
                device_id={"tensor": to},
                device_id_type=MESH,
            )
            for i, (source, target) in enumerate(zip(sources, targets))
        ]

    def start(sources, targets, c, send, recv, to):
        for copy in copies(sources, targets, c, send, recv, to):
            copy.start()

    def arrived(targets, c, send, recv):
        for copy in copies(targets, targets, c, send, recv, me):
            copy.wait_recv()

    def reduce_step(c):
        for side, inner, held, recv, to in (
            (me < root, has_low, lows, low_recv, me + 1),
            (me > root, has_high, highs, high_recv, me - 1),
        ):

            @pl.when(side & inner)
            def _():
                arrived(held, c, up_send, recv)
                for x, h in zip(xs, held):
                    piece(h, c)[...] += piece(x, c)[...]
                start(held, held, c, up_send, recv, to)

            @pl.when(side & jnp.logical_not(inner))
            def _():
                start(xs, held, c, up_send, recv, to)

        @pl.when(me == root)
        def _():
            arrived(lows, c, up_send, low_recv)
            if root < n - 1:
                arrived(highs, c, up_send, high_recv)
            for x, low, high, out in zip(xs, lows, highs, outs):
                total = piece(x, c)[...] + piece(low, c)[...]
                if root < n - 1:
                    total += piece(high, c)[...]
                piece(out, c)[...] = total
            start(outs, outs, c, low_send, total_recv, me - 1)
            if root < n - 1:
                start(outs, outs, c, high_send, total_recv, me + 1)

    def total_step(c):
        @pl.when(me != root)
        def _():
            arrived(outs, c, low_send, total_recv)

        @pl.when((me < root) & has_low)
        def _():
            start(outs, outs, c, low_send, total_recv, me - 1)

        @pl.when((me > root) & has_high)
        def _():
            start(outs, outs, c, high_send, total_recv, me + 1)

    lag = jnp.where(has_low & has_high, LAG, STEPS)

    def step(t, carry):
        @pl.when(t < STEPS)
        def _():
            reduce_step(t)

        @pl.when((t >= lag) & (t - lag < STEPS))
        def _():
            total_step(t - lag)

        return carry

    def finish():
        def drain(c, carry):
            for condition, send in (
                (me != root, up_send),
                ((me <= root) & has_low, low_send),
                ((me >= root) & has_high, high_send),
            ):

                @pl.when(condition)
                def _():
                    for copy in copies(xs, lows, c, send, low_recv, me):
                        copy.wait_send()

            return carry

        lax.fori_loop(0, STEPS, drain, 0)

    return begin, step, finish


def line_scratch(arrays):
    return [pltpu.VMEM(array.shape, jnp.float32) for array in arrays * 2] + [
        pltpu.SemaphoreType.DMA((len(arrays), STEPS))
    ] * 6


def line_sum_kernel(n, count, *refs):
    begin, step, finish = line_stages(n, refs[:count], refs[count : 2 * count], refs[2 * count :])
    begin()
    lax.fori_loop(0, 2 * STEPS, step, 0)
    finish()


def line_sum(x, extra, n, name):
    arrays = [x] if extra is None else [x, extra]
    count = len(arrays)
    shapes = [jax.ShapeDtypeStruct(array.shape, jnp.float32) for array in arrays]
    size = sum(array.size for array in arrays)
    results = pl.pallas_call(
        functools.partial(line_sum_kernel, n, count),
        out_shape=shapes,
        in_specs=[pl.BlockSpec(memory_space=pltpu.VMEM)] * count,
        out_specs=[pl.BlockSpec(memory_space=pltpu.VMEM)] * count,
        scratch_shapes=line_scratch(arrays),
        compiler_params=pltpu.CompilerParams(
            collective_id=name, has_side_effects=True, vmem_limit_bytes=40 << 20
        ),
        cost_estimate=pl.CostEstimate(
            flops=3 * size, bytes_accessed=8 * size, transcendentals=0
        ),
    )(*arrays)
    return (results[0], None) if extra is None else tuple(results)


def expert_kernel(
    parts,
    first,
    numbers,
    chained,
    count_ref,
    place_ref,
    gate_ref,
    normed_ref,
    grad_ref,
    gate_w,
    up_w,
    down_w,
    *refs,
):
    if chained:
        moe_in, back_in = refs[:2]
        refs = refs[2:]
    grads_out, refs = refs[: len(numbers)], refs[len(numbers) :]
    moe_out, back_out, gates_out = refs[:3]
    rows_ref, grads_ref, active_ref, gate_in_ref, up_in_ref, weights_ref, sems, out_sems = refs[3:]
    expert = pl.program_id(0)
    filled = count_ref[first + expert]
    length, width = normed_ref.shape
    hidden_size = gate_w.shape[2]
    sizes = (128, 256, CAP)

    def by_size(run):
        low = None
        for rows in sizes:
            fits = filled <= rows if low is None else filled > low
            if low is not None and rows != sizes[-1]:
                fits = fits & (filled <= rows)
            pl.when(fits)(functools.partial(run, rows))
            low = rows

    if chained:
        copy_moe = pltpu.make_async_copy(moe_in, moe_out, sems.at[0])
        copy_back = pltpu.make_async_copy(back_in, back_out, sems.at[1])

        @pl.when(expert == 0)
        def _():
            copy_moe.start()
            copy_back.start()

    else:

        @pl.when(expert == 0)
        def _():
            moe_out[...] = jnp.zeros_like(moe_out)
            back_out[...] = jnp.zeros_like(back_out)

    def slots(rows):
        mask = lax.broadcasted_iota(jnp.int32, (rows, length), 0) == place_ref[0]
        return mask, jnp.where(mask, 1.0, 0.0).astype(jnp.bfloat16)

    def enter(rows):
        mask, picks = slots(rows)
        rows_in = jnp.dot(picks, normed_ref[...], preferred_element_type=jnp.float32).astype(jnp.bfloat16)
        grad_rows = (
            RESIDUAL * jnp.dot(picks, grad_ref[...], preferred_element_type=jnp.float32)
        ).astype(jnp.bfloat16)
        rows_ref[:rows] = rows_in
        grads_ref[:rows] = grad_rows
        gate = jnp.sum(jnp.where(mask, gate_ref[0], 0.0), axis=1, keepdims=True)
        gate_input = jnp.dot(rows_in, gate_w[0], preferred_element_type=jnp.float32)
        up_input = jnp.dot(rows_in, up_w[0], preferred_element_type=jnp.float32)
        grad_act = right_inner(grad_rows, down_w[0])
        sigmoid_val = jax.nn.sigmoid(gate_input)
        silu_out = gate_input * sigmoid_val
        hidden = silu_out * up_input
        active_ref[:rows] = (hidden * gate).astype(jnp.bfloat16)
        column = jnp.sum(grad_act * hidden, axis=1, keepdims=True)
        gates_out[0] = jnp.sum(jnp.where(mask, column, 0.0), axis=0, keepdims=True)
        grad_hidden = grad_act * gate
        gate_in_ref[:rows] = (
            grad_hidden * up_input * sigmoid_val * (1.0 + gate_input * (1.0 - sigmoid_val))
        ).astype(jnp.bfloat16)
        up_in_ref[:rows] = (grad_hidden * silu_out).astype(jnp.bfloat16)

    by_size(enter)
    if chained:

        @pl.when(expert == 0)
        def _():
            copy_moe.wait()
            copy_back.wait()

    def leave(rows):
        column = jnp.transpose(jnp.broadcast_to(place_ref[0], (128, length)))
        column = jnp.concatenate([column] * (rows // 128), 1)
        own = lax.broadcasted_iota(jnp.int32, (length, rows), 1)
        picks = jnp.where(own == column, 1.0, 0.0).astype(jnp.bfloat16)
        moe = jnp.dot(active_ref[:rows], down_w[0], preferred_element_type=jnp.float32)
        moe_out[...] += jnp.dot(
            picks, moe.astype(jnp.bfloat16), preferred_element_type=jnp.float32
        )
        back = right_inner(gate_in_ref[:rows], gate_w[0]) + right_inner(up_in_ref[:rows], up_w[0])
        back_out[...] += jnp.dot(
            picks, back.astype(jnp.bfloat16), preferred_element_type=jnp.float32
        )

    by_size(leave)

    def copies(target, number):
        return [
            pltpu.make_async_copy(weights_ref.at[kind], target.at[number, kind], out_sems.at[kind])
            for kind in range(3)
        ]

    @pl.when(expert > 0)
    def _():
        for copy in copies(grads_out[0], 0):
            copy.wait()

    def weigh(rows):
        grads = left_inner(
            rows_ref[:rows], jnp.concatenate([gate_in_ref[:rows], up_in_ref[:rows]], 1)
        )
        weights_ref[0] = grads[:, :hidden_size]
        weights_ref[1] = grads[:, hidden_size:]
        grad_down = left_inner(active_ref[:rows], grads_ref[:rows])
        own = hidden_size // parts
        blocks = width // hidden_size
        for part in range(parts):
            for piece in range(blocks):
                at = (part * blocks + piece) * own
                weights_ref[2, at : at + own, :] = grad_down[
                    part * own : (part + 1) * own, piece * hidden_size : (piece + 1) * hidden_size
                ]

    by_size(weigh)
    start = 0
    for target, number in zip(grads_out, numbers):

        @pl.when((expert >= start) & (expert < start + number))
        def _():
            for copy in copies(target, expert - start):
                copy.start()

        start += number

    @pl.when(expert == pl.num_programs(0) - 1)
    def _():
        for copy in copies(grads_out[0], 0):
            copy.wait()


def expert_stage(parts, first, numbers, counts, places, gate_rows, normed_b, grad_b, gate_w, up_w, down_w, sums):
    number = sum(numbers)
    length, width = normed_b.shape
    hidden = gate_w.shape[2]
    experts = places.shape[0]
    chained = sums is not None
    whole = lambda e, c: (0, 0)
    row_spec = pl.BlockSpec((1, 1, length), lambda e, c: (first + e, 0, 0))
    once = pl.Buffered(1)
    f32, bf16 = jnp.float32, jnp.bfloat16
    in_specs = [
        row_spec,
        row_spec,
        pl.BlockSpec((length, width), whole, pipeline_mode=once),
        pl.BlockSpec((length, width), whole, pipeline_mode=once),
        pl.BlockSpec((1, width, hidden), lambda e, c: (first + e, 0, 0)),
        pl.BlockSpec((1, width, hidden), lambda e, c: (first + e, 0, 0)),
        pl.BlockSpec((1, hidden, width), lambda e, c: (first + e, 0, 0)),
    ]
    args = [
        counts,
        places.reshape(experts, 1, length),
        gate_rows.reshape(experts, 1, length),
        normed_b,
        grad_b,
        gate_w,
        up_w,
        down_w,
    ]
    if chained:
        in_specs += [pl.BlockSpec(memory_space=pl.ANY)] * 2
        args += [sums[0], sums[1]]
    results = pl.pallas_call(
        functools.partial(expert_kernel, parts, first, numbers, chained),
        out_shape=[jax.ShapeDtypeStruct((some, 3, width, hidden), f32) for some in numbers]
        + [
            jax.ShapeDtypeStruct((length, width), f32),
            jax.ShapeDtypeStruct((length, width), f32),
            jax.ShapeDtypeStruct((number, 1, length), f32),
        ],
        grid_spec=pltpu.PrefetchScalarGridSpec(
            num_scalar_prefetch=1,
            grid=(number,),
            in_specs=in_specs,
            out_specs=[pl.BlockSpec(memory_space=pl.ANY)] * len(numbers)
            + [
                pl.BlockSpec((length, width), whole, pipeline_mode=once),
                pl.BlockSpec((length, width), whole, pipeline_mode=once),
                pl.BlockSpec((1, 1, length), lambda e, c: (e, 0, 0)),
            ],
            scratch_shapes=[
                pltpu.VMEM((CAP, width), bf16),
                pltpu.VMEM((CAP, width), bf16),
                pltpu.VMEM((CAP, hidden), bf16),
                pltpu.VMEM((CAP, hidden), bf16),
                pltpu.VMEM((CAP, hidden), bf16),
                pltpu.VMEM((3, width, hidden), f32),
                pltpu.SemaphoreType.DMA((2,)),
                pltpu.SemaphoreType.DMA((3,)),
            ],
        ),
        compiler_params=pltpu.CompilerParams(
            dimension_semantics=("arbitrary",), vmem_limit_bytes=63 << 20
        ),
        cost_estimate=pl.CostEstimate(
            flops=number * 8 * 10**9, bytes_accessed=number * 14 * 10**6, transcendentals=0
        ),
    )(*args)
    return results[: len(numbers)], results[len(numbers) :]


PIECES = 16


def line_gather_kernel(n, x_ref, out_ref, blocks_ref, recv, up_send, down_send):
    me = lax.axis_index("tensor")
    has_low, has_high = me > 0, me < n - 1
    barrier = pltpu.get_barrier_semaphore()

    @pl.when(has_low)
    def _():
        pl.semaphore_signal(barrier, inc=1, device_id={"tensor": me - 1}, device_id_type=MESH)

    @pl.when(has_high)
    def _():
        pl.semaphore_signal(barrier, inc=1, device_id={"tensor": me + 1}, device_id_type=MESH)

    blocks_ref[me] = x_ref[...].astype(jnp.float32)
    pl.semaphore_wait(barrier, has_low.astype(jnp.int32) + has_high.astype(jnp.int32))
    rows = x_ref.shape[0] // PIECES

    def copy(block, c, send, to):
        piece = blocks_ref.at[block, pl.ds(pl.multiple_of(c * rows, rows), rows), :]
        return pltpu.make_async_remote_copy(
            src_ref=piece,
            dst_ref=piece,
            send_sem=send.at[block, c],
            recv_sem=recv.at[block, c],
            device_id={"tensor": to},
            device_id_type=MESH,
        )

    for hop in range(n):
        low, high = me - hop, me + hop

        def step(c, carry):
            @pl.when(low >= 0)
            def _():
                if hop > 0:
                    copy(low, c, up_send, me).wait_recv()

                @pl.when(has_high)
                def _():
                    copy(low, c, up_send, me + 1).start()

            @pl.when(high < n)
            def _():
                if hop > 0:
                    copy(high, c, down_send, me).wait_recv()

                @pl.when(has_low)
                def _():
                    copy(high, c, down_send, me - 1).start()

            return carry

        lax.fori_loop(0, PIECES, step, 0)
    wide = x_ref.shape[1]
    for block in range(n):
        out_ref[:, block * wide : (block + 1) * wide] = blocks_ref[block].astype(jnp.bfloat16)
    for hop in range(n):
        low, high = me - hop, me + hop

        def drain(c, carry):
            @pl.when((low >= 0) & has_high)
            def _():
                copy(low, c, up_send, me).wait_send()

            @pl.when((high < n) & has_low)
            def _():
                copy(high, c, down_send, me).wait_send()

            return carry

        lax.fori_loop(0, PIECES, drain, 0)


def line_gather(x, n, name):
    length, wide = x.shape
    full = pl.BlockSpec(memory_space=pltpu.VMEM)
    return pl.pallas_call(
        functools.partial(line_gather_kernel, n),
        out_shape=jax.ShapeDtypeStruct((length, n * wide), jnp.bfloat16),
        in_specs=[full],
        out_specs=full,
        scratch_shapes=[pltpu.VMEM((n, length, wide), jnp.float32)]
        + [pltpu.SemaphoreType.DMA((n, PIECES))] * 3,
        compiler_params=pltpu.CompilerParams(
            collective_id=name, has_side_effects=True, vmem_limit_bytes=32 << 20
        ),
        cost_estimate=pl.CostEstimate(
            flops=0, bytes_accessed=16 * n * x.size, transcendentals=0
        ),
    )(x)


BLOCK = 256


def own_rows_kernel(parts, weight_ref, out_ref):
    rows = out_ref.shape[0]
    first = lax.axis_index("dp") * rows if parts > 1 else 0
    out_ref[...] = weight_ref[pl.ds(pl.multiple_of(first, 16), rows), :].astype(jnp.float32)


def gather_out_weight(out_weight, parts):
    rows, width = out_weight.shape
    ways = parts if rows % (16 * parts) == 0 else 1
    full = pl.BlockSpec(memory_space=pltpu.VMEM)
    own = pl.pallas_call(
        functools.partial(own_rows_kernel, ways),
        out_shape=jax.ShapeDtypeStruct((rows // ways, width), jnp.float32),
        in_specs=[full],
        out_specs=full,
    )(out_weight)
    return ways, lax.all_gather(own, "tensor")


def middle_kernel(
    attended_ref, weight_all_ref, tokens_ref, gain_ref, router_ref, chosen_ref, middle_out, normed_out, gates_out, weight_ref
):
    ways, n, rows, unused = weight_all_ref.shape
    for way in range(ways):
        for block in range(n):
            at = (block * ways + way) * rows
            weight_ref[at : at + rows, :] = weight_all_ref[way, block].astype(jnp.bfloat16)
    for first in range(0, tokens_ref.shape[0], BLOCK):
        own = slice(first, first + BLOCK)
        branch = jnp.dot(attended_ref[own, :], weight_ref[...], preferred_element_type=jnp.float32)
        middle = tokens_ref[own, :].astype(jnp.float32) + RESIDUAL * branch
        middle_out[own, :] = middle
        recip = lax.rsqrt(jnp.mean(middle * middle, axis=1, keepdims=True) + EPSILON)
        normed = (middle * recip * gain_ref[...]).astype(jnp.bfloat16)
        normed_out[own, :] = normed
        logits = jnp.dot(normed, router_ref[...], preferred_element_type=jnp.float32)
        raised = jnp.where(chosen_ref[own, :] > 0.0, jnp.exp(logits), 0.0)
        gates_out[own, :] = raised / jnp.sum(raised, axis=1, keepdims=True)


def enter_middle(attended, weight_all, tokens, gain, router, chosen):
    length, width = tokens.shape
    full = pl.BlockSpec(memory_space=pltpu.VMEM)
    return pl.pallas_call(
        middle_kernel,
        out_shape=[
            jax.ShapeDtypeStruct((length, width), jnp.float32),
            jax.ShapeDtypeStruct((length, width), jnp.bfloat16),
            jax.ShapeDtypeStruct((length, router.shape[1]), jnp.float32),
        ],
        in_specs=[full] * 6,
        out_specs=[full] * 3,
        scratch_shapes=[pltpu.VMEM((attended.shape[1], width), jnp.bfloat16)],
        compiler_params=pltpu.CompilerParams(vmem_limit_bytes=56 << 20),
        cost_estimate=pl.CostEstimate(
            flops=2 * length * width * width, bytes_accessed=25 * 10**6, transcendentals=0
        ),
    )(attended, weight_all, tokens, gain.reshape(1, width), router, chosen)


def turn_kernel(
    summed_ref, grad_gates_ref, gates_ref, middle_ref, cotangent_ref, gain_ref, router_ref, grad_out, branch_out, logits_out, gain_out
):
    length, width = summed_ref.shape
    experts = grad_gates_ref.shape[0]
    gates_rows = jnp.concatenate(
        [grad_gates_ref[...], jnp.zeros((128 - experts, length), jnp.float32)], 0
    )
    gain_sum = jnp.zeros((1, width), jnp.float32)
    for first in range(0, length, BLOCK):
        own = slice(first, first + BLOCK)
        grad_gates = jnp.transpose(gates_rows[:, own])
        gates = gates_ref[own, :]
        weighted = jnp.sum(gates * grad_gates, axis=1, keepdims=True)
        grad_logits = (gates * (grad_gates - weighted)).astype(jnp.bfloat16)
        logits_out[own, :] = grad_logits
        grad = summed_ref[own, :] + right_inner(grad_logits, router_ref[...])
        middle = middle_ref[own, :]
        recip = lax.rsqrt(jnp.mean(middle * middle, axis=1, keepdims=True) + EPSILON)
        unit = middle * recip
        gain_sum += jnp.sum(grad * unit, axis=0, keepdims=True)
        scaled = grad * gain_ref[...]
        back = recip * (scaled - unit * jnp.mean(scaled * unit, axis=1, keepdims=True))
        total = cotangent_ref[own, :].astype(jnp.float32) + back
        grad_out[own, :] = total
        branch_out[own, :] = (RESIDUAL * total).astype(jnp.bfloat16)
    gain_out[...] = gain_sum


def turn_middle(summed, grad_gates, gates, middle, cotangent, gain, router):
    length, width = summed.shape
    full = pl.BlockSpec(memory_space=pltpu.VMEM)
    return pl.pallas_call(
        turn_kernel,
        out_shape=[
            jax.ShapeDtypeStruct((length, width), jnp.float32),
            jax.ShapeDtypeStruct((length, width), jnp.bfloat16),
            jax.ShapeDtypeStruct((length, gates.shape[1]), jnp.bfloat16),
            jax.ShapeDtypeStruct((1, width), jnp.float32),
        ],
        in_specs=[full] * 7,
        out_specs=[full] * 4,
        compiler_params=pltpu.CompilerParams(vmem_limit_bytes=48 << 20),
        cost_estimate=pl.CostEstimate(
            flops=40 * length * width, bytes_accessed=25 * 10**6, transcendentals=0
        ),
    )(summed, grad_gates, gates, middle, cotangent, gain.reshape(1, width), router)


SPAN = 768
ROWS = 256


def lane_halves(shape):
    return lax.broadcasted_iota(jnp.int32, shape, len(shape) - 1) // HEAD


def select_halves(tile, source, half):
    kept = jnp.where(lane_halves(tile.shape) == source, tile, 0.0)
    return kept if source == half else pltpu.roll(kept, HEAD, 1)


def spread_pairs(tile, target):
    for source in range(2):
        for half in range(2):
            target[2 * source + half] = select_halves(tile, source, half).astype(jnp.bfloat16)


def rope_tile(tile, cosine, sine_low, sine_high):
    return tile * cosine + pltpu.roll(tile, 128 - HEAD // 2, 1) * sine_low + pltpu.roll(
        tile, HEAD // 2, 1
    ) * sine_high


def rope_back_tile(tile, cosine, sine_low, sine_high):
    return (
        tile * cosine
        + pltpu.roll(tile * sine_low, HEAD // 2, 1)
        + pltpu.roll(tile * sine_high, 128 - HEAD // 2, 1)
    )


def window(block):
    first = block * ROWS
    return first, jnp.maximum(first + ROWS - SPAN, 0)


def attend_forward_kernel(
    heads,
    group,
    tokens_ref,
    gain_ref,
    query_w,
    key_w,
    value_w,
    cosine_ref,
    sine_low_ref,
    sine_high_ref,
    opening_ref,
    normed_out,
    query_out,
    key_out,
    value_out,
    attended_out,
    logsum_out,
    key_pairs,
    value_pairs,
    tiles_ref,
):
    tiles, length, unused = query_out.shape
    hidden = tokens_ref[...].astype(jnp.float32)
    recip = lax.rsqrt(jnp.mean(hidden * hidden, axis=1, keepdims=True) + EPSILON)
    normed_out[...] = (hidden * recip * gain_ref[...]).astype(jnp.bfloat16)
    cosine, sine_low, sine_high = cosine_ref[...], sine_low_ref[...], sine_high_ref[...]
    for tile in range(tiles):
        query = jnp.dot(
            normed_out[...],
            query_w[:, tile * 128 : (tile + 1) * 128],
            preferred_element_type=jnp.float32,
        )
        query_out[tile] = rope_tile(query, cosine, sine_low, sine_high).astype(jnp.bfloat16)
    key = rope_tile(
        jnp.dot(normed_out[...], key_w[...], preferred_element_type=jnp.float32),
        cosine,
        sine_low,
        sine_high,
    )
    value = jnp.dot(normed_out[...], value_w[...], preferred_element_type=jnp.float32)
    key_out[...] = key.astype(jnp.bfloat16)
    value_out[...] = value.astype(jnp.bfloat16)
    spread_pairs(key, key_pairs)
    spread_pairs(value, value_pairs)
    blocks = length // ROWS
    tiles_ref[...] = jnp.zeros_like(tiles_ref)

    def unit(step, carry):
        head, block = step // blocks, step % blocks
        tile, half = head // 2, head % 2
        pair = 2 * (head // group) + half
        first, low = window(block)
        rows = pl.ds(pl.multiple_of(first, ROWS), ROWS)
        span = pl.ds(pl.multiple_of(low, ROWS), SPAN)
        scores = right_inner(query_out[tile, rows, :], key_pairs[pair, span, :])
        columns = low + lax.broadcasted_iota(jnp.int32, (ROWS, SPAN), 1)
        own = first + lax.broadcasted_iota(jnp.int32, (ROWS, SPAN), 0)
        allowed = (columns >= opening_ref[rows, :]) & (columns <= own)
        raised = jnp.where(allowed, jnp.exp(ATTN_SCALE * scores), 0.0)
        total = jnp.sum(raised, axis=1, keepdims=True)
        product = jnp.dot(
            raised.astype(jnp.bfloat16), value_pairs[pair, span, :], preferred_element_type=jnp.float32
        )
        tiles_ref[tile, rows, :] += product / total
        wide = jnp.broadcast_to(jnp.log(total), (ROWS, 128))
        logsum_out[head, :, rows] = jnp.transpose(wide)[:1]
        return carry

    lax.fori_loop(0, heads * blocks, unit, 0)
    for tile in range(tiles):
        attended_out[:, tile * 128 : (tile + 1) * 128] = tiles_ref[tile].astype(jnp.bfloat16)


def attend_forward(tokens, gain, query_w, key_w, value_w, tables, opening, heads, group):
    length, width = tokens.shape
    wide = query_w.shape[1]
    tiles = wide // 128
    bf16, f32 = jnp.bfloat16, jnp.float32
    full = pl.BlockSpec(memory_space=pltpu.VMEM)
    return pl.pallas_call(
        functools.partial(attend_forward_kernel, heads, group),
        out_shape=[
            jax.ShapeDtypeStruct((length, width), bf16),
            jax.ShapeDtypeStruct((tiles, length, 128), bf16),
            jax.ShapeDtypeStruct((length, 128), bf16),
            jax.ShapeDtypeStruct((length, 128), bf16),
            jax.ShapeDtypeStruct((length, wide), bf16),
            jax.ShapeDtypeStruct((heads, 1, length), f32),
        ],
        in_specs=[full] * 9,
        out_specs=[full] * 6,
        scratch_shapes=[
            pltpu.VMEM((4, length, 128), bf16),
            pltpu.VMEM((4, length, 128), bf16),
            pltpu.VMEM((tiles, length, 128), f32),
        ],
        compiler_params=pltpu.CompilerParams(vmem_limit_bytes=48 << 20),
        cost_estimate=pl.CostEstimate(
            flops=8 * 10**9, bytes_accessed=12 * 10**6, transcendentals=5 * 10**6
        ),
    )(tokens, gain.reshape(1, width), query_w, key_w, value_w, *tables, opening.reshape(length, 1))


def attend_backward_kernel(
    n,
    heads,
    group,
    branch_ref,
    out_w,
    query_ref,
    key_ref,
    value_ref,
    attended_ref,
    logsum_ref,
    query_w,
    key_w,
    value_w,
    cosine_ref,
    sine_low_ref,
    sine_high_ref,
    opening_ref,
    tokens_ref,
    moe_ref,
    grads_out,
    normed_out,
    gain_out,
    moe_out,
    key_pairs,
    value_pairs,
    attend_grads,
    query_grads,
    key_grads,
    value_grads,
    delta_ref,
    *line,
):
    tiles, length, unused = query_ref.shape
    line_start, line_step, line_end = line_stages(n, [moe_ref], [moe_out], line)
    line_start()
    blocks = length // ROWS
    units = heads * blocks
    taken = 0

    def run_line(steps):
        nonlocal taken
        until = min(taken + steps, 2 * STEPS)
        lax.fori_loop(taken, until, line_step, 0)
        taken = until

    run_line(2)
    spread_pairs(key_ref[...].astype(jnp.float32), key_pairs)
    spread_pairs(value_ref[...].astype(jnp.float32), value_pairs)
    halves = (
        lax.broadcasted_iota(jnp.int32, (8, 128), 0) == lane_halves((8, 128))
    ).astype(jnp.float32)
    for tile in range(tiles):
        lanes = slice(tile * 128, (tile + 1) * 128)
        grad = right_inner(branch_ref[...], out_w[lanes, :]).astype(jnp.bfloat16)
        attend_grads[tile] = grad
        products = grad.astype(jnp.float32) * attended_ref[:, lanes].astype(jnp.float32)
        sums = lax.dot_general(
            halves,
            products,
            (((1,), (1,)), ((), ())),
            precision=lax.Precision.HIGHEST,
            preferred_element_type=jnp.float32,
        )
        delta_ref[2 * tile] = sums[0:1]
        delta_ref[2 * tile + 1] = sums[1:2]
        run_line(2)
    query_grads[...] = jnp.zeros_like(query_grads)
    key_grads[...] = jnp.zeros_like(key_grads)
    value_grads[...] = jnp.zeros_like(value_grads)
    before, each = taken, (2 * STEPS - 8 - taken) // units
    taken += units * each

    def unit(step, carry):
        lax.fori_loop(before + step * each, before + step * each + each, line_step, 0)
        head, block = step // blocks, step % blocks
        tile, half = head // 2, head % 2
        pair = 2 * (head // group) + half
        first, low = window(block)
        rows = pl.ds(pl.multiple_of(first, ROWS), ROWS)
        span = pl.ds(pl.multiple_of(low, ROWS), SPAN)
        keys = key_pairs[pair, span, :]
        query = query_ref[tile, rows, :]
        grad = attend_grads[tile, rows, :]
        scores = right_inner(keys, query)
        columns = low + lax.broadcasted_iota(jnp.int32, (SPAN, ROWS), 0)
        own = first + lax.broadcasted_iota(jnp.int32, (SPAN, ROWS), 1)
        allowed = (columns >= opening_ref[:, rows]) & (columns <= own)
        probs = jnp.where(
            allowed, jnp.exp(ATTN_SCALE * scores - logsum_ref[head, :, rows]), 0.0
        )
        grad_probs = right_inner(value_pairs[pair, span, :], grad)
        grad_scores = (probs * (grad_probs - delta_ref[head, :, rows])).astype(jnp.bfloat16)
        value_grads[pair, span, :] += jnp.dot(
            probs.astype(jnp.bfloat16), grad, preferred_element_type=jnp.float32
        )
        key_grads[pair, span, :] += jnp.dot(
            grad_scores, query, preferred_element_type=jnp.float32
        )
        query_grads[tile, rows, :] += left_inner(grad_scores, keys)
        return carry

    lax.fori_loop(0, units, unit, 0)
    cosine, sine_low, sine_high = cosine_ref[...], sine_low_ref[...], sine_high_ref[...]
    wide = tiles * 128
    for tile in range(tiles):
        grads_out[:, tile * 128 : (tile + 1) * 128] = rope_back_tile(
            ATTN_SCALE * query_grads[tile], cosine, sine_low, sine_high
        ).astype(jnp.bfloat16)
    totals = []
    for grads in (key_grads, value_grads):
        totals.append(
            sum(
                select_halves(grads[2 * source + half], half, source)
                for source in range(2)
                for half in range(2)
            )
        )
    grads_out[:, wide : wide + 128] = rope_back_tile(
        ATTN_SCALE * totals[0], cosine, sine_low, sine_high
    ).astype(jnp.bfloat16)
    grads_out[:, wide + 128 : wide + 256] = totals[1].astype(jnp.bfloat16)
    gain_sum = jnp.zeros((1, normed_out.shape[1]), jnp.float32)
    for block in range(blocks):
        rows = slice(block * ROWS, (block + 1) * ROWS)
        normed = (
            right_inner(grads_out[rows, :wide], query_w[...])
            + right_inner(grads_out[rows, wide : wide + 128], key_w[...])
            + right_inner(grads_out[rows, wide + 128 :], value_w[...])
        )
        normed_out[rows, :] = normed
        hidden = tokens_ref[rows, :].astype(jnp.float32)
        recip = lax.rsqrt(jnp.mean(hidden * hidden, axis=1, keepdims=True) + EPSILON)
        gain_sum += jnp.sum(normed * (hidden * recip), axis=0, keepdims=True)
        run_line(2)
    gain_out[...] = gain_sum
    run_line(2 * STEPS)
    line_end()


def attend_backward(
    n, branch, out_w, query, key, value, attended, logsum, query_w, key_w, value_w, tables, opening, tokens, moe,
    heads, group, name,
):
    length, width = branch.shape
    tiles = query.shape[0]
    wide = tiles * 128
    bf16, f32 = jnp.bfloat16, jnp.float32
    full = pl.BlockSpec(memory_space=pltpu.VMEM)
    return pl.pallas_call(
        functools.partial(attend_backward_kernel, n, heads, group),
        out_shape=[
            jax.ShapeDtypeStruct((length, wide + 256), bf16),
            jax.ShapeDtypeStruct((length, width), f32),
            jax.ShapeDtypeStruct((1, width), f32),
            jax.ShapeDtypeStruct((length, width), f32),
        ],
        in_specs=[full] * 16,
        out_specs=[full] * 4,
        scratch_shapes=[
            pltpu.VMEM((4, length, 128), bf16),
            pltpu.VMEM((4, length, 128), bf16),
            pltpu.VMEM((tiles, length, 128), bf16),
            pltpu.VMEM((tiles, length, 128), f32),
            pltpu.VMEM((4, length, 128), f32),
            pltpu.VMEM((4, length, 128), f32),
            pltpu.VMEM((2 * tiles, 1, length), f32),
        ]
        + line_scratch([moe]),
        compiler_params=pltpu.CompilerParams(
            collective_id=name, has_side_effects=True, vmem_limit_bytes=62 << 20
        ),
        cost_estimate=pl.CostEstimate(
            flops=12 * 10**9, bytes_accessed=30 * 10**6, transcendentals=5 * 10**6
        ),
    )(
        branch, out_w, query, key, value, attended, logsum, query_w, key_w, value_w, *tables,
        opening.reshape(1, length), tokens, moe,
    )


def finish_kernel(
    n,
    parts,
    local_ref,
    normed_ref,
    grads_ref,
    branch_ref,
    attended_ref,
    normed_two_ref,
    logits_ref,
    gain_ref,
    first_gain_ref,
    normed_out,
    query_out,
    key_out,
    value_out,
    branch_out,
    router_out,
    gain_out,
    first_gain_out,
    weights_ref,
    gains_ref,
    gain_send,
    gain_recv,
    *scratch,
):
    levels = parts.bit_length() - 1
    held = scratch[:levels]
    sends, recvs = scratch[levels : levels + 2]
    line_start, line_step, line_end = line_stages(n, [local_ref], [normed_out], scratch[levels + 2 :])
    me = lax.axis_index("dp")
    width = normed_ref.shape[1]
    own = width // parts
    wide, attended_wide = grads_ref.shape[1], attended_ref.shape[1]
    mine = lax.axis_index("tensor")
    line_start(
        [{"dp": jnp.bitwise_xor(me, 1 << level)} for level in range(levels)]
        + [{"tensor": lax.rem(mine + ahead, n)} for ahead in range(1, n)]
    )

    def run_line(first, last):
        lax.fori_loop(first, last, line_step, 0)

    run_line(0, 2)
    pieces = 4
    block = width // pieces
    for piece in range(pieces):
        rows = slice(piece * block, (piece + 1) * block)
        weights_ref[rows, :wide] = left_inner(normed_ref[:, rows], grads_ref[...])
        weights_ref[rows, wide : wide + attended_wide] = left_inner(
            branch_ref[:, rows], attended_ref[...]
        )
        gain = jnp.transpose(jnp.broadcast_to(gain_ref[:, rows], (128, block)))
        first_gain = jnp.transpose(jnp.broadcast_to(first_gain_ref[:, rows], (128, block)))
        lanes = lax.broadcasted_iota(jnp.int32, (block, 128), 1)
        weights_ref[rows, wide + attended_wide :] = jnp.where(
            lanes == 127,
            gain,
            jnp.where(
                lanes == 126, first_gain, left_inner(normed_two_ref[:, rows], logits_ref[...])
            ),
        )
        run_line(2 + 2 * piece, 4 + 2 * piece)
    done = 2 + 2 * pieces

    columns = weights_ref.shape[1]
    middle = columns // 256 * 128
    orders = (
        (slice(0, middle), list(range(levels))),
        (slice(middle, columns), [0] + list(range(levels - 1, 0, -1))),
    )

    def shard(number, lanes):
        return weights_ref.at[pl.ds(pl.multiple_of(number * own, own), own), lanes]

    def numbers(order, level, peer):
        fixed = sum(1 << bit for bit in order[: level + 1])
        base = jnp.bitwise_and(peer, fixed)
        free = order[level + 1 :]
        return [
            base + sum(((i >> place) & 1) << bit for place, bit in enumerate(free))
            for i in range(1 << len(free))
        ]

    def copies(level):
        made = []
        for side, (lanes, order) in enumerate(orders):
            peer = jnp.bitwise_xor(me, 1 << order[level])
            for i, number in enumerate(numbers(order, level, peer)):
                made.append(
                    pltpu.make_async_remote_copy(
                        src_ref=shard(number, lanes),
                        dst_ref=held[level].at[i, :, lanes],
                        send_sem=sends.at[side, level, i],
                        recv_sem=recvs.at[side, level, i],
                        device_id={"dp": peer},
                        device_id_type=MESH,
                    )
                )
        return made

    stops = [6, 28, 18, 2]
    for level in range(levels):
        for copy in copies(level):
            copy.start()
        until = done + stops[level]
        run_line(done, until)
        done = until
        for copy in copies(level):
            copy.wait_recv()
        for lanes, order in orders:
            for i, number in enumerate(numbers(order, level, me)):
                target = shard(number, lanes)
                target[...] += held[level][i, :, lanes]
    everything = slice(0, columns)
    gains_ref[0] = shard(me, slice(wide + attended_wide, columns))[...]
    gain_copies = [
        pltpu.make_async_remote_copy(
            src_ref=gains_ref.at[0],
            dst_ref=gains_ref.at[ahead],
            send_sem=gain_send.at[ahead],
            recv_sem=gain_recv.at[ahead],
            device_id={"tensor": lax.rem(mine + ahead, n)},
            device_id_type=MESH,
        )
        for ahead in range(1, n)
    ]
    for copy in gain_copies:
        copy.start()
    kept = shard(me, everything)
    query_out[...] = kept[:, : query_out.shape[1]]
    key_out[...] = kept[:, wide - 256 : wide - 256 + key_out.shape[1]]
    value_out[...] = kept[:, wide - 128 : wide - 128 + value_out.shape[1]]
    branch_out[...] = jnp.transpose(kept[:, wide : wide + attended_wide])[: branch_out.shape[0]]
    router_out[...] = gains_ref[0][:, : router_out.shape[1]]
    run_line(done, 2 * STEPS)
    total = gains_ref[0]
    for ahead, copy in enumerate(gain_copies, 1):
        copy.wait_recv()
        total = total + gains_ref[ahead]
    gain_out[...] = jnp.transpose(gains_ref[0])[127:]
    first_gain_out[...] = jnp.transpose(total)[126:127]
    for level in range(levels):
        for copy in copies(level):
            copy.wait_send()
    for copy in gain_copies:
        copy.wait_send()
    line_end()


def finish(
    n, parts, grad_local, normed_b, grads_wide, branch_b, attended, normed_two_b, grad_logits_b, gain_grad, first_gain_grad,
    wide_q, wide_k, experts, name,
):
    length, width = normed_b.shape
    columns = grads_wide.shape[1] + attended.shape[1] + 128
    full = pl.BlockSpec(memory_space=pltpu.VMEM)
    levels = parts.bit_length() - 1
    own = width // parts
    f32 = jnp.float32
    shapes = [(length, width), (own, wide_q), (own, wide_k), (own, wide_k), (wide_q, own)]
    shapes += [(own, experts), (1, own), (1, own)]
    return pl.pallas_call(
        functools.partial(finish_kernel, n, parts),
        out_shape=[jax.ShapeDtypeStruct(shape, f32) for shape in shapes],
        in_specs=[full] * 9,
        out_specs=[full] * 8,
        scratch_shapes=[
            pltpu.VMEM((width, columns), f32),
            pltpu.VMEM((n, own, 128), f32),
            pltpu.SemaphoreType.DMA((n,)),
            pltpu.SemaphoreType.DMA((n,)),
        ]
        + [pltpu.VMEM((parts >> (level + 1), own, columns), f32) for level in range(levels)]
        + [pltpu.SemaphoreType.DMA((2, levels, parts // 2))] * 2
        + line_scratch([grad_local]),
        compiler_params=pltpu.CompilerParams(
            collective_id=name, has_side_effects=True, vmem_limit_bytes=62 << 20
        ),
        cost_estimate=pl.CostEstimate(
            flops=2 * length * width * columns, bytes_accessed=50 * 10**6, transcendentals=0
        ),
    )(
        grad_local, normed_b, grads_wide, branch_b, attended, normed_two_b, grad_logits_b, gain_grad,
        first_gain_grad,
    )


def place_kernel(shards_ref, *refs):
    gate_out, up_out, down_out = refs[-3:]
    gate_out[0] = shards_ref[0, 0]
    up_out[0] = shards_ref[0, 1]
    rows, hidden = down_out.shape[1], shards_ref.shape[3]
    for piece in range(down_out.shape[2] // hidden):
        down_out[0, :, piece * hidden : (piece + 1) * hidden] = shards_ref[
            0, 2, piece * rows : (piece + 1) * rows, :
        ]


def place_shards(parts, shards, first, experts, before):
    number, unused, rows, hidden = shards.shape
    down_rows = hidden // parts
    width = rows * parts
    shapes = [(experts, rows, hidden), (experts, rows, hidden), (experts, down_rows, width)]
    spec = lambda shape: pl.BlockSpec((1,) + shape[1:], lambda e: (first + e, 0, 0))
    args, extra, aliases = [shards], [], {}
    if before is not None:
        args += list(before)
        extra = [pl.BlockSpec(memory_space=pl.ANY)] * 3
        aliases = {1: 0, 2: 1, 3: 2}
    return pl.pallas_call(
        place_kernel,
        out_shape=[jax.ShapeDtypeStruct(shape, jnp.float32) for shape in shapes],
        grid=(number,),
        in_specs=[pl.BlockSpec((1, 3, rows, hidden), lambda e: (e, 0, 0, 0))] + extra,
        out_specs=[spec(shape) for shape in shapes],
        input_output_aliases=aliases,
        cost_estimate=pl.CostEstimate(
            flops=0, bytes_accessed=8 * shards.size, transcendentals=0
        ),
    )(*args)


def on_device(
    ring,
    tokens,
    cotangent,
    segment_ids,
    routes,
    attn_gain,
    query_weight,
    key_weight,
    value_weight,
    out_weight,
    ffn_gain,
    router_weight,
    gate_weight,
    up_weight,
    down_weight,
):
    length = tokens.shape[0]
    width = tokens.shape[1]
    segment = segment_ids[0]
    heads_local = query_weight.shape[1] // HEAD
    kv_local = key_weight.shape[1] // HEAD
    group_size = heads_local // kv_local
    experts_all = router_weight.shape[1]
    experts_local = gate_weight.shape[0]
    parts = lax.axis_size("dp")
    opening = doc_openings(segment)
    tables = rope_tables(opening, HEAD)
    query_w, key_w, value_w = (pad_columns(w) for w in (query_weight, key_weight, value_weight))
    out_w = jnp.transpose(pad_columns(jnp.transpose(out_weight)))
    hidden_in = tokens.astype(jnp.float32)
    ways, out_rows = gather_out_weight(out_weight, parts)
    normed_b, queries, keys, values, attended, logsum = attend_forward(
        tokens, attn_gain, query_w, key_w, value_w, tables, opening, heads_local, group_size
    )
    all_ids = jnp.arange(experts_all, dtype=jnp.int32)
    chosen = jnp.sum((routes[:, :, None] == all_ids[None, None, :]).astype(jnp.int32), axis=1) > 0
    first_expert = lax.axis_index("tensor") * experts_local
    local_ids = first_expert + jnp.arange(experts_local, dtype=jnp.int32)
    picked = jnp.sum((routes[None, :, :] == local_ids[:, None, None]).astype(jnp.int32), axis=2)
    places_in = slot_places(picked)
    counts = jnp.sum(picked, axis=1)
    out_rows, attended = lax.optimization_barrier((out_rows, attended))
    out_all = lax.all_gather(out_rows, "dp") if ways > 1 else out_rows[None]
    attended_all = line_gather(attended, ring, 1)
    attended_all = attended_all.reshape(length, ring, attended.shape[1])
    attended_all = attended_all[:, :, : heads_local * HEAD].reshape(length, -1)
    router_w = pad_columns(router_weight)
    middle, normed_two_b, gate_probs = enter_middle(
        attended_all, out_all, tokens, ffn_gain, router_w, pad_columns(chosen.astype(jnp.float32))
    )
    gate_rows = jnp.transpose(lax.dynamic_slice_in_dim(gate_probs, first_expert, experts_local, 1))
    numbers = (max(1, experts_local // 10), max(1, 3 * experts_local // 10))
    numbers += (experts_local - sum(numbers),)
    (grads_first,), sums = expert_stage(
        parts, 0, numbers[:1], counts, places_in, gate_rows, normed_two_b, cotangent,
        gate_weight, up_weight, down_weight, None,
    )
    shards_first = lax.psum_scatter(grads_first, "dp", scatter_dimension=2, tiled=True)
    (grads_middle, grads_last), sums_last = expert_stage(
        parts, numbers[0], numbers[1:], counts, places_in, gate_rows, normed_two_b, cotangent,
        gate_weight, up_weight, down_weight, sums,
    )
    shards_first, grads_middle = lax.optimization_barrier((shards_first, grads_middle))
    shards_middle = lax.psum_scatter(grads_middle, "dp", scatter_dimension=2, tiled=True)
    moe_part, grad_normed_part, unused = sums_last
    grad_gates_local = jnp.concatenate([sums[2], sums_last[2]], 0)
    grad_gates_part = lax.dynamic_update_slice_in_dim(
        jnp.zeros((experts_all, length), jnp.float32),
        grad_gates_local.reshape(experts_local, length),
        first_expert,
        0,
    ).reshape(-1, 128)
    grad_gates_part = jnp.pad(grad_gates_part, ((0, GATE_ROWS - grad_gates_part.shape[0]), (0, 0)))
    shards_first, grad_normed_part = lax.optimization_barrier((shards_first, grad_normed_part))
    grad_normed_sum, gates_sum = line_sum(grad_normed_part, grad_gates_part, ring, 2)
    grad_gates = gates_sum[: experts_all * length // 128].reshape(experts_all, length)
    grad_middle, grad_branch_b, grad_logits_b, grad_ffn_gain = turn_middle(
        grad_normed_sum, grad_gates, gate_probs, middle, cotangent, ffn_gain, router_w
    )
    shards_middle, grads_last, grad_branch_b = lax.optimization_barrier(
        (shards_middle, grads_last, grad_branch_b)
    )
    shards_last = lax.psum_scatter(grads_last, "dp", scatter_dimension=2, tiled=True)
    grads_wide, grad_normed_local, first_gain, moe_out = attend_backward(
        ring, grad_branch_b, out_w, queries, keys, values, attended, logsum,
        query_w, key_w, value_w, tables, opening, tokens, moe_part, heads_local, group_size, 3,
    )
    output = (middle + RESIDUAL * moe_out).astype(jnp.bfloat16)
    wide_q, wide_k = heads_local * HEAD, kv_local * HEAD
    grad_normed, *small = finish(
        ring, parts, grad_normed_local, normed_b, grads_wide, grad_branch_b, attended, normed_two_b,
        grad_logits_b, grad_ffn_gain, first_gain, wide_q, wide_k, experts_all, 4,
    )
    grad_query, grad_key, grad_value, grad_out, grad_router, grad_ffn_gain, grad_attn_gain = small
    recip_one = lax.rsqrt(jnp.mean(hidden_in * hidden_in, axis=-1, keepdims=True) + EPSILON)
    unit_one = hidden_in * recip_one
    scaled = grad_normed * attn_gain
    inner = jnp.mean(scaled * unit_one, axis=-1, keepdims=True)
    grad_tokens = grad_middle + recip_one * (scaled - unit_one * inner)
    shards_last, grad_tokens = lax.optimization_barrier((shards_last, grad_tokens))
    grads_placed = place_shards(parts, shards_first, 0, experts_local, None)
    grads_placed = place_shards(parts, shards_middle, numbers[0], experts_local, grads_placed)
    grad_gate, grad_up, grad_down = place_shards(
        parts, shards_last, numbers[0] + numbers[1], experts_local, grads_placed
    )
    return (
        output,
        grad_tokens,
        grad_attn_gain.reshape(-1),
        grad_query,
        grad_key,
        grad_value,
        grad_out,
        grad_ffn_gain.reshape(-1),
        grad_router,
        grad_gate,
        grad_up,
        grad_down,
    )


def solution(mesh):
    return jax.shard_map(
        functools.partial(on_device, mesh.shape["tensor"]),
        mesh=mesh,
        in_specs=(
            P("dp", None),
            P("dp", None),
            P("dp", None),
            P("dp", None),
            P(),
            P(None, "tensor"),
            P(None, "tensor"),
            P(None, "tensor"),
            P("tensor", None),
            P(),
            P(),
            P("tensor", None, None),
            P("tensor", None, None),
            P("tensor", None, None),
        ),
        out_specs=(
            P("dp", None),
            P("dp", None),
            P("dp"),
            P("dp", "tensor"),
            P("dp", "tensor"),
            P("dp", "tensor"),
            P("tensor", "dp"),
            P("dp"),
            P("dp", None),
            P("tensor", "dp", None),
            P("tensor", "dp", None),
            P("tensor", "dp", None),
        ),
        check_vma=False,
    )
```

```python
import functools

import jax
import jax.numpy as jnp
from jax import lax
from jax.experimental import pallas as pl
from jax.experimental.pallas import tpu as pltpu
from jax.sharding import PartitionSpec as P

MESH = pl.DeviceIdType.MESH

HEAD = 64
CAP = 384


EPSILON = 1e-06
RESIDUAL = 0.22
ATTN_SCALE = 0.015625
ROPE_BASE = 10000.0


def left_inner(first, second):
    return lax.dot_general(
        first, second, (((0,), (0,)), ((), ())), preferred_element_type=jnp.float32
    )


def right_inner(first, second):
    return lax.dot_general(
        first, second, (((1,), (1,)), ((), ())), preferred_element_type=jnp.float32
    )


def doc_openings(segment):
    return jnp.sum((segment[None, :] < segment[:, None]).astype(jnp.int32), axis=1)


def rope_tables(opening, head_size):
    halfway = head_size // 2
    spread = jnp.arange(halfway, dtype=jnp.float32) * (2.0 / head_size)
    inverse = jnp.power(ROPE_BASE, -spread)
    places = jnp.arange(opening.shape[0], dtype=jnp.int32)
    angles = (places - opening).astype(jnp.float32)[:, None] * inverse[None, :]
    cosine, sine = jnp.cos(angles), jnp.sin(angles)
    none = jnp.zeros_like(sine)
    return (
        jnp.concatenate([cosine] * 4, 1),
        jnp.concatenate([-sine, none] * 2, 1),
        jnp.concatenate([none, sine] * 2, 1),
    )


def pad_columns(weight):
    missing = -weight.shape[1] % 128
    return weight if missing == 0 else jnp.pad(weight, ((0, 0), (0, missing)))


def rms_forward(hidden, gain):
    recip = lax.rsqrt(jnp.mean(hidden * hidden, axis=-1, keepdims=True) + EPSILON)
    unit = hidden * recip
    return (unit * gain, unit, recip)


def rms_backward(gradient, unit, recip, gain):
    gain_grad = jnp.sum(gradient * unit, axis=0)
    scaled = gradient * gain
    return (recip * (scaled - unit * jnp.mean(scaled * unit, axis=-1, keepdims=True)), gain_grad)


def slot_places(picked):
    length = picked.shape[1]
    tokens = jnp.arange(length, dtype=jnp.int32)
    earlier = (tokens[:, None] < tokens[None, :]).astype(jnp.bfloat16)
    before = jnp.dot(picked.astype(jnp.bfloat16), earlier, preferred_element_type=jnp.float32)
    return jnp.where(picked > 0, before.astype(jnp.int32), -1)


STEPS = 32
LAG = 2


def line_stages(n, xs, outs, scratch, done=None):
    count = len(xs)
    lows, highs = scratch[:count], scratch[count : 2 * count]
    low_recv, high_recv, total_recv, up_send, low_send, high_send = scratch[2 * count :]
    me = lax.axis_index("tensor")
    root = n // 2
    has_low, has_high = me > 0, me < n - 1

    def begin(others=()):
        barrier = pltpu.get_barrier_semaphore()
        for other in others:
            pl.semaphore_signal(barrier, inc=1, device_id=other, device_id_type=MESH)

        @pl.when(has_low)
        def _():
            pl.semaphore_signal(barrier, inc=1, device_id={"tensor": me - 1}, device_id_type=MESH)

        @pl.when(has_high)
        def _():
            pl.semaphore_signal(barrier, inc=1, device_id={"tensor": me + 1}, device_id_type=MESH)

        pl.semaphore_wait(
            barrier, len(others) + has_low.astype(jnp.int32) + has_high.astype(jnp.int32)
        )

    def piece(ref, c):
        rows = ref.shape[0] // STEPS
        return ref.at[pl.ds(pl.multiple_of(c * rows, rows), rows), :]

    def copies(sources, targets, c, send, recv, to):
        return [
            pltpu.make_async_remote_copy(
                src_ref=piece(source, c),
                dst_ref=piece(target, c),
                send_sem=send.at[i, c],
                recv_sem=recv.at[i, c],
                device_id={"tensor": to},
                device_id_type=MESH,
            )
            for i, (source, target) in enumerate(zip(sources, targets))
        ]

    def start(sources, targets, c, send, recv, to):
        for copy in copies(sources, targets, c, send, recv, to):
            copy.start()

    def arrived(targets, c, send, recv):
        for copy in copies(targets, targets, c, send, recv, me):
            copy.wait_recv()

    def reduce_step(c):
        for side, inner, held, recv, to in (
            (me < root, has_low, lows, low_recv, me + 1),
            (me > root, has_high, highs, high_recv, me - 1),
        ):

            @pl.when(side & inner)
            def _():
                arrived(held, c, up_send, recv)
                for x, h in zip(xs, held):
                    piece(h, c)[...] += piece(x, c)[...]
                start(held, held, c, up_send, recv, to)

            @pl.when(side & jnp.logical_not(inner))
            def _():
                start(xs, held, c, up_send, recv, to)

        @pl.when(me == root)
        def _():
            arrived(lows, c, up_send, low_recv)
            if root < n - 1:
                arrived(highs, c, up_send, high_recv)
            for x, low, high, out in zip(xs, lows, highs, outs):
                total = piece(x, c)[...] + piece(low, c)[...]
                if root < n - 1:
                    total += piece(high, c)[...]
                piece(out, c)[...] = total
            start(outs, outs, c, low_send, total_recv, me - 1)
            if root < n - 1:
                start(outs, outs, c, high_send, total_recv, me + 1)
            if done is not None:
                done(c)

    def total_step(c):
        @pl.when(me != root)
        def _():
            arrived(outs, c, low_send, total_recv)

        @pl.when((me < root) & has_low)
        def _():
            start(outs, outs, c, low_send, total_recv, me - 1)

        @pl.when((me > root) & has_high)
        def _():
            start(outs, outs, c, high_send, total_recv, me + 1)

        if done is not None:

            @pl.when(me != root)
            def _():
                done(c)

    lag = jnp.where(has_low & has_high, LAG, STEPS)

    def step(t, carry):
        @pl.when(t < STEPS)
        def _():
            reduce_step(t)

        @pl.when((t >= lag) & (t - lag < STEPS))
        def _():
            total_step(t - lag)

        return carry

    def finish():
        def drain(c, carry):
            for condition, send in (
                (me != root, up_send),
                ((me <= root) & has_low, low_send),
                ((me >= root) & has_high, high_send),
            ):

                @pl.when(condition)
                def _():
                    for copy in copies(xs, lows, c, send, low_recv, me):
                        copy.wait_send()

            return carry

        lax.fori_loop(0, STEPS, drain, 0)

    return begin, step, finish


def line_scratch(arrays):
    return [pltpu.VMEM(array.shape, jnp.float32) for array in arrays * 2] + [
        pltpu.SemaphoreType.DMA((len(arrays), STEPS))
    ] * 6


def expert_kernel(
    parts,
    first,
    numbers,
    chained,
    count_ref,
    place_ref,
    gate_ref,
    normed_ref,
    grad_ref,
    gate_w,
    up_w,
    down_w,
    *refs,
):
    if chained:
        moe_in, back_in = refs[:2]
        refs = refs[2:]
    grads_out, refs = refs[: len(numbers)], refs[len(numbers) :]
    moe_out, back_out, gates_out = refs[:3]
    rows_ref, grads_ref, active_ref, gate_in_ref, up_in_ref, weights_ref, sems, out_sems = refs[3:]
    expert = pl.program_id(0)
    filled = count_ref[first + expert]
    length, width = normed_ref.shape
    hidden_size = gate_w.shape[2]
    sizes = (128, 256, CAP)

    def by_size(run):
        low = None
        for rows in sizes:
            fits = filled <= rows if low is None else filled > low
            if low is not None and rows != sizes[-1]:
                fits = fits & (filled <= rows)
            pl.when(fits)(functools.partial(run, rows))
            low = rows

    if chained:
        copy_moe = pltpu.make_async_copy(moe_in, moe_out, sems.at[0])
        copy_back = pltpu.make_async_copy(back_in, back_out, sems.at[1])

        @pl.when(expert == 0)
        def _():
            copy_moe.start()
            copy_back.start()

    else:

        @pl.when(expert == 0)
        def _():
            moe_out[...] = jnp.zeros_like(moe_out)
            back_out[...] = jnp.zeros_like(back_out)

    def slots(rows):
        mask = lax.broadcasted_iota(jnp.int32, (rows, length), 0) == place_ref[0]
        return mask, jnp.where(mask, 1.0, 0.0).astype(jnp.bfloat16)

    def enter(rows):
        mask, picks = slots(rows)
        rows_in = jnp.dot(picks, normed_ref[...], preferred_element_type=jnp.float32).astype(jnp.bfloat16)
        grad_rows = (
            RESIDUAL * jnp.dot(picks, grad_ref[...], preferred_element_type=jnp.float32)
        ).astype(jnp.bfloat16)
        rows_ref[:rows] = rows_in
        grads_ref[:rows] = grad_rows
        gate = jnp.sum(jnp.where(mask, gate_ref[0], 0.0), axis=1, keepdims=True)
        gate_input = jnp.dot(rows_in, gate_w[0], preferred_element_type=jnp.float32)
        up_input = jnp.dot(rows_in, up_w[0], preferred_element_type=jnp.float32)
        grad_act = right_inner(grad_rows, down_w[0])
        sigmoid_val = jax.nn.sigmoid(gate_input)
        silu_out = gate_input * sigmoid_val
        hidden = silu_out * up_input
        active_ref[:rows] = (hidden * gate).astype(jnp.bfloat16)
        column = jnp.sum(grad_act * hidden, axis=1, keepdims=True)
        gates_out[0] = jnp.sum(jnp.where(mask, column, 0.0), axis=0, keepdims=True)
        grad_hidden = grad_act * gate
        gate_in_ref[:rows] = (
            grad_hidden * up_input * sigmoid_val * (1.0 + gate_input * (1.0 - sigmoid_val))
        ).astype(jnp.bfloat16)
        up_in_ref[:rows] = (grad_hidden * silu_out).astype(jnp.bfloat16)

    by_size(enter)
    if chained:

        @pl.when(expert == 0)
        def _():
            copy_moe.wait()
            copy_back.wait()

    def leave(rows):
        column = jnp.transpose(jnp.broadcast_to(place_ref[0], (128, length)))
        column = jnp.concatenate([column] * (rows // 128), 1)
        own = lax.broadcasted_iota(jnp.int32, (length, rows), 1)
        picks = jnp.where(own == column, 1.0, 0.0).astype(jnp.bfloat16)
        moe = jnp.dot(active_ref[:rows], down_w[0], preferred_element_type=jnp.float32)
        moe_out[...] += jnp.dot(
            picks, moe.astype(jnp.bfloat16), preferred_element_type=jnp.float32
        )
        back = right_inner(gate_in_ref[:rows], gate_w[0]) + right_inner(up_in_ref[:rows], up_w[0])
        back_out[...] += jnp.dot(
            picks, back.astype(jnp.bfloat16), preferred_element_type=jnp.float32
        )

    by_size(leave)

    def copies(target, number):
        return [
            pltpu.make_async_copy(weights_ref.at[kind], target.at[number, kind], out_sems.at[kind])
            for kind in range(3)
        ]

    @pl.when(expert > 0)
    def _():
        for copy in copies(grads_out[0], 0):
            copy.wait()

    def weigh(rows):
        grads = left_inner(
            rows_ref[:rows], jnp.concatenate([gate_in_ref[:rows], up_in_ref[:rows]], 1)
        )
        weights_ref[0] = grads[:, :hidden_size]
        weights_ref[1] = grads[:, hidden_size:]
        grad_down = left_inner(active_ref[:rows], grads_ref[:rows])
        own = hidden_size // parts
        blocks = width // hidden_size
        for part in range(parts):
            for piece in range(blocks):
                at = (part * blocks + piece) * own
                weights_ref[2, at : at + own, :] = grad_down[
                    part * own : (part + 1) * own, piece * hidden_size : (piece + 1) * hidden_size
                ]

    by_size(weigh)
    start = 0
    for target, number in zip(grads_out, numbers):

        @pl.when((expert >= start) & (expert < start + number))
        def _():
            for copy in copies(target, expert - start):
                copy.start()

        start += number

    @pl.when(expert == pl.num_programs(0) - 1)
    def _():
        for copy in copies(grads_out[0], 0):
            copy.wait()


def expert_stage(parts, first, numbers, counts, places, gate_rows, normed_b, grad_b, gate_w, up_w, down_w, sums):
    number = sum(numbers)
    length, width = normed_b.shape
    hidden = gate_w.shape[2]
    experts = places.shape[0]
    chained = sums is not None
    whole = lambda e, c: (0, 0)
    row_spec = pl.BlockSpec((1, 1, length), lambda e, c: (first + e, 0, 0))
    once = pl.Buffered(1)
    f32, bf16 = jnp.float32, jnp.bfloat16
    in_specs = [
        row_spec,
        row_spec,
        pl.BlockSpec((length, width), whole, pipeline_mode=once),
        pl.BlockSpec((length, width), whole, pipeline_mode=once),
        pl.BlockSpec((1, width, hidden), lambda e, c: (first + e, 0, 0)),
        pl.BlockSpec((1, width, hidden), lambda e, c: (first + e, 0, 0)),
        pl.BlockSpec((1, hidden, width), lambda e, c: (first + e, 0, 0)),
    ]
    args = [
        counts,
        places.reshape(experts, 1, length),
        gate_rows.reshape(experts, 1, length),
        normed_b,
        grad_b,
        gate_w,
        up_w,
        down_w,
    ]
    if chained:
        in_specs += [pl.BlockSpec(memory_space=pl.ANY)] * 2
        args += [sums[0], sums[1]]
    results = pl.pallas_call(
        functools.partial(expert_kernel, parts, first, numbers, chained),
        out_shape=[jax.ShapeDtypeStruct((some, 3, width, hidden), f32) for some in numbers]
        + [
            jax.ShapeDtypeStruct((length, width), f32),
            jax.ShapeDtypeStruct((length, width), f32),
            jax.ShapeDtypeStruct((number, 1, length), f32),
        ],
        grid_spec=pltpu.PrefetchScalarGridSpec(
            num_scalar_prefetch=1,
            grid=(number,),
            in_specs=in_specs,
            out_specs=[pl.BlockSpec(memory_space=pl.ANY)] * len(numbers)
            + [
                pl.BlockSpec((length, width), whole, pipeline_mode=once),
                pl.BlockSpec((length, width), whole, pipeline_mode=once),
                pl.BlockSpec((1, 1, length), lambda e, c: (e, 0, 0)),
            ],
            scratch_shapes=[
                pltpu.VMEM((CAP, width), bf16),
                pltpu.VMEM((CAP, width), bf16),
                pltpu.VMEM((CAP, hidden), bf16),
                pltpu.VMEM((CAP, hidden), bf16),
                pltpu.VMEM((CAP, hidden), bf16),
                pltpu.VMEM((3, width, hidden), f32),
                pltpu.SemaphoreType.DMA((2,)),
                pltpu.SemaphoreType.DMA((3,)),
            ],
        ),
        compiler_params=pltpu.CompilerParams(
            dimension_semantics=("arbitrary",), vmem_limit_bytes=63 << 20
        ),
        cost_estimate=pl.CostEstimate(
            flops=number * 8 * 10**9, bytes_accessed=number * 14 * 10**6, transcendentals=0
        ),
    )(*args)
    return results[: len(numbers)], results[len(numbers) :]


PIECES = 16


def line_gather_kernel(n, x_ref, out_ref, blocks_ref, recv, up_send, down_send):
    me = lax.axis_index("tensor")
    has_low, has_high = me > 0, me < n - 1
    barrier = pltpu.get_barrier_semaphore()

    @pl.when(has_low)
    def _():
        pl.semaphore_signal(barrier, inc=1, device_id={"tensor": me - 1}, device_id_type=MESH)

    @pl.when(has_high)
    def _():
        pl.semaphore_signal(barrier, inc=1, device_id={"tensor": me + 1}, device_id_type=MESH)

    blocks_ref[me] = x_ref[...].astype(jnp.float32)
    pl.semaphore_wait(barrier, has_low.astype(jnp.int32) + has_high.astype(jnp.int32))
    rows = x_ref.shape[0] // PIECES

    def copy(block, c, send, to):
        piece = blocks_ref.at[block, pl.ds(pl.multiple_of(c * rows, rows), rows), :]
        return pltpu.make_async_remote_copy(
            src_ref=piece,
            dst_ref=piece,
            send_sem=send.at[block, c],
            recv_sem=recv.at[block, c],
            device_id={"tensor": to},
            device_id_type=MESH,
        )

    for hop in range(n):
        low, high = me - hop, me + hop

        def step(c, carry):
            @pl.when(low >= 0)
            def _():
                if hop > 0:
                    copy(low, c, up_send, me).wait_recv()

                @pl.when(has_high)
                def _():
                    copy(low, c, up_send, me + 1).start()

            @pl.when(high < n)
            def _():
                if hop > 0:
                    copy(high, c, down_send, me).wait_recv()

                @pl.when(has_low)
                def _():
                    copy(high, c, down_send, me - 1).start()

            return carry

        lax.fori_loop(0, PIECES, step, 0)
    wide = x_ref.shape[1]
    for block in range(n):
        out_ref[:, block * wide : (block + 1) * wide] = blocks_ref[block].astype(jnp.bfloat16)
    for hop in range(n):
        low, high = me - hop, me + hop

        def drain(c, carry):
            @pl.when((low >= 0) & has_high)
            def _():
                copy(low, c, up_send, me).wait_send()

            @pl.when((high < n) & has_low)
            def _():
                copy(high, c, down_send, me).wait_send()

            return carry

        lax.fori_loop(0, PIECES, drain, 0)


def line_gather(x, n, name):
    length, wide = x.shape
    full = pl.BlockSpec(memory_space=pltpu.VMEM)
    return pl.pallas_call(
        functools.partial(line_gather_kernel, n),
        out_shape=jax.ShapeDtypeStruct((length, n * wide), jnp.bfloat16),
        in_specs=[full],
        out_specs=full,
        scratch_shapes=[pltpu.VMEM((n, length, wide), jnp.float32)]
        + [pltpu.SemaphoreType.DMA((n, PIECES))] * 3,
        compiler_params=pltpu.CompilerParams(
            collective_id=name, has_side_effects=True, vmem_limit_bytes=32 << 20
        ),
        cost_estimate=pl.CostEstimate(
            flops=0, bytes_accessed=16 * n * x.size, transcendentals=0
        ),
    )(x)


BLOCK = 256


def own_rows_kernel(parts, weight_ref, out_ref):
    rows = out_ref.shape[0]
    first = lax.axis_index("dp") * rows if parts > 1 else 0
    out_ref[...] = weight_ref[pl.ds(pl.multiple_of(first, 16), rows), :].astype(jnp.float32)


def gather_out_weight(out_weight, parts):
    rows, width = out_weight.shape
    ways = parts if rows % (16 * parts) == 0 else 1
    full = pl.BlockSpec(memory_space=pltpu.VMEM)
    own = pl.pallas_call(
        functools.partial(own_rows_kernel, ways),
        out_shape=jax.ShapeDtypeStruct((rows // ways, width), jnp.float32),
        in_specs=[full],
        out_specs=full,
    )(out_weight)
    return ways, lax.all_gather(own, "tensor")


def middle_kernel(
    attended_ref, weight_all_ref, tokens_ref, gain_ref, router_ref, chosen_ref, middle_out, normed_out, gates_out, weight_ref
):
    ways, n, rows, unused = weight_all_ref.shape

    @pl.when(pl.program_id(0) == 0)
    def _():
        for way in range(ways):
            for block in range(n):
                at = (block * ways + way) * rows
                weight_ref[at : at + rows, :] = weight_all_ref[way, block].astype(jnp.bfloat16)

    branch = jnp.dot(attended_ref[...], weight_ref[...], preferred_element_type=jnp.float32)
    middle = tokens_ref[...].astype(jnp.float32) + RESIDUAL * branch
    middle_out[...] = middle
    recip = lax.rsqrt(jnp.mean(middle * middle, axis=1, keepdims=True) + EPSILON)
    normed = (middle * recip * gain_ref[...]).astype(jnp.bfloat16)
    normed_out[...] = normed
    logits = jnp.dot(normed, router_ref[...], preferred_element_type=jnp.float32)
    raised = jnp.where(chosen_ref[...] > 0.0, jnp.exp(logits), 0.0)
    gates_out[...] = raised / jnp.sum(raised, axis=1, keepdims=True)


def enter_middle(attended, weight_all, tokens, gain, router, chosen):
    length, width = tokens.shape
    rows = lambda columns: pl.BlockSpec((BLOCK, columns), lambda i: (i, 0))
    whole = lambda shape: pl.BlockSpec(
        shape, lambda i: (0,) * len(shape), pipeline_mode=pl.Buffered(1)
    )
    experts = router.shape[1]
    return pl.pallas_call(
        middle_kernel,
        out_shape=[
            jax.ShapeDtypeStruct((length, width), jnp.float32),
            jax.ShapeDtypeStruct((length, width), jnp.bfloat16),
            jax.ShapeDtypeStruct((length, experts), jnp.float32),
        ],
        grid=(length // BLOCK,),
        in_specs=[
            rows(attended.shape[1]),
            whole(weight_all.shape),
            rows(width),
            whole((1, width)),
            whole(router.shape),
            rows(experts),
        ],
        out_specs=[rows(width), rows(width), rows(experts)],
        scratch_shapes=[pltpu.VMEM((attended.shape[1], width), jnp.bfloat16)],
        compiler_params=pltpu.CompilerParams(
            dimension_semantics=("arbitrary",), vmem_limit_bytes=48 << 20
        ),
        cost_estimate=pl.CostEstimate(
            flops=2 * length * width * width, bytes_accessed=25 * 10**6, transcendentals=0
        ),
    )(attended, weight_all, tokens, gain.reshape(1, width), router, chosen)


def turn_kernel(
    n,
    part_ref,
    gates_part_ref,
    gates_ref,
    middle_ref,
    cotangent_ref,
    gain_ref,
    router_ref,
    grad_out,
    branch_out,
    logits_out,
    gain_out,
    summed_ref,
    grad_gates_ref,
    *line,
):
    rows = part_ref.shape[0] // STEPS

    def done(c):
        own = pl.ds(pl.multiple_of(c * rows, rows), rows)
        gates, grad_gates = gates_ref[own, :], grad_gates_ref[own, :]
        weighted = jnp.sum(gates * grad_gates, axis=1, keepdims=True)
        grad_logits = (gates * (grad_gates - weighted)).astype(jnp.bfloat16)
        logits_out[own, :] = grad_logits
        grad = summed_ref[own, :] + right_inner(grad_logits, router_ref[...])
        middle = middle_ref[own, :]
        recip = lax.rsqrt(jnp.mean(middle * middle, axis=1, keepdims=True) + EPSILON)
        unit = middle * recip
        gain_out[...] += jnp.sum(grad * unit, axis=0, keepdims=True)
        scaled = grad * gain_ref[...]
        back = recip * (scaled - unit * jnp.mean(scaled * unit, axis=1, keepdims=True))
        total = cotangent_ref[own, :].astype(jnp.float32) + back
        grad_out[own, :] = total
        branch_out[own, :] = (RESIDUAL * total).astype(jnp.bfloat16)

    begin, step, finish = line_stages(
        n, [part_ref, gates_part_ref], [summed_ref, grad_gates_ref], line, done
    )
    begin()
    gain_out[...] = jnp.zeros_like(gain_out)
    lax.fori_loop(0, 2 * STEPS, step, 0)
    finish()


def turn_middle(n, part, gates_part, gates, middle, cotangent, gain, router, name):
    length, width = part.shape
    full = pl.BlockSpec(memory_space=pltpu.VMEM)
    f32 = jnp.float32
    return pl.pallas_call(
        functools.partial(turn_kernel, n),
        out_shape=[
            jax.ShapeDtypeStruct((length, width), f32),
            jax.ShapeDtypeStruct((length, width), jnp.bfloat16),
            jax.ShapeDtypeStruct(gates.shape, jnp.bfloat16),
            jax.ShapeDtypeStruct((1, width), f32),
        ],
        in_specs=[full] * 7,
        out_specs=[full] * 4,
        scratch_shapes=[pltpu.VMEM(part.shape, f32), pltpu.VMEM(gates.shape, f32)]
        + line_scratch([part, gates_part]),
        compiler_params=pltpu.CompilerParams(
            collective_id=name, has_side_effects=True, vmem_limit_bytes=58 << 20
        ),
        cost_estimate=pl.CostEstimate(
            flops=40 * length * width, bytes_accessed=60 * 10**6, transcendentals=0
        ),
    )(part, gates_part, gates, middle, cotangent, gain.reshape(1, width), router)


SPAN = 768
ROWS = 256


def lane_halves(shape):
    return lax.broadcasted_iota(jnp.int32, shape, len(shape) - 1) // HEAD


def select_halves(tile, source, half):
    kept = jnp.where(lane_halves(tile.shape) == source, tile, 0.0)
    return kept if source == half else pltpu.roll(kept, HEAD, 1)


def spread_pairs(tile, target):
    for source in range(2):
        for half in range(2):
            target[2 * source + half] = select_halves(tile, source, half).astype(jnp.bfloat16)


def rope_tile(tile, cosine, sine_low, sine_high):
    return tile * cosine + pltpu.roll(tile, 128 - HEAD // 2, 1) * sine_low + pltpu.roll(
        tile, HEAD // 2, 1
    ) * sine_high


def rope_back_tile(tile, cosine, sine_low, sine_high):
    return (
        tile * cosine
        + pltpu.roll(tile * sine_low, HEAD // 2, 1)
        + pltpu.roll(tile * sine_high, 128 - HEAD // 2, 1)
    )


def window(block):
    first = block * ROWS
    return first, jnp.maximum(first + ROWS - SPAN, 0)


def attend_forward_kernel(
    heads,
    group,
    tokens_ref,
    gain_ref,
    query_w,
    key_w,
    value_w,
    cosine_ref,
    sine_low_ref,
    sine_high_ref,
    opening_ref,
    normed_out,
    query_out,
    key_out,
    value_out,
    attended_out,
    logsum_out,
    key_pairs,
    value_pairs,
    tiles_ref,
):
    tiles, length, unused = query_out.shape
    hidden = tokens_ref[...].astype(jnp.float32)
    recip = lax.rsqrt(jnp.mean(hidden * hidden, axis=1, keepdims=True) + EPSILON)
    normed_out[...] = (hidden * recip * gain_ref[...]).astype(jnp.bfloat16)
    cosine, sine_low, sine_high = cosine_ref[...], sine_low_ref[...], sine_high_ref[...]
    for tile in range(tiles):
        query = jnp.dot(
            normed_out[...],
            query_w[:, tile * 128 : (tile + 1) * 128],
            preferred_element_type=jnp.float32,
        )
        query_out[tile] = rope_tile(query, cosine, sine_low, sine_high).astype(jnp.bfloat16)
    key = rope_tile(
        jnp.dot(normed_out[...], key_w[...], preferred_element_type=jnp.float32),
        cosine,
        sine_low,
        sine_high,
    )
    value = jnp.dot(normed_out[...], value_w[...], preferred_element_type=jnp.float32)
    key_out[...] = key.astype(jnp.bfloat16)
    value_out[...] = value.astype(jnp.bfloat16)
    spread_pairs(key, key_pairs)
    spread_pairs(value, value_pairs)
    blocks = length // ROWS
    tiles_ref[...] = jnp.zeros_like(tiles_ref)

    def unit(step, carry):
        head, block = step // blocks, step % blocks
        tile, half = head // 2, head % 2
        pair = 2 * (head // group) + half
        first, low = window(block)
        rows = pl.ds(pl.multiple_of(first, ROWS), ROWS)
        span = pl.ds(pl.multiple_of(low, ROWS), SPAN)
        scores = right_inner(query_out[tile, rows, :], key_pairs[pair, span, :])
        columns = low + lax.broadcasted_iota(jnp.int32, (ROWS, SPAN), 1)
        own = first + lax.broadcasted_iota(jnp.int32, (ROWS, SPAN), 0)
        allowed = (columns >= opening_ref[rows, :]) & (columns <= own)
        raised = jnp.where(allowed, jnp.exp(ATTN_SCALE * scores), 0.0)
        total = jnp.sum(raised, axis=1, keepdims=True)
        product = jnp.dot(
            raised.astype(jnp.bfloat16), value_pairs[pair, span, :], preferred_element_type=jnp.float32
        )
        tiles_ref[tile, rows, :] += product / total
        wide = jnp.broadcast_to(jnp.log(total), (ROWS, 128))
        logsum_out[head, :, rows] = jnp.transpose(wide)[:1]
        return carry

    lax.fori_loop(0, heads * blocks, unit, 0)
    for tile in range(tiles):
        attended_out[:, tile * 128 : (tile + 1) * 128] = tiles_ref[tile].astype(jnp.bfloat16)


def attend_forward(tokens, gain, query_w, key_w, value_w, tables, opening, heads, group):
    length, width = tokens.shape
    wide = query_w.shape[1]
    tiles = wide // 128
    bf16, f32 = jnp.bfloat16, jnp.float32
    full = pl.BlockSpec(memory_space=pltpu.VMEM)
    return pl.pallas_call(
        functools.partial(attend_forward_kernel, heads, group),
        out_shape=[
            jax.ShapeDtypeStruct((length, width), bf16),
            jax.ShapeDtypeStruct((tiles, length, 128), bf16),
            jax.ShapeDtypeStruct((length, 128), bf16),
            jax.ShapeDtypeStruct((length, 128), bf16),
            jax.ShapeDtypeStruct((length, wide), bf16),
            jax.ShapeDtypeStruct((heads, 1, length), f32),
        ],
        in_specs=[full] * 9,
        out_specs=[full] * 6,
        scratch_shapes=[
            pltpu.VMEM((4, length, 128), bf16),
            pltpu.VMEM((4, length, 128), bf16),
            pltpu.VMEM((tiles, length, 128), f32),
        ],
        compiler_params=pltpu.CompilerParams(vmem_limit_bytes=48 << 20),
        cost_estimate=pl.CostEstimate(
            flops=8 * 10**9, bytes_accessed=12 * 10**6, transcendentals=5 * 10**6
        ),
    )(tokens, gain.reshape(1, width), query_w, key_w, value_w, *tables, opening.reshape(length, 1))


def attend_backward_kernel(
    n,
    heads,
    group,
    branch_ref,
    out_w,
    query_ref,
    key_ref,
    value_ref,
    attended_ref,
    logsum_ref,
    query_w,
    key_w,
    value_w,
    cosine_ref,
    sine_low_ref,
    sine_high_ref,
    opening_ref,
    tokens_ref,
    moe_ref,
    middle_ref,
    grads_out,
    normed_out,
    gain_out,
    output_ref,
    moe_sum,
    middle_rows,
    middle_sems,
    key_pairs,
    value_pairs,
    attend_grads,
    query_grads,
    key_grads,
    value_grads,
    delta_ref,
    *line,
):
    tiles, length, unused = query_ref.shape
    share = length // STEPS

    def share_rows(c):
        return pl.ds(pl.multiple_of(c * share, share), share)

    def fetch(c):
        slot = lax.rem(c, 2)
        return pltpu.make_async_copy(
            middle_ref.at[share_rows(c), :], middle_rows.at[slot], middle_sems.at[slot]
        )

    def done(c):
        fetch(c).wait()

        @pl.when(c + 1 < STEPS)
        def _():
            fetch(c + 1).start()

        total = middle_rows[lax.rem(c, 2)] + RESIDUAL * moe_sum[share_rows(c), :]
        output_ref[share_rows(c), :] = total.astype(jnp.bfloat16)

    line_start, line_step, line_end = line_stages(n, [moe_ref], [moe_sum], line, done)
    line_start()
    fetch(jnp.int32(0)).start()
    blocks = length // ROWS
    units = heads * blocks
    taken = 0

    def run_line(steps):
        nonlocal taken
        until = min(taken + steps, 2 * STEPS)
        lax.fori_loop(taken, until, line_step, 0)
        taken = until

    run_line(2)
    spread_pairs(key_ref[...].astype(jnp.float32), key_pairs)
    spread_pairs(value_ref[...].astype(jnp.float32), value_pairs)
    halves = (
        lax.broadcasted_iota(jnp.int32, (8, 128), 0) == lane_halves((8, 128))
    ).astype(jnp.float32)
    for tile in range(tiles):
        lanes = slice(tile * 128, (tile + 1) * 128)
        grad = right_inner(branch_ref[...], out_w[lanes, :]).astype(jnp.bfloat16)
        attend_grads[tile] = grad
        products = grad.astype(jnp.float32) * attended_ref[:, lanes].astype(jnp.float32)
        sums = lax.dot_general(
            halves,
            products,
            (((1,), (1,)), ((), ())),
            precision=lax.Precision.HIGHEST,
            preferred_element_type=jnp.float32,
        )
        delta_ref[2 * tile] = sums[0:1]
        delta_ref[2 * tile + 1] = sums[1:2]
        run_line(2)
    query_grads[...] = jnp.zeros_like(query_grads)
    key_grads[...] = jnp.zeros_like(key_grads)
    value_grads[...] = jnp.zeros_like(value_grads)
    before, each = taken, (2 * STEPS - 8 - taken) // units
    taken += units * each

    def unit(step, carry):
        lax.fori_loop(before + step * each, before + step * each + each, line_step, 0)
        head, block = step // blocks, step % blocks
        tile, half = head // 2, head % 2
        pair = 2 * (head // group) + half
        first, low = window(block)
        rows = pl.ds(pl.multiple_of(first, ROWS), ROWS)
        span = pl.ds(pl.multiple_of(low, ROWS), SPAN)
        keys = key_pairs[pair, span, :]
        query = query_ref[tile, rows, :]
        grad = attend_grads[tile, rows, :]
        scores = right_inner(keys, query)
        columns = low + lax.broadcasted_iota(jnp.int32, (SPAN, ROWS), 0)
        own = first + lax.broadcasted_iota(jnp.int32, (SPAN, ROWS), 1)
        allowed = (columns >= opening_ref[:, rows]) & (columns <= own)
        probs = jnp.where(
            allowed, jnp.exp(ATTN_SCALE * scores - logsum_ref[head, :, rows]), 0.0
        )
        grad_probs = right_inner(value_pairs[pair, span, :], grad)
        grad_scores = (probs * (grad_probs - delta_ref[head, :, rows])).astype(jnp.bfloat16)
        value_grads[pair, span, :] += jnp.dot(
            probs.astype(jnp.bfloat16), grad, preferred_element_type=jnp.float32
        )
        key_grads[pair, span, :] += jnp.dot(
            grad_scores, query, preferred_element_type=jnp.float32
        )
        query_grads[tile, rows, :] += left_inner(grad_scores, keys)
        return carry

    lax.fori_loop(0, units, unit, 0)
    cosine, sine_low, sine_high = cosine_ref[...], sine_low_ref[...], sine_high_ref[...]
    wide = tiles * 128
    for tile in range(tiles):
        grads_out[:, tile * 128 : (tile + 1) * 128] = rope_back_tile(
            ATTN_SCALE * query_grads[tile], cosine, sine_low, sine_high
        ).astype(jnp.bfloat16)
    totals = []
    for grads in (key_grads, value_grads):
        totals.append(
            sum(
                select_halves(grads[2 * source + half], half, source)
                for source in range(2)
                for half in range(2)
            )
        )
    grads_out[:, wide : wide + 128] = rope_back_tile(
        ATTN_SCALE * totals[0], cosine, sine_low, sine_high
    ).astype(jnp.bfloat16)
    grads_out[:, wide + 128 : wide + 256] = totals[1].astype(jnp.bfloat16)
    gain_sum = jnp.zeros((1, normed_out.shape[1]), jnp.float32)
    for block in range(blocks):
        rows = slice(block * ROWS, (block + 1) * ROWS)
        normed = (
            right_inner(grads_out[rows, :wide], query_w[...])
            + right_inner(grads_out[rows, wide : wide + 128], key_w[...])
            + right_inner(grads_out[rows, wide + 128 :], value_w[...])
        )
        normed_out[rows, :] = normed
        hidden = tokens_ref[rows, :].astype(jnp.float32)
        recip = lax.rsqrt(jnp.mean(hidden * hidden, axis=1, keepdims=True) + EPSILON)
        gain_sum += jnp.sum(normed * (hidden * recip), axis=0, keepdims=True)
        run_line(2)
    gain_out[...] = gain_sum
    run_line(2 * STEPS)
    line_end()


def attend_backward(
    n, branch, out_w, query, key, value, attended, logsum, query_w, key_w, value_w, tables, opening, tokens, moe, middle,
    heads, group, name,
):
    length, width = branch.shape
    tiles = query.shape[0]
    wide = tiles * 128
    bf16, f32 = jnp.bfloat16, jnp.float32
    full = pl.BlockSpec(memory_space=pltpu.VMEM)
    return pl.pallas_call(
        functools.partial(attend_backward_kernel, n, heads, group),
        out_shape=[
            jax.ShapeDtypeStruct((length, wide + 256), bf16),
            jax.ShapeDtypeStruct((length, width), f32),
            jax.ShapeDtypeStruct((1, width), f32),
            jax.ShapeDtypeStruct((length, width), bf16),
        ],
        in_specs=[full] * 16 + [pl.BlockSpec(memory_space=pl.ANY)],
        out_specs=[full] * 4,
        scratch_shapes=[
            pltpu.VMEM((length, width), f32),
            pltpu.VMEM((2, length // STEPS, width), f32),
            pltpu.SemaphoreType.DMA((2,)),
            pltpu.VMEM((4, length, 128), bf16),
            pltpu.VMEM((4, length, 128), bf16),
            pltpu.VMEM((tiles, length, 128), bf16),
            pltpu.VMEM((tiles, length, 128), f32),
            pltpu.VMEM((4, length, 128), f32),
            pltpu.VMEM((4, length, 128), f32),
            pltpu.VMEM((2 * tiles, 1, length), f32),
        ]
        + line_scratch([moe]),
        compiler_params=pltpu.CompilerParams(
            collective_id=name, has_side_effects=True, vmem_limit_bytes=63 << 20
        ),
        cost_estimate=pl.CostEstimate(
            flops=12 * 10**9, bytes_accessed=30 * 10**6, transcendentals=5 * 10**6
        ),
    )(
        branch, out_w, query, key, value, attended, logsum, query_w, key_w, value_w, *tables,
        opening.reshape(1, length), tokens, moe, middle,
    )


def finish_kernel(
    n,
    parts,
    local_ref,
    normed_ref,
    grads_ref,
    branch_ref,
    attended_ref,
    normed_two_ref,
    logits_ref,
    gain_ref,
    first_gain_ref,
    normed_out,
    query_out,
    key_out,
    value_out,
    branch_out,
    router_out,
    gain_out,
    first_gain_out,
    weights_ref,
    gains_ref,
    gain_send,
    gain_recv,
    *scratch,
):
    levels = parts.bit_length() - 1
    held = scratch[:levels]
    sends, recvs = scratch[levels : levels + 2]
    line_start, line_step, line_end = line_stages(n, [local_ref], [normed_out], scratch[levels + 2 :])
    me = lax.axis_index("dp")
    width = normed_ref.shape[1]
    own = width // parts
    wide, attended_wide = grads_ref.shape[1], attended_ref.shape[1]
    mine = lax.axis_index("tensor")
    line_start(
        [{"dp": jnp.bitwise_xor(me, 1 << level)} for level in range(levels)]
        + [{"tensor": lax.rem(mine + ahead, n)} for ahead in range(1, n)]
    )

    def run_line(first, last):
        lax.fori_loop(first, last, line_step, 0)

    run_line(0, 2)
    pieces = 4
    block = width // pieces
    for piece in range(pieces):
        rows = slice(piece * block, (piece + 1) * block)
        weights_ref[rows, :wide] = left_inner(normed_ref[:, rows], grads_ref[...])
        weights_ref[rows, wide : wide + attended_wide] = left_inner(
            branch_ref[:, rows], attended_ref[...]
        )
        gain = jnp.transpose(jnp.broadcast_to(gain_ref[:, rows], (128, block)))
        first_gain = jnp.transpose(jnp.broadcast_to(first_gain_ref[:, rows], (128, block)))
        lanes = lax.broadcasted_iota(jnp.int32, (block, 128), 1)
        weights_ref[rows, wide + attended_wide :] = jnp.where(
            lanes == 127,
            gain,
            jnp.where(
                lanes == 126, first_gain, left_inner(normed_two_ref[:, rows], logits_ref[...])
            ),
        )
        run_line(2 + 2 * piece, 4 + 2 * piece)
    done = 2 + 2 * pieces

    columns = weights_ref.shape[1]
    middle = columns // 256 * 128
    orders = (
        (slice(0, middle), list(range(levels))),
        (slice(middle, columns), [0] + list(range(levels - 1, 0, -1))),
    )

    def shard(number, lanes):
        return weights_ref.at[pl.ds(pl.multiple_of(number * own, own), own), lanes]

    def numbers(order, level, peer):
        fixed = sum(1 << bit for bit in order[: level + 1])
        base = jnp.bitwise_and(peer, fixed)
        free = order[level + 1 :]
        return [
            base + sum(((i >> place) & 1) << bit for place, bit in enumerate(free))
            for i in range(1 << len(free))
        ]

    def copies(level):
        made = []
        for side, (lanes, order) in enumerate(orders):
            peer = jnp.bitwise_xor(me, 1 << order[level])
            for i, number in enumerate(numbers(order, level, peer)):
                made.append(
                    pltpu.make_async_remote_copy(
                        src_ref=shard(number, lanes),
                        dst_ref=held[level].at[i, :, lanes],
                        send_sem=sends.at[side, level, i],
                        recv_sem=recvs.at[side, level, i],
                        device_id={"dp": peer},
                        device_id_type=MESH,
                    )
                )
        return made

    stops = [6, 28, 18, 2]
    for level in range(levels):
        for copy in copies(level):
            copy.start()
        until = done + stops[level]
        run_line(done, until)
        done = until
        for copy in copies(level):
            copy.wait_recv()
        for lanes, order in orders:
            for i, number in enumerate(numbers(order, level, me)):
                target = shard(number, lanes)
                target[...] += held[level][i, :, lanes]
    everything = slice(0, columns)
    gains_ref[0] = shard(me, slice(wide + attended_wide, columns))[...]
    gain_copies = [
        pltpu.make_async_remote_copy(
            src_ref=gains_ref.at[0],
            dst_ref=gains_ref.at[ahead],
            send_sem=gain_send.at[ahead],
            recv_sem=gain_recv.at[ahead],
            device_id={"tensor": lax.rem(mine + ahead, n)},
            device_id_type=MESH,
        )
        for ahead in range(1, n)
    ]
    for copy in gain_copies:
        copy.start()
    kept = shard(me, everything)
    query_out[...] = kept[:, : query_out.shape[1]]
    key_out[...] = kept[:, wide - 256 : wide - 256 + key_out.shape[1]]
    value_out[...] = kept[:, wide - 128 : wide - 128 + value_out.shape[1]]
    branch_out[...] = jnp.transpose(kept[:, wide : wide + attended_wide])[: branch_out.shape[0]]
    router_out[...] = gains_ref[0][:, : router_out.shape[1]]
    run_line(done, 2 * STEPS)
    total = gains_ref[0]
    for ahead, copy in enumerate(gain_copies, 1):
        copy.wait_recv()
        total = total + gains_ref[ahead]
    gain_out[...] = jnp.transpose(gains_ref[0])[127:]
    first_gain_out[...] = jnp.transpose(total)[126:127]
    for level in range(levels):
        for copy in copies(level):
            copy.wait_send()
    for copy in gain_copies:
        copy.wait_send()
    line_end()


def finish(
    n, parts, grad_local, normed_b, grads_wide, branch_b, attended, normed_two_b, grad_logits_b, gain_grad, first_gain_grad,
    wide_q, wide_k, experts, name,
):
    length, width = normed_b.shape
    columns = grads_wide.shape[1] + attended.shape[1] + 128
    full = pl.BlockSpec(memory_space=pltpu.VMEM)
    levels = parts.bit_length() - 1
    own = width // parts
    f32 = jnp.float32
    shapes = [(length, width), (own, wide_q), (own, wide_k), (own, wide_k), (wide_q, own)]
    shapes += [(own, experts), (1, own), (1, own)]
    return pl.pallas_call(
        functools.partial(finish_kernel, n, parts),
        out_shape=[jax.ShapeDtypeStruct(shape, f32) for shape in shapes],
        in_specs=[full] * 9,
        out_specs=[full] * 8,
        scratch_shapes=[
            pltpu.VMEM((width, columns), f32),
            pltpu.VMEM((n, own, 128), f32),
            pltpu.SemaphoreType.DMA((n,)),
            pltpu.SemaphoreType.DMA((n,)),
        ]
        + [pltpu.VMEM((parts >> (level + 1), own, columns), f32) for level in range(levels)]
        + [pltpu.SemaphoreType.DMA((2, levels, parts // 2))] * 2
        + line_scratch([grad_local]),
        compiler_params=pltpu.CompilerParams(
            collective_id=name, has_side_effects=True, vmem_limit_bytes=62 << 20
        ),
        cost_estimate=pl.CostEstimate(
            flops=2 * length * width * columns, bytes_accessed=50 * 10**6, transcendentals=0
        ),
    )(
        grad_local, normed_b, grads_wide, branch_b, attended, normed_two_b, grad_logits_b, gain_grad,
        first_gain_grad,
    )


def place_kernel(shards_ref, *refs):
    gate_out, up_out, down_out = refs[-3:]
    gate_out[0] = shards_ref[0, 0]
    up_out[0] = shards_ref[0, 1]
    rows, hidden = down_out.shape[1], shards_ref.shape[3]
    for piece in range(down_out.shape[2] // hidden):
        down_out[0, :, piece * hidden : (piece + 1) * hidden] = shards_ref[
            0, 2, piece * rows : (piece + 1) * rows, :
        ]


def place_shards(parts, shards, first, experts, before):
    number, unused, rows, hidden = shards.shape
    down_rows = hidden // parts
    width = rows * parts
    shapes = [(experts, rows, hidden), (experts, rows, hidden), (experts, down_rows, width)]
    spec = lambda shape: pl.BlockSpec((1,) + shape[1:], lambda e: (first + e, 0, 0))
    args, extra, aliases = [shards], [], {}
    if before is not None:
        args += list(before)
        extra = [pl.BlockSpec(memory_space=pl.ANY)] * 3
        aliases = {1: 0, 2: 1, 3: 2}
    return pl.pallas_call(
        place_kernel,
        out_shape=[jax.ShapeDtypeStruct(shape, jnp.float32) for shape in shapes],
        grid=(number,),
        in_specs=[pl.BlockSpec((1, 3, rows, hidden), lambda e: (e, 0, 0, 0))] + extra,
        out_specs=[spec(shape) for shape in shapes],
        input_output_aliases=aliases,
        cost_estimate=pl.CostEstimate(
            flops=0, bytes_accessed=8 * shards.size, transcendentals=0
        ),
    )(*args)


def on_device(
    ring,
    tokens,
    cotangent,
    segment_ids,
    routes,
    attn_gain,
    query_weight,
    key_weight,
    value_weight,
    out_weight,
    ffn_gain,
    router_weight,
    gate_weight,
    up_weight,
    down_weight,
):
    length = tokens.shape[0]
    width = tokens.shape[1]
    segment = segment_ids[0]
    heads_local = query_weight.shape[1] // HEAD
    kv_local = key_weight.shape[1] // HEAD
    group_size = heads_local // kv_local
    experts_all = router_weight.shape[1]
    experts_local = gate_weight.shape[0]
    parts = lax.axis_size("dp")
    opening = doc_openings(segment)
    tables = rope_tables(opening, HEAD)
    query_w, key_w, value_w = (pad_columns(w) for w in (query_weight, key_weight, value_weight))
    out_w = jnp.transpose(pad_columns(jnp.transpose(out_weight)))
    hidden_in = tokens.astype(jnp.float32)
    ways, out_rows = gather_out_weight(out_weight, parts)
    normed_b, queries, keys, values, attended, logsum = attend_forward(
        tokens, attn_gain, query_w, key_w, value_w, tables, opening, heads_local, group_size
    )
    all_ids = jnp.arange(experts_all, dtype=jnp.int32)
    chosen = jnp.sum((routes[:, :, None] == all_ids[None, None, :]).astype(jnp.int32), axis=1) > 0
    first_expert = lax.axis_index("tensor") * experts_local
    local_ids = first_expert + jnp.arange(experts_local, dtype=jnp.int32)
    picked = jnp.sum((routes[None, :, :] == local_ids[:, None, None]).astype(jnp.int32), axis=2)
    places_in = slot_places(picked)
    counts = jnp.sum(picked, axis=1)
    out_rows, attended = lax.optimization_barrier((out_rows, attended))
    out_all = lax.all_gather(out_rows, "dp") if ways > 1 else out_rows[None]
    attended_all = line_gather(attended, ring, 1)
    attended_all = attended_all.reshape(length, ring, attended.shape[1])
    attended_all = attended_all[:, :, : heads_local * HEAD].reshape(length, -1)
    router_w = pad_columns(router_weight)
    middle, normed_two_b, gate_probs = enter_middle(
        attended_all, out_all, tokens, ffn_gain, router_w, pad_columns(chosen.astype(jnp.float32))
    )
    gate_rows = jnp.transpose(lax.dynamic_slice_in_dim(gate_probs, first_expert, experts_local, 1))
    numbers = (max(1, experts_local // 10),)
    numbers += (experts_local - numbers[0],)
    (grads_first,), sums = expert_stage(
        parts, 0, numbers[:1], counts, places_in, gate_rows, normed_two_b, cotangent,
        gate_weight, up_weight, down_weight, None,
    )
    shards_first = lax.psum_scatter(grads_first, "dp", scatter_dimension=2, tiled=True)
    (grads_last,), sums_last = expert_stage(
        parts, numbers[0], numbers[1:], counts, places_in, gate_rows, normed_two_b, cotangent,
        gate_weight, up_weight, down_weight, sums,
    )
    moe_part, grad_normed_part, unused = sums_last
    shards_first, grads_last, grad_normed_part = lax.optimization_barrier(
        (shards_first, grads_last, grad_normed_part)
    )
    shards_last = lax.psum_scatter(grads_last, "dp", scatter_dimension=2, tiled=True)
    grad_gates_local = jnp.concatenate([sums[2], sums_last[2]], 0).reshape(experts_local, length)
    grad_gates_part = lax.dynamic_update_slice_in_dim(
        jnp.zeros(gate_probs.shape, jnp.float32), jnp.transpose(grad_gates_local), first_expert, 1
    )
    grad_middle, grad_branch_b, grad_logits_b, grad_ffn_gain = turn_middle(
        ring, grad_normed_part, grad_gates_part, gate_probs, middle, cotangent, ffn_gain, router_w, 2
    )
    grads_wide, grad_normed_local, first_gain, output = attend_backward(
        ring, grad_branch_b, out_w, queries, keys, values, attended, logsum,
        query_w, key_w, value_w, tables, opening, tokens, moe_part, middle, heads_local, group_size, 3,
    )
    wide_q, wide_k = heads_local * HEAD, kv_local * HEAD
    grad_normed, *small = finish(
        ring, parts, grad_normed_local, normed_b, grads_wide, grad_branch_b, attended, normed_two_b,
        grad_logits_b, grad_ffn_gain, first_gain, wide_q, wide_k, experts_all, 4,
    )
    grad_query, grad_key, grad_value, grad_out, grad_router, grad_ffn_gain, grad_attn_gain = small
    recip_one = lax.rsqrt(jnp.mean(hidden_in * hidden_in, axis=-1, keepdims=True) + EPSILON)
    unit_one = hidden_in * recip_one
    scaled = grad_normed * attn_gain
    inner = jnp.mean(scaled * unit_one, axis=-1, keepdims=True)
    grad_tokens = grad_middle + recip_one * (scaled - unit_one * inner)
    shards_last, grad_tokens = lax.optimization_barrier((shards_last, grad_tokens))
    grads_placed = place_shards(parts, shards_first, 0, experts_local, None)
    grad_gate, grad_up, grad_down = place_shards(
        parts, shards_last, numbers[0], experts_local, grads_placed
    )
    return (
        output,
        grad_tokens,
        grad_attn_gain.reshape(-1),
        grad_query,
        grad_key,
        grad_value,
        grad_out,
        grad_ffn_gain.reshape(-1),
        grad_router,
        grad_gate,
        grad_up,
        grad_down,
    )


def solution(mesh):
    return jax.shard_map(
        functools.partial(on_device, mesh.shape["tensor"]),
        mesh=mesh,
        in_specs=(
            P("dp", None),
            P("dp", None),
            P("dp", None),
            P("dp", None),
            P(),
            P(None, "tensor"),
            P(None, "tensor"),
            P(None, "tensor"),
            P("tensor", None),
            P(),
            P(),
            P("tensor", None, None),
            P("tensor", None, None),
            P("tensor", None, None),
        ),
        out_specs=(
            P("dp", None),
            P("dp", None),
            P("dp"),
            P("dp", "tensor"),
            P("dp", "tensor"),
            P("dp", "tensor"),
            P("tensor", "dp"),
            P("dp"),
            P("dp", None),
            P("tensor", "dp", None),
            P("tensor", "dp", None),
            P("tensor", "dp", None),
        ),
        check_vma=False,
    )
```

```python
import functools

import jax
import jax.numpy as jnp
from jax import lax
from jax.experimental import pallas as pl
from jax.experimental.pallas import tpu as pltpu
from jax.sharding import PartitionSpec as P

MESH = pl.DeviceIdType.MESH

HEAD = 64
CAP = 384


EPSILON = 1e-06
RESIDUAL = 0.22
ATTN_SCALE = 0.015625
ROPE_BASE = 10000.0


def left_inner(first, second):
    return lax.dot_general(
        first, second, (((0,), (0,)), ((), ())), preferred_element_type=jnp.float32
    )


def right_inner(first, second):
    return lax.dot_general(
        first, second, (((1,), (1,)), ((), ())), preferred_element_type=jnp.float32
    )


def doc_openings(segment):
    return jnp.sum((segment[None, :] < segment[:, None]).astype(jnp.int32), axis=1)


def rope_tables(opening, head_size):
    halfway = head_size // 2
    spread = jnp.arange(halfway, dtype=jnp.float32) * (2.0 / head_size)
    inverse = jnp.power(ROPE_BASE, -spread)
    places = jnp.arange(opening.shape[0], dtype=jnp.int32)
    angles = (places - opening).astype(jnp.float32)[:, None] * inverse[None, :]
    cosine, sine = jnp.cos(angles), jnp.sin(angles)
    none = jnp.zeros_like(sine)
    return (
        jnp.concatenate([cosine] * 4, 1),
        jnp.concatenate([-sine, none] * 2, 1),
        jnp.concatenate([none, sine] * 2, 1),
    )


def pad_columns(weight):
    missing = -weight.shape[1] % 128
    return weight if missing == 0 else jnp.pad(weight, ((0, 0), (0, missing)))


def rms_forward(hidden, gain):
    recip = lax.rsqrt(jnp.mean(hidden * hidden, axis=-1, keepdims=True) + EPSILON)
    unit = hidden * recip
    return (unit * gain, unit, recip)


def rms_backward(gradient, unit, recip, gain):
    gain_grad = jnp.sum(gradient * unit, axis=0)
    scaled = gradient * gain
    return (recip * (scaled - unit * jnp.mean(scaled * unit, axis=-1, keepdims=True)), gain_grad)


def slot_places(picked):
    length = picked.shape[1]
    tokens = jnp.arange(length, dtype=jnp.int32)
    earlier = (tokens[:, None] < tokens[None, :]).astype(jnp.bfloat16)
    before = jnp.dot(picked.astype(jnp.bfloat16), earlier, preferred_element_type=jnp.float32)
    return jnp.where(picked > 0, before.astype(jnp.int32), -1)


STEPS = 32
LAG = 2


def line_stages(n, xs, outs, scratch, done=None, whole=0):
    count = len(xs)
    lows, highs = scratch[:count], scratch[count : 2 * count]
    low_recv, high_recv, total_recv, up_send, low_send, high_send = scratch[2 * count :]
    me = lax.axis_index("tensor")
    root = n // 2
    has_low, has_high = me > 0, me < n - 1

    def begin(others=()):
        barrier = pltpu.get_barrier_semaphore()
        for other in others:
            pl.semaphore_signal(barrier, inc=1, device_id=other, device_id_type=MESH)

        @pl.when(has_low)
        def _():
            pl.semaphore_signal(barrier, inc=1, device_id={"tensor": me - 1}, device_id_type=MESH)

        @pl.when(has_high)
        def _():
            pl.semaphore_signal(barrier, inc=1, device_id={"tensor": me + 1}, device_id_type=MESH)

        pl.semaphore_wait(
            barrier, len(others) + has_low.astype(jnp.int32) + has_high.astype(jnp.int32)
        )

    def piece(ref, c):
        rows = ref.shape[0] // STEPS
        return ref.at[pl.ds(pl.multiple_of(c * rows, rows), rows), :]

    cut = count - whole

    def copies(sources, targets, c, send, recv, to, uncut):
        return [
            pltpu.make_async_remote_copy(
                src_ref=source if uncut else piece(source, c),
                dst_ref=target if uncut else piece(target, c),
                send_sem=send.at[i, c],
                recv_sem=recv.at[i, c],
                device_id={"tensor": to},
                device_id_type=MESH,
            )
            for i, (source, target) in enumerate(zip(sources, targets))
            if (i >= cut) == uncut
        ]

    def each(sources, targets, c, send, recv, to, act):
        for copy in copies(sources, targets, c, send, recv, to, False):
            act(copy)
        if whole:

            @pl.when(c == 0)
            def _():
                for copy in copies(sources, targets, 0, send, recv, to, True):
                    act(copy)

    def start(sources, targets, c, send, recv, to):
        each(sources, targets, c, send, recv, to, lambda copy: copy.start())

    def arrived(targets, c, send, recv):
        each(targets, targets, c, send, recv, me, lambda copy: copy.wait_recv())

    def add(c, terms, targets):
        for i, target in enumerate(targets):
            if i < cut:
                piece(target, c)[...] = functools.reduce(
                    jnp.add, [piece(term[i], c)[...] for term in terms]
                )
            else:

                @pl.when(c == 0)
                def _():
                    target[...] = functools.reduce(jnp.add, [term[i][...] for term in terms])

    def reduce_step(c):
        for side, inner, held, recv, to in (
            (me < root, has_low, lows, low_recv, me + 1),
            (me > root, has_high, highs, high_recv, me - 1),
        ):

            @pl.when(side & inner)
            def _():
                arrived(held, c, up_send, recv)
                add(c, (held, xs), held)
                start(held, held, c, up_send, recv, to)

            @pl.when(side & jnp.logical_not(inner))
            def _():
                start(xs, held, c, up_send, recv, to)

        @pl.when(me == root)
        def _():
            arrived(lows, c, up_send, low_recv)
            if root < n - 1:
                arrived(highs, c, up_send, high_recv)
            add(c, (xs, lows, highs) if root < n - 1 else (xs, lows), outs)
            start(outs, outs, c, low_send, total_recv, me - 1)
            if root < n - 1:
                start(outs, outs, c, high_send, total_recv, me + 1)
            if done is not None:
                done(c)

    def total_step(c):
        @pl.when(me != root)
        def _():
            arrived(outs, c, low_send, total_recv)

        @pl.when((me < root) & has_low)
        def _():
            start(outs, outs, c, low_send, total_recv, me - 1)

        @pl.when((me > root) & has_high)
        def _():
            start(outs, outs, c, high_send, total_recv, me + 1)

        if done is not None:

            @pl.when(me != root)
            def _():
                done(c)

    lag = jnp.where(has_low & has_high, LAG, STEPS)

    def step(t, carry):
        @pl.when(t < STEPS)
        def _():
            reduce_step(t)

        @pl.when((t >= lag) & (t - lag < STEPS))
        def _():
            total_step(t - lag)

        return carry

    def finish():
        def drain(c, carry):
            for condition, send in (
                (me != root, up_send),
                ((me <= root) & has_low, low_send),
                ((me >= root) & has_high, high_send),
            ):

                @pl.when(condition)
                def _():
                    each(xs, lows, c, send, low_recv, me, lambda copy: copy.wait_send())

            return carry

        lax.fori_loop(0, STEPS, drain, 0)

    return begin, step, finish


def line_scratch(arrays):
    return [pltpu.VMEM(array.shape, jnp.float32) for array in arrays * 2] + [
        pltpu.SemaphoreType.DMA((len(arrays), STEPS))
    ] * 6


def expert_kernel(
    parts,
    first,
    numbers,
    chained,
    count_ref,
    place_ref,
    gate_ref,
    normed_ref,
    grad_ref,
    gate_w,
    up_w,
    down_w,
    *refs,
):
    if chained:
        moe_in, back_in = refs[:2]
        refs = refs[2:]
    grads_out, refs = refs[: len(numbers)], refs[len(numbers) :]
    moe_out, back_out, gates_out = refs[:3]
    rows_ref, grads_ref, active_ref, gate_in_ref, up_in_ref, weights_ref, sems, out_sems = refs[3:]
    expert = pl.program_id(0)
    filled = count_ref[first + expert]
    length, width = normed_ref.shape
    hidden_size = gate_w.shape[2]
    sizes = (128, 256, CAP)

    def by_size(run):
        low = None
        for rows in sizes:
            fits = filled <= rows if low is None else filled > low
            if low is not None and rows != sizes[-1]:
                fits = fits & (filled <= rows)
            pl.when(fits)(functools.partial(run, rows))
            low = rows

    if chained:
        copy_moe = pltpu.make_async_copy(moe_in, moe_out, sems.at[0])
        copy_back = pltpu.make_async_copy(back_in, back_out, sems.at[1])

        @pl.when(expert == 0)
        def _():
            copy_moe.start()
            copy_back.start()

    else:

        @pl.when(expert == 0)
        def _():
            moe_out[...] = jnp.zeros_like(moe_out)
            back_out[...] = jnp.zeros_like(back_out)

    def slots(rows):
        mask = lax.broadcasted_iota(jnp.int32, (rows, length), 0) == place_ref[0]
        return mask, jnp.where(mask, 1.0, 0.0).astype(jnp.bfloat16)

    def enter(rows):
        mask, picks = slots(rows)
        rows_in = jnp.dot(picks, normed_ref[...], preferred_element_type=jnp.float32).astype(jnp.bfloat16)
        grad_rows = (
            RESIDUAL * jnp.dot(picks, grad_ref[...], preferred_element_type=jnp.float32)
        ).astype(jnp.bfloat16)
        rows_ref[:rows] = rows_in
        grads_ref[:rows] = grad_rows
        gate = jnp.sum(jnp.where(mask, gate_ref[0], 0.0), axis=1, keepdims=True)
        gate_input = jnp.dot(rows_in, gate_w[0], preferred_element_type=jnp.float32)
        up_input = jnp.dot(rows_in, up_w[0], preferred_element_type=jnp.float32)
        grad_act = right_inner(grad_rows, down_w[0])
        sigmoid_val = jax.nn.sigmoid(gate_input)
        silu_out = gate_input * sigmoid_val
        hidden = silu_out * up_input
        active_ref[:rows] = (hidden * gate).astype(jnp.bfloat16)
        column = jnp.sum(grad_act * hidden, axis=1, keepdims=True)
        gates_out[0] = jnp.sum(jnp.where(mask, column, 0.0), axis=0, keepdims=True)
        grad_hidden = grad_act * gate
        gate_in_ref[:rows] = (
            grad_hidden * up_input * sigmoid_val * (1.0 + gate_input * (1.0 - sigmoid_val))
        ).astype(jnp.bfloat16)
        up_in_ref[:rows] = (grad_hidden * silu_out).astype(jnp.bfloat16)

    by_size(enter)
    if chained:

        @pl.when(expert == 0)
        def _():
            copy_moe.wait()
            copy_back.wait()

    def leave(rows):
        column = jnp.transpose(jnp.broadcast_to(place_ref[0], (128, length)))
        column = jnp.concatenate([column] * (rows // 128), 1)
        own = lax.broadcasted_iota(jnp.int32, (length, rows), 1)
        picks = jnp.where(own == column, 1.0, 0.0).astype(jnp.bfloat16)
        moe = jnp.dot(active_ref[:rows], down_w[0], preferred_element_type=jnp.float32)
        moe_out[...] += jnp.dot(
            picks, moe.astype(jnp.bfloat16), preferred_element_type=jnp.float32
        )
        back = right_inner(gate_in_ref[:rows], gate_w[0]) + right_inner(up_in_ref[:rows], up_w[0])
        back_out[...] += jnp.dot(
            picks, back.astype(jnp.bfloat16), preferred_element_type=jnp.float32
        )

    by_size(leave)

    def copies(target, number):
        return [
            pltpu.make_async_copy(weights_ref.at[kind], target.at[number, kind], out_sems.at[kind])
            for kind in range(3)
        ]

    @pl.when(expert > 0)
    def _():
        for copy in copies(grads_out[0], 0):
            copy.wait()

    def weigh(rows):
        grads = left_inner(
            rows_ref[:rows], jnp.concatenate([gate_in_ref[:rows], up_in_ref[:rows]], 1)
        )
        weights_ref[0] = grads[:, :hidden_size]
        weights_ref[1] = grads[:, hidden_size:]
        grad_down = left_inner(active_ref[:rows], grads_ref[:rows])
        own = hidden_size // parts
        blocks = width // hidden_size
        for part in range(parts):
            for piece in range(blocks):
                at = (part * blocks + piece) * own
                weights_ref[2, at : at + own, :] = grad_down[
                    part * own : (part + 1) * own, piece * hidden_size : (piece + 1) * hidden_size
                ]

    by_size(weigh)
    start = 0
    for target, number in zip(grads_out, numbers):

        @pl.when((expert >= start) & (expert < start + number))
        def _():
            for copy in copies(target, expert - start):
                copy.start()

        start += number

    @pl.when(expert == pl.num_programs(0) - 1)
    def _():
        for copy in copies(grads_out[0], 0):
            copy.wait()


def expert_stage(parts, first, numbers, counts, places, gate_rows, normed_b, grad_b, gate_w, up_w, down_w, sums):
    number = sum(numbers)
    length, width = normed_b.shape
    hidden = gate_w.shape[2]
    experts = places.shape[0]
    chained = sums is not None
    whole = lambda e, c: (0, 0)
    row_spec = pl.BlockSpec((1, 1, length), lambda e, c: (first + e, 0, 0))
    once = pl.Buffered(1)
    f32, bf16 = jnp.float32, jnp.bfloat16
    in_specs = [
        row_spec,
        row_spec,
        pl.BlockSpec((length, width), whole, pipeline_mode=once),
        pl.BlockSpec((length, width), whole, pipeline_mode=once),
        pl.BlockSpec((1, width, hidden), lambda e, c: (first + e, 0, 0)),
        pl.BlockSpec((1, width, hidden), lambda e, c: (first + e, 0, 0)),
        pl.BlockSpec((1, hidden, width), lambda e, c: (first + e, 0, 0)),
    ]
    args = [
        counts,
        places.reshape(experts, 1, length),
        gate_rows.reshape(experts, 1, length),
        normed_b,
        grad_b,
        gate_w,
        up_w,
        down_w,
    ]
    if chained:
        in_specs += [pl.BlockSpec(memory_space=pl.ANY)] * 2
        args += [sums[0], sums[1]]
    results = pl.pallas_call(
        functools.partial(expert_kernel, parts, first, numbers, chained),
        out_shape=[jax.ShapeDtypeStruct((some, 3, width, hidden), f32) for some in numbers]
        + [
            jax.ShapeDtypeStruct((length, width), f32),
            jax.ShapeDtypeStruct((length, width), f32),
            jax.ShapeDtypeStruct((number, 1, length), f32),
        ],
        grid_spec=pltpu.PrefetchScalarGridSpec(
            num_scalar_prefetch=1,
            grid=(number,),
            in_specs=in_specs,
            out_specs=[pl.BlockSpec(memory_space=pl.ANY)] * len(numbers)
            + [
                pl.BlockSpec((length, width), whole, pipeline_mode=once),
                pl.BlockSpec((length, width), whole, pipeline_mode=once),
                pl.BlockSpec((1, 1, length), lambda e, c: (e, 0, 0)),
            ],
            scratch_shapes=[
                pltpu.VMEM((CAP, width), bf16),
                pltpu.VMEM((CAP, width), bf16),
                pltpu.VMEM((CAP, hidden), bf16),
                pltpu.VMEM((CAP, hidden), bf16),
                pltpu.VMEM((CAP, hidden), bf16),
                pltpu.VMEM((3, width, hidden), f32),
                pltpu.SemaphoreType.DMA((2,)),
                pltpu.SemaphoreType.DMA((3,)),
            ],
        ),
        compiler_params=pltpu.CompilerParams(
            dimension_semantics=("arbitrary",), vmem_limit_bytes=63 << 20
        ),
        cost_estimate=pl.CostEstimate(
            flops=number * 8 * 10**9, bytes_accessed=number * 14 * 10**6, transcendentals=0
        ),
    )(*args)
    return results[: len(numbers)], results[len(numbers) :]


PIECES = 16


def line_gather_kernel(n, x_ref, out_ref, blocks_ref, recv, up_send, down_send):
    me = lax.axis_index("tensor")
    has_low, has_high = me > 0, me < n - 1
    barrier = pltpu.get_barrier_semaphore()

    @pl.when(has_low)
    def _():
        pl.semaphore_signal(barrier, inc=1, device_id={"tensor": me - 1}, device_id_type=MESH)

    @pl.when(has_high)
    def _():
        pl.semaphore_signal(barrier, inc=1, device_id={"tensor": me + 1}, device_id_type=MESH)

    blocks_ref[me] = x_ref[...].astype(jnp.float32)
    pl.semaphore_wait(barrier, has_low.astype(jnp.int32) + has_high.astype(jnp.int32))
    rows = x_ref.shape[0] // PIECES

    def copy(block, c, send, to):
        piece = blocks_ref.at[block, pl.ds(pl.multiple_of(c * rows, rows), rows), :]
        return pltpu.make_async_remote_copy(
            src_ref=piece,
            dst_ref=piece,
            send_sem=send.at[block, c],
            recv_sem=recv.at[block, c],
            device_id={"tensor": to},
            device_id_type=MESH,
        )

    for hop in range(n):
        low, high = me - hop, me + hop

        def step(c, carry):
            @pl.when(low >= 0)
            def _():
                if hop > 0:
                    copy(low, c, up_send, me).wait_recv()

                @pl.when(has_high)
                def _():
                    copy(low, c, up_send, me + 1).start()

            @pl.when(high < n)
            def _():
                if hop > 0:
                    copy(high, c, down_send, me).wait_recv()

                @pl.when(has_low)
                def _():
                    copy(high, c, down_send, me - 1).start()

            return carry

        lax.fori_loop(0, PIECES, step, 0)
    wide = x_ref.shape[1]
    for block in range(n):
        out_ref[:, block * wide : (block + 1) * wide] = blocks_ref[block].astype(jnp.bfloat16)
    for hop in range(n):
        low, high = me - hop, me + hop

        def drain(c, carry):
            @pl.when((low >= 0) & has_high)
            def _():
                copy(low, c, up_send, me).wait_send()

            @pl.when((high < n) & has_low)
            def _():
                copy(high, c, down_send, me).wait_send()

            return carry

        lax.fori_loop(0, PIECES, drain, 0)


def line_gather(x, n, name):
    length, wide = x.shape
    full = pl.BlockSpec(memory_space=pltpu.VMEM)
    return pl.pallas_call(
        functools.partial(line_gather_kernel, n),
        out_shape=jax.ShapeDtypeStruct((length, n * wide), jnp.bfloat16),
        in_specs=[full],
        out_specs=full,
        scratch_shapes=[pltpu.VMEM((n, length, wide), jnp.float32)]
        + [pltpu.SemaphoreType.DMA((n, PIECES))] * 3,
        compiler_params=pltpu.CompilerParams(
            collective_id=name, has_side_effects=True, vmem_limit_bytes=32 << 20
        ),
        cost_estimate=pl.CostEstimate(
            flops=0, bytes_accessed=16 * n * x.size, transcendentals=0
        ),
    )(x)


BLOCK = 256


def own_rows_kernel(parts, weight_ref, out_ref):
    rows = out_ref.shape[0]
    first = lax.axis_index("dp") * rows if parts > 1 else 0
    out_ref[...] = weight_ref[pl.ds(pl.multiple_of(first, 16), rows), :].astype(jnp.float32)


def gather_out_weight(out_weight, parts):
    rows, width = out_weight.shape
    ways = parts if rows % (16 * parts) == 0 else 1
    full = pl.BlockSpec(memory_space=pltpu.VMEM)
    own = pl.pallas_call(
        functools.partial(own_rows_kernel, ways),
        out_shape=jax.ShapeDtypeStruct((rows // ways, width), jnp.float32),
        in_specs=[full],
        out_specs=full,
    )(out_weight)
    return ways, lax.all_gather(own, "tensor")


def middle_kernel(
    attended_ref, weight_all_ref, tokens_ref, gain_ref, router_ref, chosen_ref, middle_out, normed_out, gates_out, weight_ref
):
    ways, n, rows, unused = weight_all_ref.shape

    @pl.when(pl.program_id(0) == 0)
    def _():
        for way in range(ways):
            for block in range(n):
                at = (block * ways + way) * rows
                weight_ref[at : at + rows, :] = weight_all_ref[way, block].astype(jnp.bfloat16)

    branch = jnp.dot(attended_ref[...], weight_ref[...], preferred_element_type=jnp.float32)
    middle = tokens_ref[...].astype(jnp.float32) + RESIDUAL * branch
    middle_out[...] = middle
    recip = lax.rsqrt(jnp.mean(middle * middle, axis=1, keepdims=True) + EPSILON)
    normed = (middle * recip * gain_ref[...]).astype(jnp.bfloat16)
    normed_out[...] = normed
    logits = jnp.dot(normed, router_ref[...], preferred_element_type=jnp.float32)
    raised = jnp.where(chosen_ref[...] > 0.0, jnp.exp(logits), 0.0)
    gates_out[...] = raised / jnp.sum(raised, axis=1, keepdims=True)


def enter_middle(attended, weight_all, tokens, gain, router, chosen):
    length, width = tokens.shape
    rows = lambda columns: pl.BlockSpec((BLOCK, columns), lambda i: (i, 0))
    whole = lambda shape: pl.BlockSpec(
        shape, lambda i: (0,) * len(shape), pipeline_mode=pl.Buffered(1)
    )
    experts = router.shape[1]
    return pl.pallas_call(
        middle_kernel,
        out_shape=[
            jax.ShapeDtypeStruct((length, width), jnp.float32),
            jax.ShapeDtypeStruct((length, width), jnp.bfloat16),
            jax.ShapeDtypeStruct((length, experts), jnp.float32),
        ],
        grid=(length // BLOCK,),
        in_specs=[
            rows(attended.shape[1]),
            whole(weight_all.shape),
            rows(width),
            whole((1, width)),
            whole(router.shape),
            rows(experts),
        ],
        out_specs=[rows(width), rows(width), rows(experts)],
        scratch_shapes=[pltpu.VMEM((attended.shape[1], width), jnp.bfloat16)],
        compiler_params=pltpu.CompilerParams(
            dimension_semantics=("arbitrary",), vmem_limit_bytes=48 << 20
        ),
        cost_estimate=pl.CostEstimate(
            flops=2 * length * width * width, bytes_accessed=25 * 10**6, transcendentals=0
        ),
    )(attended, weight_all, tokens, gain.reshape(1, width), router, chosen)


def turn_kernel(
    n,
    part_ref,
    gates_part_ref,
    gates_ref,
    middle_ref,
    cotangent_ref,
    gain_ref,
    router_ref,
    grad_out,
    branch_out,
    logits_out,
    gain_out,
    summed_ref,
    gates_rows_ref,
    grad_gates_ref,
    *line,
):
    length = part_ref.shape[0]
    rows = length // STEPS

    def done(c):
        @pl.when(c == 0)
        def _():
            experts = gates_rows_ref.shape[0]
            empty = jnp.zeros((grad_gates_ref.shape[1] - experts, length), jnp.float32)
            grad_gates_ref[...] = jnp.transpose(
                jnp.concatenate([gates_rows_ref[...], empty], 0)
            )

        own = pl.ds(pl.multiple_of(c * rows, rows), rows)
        gates, grad_gates = gates_ref[own, :], grad_gates_ref[own, :]
        weighted = jnp.sum(gates * grad_gates, axis=1, keepdims=True)
        grad_logits = (gates * (grad_gates - weighted)).astype(jnp.bfloat16)
        logits_out[own, :] = grad_logits
        grad = summed_ref[own, :] + right_inner(grad_logits, router_ref[...])
        middle = middle_ref[own, :]
        recip = lax.rsqrt(jnp.mean(middle * middle, axis=1, keepdims=True) + EPSILON)
        unit = middle * recip
        gain_out[...] += jnp.sum(grad * unit, axis=0, keepdims=True)
        scaled = grad * gain_ref[...]
        back = recip * (scaled - unit * jnp.mean(scaled * unit, axis=1, keepdims=True))
        total = cotangent_ref[own, :].astype(jnp.float32) + back
        grad_out[own, :] = total
        branch_out[own, :] = (RESIDUAL * total).astype(jnp.bfloat16)

    begin, step, finish = line_stages(
        n, [part_ref, gates_part_ref], [summed_ref, gates_rows_ref], line, done, 1
    )
    begin()
    gain_out[...] = jnp.zeros_like(gain_out)
    lax.fori_loop(0, 2 * STEPS, step, 0)
    finish()


def turn_middle(n, part, gates_part, gates, middle, cotangent, gain, router, name):
    length, width = part.shape
    full = pl.BlockSpec(memory_space=pltpu.VMEM)
    f32 = jnp.float32
    return pl.pallas_call(
        functools.partial(turn_kernel, n),
        out_shape=[
            jax.ShapeDtypeStruct((length, width), f32),
            jax.ShapeDtypeStruct((length, width), jnp.bfloat16),
            jax.ShapeDtypeStruct(gates.shape, jnp.bfloat16),
            jax.ShapeDtypeStruct((1, width), f32),
        ],
        in_specs=[full] * 7,
        out_specs=[full] * 4,
        scratch_shapes=[
            pltpu.VMEM(part.shape, f32),
            pltpu.VMEM(gates_part.shape, f32),
            pltpu.VMEM(gates.shape, f32),
        ]
        + line_scratch([part, gates_part]),
        compiler_params=pltpu.CompilerParams(
            collective_id=name, has_side_effects=True, vmem_limit_bytes=58 << 20
        ),
        cost_estimate=pl.CostEstimate(
            flops=40 * length * width, bytes_accessed=60 * 10**6, transcendentals=0
        ),
    )(part, gates_part, gates, middle, cotangent, gain.reshape(1, width), router)


def last_kernel(summed_ref, tokens_ref, middle_ref, gain_ref, out_ref):
    hidden = tokens_ref[...].astype(jnp.float32)
    recip = lax.rsqrt(jnp.mean(hidden * hidden, axis=1, keepdims=True) + EPSILON)
    unit = hidden * recip
    scaled = summed_ref[...] * gain_ref[...]
    inner = jnp.mean(scaled * unit, axis=1, keepdims=True)
    out_ref[...] = middle_ref[...] + recip * (scaled - unit * inner)


def leave_first(summed, tokens, grad_middle, gain):
    length, width = tokens.shape
    rows = pl.BlockSpec((BLOCK // 2, width), lambda i: (i, 0))
    return pl.pallas_call(
        last_kernel,
        out_shape=jax.ShapeDtypeStruct((length, width), jnp.float32),
        grid=(2 * length // BLOCK,),
        in_specs=[rows, rows, rows, pl.BlockSpec((1, width), lambda i: (0, 0))],
        out_specs=rows,
        compiler_params=pltpu.CompilerParams(vmem_limit_bytes=16 << 20),
        cost_estimate=pl.CostEstimate(
            flops=10 * length * width, bytes_accessed=14 * length * width, transcendentals=0
        ),
    )(summed, tokens, grad_middle, gain.reshape(1, width))


SPAN = 768
ROWS = 256


def lane_halves(shape):
    return lax.broadcasted_iota(jnp.int32, shape, len(shape) - 1) // HEAD


def select_halves(tile, source, half):
    kept = jnp.where(lane_halves(tile.shape) == source, tile, 0.0)
    return kept if source == half else pltpu.roll(kept, HEAD, 1)


def spread_pairs(tile, target):
    for source in range(2):
        for half in range(2):
            target[2 * source + half] = select_halves(tile, source, half).astype(jnp.bfloat16)


def rope_tile(tile, cosine, sine_low, sine_high):
    return tile * cosine + pltpu.roll(tile, 128 - HEAD // 2, 1) * sine_low + pltpu.roll(
        tile, HEAD // 2, 1
    ) * sine_high


def rope_back_tile(tile, cosine, sine_low, sine_high):
    return (
        tile * cosine
        + pltpu.roll(tile * sine_low, HEAD // 2, 1)
        + pltpu.roll(tile * sine_high, 128 - HEAD // 2, 1)
    )


def window(block):
    first = block * ROWS
    return first, jnp.maximum(first + ROWS - SPAN, 0)


def attend_forward_kernel(
    heads,
    group,
    tokens_ref,
    gain_ref,
    query_w,
    key_w,
    value_w,
    cosine_ref,
    sine_low_ref,
    sine_high_ref,
    opening_ref,
    normed_out,
    query_out,
    key_out,
    value_out,
    attended_out,
    logsum_out,
    key_pairs,
    value_pairs,
    tiles_ref,
):
    tiles, length, unused = query_out.shape
    hidden = tokens_ref[...].astype(jnp.float32)
    recip = lax.rsqrt(jnp.mean(hidden * hidden, axis=1, keepdims=True) + EPSILON)
    normed_out[...] = (hidden * recip * gain_ref[...]).astype(jnp.bfloat16)
    cosine, sine_low, sine_high = cosine_ref[...], sine_low_ref[...], sine_high_ref[...]
    for tile in range(tiles):
        query = jnp.dot(
            normed_out[...],
            query_w[:, tile * 128 : (tile + 1) * 128],
            preferred_element_type=jnp.float32,
        )
        query_out[tile] = rope_tile(query, cosine, sine_low, sine_high).astype(jnp.bfloat16)
    key = rope_tile(
        jnp.dot(normed_out[...], key_w[...], preferred_element_type=jnp.float32),
        cosine,
        sine_low,
        sine_high,
    )
    value = jnp.dot(normed_out[...], value_w[...], preferred_element_type=jnp.float32)
    key_out[...] = key.astype(jnp.bfloat16)
    value_out[...] = value.astype(jnp.bfloat16)
    spread_pairs(key, key_pairs)
    spread_pairs(value, value_pairs)
    blocks = length // ROWS
    tiles_ref[...] = jnp.zeros_like(tiles_ref)

    def unit(step, carry):
        head, block = step // blocks, step % blocks
        tile, half = head // 2, head % 2
        pair = 2 * (head // group) + half
        first, low = window(block)
        rows = pl.ds(pl.multiple_of(first, ROWS), ROWS)
        span = pl.ds(pl.multiple_of(low, ROWS), SPAN)
        scores = right_inner(query_out[tile, rows, :], key_pairs[pair, span, :])
        columns = low + lax.broadcasted_iota(jnp.int32, (ROWS, SPAN), 1)
        own = first + lax.broadcasted_iota(jnp.int32, (ROWS, SPAN), 0)
        allowed = (columns >= opening_ref[rows, :]) & (columns <= own)
        raised = jnp.where(allowed, jnp.exp(ATTN_SCALE * scores), 0.0)
        total = jnp.sum(raised, axis=1, keepdims=True)
        product = jnp.dot(
            raised.astype(jnp.bfloat16), value_pairs[pair, span, :], preferred_element_type=jnp.float32
        )
        tiles_ref[tile, rows, :] += product / total
        wide = jnp.broadcast_to(jnp.log(total), (ROWS, 128))
        logsum_out[head, :, rows] = jnp.transpose(wide)[:1]
        return carry

    lax.fori_loop(0, heads * blocks, unit, 0)
    for tile in range(tiles):
        attended_out[:, tile * 128 : (tile + 1) * 128] = tiles_ref[tile].astype(jnp.bfloat16)


def attend_forward(tokens, gain, query_w, key_w, value_w, tables, opening, heads, group):
    length, width = tokens.shape
    wide = query_w.shape[1]
    tiles = wide // 128
    bf16, f32 = jnp.bfloat16, jnp.float32
    full = pl.BlockSpec(memory_space=pltpu.VMEM)
    return pl.pallas_call(
        functools.partial(attend_forward_kernel, heads, group),
        out_shape=[
            jax.ShapeDtypeStruct((length, width), bf16),
            jax.ShapeDtypeStruct((tiles, length, 128), bf16),
            jax.ShapeDtypeStruct((length, 128), bf16),
            jax.ShapeDtypeStruct((length, 128), bf16),
            jax.ShapeDtypeStruct((length, wide), bf16),
            jax.ShapeDtypeStruct((heads, 1, length), f32),
        ],
        in_specs=[full] * 9,
        out_specs=[full] * 6,
        scratch_shapes=[
            pltpu.VMEM((4, length, 128), bf16),
            pltpu.VMEM((4, length, 128), bf16),
            pltpu.VMEM((tiles, length, 128), f32),
        ],
        compiler_params=pltpu.CompilerParams(vmem_limit_bytes=48 << 20),
        cost_estimate=pl.CostEstimate(
            flops=8 * 10**9, bytes_accessed=12 * 10**6, transcendentals=5 * 10**6
        ),
    )(tokens, gain.reshape(1, width), query_w, key_w, value_w, *tables, opening.reshape(length, 1))


def attend_backward_kernel(
    n,
    heads,
    group,
    branch_ref,
    out_w,
    query_ref,
    key_ref,
    value_ref,
    attended_ref,
    logsum_ref,
    query_w,
    key_w,
    value_w,
    cosine_ref,
    sine_low_ref,
    sine_high_ref,
    opening_ref,
    tokens_ref,
    moe_ref,
    middle_ref,
    grads_out,
    normed_out,
    gain_out,
    output_ref,
    moe_sum,
    middle_rows,
    middle_sems,
    key_pairs,
    value_pairs,
    attend_grads,
    query_grads,
    key_grads,
    value_grads,
    delta_ref,
    *line,
):
    tiles, length, unused = query_ref.shape
    share = length // STEPS

    def share_rows(c):
        return pl.ds(pl.multiple_of(c * share, share), share)

    def fetch(c):
        slot = lax.rem(c, 2)
        return pltpu.make_async_copy(
            middle_ref.at[share_rows(c), :], middle_rows.at[slot], middle_sems.at[slot]
        )

    def done(c):
        fetch(c).wait()

        @pl.when(c + 1 < STEPS)
        def _():
            fetch(c + 1).start()

        total = middle_rows[lax.rem(c, 2)] + RESIDUAL * moe_sum[share_rows(c), :]
        output_ref[share_rows(c), :] = total.astype(jnp.bfloat16)

    line_start, line_step, line_end = line_stages(n, [moe_ref], [moe_sum], line, done)
    line_start()
    fetch(jnp.int32(0)).start()
    blocks = length // ROWS
    units = heads * blocks
    taken = 0

    def run_line(steps):
        nonlocal taken
        until = min(taken + steps, 2 * STEPS)
        lax.fori_loop(taken, until, line_step, 0)
        taken = until

    run_line(2)
    spread_pairs(key_ref[...].astype(jnp.float32), key_pairs)
    spread_pairs(value_ref[...].astype(jnp.float32), value_pairs)
    halves = (
        lax.broadcasted_iota(jnp.int32, (8, 128), 0) == lane_halves((8, 128))
    ).astype(jnp.float32)
    for tile in range(tiles):
        lanes = slice(tile * 128, (tile + 1) * 128)
        grad = right_inner(branch_ref[...], out_w[lanes, :]).astype(jnp.bfloat16)
        attend_grads[tile] = grad
        products = grad.astype(jnp.float32) * attended_ref[:, lanes].astype(jnp.float32)
        sums = lax.dot_general(
            halves,
            products,
            (((1,), (1,)), ((), ())),
            precision=lax.Precision.HIGHEST,
            preferred_element_type=jnp.float32,
        )
        delta_ref[2 * tile] = sums[0:1]
        delta_ref[2 * tile + 1] = sums[1:2]
        run_line(2)
    query_grads[...] = jnp.zeros_like(query_grads)
    key_grads[...] = jnp.zeros_like(key_grads)
    value_grads[...] = jnp.zeros_like(value_grads)
    before, each = taken, (2 * STEPS - 8 - taken) // units
    taken += units * each

    def unit(step, carry):
        lax.fori_loop(before + step * each, before + step * each + each, line_step, 0)
        head, block = step // blocks, step % blocks
        tile, half = head // 2, head % 2
        pair = 2 * (head // group) + half
        first, low = window(block)
        rows = pl.ds(pl.multiple_of(first, ROWS), ROWS)
        span = pl.ds(pl.multiple_of(low, ROWS), SPAN)
        keys = key_pairs[pair, span, :]
        query = query_ref[tile, rows, :]
        grad = attend_grads[tile, rows, :]
        scores = right_inner(keys, query)
        columns = low + lax.broadcasted_iota(jnp.int32, (SPAN, ROWS), 0)
        own = first + lax.broadcasted_iota(jnp.int32, (SPAN, ROWS), 1)
        allowed = (columns >= opening_ref[:, rows]) & (columns <= own)
        probs = jnp.where(
            allowed, jnp.exp(ATTN_SCALE * scores - logsum_ref[head, :, rows]), 0.0
        )
        grad_probs = right_inner(value_pairs[pair, span, :], grad)
        grad_scores = (probs * (grad_probs - delta_ref[head, :, rows])).astype(jnp.bfloat16)
        value_grads[pair, span, :] += jnp.dot(
            probs.astype(jnp.bfloat16), grad, preferred_element_type=jnp.float32
        )
        key_grads[pair, span, :] += jnp.dot(
            grad_scores, query, preferred_element_type=jnp.float32
        )
        query_grads[tile, rows, :] += left_inner(grad_scores, keys)
        return carry

    lax.fori_loop(0, units, unit, 0)
    cosine, sine_low, sine_high = cosine_ref[...], sine_low_ref[...], sine_high_ref[...]
    wide = tiles * 128
    for tile in range(tiles):
        grads_out[:, tile * 128 : (tile + 1) * 128] = rope_back_tile(
            ATTN_SCALE * query_grads[tile], cosine, sine_low, sine_high
        ).astype(jnp.bfloat16)
    totals = []
    for grads in (key_grads, value_grads):
        totals.append(
            sum(
                select_halves(grads[2 * source + half], half, source)
                for source in range(2)
                for half in range(2)
            )
        )
    grads_out[:, wide : wide + 128] = rope_back_tile(
        ATTN_SCALE * totals[0], cosine, sine_low, sine_high
    ).astype(jnp.bfloat16)
    grads_out[:, wide + 128 : wide + 256] = totals[1].astype(jnp.bfloat16)
    gain_sum = jnp.zeros((1, normed_out.shape[1]), jnp.float32)
    for block in range(blocks):
        rows = slice(block * ROWS, (block + 1) * ROWS)
        normed = (
            right_inner(grads_out[rows, :wide], query_w[...])
            + right_inner(grads_out[rows, wide : wide + 128], key_w[...])
            + right_inner(grads_out[rows, wide + 128 :], value_w[...])
        )
        normed_out[rows, :] = normed
        hidden = tokens_ref[rows, :].astype(jnp.float32)
        recip = lax.rsqrt(jnp.mean(hidden * hidden, axis=1, keepdims=True) + EPSILON)
        gain_sum += jnp.sum(normed * (hidden * recip), axis=0, keepdims=True)
        run_line(2)
    gain_out[...] = gain_sum
    run_line(2 * STEPS)
    line_end()


def attend_backward(
    n, branch, out_w, query, key, value, attended, logsum, query_w, key_w, value_w, tables, opening, tokens, moe, middle,
    heads, group, name,
):
    length, width = branch.shape
    tiles = query.shape[0]
    wide = tiles * 128
    bf16, f32 = jnp.bfloat16, jnp.float32
    full = pl.BlockSpec(memory_space=pltpu.VMEM)
    return pl.pallas_call(
        functools.partial(attend_backward_kernel, n, heads, group),
        out_shape=[
            jax.ShapeDtypeStruct((length, wide + 256), bf16),
            jax.ShapeDtypeStruct((length, width), f32),
            jax.ShapeDtypeStruct((1, width), f32),
            jax.ShapeDtypeStruct((length, width), bf16),
        ],
        in_specs=[full] * 16 + [pl.BlockSpec(memory_space=pl.ANY)],
        out_specs=[full] * 4,
        scratch_shapes=[
            pltpu.VMEM((length, width), f32),
            pltpu.VMEM((2, length // STEPS, width), f32),
            pltpu.SemaphoreType.DMA((2,)),
            pltpu.VMEM((4, length, 128), bf16),
            pltpu.VMEM((4, length, 128), bf16),
            pltpu.VMEM((tiles, length, 128), bf16),
            pltpu.VMEM((tiles, length, 128), f32),
            pltpu.VMEM((4, length, 128), f32),
            pltpu.VMEM((4, length, 128), f32),
            pltpu.VMEM((2 * tiles, 1, length), f32),
        ]
        + line_scratch([moe]),
        compiler_params=pltpu.CompilerParams(
            collective_id=name, has_side_effects=True, vmem_limit_bytes=63 << 20
        ),
        cost_estimate=pl.CostEstimate(
            flops=12 * 10**9, bytes_accessed=30 * 10**6, transcendentals=5 * 10**6
        ),
    )(
        branch, out_w, query, key, value, attended, logsum, query_w, key_w, value_w, *tables,
        opening.reshape(1, length), tokens, moe, middle,
    )


def finish_kernel(
    n,
    parts,
    local_ref,
    normed_ref,
    grads_ref,
    branch_ref,
    attended_ref,
    normed_two_ref,
    logits_ref,
    gain_ref,
    first_gain_ref,
    normed_out,
    query_out,
    key_out,
    value_out,
    branch_out,
    router_out,
    gain_out,
    first_gain_out,
    weights_ref,
    gains_ref,
    gain_send,
    gain_recv,
    *scratch,
):
    levels = parts.bit_length() - 1
    held = scratch[:levels]
    sends, recvs = scratch[levels : levels + 2]
    line_start, line_step, line_end = line_stages(n, [local_ref], [normed_out], scratch[levels + 2 :])
    me = lax.axis_index("dp")
    width = normed_ref.shape[1]
    own = width // parts
    wide, attended_wide = grads_ref.shape[1], attended_ref.shape[1]
    mine = lax.axis_index("tensor")
    line_start(
        [{"dp": jnp.bitwise_xor(me, 1 << level)} for level in range(levels)]
        + [{"tensor": lax.rem(mine + ahead, n)} for ahead in range(1, n)]
    )

    def run_line(first, last):
        lax.fori_loop(first, last, line_step, 0)

    run_line(0, 2)
    pieces = 4
    block = width // pieces
    for piece in range(pieces):
        rows = slice(piece * block, (piece + 1) * block)
        weights_ref[rows, :wide] = left_inner(normed_ref[:, rows], grads_ref[...])
        weights_ref[rows, wide : wide + attended_wide] = left_inner(
            branch_ref[:, rows], attended_ref[...]
        )
        gain = jnp.transpose(jnp.broadcast_to(gain_ref[:, rows], (128, block)))
        first_gain = jnp.transpose(jnp.broadcast_to(first_gain_ref[:, rows], (128, block)))
        lanes = lax.broadcasted_iota(jnp.int32, (block, 128), 1)
        weights_ref[rows, wide + attended_wide :] = jnp.where(
            lanes == 127,
            gain,
            jnp.where(
                lanes == 126, first_gain, left_inner(normed_two_ref[:, rows], logits_ref[...])
            ),
        )
        run_line(2 + 2 * piece, 4 + 2 * piece)
    done = 2 + 2 * pieces

    columns = weights_ref.shape[1]
    middle = columns // 256 * 128
    orders = (
        (slice(0, middle), list(range(levels))),
        (slice(middle, columns), [0] + list(range(levels - 1, 0, -1))),
    )

    def shard(number, lanes):
        return weights_ref.at[pl.ds(pl.multiple_of(number * own, own), own), lanes]

    def numbers(order, level, peer):
        fixed = sum(1 << bit for bit in order[: level + 1])
        base = jnp.bitwise_and(peer, fixed)
        free = order[level + 1 :]
        return [
            base + sum(((i >> place) & 1) << bit for place, bit in enumerate(free))
            for i in range(1 << len(free))
        ]

    def copies(level):
        made = []
        for side, (lanes, order) in enumerate(orders):
            peer = jnp.bitwise_xor(me, 1 << order[level])
            for i, number in enumerate(numbers(order, level, peer)):
                made.append(
                    pltpu.make_async_remote_copy(
                        src_ref=shard(number, lanes),
                        dst_ref=held[level].at[i, :, lanes],
                        send_sem=sends.at[side, level, i],
                        recv_sem=recvs.at[side, level, i],
                        device_id={"dp": peer},
                        device_id_type=MESH,
                    )
                )
        return made

    stops = [6] + [42] * (levels > 1) + [4, 0, 0]
    for level in range(levels):
        for copy in copies(level):
            copy.start()
        until = done + stops[level]
        run_line(done, until)
        done = until
        for copy in copies(level):
            copy.wait_recv()
        for lanes, order in orders:
            for i, number in enumerate(numbers(order, level, me)):
                target = shard(number, lanes)
                target[...] += held[level][i, :, lanes]
    everything = slice(0, columns)
    gains_ref[0] = shard(me, slice(wide + attended_wide, columns))[...]
    gain_copies = [
        pltpu.make_async_remote_copy(
            src_ref=gains_ref.at[0],
            dst_ref=gains_ref.at[ahead],
            send_sem=gain_send.at[ahead],
            recv_sem=gain_recv.at[ahead],
            device_id={"tensor": lax.rem(mine + ahead, n)},
            device_id_type=MESH,
        )
        for ahead in range(1, n)
    ]
    for copy in gain_copies:
        copy.start()
    kept = shard(me, everything)
    query_out[...] = kept[:, : query_out.shape[1]]
    key_out[...] = kept[:, wide - 256 : wide - 256 + key_out.shape[1]]
    value_out[...] = kept[:, wide - 128 : wide - 128 + value_out.shape[1]]
    branch_out[...] = kept[:, wide : wide + branch_out.shape[1]]
    router_out[...] = jnp.transpose(gains_ref[0])[: router_out.shape[0]]
    run_line(done, 2 * STEPS)
    total = gains_ref[0]
    for ahead, copy in enumerate(gain_copies, 1):
        copy.wait_recv()
        total = total + gains_ref[ahead]
    gain_out[...] = jnp.transpose(gains_ref[0])[127:]
    first_gain_out[...] = jnp.transpose(total)[126:127]
    for level in range(levels):
        for copy in copies(level):
            copy.wait_send()
    for copy in gain_copies:
        copy.wait_send()
    line_end()


def finish(
    n, parts, grad_local, normed_b, grads_wide, branch_b, attended, normed_two_b, grad_logits_b, gain_grad, first_gain_grad,
    wide_q, wide_k, experts, name,
):
    length, width = normed_b.shape
    columns = grads_wide.shape[1] + attended.shape[1] + 128
    full = pl.BlockSpec(memory_space=pltpu.VMEM)
    levels = parts.bit_length() - 1
    own = width // parts
    f32 = jnp.float32
    shapes = [(length, width), (own, wide_q), (own, wide_k), (own, wide_k), (own, wide_q)]
    shapes += [(experts, own), (1, own), (1, own)]
    return pl.pallas_call(
        functools.partial(finish_kernel, n, parts),
        out_shape=[jax.ShapeDtypeStruct(shape, f32) for shape in shapes],
        in_specs=[full] * 9,
        out_specs=[full] * 8,
        scratch_shapes=[
            pltpu.VMEM((width, columns), f32),
            pltpu.VMEM((n, own, 128), f32),
            pltpu.SemaphoreType.DMA((n,)),
            pltpu.SemaphoreType.DMA((n,)),
        ]
        + [pltpu.VMEM((parts >> (level + 1), own, columns), f32) for level in range(levels)]
        + [pltpu.SemaphoreType.DMA((2, levels, parts // 2))] * 2
        + line_scratch([grad_local]),
        compiler_params=pltpu.CompilerParams(
            collective_id=name, has_side_effects=True, vmem_limit_bytes=62 << 20
        ),
        cost_estimate=pl.CostEstimate(
            flops=2 * length * width * columns, bytes_accessed=50 * 10**6, transcendentals=0
        ),
    )(
        grad_local, normed_b, grads_wide, branch_b, attended, normed_two_b, grad_logits_b, gain_grad,
        first_gain_grad,
    )


def place_kernel(shards_ref, *refs):
    gate_out, up_out, down_out = refs[-3:]
    gate_out[0] = shards_ref[0, 0]
    up_out[0] = shards_ref[0, 1]
    rows, hidden = down_out.shape[1], shards_ref.shape[3]
    for piece in range(down_out.shape[2] // hidden):
        down_out[0, :, piece * hidden : (piece + 1) * hidden] = shards_ref[
            0, 2, piece * rows : (piece + 1) * rows, :
        ]


def place_shards(parts, shards, first, experts, before):
    number, unused, rows, hidden = shards.shape
    down_rows = hidden // parts
    width = rows * parts
    shapes = [(experts, rows, hidden), (experts, rows, hidden), (experts, down_rows, width)]
    spec = lambda shape: pl.BlockSpec((1,) + shape[1:], lambda e: (first + e, 0, 0))
    args, extra, aliases = [shards], [], {}
    if before is not None:
        args += list(before)
        extra = [pl.BlockSpec(memory_space=pl.ANY)] * 3
        aliases = {1: 0, 2: 1, 3: 2}
    return pl.pallas_call(
        place_kernel,
        out_shape=[jax.ShapeDtypeStruct(shape, jnp.float32) for shape in shapes],
        grid=(number,),
        in_specs=[pl.BlockSpec((1, 3, rows, hidden), lambda e: (e, 0, 0, 0))] + extra,
        out_specs=[spec(shape) for shape in shapes],
        input_output_aliases=aliases,
        cost_estimate=pl.CostEstimate(
            flops=0, bytes_accessed=8 * shards.size, transcendentals=0
        ),
    )(*args)


def on_device(
    ring,
    tokens,
    cotangent,
    segment_ids,
    routes,
    attn_gain,
    query_weight,
    key_weight,
    value_weight,
    out_weight,
    ffn_gain,
    router_weight,
    gate_weight,
    up_weight,
    down_weight,
):
    length = tokens.shape[0]
    width = tokens.shape[1]
    segment = segment_ids[0]
    heads_local = query_weight.shape[1] // HEAD
    kv_local = key_weight.shape[1] // HEAD
    group_size = heads_local // kv_local
    experts_all = router_weight.shape[1]
    experts_local = gate_weight.shape[0]
    parts = lax.axis_size("dp")
    opening = doc_openings(segment)
    tables = rope_tables(opening, HEAD)
    query_w, key_w, value_w = (pad_columns(w) for w in (query_weight, key_weight, value_weight))
    out_w = jnp.transpose(pad_columns(jnp.transpose(out_weight)))
    ways, out_rows = gather_out_weight(out_weight, parts)
    normed_b, queries, keys, values, attended, logsum = attend_forward(
        tokens, attn_gain, query_w, key_w, value_w, tables, opening, heads_local, group_size
    )
    all_ids = jnp.arange(experts_all, dtype=jnp.int32)
    chosen = jnp.sum((routes[:, :, None] == all_ids[None, None, :]).astype(jnp.int32), axis=1) > 0
    first_expert = lax.axis_index("tensor") * experts_local
    local_ids = first_expert + jnp.arange(experts_local, dtype=jnp.int32)
    picked = jnp.sum((routes[None, :, :] == local_ids[:, None, None]).astype(jnp.int32), axis=2)
    places_in = slot_places(picked)
    counts = jnp.sum(picked, axis=1)
    out_rows, attended = lax.optimization_barrier((out_rows, attended))
    out_all = lax.all_gather(out_rows, "dp") if ways > 1 else out_rows[None]
    attended_all = line_gather(attended, ring, 1)
    attended_all = attended_all.reshape(length, ring, attended.shape[1])
    attended_all = attended_all[:, :, : heads_local * HEAD].reshape(length, -1)
    router_w = pad_columns(router_weight)
    middle, normed_two_b, gate_probs = enter_middle(
        attended_all, out_all, tokens, ffn_gain, router_w, pad_columns(chosen.astype(jnp.float32))
    )
    gate_rows = jnp.transpose(lax.dynamic_slice_in_dim(gate_probs, first_expert, experts_local, 1))
    numbers = (max(1, experts_local // 10),)
    numbers += (experts_local - numbers[0],)
    (grads_first,), sums = expert_stage(
        parts, 0, numbers[:1], counts, places_in, gate_rows, normed_two_b, cotangent,
        gate_weight, up_weight, down_weight, None,
    )
    shards_first = lax.psum_scatter(grads_first, "dp", scatter_dimension=2, tiled=True)
    (grads_last,), sums_last = expert_stage(
        parts, numbers[0], numbers[1:], counts, places_in, gate_rows, normed_two_b, cotangent,
        gate_weight, up_weight, down_weight, sums,
    )
    moe_part, grad_normed_part, unused = sums_last
    shards_first, grads_last, grad_normed_part = lax.optimization_barrier(
        (shards_first, grads_last, grad_normed_part)
    )
    shards_last = lax.psum_scatter(grads_last, "dp", scatter_dimension=2, tiled=True)
    grad_gates_local = jnp.concatenate([sums[2], sums_last[2]], 0).reshape(experts_local, length)
    grad_gates_part = lax.dynamic_update_slice_in_dim(
        jnp.zeros((experts_all, length), jnp.float32), grad_gates_local, first_expert, 0
    )
    grad_middle, grad_branch_b, grad_logits_b, grad_ffn_gain = turn_middle(
        ring, grad_normed_part, grad_gates_part, gate_probs, middle, cotangent, ffn_gain, router_w, 2
    )
    grads_wide, grad_normed_local, first_gain, output = attend_backward(
        ring, grad_branch_b, out_w, queries, keys, values, attended, logsum,
        query_w, key_w, value_w, tables, opening, tokens, moe_part, middle, heads_local, group_size, 3,
    )
    wide_q, wide_k = heads_local * HEAD, kv_local * HEAD
    grads_placed = place_shards(parts, shards_first, 0, experts_local, None)
    grads_placed, grads_wide = lax.optimization_barrier((grads_placed, grads_wide))
    grad_normed, *small = finish(
        ring, parts, grad_normed_local, normed_b, grads_wide, grad_branch_b, attended, normed_two_b,
        grad_logits_b, grad_ffn_gain, first_gain, wide_q, wide_k, experts_all, 4,
    )
    grad_query, grad_key, grad_value, grad_out, grad_router, grad_ffn_gain, grad_attn_gain = small
    grad_tokens = leave_first(grad_normed, tokens, grad_middle, attn_gain)
    shards_last, grad_tokens = lax.optimization_barrier((shards_last, grad_tokens))
    grad_gate, grad_up, grad_down = place_shards(
        parts, shards_last, numbers[0], experts_local, grads_placed
    )
    return (
        output,
        grad_tokens,
        grad_attn_gain.reshape(-1),
        grad_query,
        grad_key,
        grad_value,
        jnp.transpose(grad_out),
        grad_ffn_gain.reshape(-1),
        jnp.transpose(grad_router),
        grad_gate,
        grad_up,
        grad_down,
    )


def solution(mesh):
    return jax.shard_map(
        functools.partial(on_device, mesh.shape["tensor"]),
        mesh=mesh,
        in_specs=(
            P("dp", None),
            P("dp", None),
            P("dp", None),
            P("dp", None),
            P(),
            P(None, "tensor"),
            P(None, "tensor"),
            P(None, "tensor"),
            P("tensor", None),
            P(),
            P(),
            P("tensor", None, None),
            P("tensor", None, None),
            P("tensor", None, None),
        ),
        out_specs=(
            P("dp", None),
            P("dp", None),
            P("dp"),
            P("dp", "tensor"),
            P("dp", "tensor"),
            P("dp", "tensor"),
            P("tensor", "dp"),
            P("dp"),
            P("dp", None),
            P("tensor", "dp", None),
            P("tensor", "dp", None),
            P("tensor", "dp", None),
        ),
        check_vma=False,
    )
```

```python
import functools

import jax
import jax.numpy as jnp
from jax import lax
from jax.experimental import pallas as pl
from jax.experimental.pallas import tpu as pltpu
from jax.sharding import PartitionSpec as P

MESH = pl.DeviceIdType.MESH

HEAD = 64
CAP = 384


EPSILON = 1e-06
RESIDUAL = 0.22
ATTN_SCALE = 0.015625
ROPE_BASE = 10000.0


def left_inner(first, second):
    return lax.dot_general(
        first, second, (((0,), (0,)), ((), ())), preferred_element_type=jnp.float32
    )


def right_inner(first, second):
    return lax.dot_general(
        first, second, (((1,), (1,)), ((), ())), preferred_element_type=jnp.float32
    )


def doc_openings(segment):
    return jnp.sum((segment[None, :] < segment[:, None]).astype(jnp.int32), axis=1)


def rope_tables(opening, head_size):
    halfway = head_size // 2
    spread = jnp.arange(halfway, dtype=jnp.float32) * (2.0 / head_size)
    inverse = jnp.power(ROPE_BASE, -spread)
    places = jnp.arange(opening.shape[0], dtype=jnp.int32)
    angles = (places - opening).astype(jnp.float32)[:, None] * inverse[None, :]
    cosine, sine = jnp.cos(angles), jnp.sin(angles)
    none = jnp.zeros_like(sine)
    return (
        jnp.concatenate([cosine] * 4, 1),
        jnp.concatenate([-sine, none] * 2, 1),
        jnp.concatenate([none, sine] * 2, 1),
    )


def pad_columns(weight):
    missing = -weight.shape[1] % 128
    return weight if missing == 0 else jnp.pad(weight, ((0, 0), (0, missing)))


def rms_forward(hidden, gain):
    recip = lax.rsqrt(jnp.mean(hidden * hidden, axis=-1, keepdims=True) + EPSILON)
    unit = hidden * recip
    return (unit * gain, unit, recip)


def rms_backward(gradient, unit, recip, gain):
    gain_grad = jnp.sum(gradient * unit, axis=0)
    scaled = gradient * gain
    return (recip * (scaled - unit * jnp.mean(scaled * unit, axis=-1, keepdims=True)), gain_grad)


def slot_places(picked):
    length = picked.shape[1]
    tokens = jnp.arange(length, dtype=jnp.int32)
    earlier = (tokens[:, None] < tokens[None, :]).astype(jnp.bfloat16)
    before = jnp.dot(picked.astype(jnp.bfloat16), earlier, preferred_element_type=jnp.float32)
    return jnp.where(picked > 0, before.astype(jnp.int32), -1)


STEPS = 32
LAG = 2


def line_stages(n, xs, outs, scratch, done=None, whole=0):
    count = len(xs)
    lows, highs = scratch[:count], scratch[count : 2 * count]
    low_recv, high_recv, total_recv, up_send, low_send, high_send = scratch[2 * count :]
    me = lax.axis_index("tensor")
    root = n // 2
    has_low, has_high = me > 0, me < n - 1

    def begin(others=()):
        barrier = pltpu.get_barrier_semaphore()
        for other in others:
            pl.semaphore_signal(barrier, inc=1, device_id=other, device_id_type=MESH)

        @pl.when(has_low)
        def _():
            pl.semaphore_signal(barrier, inc=1, device_id={"tensor": me - 1}, device_id_type=MESH)

        @pl.when(has_high)
        def _():
            pl.semaphore_signal(barrier, inc=1, device_id={"tensor": me + 1}, device_id_type=MESH)

        pl.semaphore_wait(
            barrier, len(others) + has_low.astype(jnp.int32) + has_high.astype(jnp.int32)
        )

    def piece(ref, c):
        rows = ref.shape[0] // STEPS
        return ref.at[pl.ds(pl.multiple_of(c * rows, rows), rows), :]

    cut = count - whole

    def copies(sources, targets, c, send, recv, to, uncut):
        return [
            pltpu.make_async_remote_copy(
                src_ref=source if uncut else piece(source, c),
                dst_ref=target if uncut else piece(target, c),
                send_sem=send.at[i, c],
                recv_sem=recv.at[i, c],
                device_id={"tensor": to},
                device_id_type=MESH,
            )
            for i, (source, target) in enumerate(zip(sources, targets))
            if (i >= cut) == uncut
        ]

    def each(sources, targets, c, send, recv, to, act):
        for copy in copies(sources, targets, c, send, recv, to, False):
            act(copy)
        if whole:

            @pl.when(c == 0)
            def _():
                for copy in copies(sources, targets, 0, send, recv, to, True):
                    act(copy)

    def start(sources, targets, c, send, recv, to):
        each(sources, targets, c, send, recv, to, lambda copy: copy.start())

    def arrived(targets, c, send, recv):
        each(targets, targets, c, send, recv, me, lambda copy: copy.wait_recv())

    def add(c, terms, targets):
        for i, target in enumerate(targets):
            if i < cut:
                piece(target, c)[...] = functools.reduce(
                    jnp.add, [piece(term[i], c)[...] for term in terms]
                )
            else:

                @pl.when(c == 0)
                def _():
                    target[...] = functools.reduce(jnp.add, [term[i][...] for term in terms])

    def reduce_step(c):
        for side, inner, held, recv, to in (
            (me < root, has_low, lows, low_recv, me + 1),
            (me > root, has_high, highs, high_recv, me - 1),
        ):

            @pl.when(side & inner)
            def _():
                arrived(held, c, up_send, recv)
                add(c, (held, xs), held)
                start(held, held, c, up_send, recv, to)

            @pl.when(side & jnp.logical_not(inner))
            def _():
                start(xs, held, c, up_send, recv, to)

        @pl.when(me == root)
        def _():
            arrived(lows, c, up_send, low_recv)
            if root < n - 1:
                arrived(highs, c, up_send, high_recv)
            add(c, (xs, lows, highs) if root < n - 1 else (xs, lows), outs)
            start(outs, outs, c, low_send, total_recv, me - 1)
            if root < n - 1:
                start(outs, outs, c, high_send, total_recv, me + 1)
            if done is not None:
                done(c)

    def total_step(c):
        @pl.when(me != root)
        def _():
            arrived(outs, c, low_send, total_recv)

        @pl.when((me < root) & has_low)
        def _():
            start(outs, outs, c, low_send, total_recv, me - 1)

        @pl.when((me > root) & has_high)
        def _():
            start(outs, outs, c, high_send, total_recv, me + 1)

        if done is not None:

            @pl.when(me != root)
            def _():
                done(c)

    lag = jnp.where(has_low & has_high, LAG, STEPS)

    def step(t, carry):
        @pl.when(t < STEPS)
        def _():
            reduce_step(t)

        @pl.when((t >= lag) & (t - lag < STEPS))
        def _():
            total_step(t - lag)

        return carry

    def finish():
        def drain(c, carry):
            for condition, send in (
                (me != root, up_send),
                ((me <= root) & has_low, low_send),
                ((me >= root) & has_high, high_send),
            ):

                @pl.when(condition)
                def _():
                    each(xs, lows, c, send, low_recv, me, lambda copy: copy.wait_send())

            return carry

        lax.fori_loop(0, STEPS, drain, 0)

    return begin, step, finish


def line_scratch(arrays):
    return [pltpu.VMEM(array.shape, jnp.float32) for array in arrays * 2] + [
        pltpu.SemaphoreType.DMA((len(arrays), STEPS))
    ] * 6


def expert_kernel(
    parts,
    first,
    numbers,
    chained,
    count_ref,
    place_ref,
    gate_ref,
    normed_ref,
    grad_ref,
    gate_w,
    up_w,
    down_w,
    *refs,
):
    if chained:
        moe_in, back_in, early_in = refs[:3]
        refs = refs[3:]
    grads_out, refs = refs[: len(numbers)], refs[len(numbers) :]
    moe_out, back_out, gates_out = refs[:3]
    rows_ref, grads_ref, active_ref, gate_in_ref, up_in_ref, weights_ref, sems, out_sems = refs[3:]
    expert = pl.program_id(0)
    filled = count_ref[first + expert]
    length, width = normed_ref.shape
    hidden_size = gate_w.shape[2]
    sizes = (128, 256, CAP)

    def by_size(run):
        low = None
        for rows in sizes:
            fits = filled <= rows if low is None else filled > low
            if low is not None and rows != sizes[-1]:
                fits = fits & (filled <= rows)
            pl.when(fits)(functools.partial(run, rows))
            low = rows

    if chained:
        copy_moe = pltpu.make_async_copy(moe_in, moe_out, sems.at[0])
        copy_back = pltpu.make_async_copy(back_in, back_out, sems.at[1])
        early = early_in.shape[0]
        copy_early = pltpu.make_async_copy(early_in, grads_out[0].at[:early], sems.at[2])

        @pl.when(expert == 0)
        def _():
            copy_moe.start()
            copy_back.start()
            copy_early.start()

    else:

        @pl.when(expert == 0)
        def _():
            moe_out[...] = jnp.zeros_like(moe_out)
            back_out[...] = jnp.zeros_like(back_out)

    def slots(rows):
        mask = lax.broadcasted_iota(jnp.int32, (rows, length), 0) == place_ref[0]
        return mask, jnp.where(mask, 1.0, 0.0).astype(jnp.bfloat16)

    def enter(rows):
        mask, picks = slots(rows)
        rows_in = jnp.dot(picks, normed_ref[...], preferred_element_type=jnp.float32).astype(jnp.bfloat16)
        grad_rows = (
            RESIDUAL * jnp.dot(picks, grad_ref[...], preferred_element_type=jnp.float32)
        ).astype(jnp.bfloat16)
        rows_ref[:rows] = rows_in
        grads_ref[:rows] = grad_rows
        gate = jnp.sum(jnp.where(mask, gate_ref[0], 0.0), axis=1, keepdims=True)
        gate_input = jnp.dot(rows_in, gate_w[0], preferred_element_type=jnp.float32)
        up_input = jnp.dot(rows_in, up_w[0], preferred_element_type=jnp.float32)
        grad_act = right_inner(grad_rows, down_w[0])
        sigmoid_val = jax.nn.sigmoid(gate_input)
        silu_out = gate_input * sigmoid_val
        hidden = silu_out * up_input
        active_ref[:rows] = (hidden * gate).astype(jnp.bfloat16)
        column = jnp.sum(grad_act * hidden, axis=1, keepdims=True)
        gates_out[0] = jnp.sum(jnp.where(mask, column, 0.0), axis=0, keepdims=True)
        grad_hidden = grad_act * gate
        gate_in_ref[:rows] = (
            grad_hidden * up_input * sigmoid_val * (1.0 + gate_input * (1.0 - sigmoid_val))
        ).astype(jnp.bfloat16)
        up_in_ref[:rows] = (grad_hidden * silu_out).astype(jnp.bfloat16)

    by_size(enter)
    if chained:

        @pl.when(expert == 0)
        def _():
            copy_moe.wait()
            copy_back.wait()
            copy_early.wait()

    def leave(rows):
        column = jnp.transpose(jnp.broadcast_to(place_ref[0], (128, length)))
        column = jnp.concatenate([column] * (rows // 128), 1)
        own = lax.broadcasted_iota(jnp.int32, (length, rows), 1)
        picks = jnp.where(own == column, 1.0, 0.0).astype(jnp.bfloat16)
        moe = jnp.dot(active_ref[:rows], down_w[0], preferred_element_type=jnp.float32)
        moe_out[...] += jnp.dot(
            picks, moe.astype(jnp.bfloat16), preferred_element_type=jnp.float32
        )
        back = right_inner(gate_in_ref[:rows], gate_w[0]) + right_inner(up_in_ref[:rows], up_w[0])
        back_out[...] += jnp.dot(
            picks, back.astype(jnp.bfloat16), preferred_element_type=jnp.float32
        )

    by_size(leave)

    def copy_out(target, at, kind):
        return pltpu.make_async_copy(weights_ref.at[kind], target.at[at], out_sems.at[kind])

    @pl.when(expert > 0)
    def _():
        for kind in range(3):
            copy_out(grads_out[0], 0, kind).wait()

    def weigh(rows):
        grads = left_inner(
            rows_ref[:rows], jnp.concatenate([gate_in_ref[:rows], up_in_ref[:rows]], 1)
        )
        weights_ref[0] = grads[:, :hidden_size]
        weights_ref[1] = grads[:, hidden_size:]
        grad_down = left_inner(active_ref[:rows], grads_ref[:rows])
        own = hidden_size // parts
        blocks = width // hidden_size
        for part in range(parts):
            for piece in range(blocks):
                at = (part * blocks + piece) * own
                weights_ref[2, at : at + own, :] = grad_down[
                    part * own : (part + 1) * own, piece * hidden_size : (piece + 1) * hidden_size
                ]

    by_size(weigh)
    for kind in range(3):
        start = -early_in.shape[0] if chained else 0
        for target, number in zip(grads_out, numbers):
            at = 3 * expert + kind - start

            @pl.when((at >= 0) & (at < number))
            def _():
                copy_out(target, at, kind).start()

            start += number

    @pl.when(expert == pl.num_programs(0) - 1)
    def _():
        for kind in range(3):
            copy_out(grads_out[0], 0, kind).wait()


def expert_stage(parts, first, number, numbers, counts, places, gate_rows, normed_b, grad_b, gate_w, up_w, down_w, sums):
    length, width = normed_b.shape
    hidden = gate_w.shape[2]
    experts = places.shape[0]
    chained = sums is not None
    whole = lambda e, c: (0, 0)
    row_spec = pl.BlockSpec((1, 1, length), lambda e, c: (first + e, 0, 0))
    once = pl.Buffered(1)
    f32, bf16 = jnp.float32, jnp.bfloat16
    in_specs = [
        row_spec,
        row_spec,
        pl.BlockSpec((length, width), whole, pipeline_mode=once),
        pl.BlockSpec((length, width), whole, pipeline_mode=once),
        pl.BlockSpec((1, width, hidden), lambda e, c: (first + e, 0, 0)),
        pl.BlockSpec((1, width, hidden), lambda e, c: (first + e, 0, 0)),
        pl.BlockSpec((1, hidden, width), lambda e, c: (first + e, 0, 0)),
    ]
    args = [
        counts,
        places.reshape(experts, 1, length),
        gate_rows.reshape(experts, 1, length),
        normed_b,
        grad_b,
        gate_w,
        up_w,
        down_w,
    ]
    if chained:
        in_specs += [pl.BlockSpec(memory_space=pl.ANY)] * 3
        args += list(sums)
    results = pl.pallas_call(
        functools.partial(expert_kernel, parts, first, numbers, chained),
        out_shape=[jax.ShapeDtypeStruct((some, width, hidden), f32) for some in numbers]
        + [
            jax.ShapeDtypeStruct((length, width), f32),
            jax.ShapeDtypeStruct((length, width), f32),
            jax.ShapeDtypeStruct((number, 1, length), f32),
        ],
        grid_spec=pltpu.PrefetchScalarGridSpec(
            num_scalar_prefetch=1,
            grid=(number,),
            in_specs=in_specs,
            out_specs=[pl.BlockSpec(memory_space=pl.ANY)] * len(numbers)
            + [
                pl.BlockSpec((length, width), whole, pipeline_mode=once),
                pl.BlockSpec((length, width), whole, pipeline_mode=once),
                pl.BlockSpec((1, 1, length), lambda e, c: (e, 0, 0)),
            ],
            scratch_shapes=[
                pltpu.VMEM((CAP, width), bf16),
                pltpu.VMEM((CAP, width), bf16),
                pltpu.VMEM((CAP, hidden), bf16),
                pltpu.VMEM((CAP, hidden), bf16),
                pltpu.VMEM((CAP, hidden), bf16),
                pltpu.VMEM((3, width, hidden), f32),
                pltpu.SemaphoreType.DMA((3,)),
                pltpu.SemaphoreType.DMA((3,)),
            ],
        ),
        compiler_params=pltpu.CompilerParams(
            dimension_semantics=("arbitrary",), vmem_limit_bytes=63 << 20
        ),
        cost_estimate=pl.CostEstimate(
            flops=number * 8 * 10**9, bytes_accessed=number * 14 * 10**6, transcendentals=0
        ),
    )(*args)
    return results[: len(numbers)], results[len(numbers) :]


PIECES = 16


def line_gather_kernel(n, x_ref, out_ref, blocks_ref, recv, up_send, down_send):
    me = lax.axis_index("tensor")
    has_low, has_high = me > 0, me < n - 1
    barrier = pltpu.get_barrier_semaphore()

    @pl.when(has_low)
    def _():
        pl.semaphore_signal(barrier, inc=1, device_id={"tensor": me - 1}, device_id_type=MESH)

    @pl.when(has_high)
    def _():
        pl.semaphore_signal(barrier, inc=1, device_id={"tensor": me + 1}, device_id_type=MESH)

    blocks_ref[me] = x_ref[...].astype(jnp.float32)
    pl.semaphore_wait(barrier, has_low.astype(jnp.int32) + has_high.astype(jnp.int32))
    rows = x_ref.shape[0] // PIECES

    def copy(block, c, send, to):
        piece = blocks_ref.at[block, pl.ds(pl.multiple_of(c * rows, rows), rows), :]
        return pltpu.make_async_remote_copy(
            src_ref=piece,
            dst_ref=piece,
            send_sem=send.at[block, c],
            recv_sem=recv.at[block, c],
            device_id={"tensor": to},
            device_id_type=MESH,
        )

    for hop in range(n):
        low, high = me - hop, me + hop

        def step(c, carry):
            @pl.when(low >= 0)
            def _():
                if hop > 0:
                    copy(low, c, up_send, me).wait_recv()

                @pl.when(has_high)
                def _():
                    copy(low, c, up_send, me + 1).start()

            @pl.when(high < n)
            def _():
                if hop > 0:
                    copy(high, c, down_send, me).wait_recv()

                @pl.when(has_low)
                def _():
                    copy(high, c, down_send, me - 1).start()

            return carry

        lax.fori_loop(0, PIECES, step, 0)
    wide = x_ref.shape[1]
    for block in range(n):
        out_ref[:, block * wide : (block + 1) * wide] = blocks_ref[block].astype(jnp.bfloat16)
    for hop in range(n):
        low, high = me - hop, me + hop

        def drain(c, carry):
            @pl.when((low >= 0) & has_high)
            def _():
                copy(low, c, up_send, me).wait_send()

            @pl.when((high < n) & has_low)
            def _():
                copy(high, c, down_send, me).wait_send()

            return carry

        lax.fori_loop(0, PIECES, drain, 0)


def line_gather(x, n, name):
    length, wide = x.shape
    full = pl.BlockSpec(memory_space=pltpu.VMEM)
    return pl.pallas_call(
        functools.partial(line_gather_kernel, n),
        out_shape=jax.ShapeDtypeStruct((length, n * wide), jnp.bfloat16),
        in_specs=[full],
        out_specs=full,
        scratch_shapes=[pltpu.VMEM((n, length, wide), jnp.float32)]
        + [pltpu.SemaphoreType.DMA((n, PIECES))] * 3,
        compiler_params=pltpu.CompilerParams(
            collective_id=name, has_side_effects=True, vmem_limit_bytes=32 << 20
        ),
        cost_estimate=pl.CostEstimate(
            flops=0, bytes_accessed=16 * n * x.size, transcendentals=0
        ),
    )(x)


BLOCK = 256


def own_rows_kernel(parts, weight_ref, out_ref):
    rows = out_ref.shape[0]
    first = lax.axis_index("dp") * rows if parts > 1 else 0
    out_ref[...] = weight_ref[pl.ds(pl.multiple_of(first, 16), rows), :].astype(jnp.float32)


def gather_out_weight(out_weight, parts):
    rows, width = out_weight.shape
    ways = parts if rows % (16 * parts) == 0 else 1
    full = pl.BlockSpec(memory_space=pltpu.VMEM)
    own = pl.pallas_call(
        functools.partial(own_rows_kernel, ways),
        out_shape=jax.ShapeDtypeStruct((rows // ways, width), jnp.float32),
        in_specs=[full],
        out_specs=full,
    )(out_weight)
    return ways, lax.all_gather(own, "tensor")


def middle_kernel(
    attended_ref, weight_all_ref, tokens_ref, gain_ref, router_ref, chosen_ref, middle_out, normed_out, gates_out, weight_ref
):
    ways, n, rows, unused = weight_all_ref.shape

    @pl.when(pl.program_id(0) == 0)
    def _():
        for way in range(ways):
            for block in range(n):
                at = (block * ways + way) * rows
                weight_ref[at : at + rows, :] = weight_all_ref[way, block].astype(jnp.bfloat16)

    branch = jnp.dot(attended_ref[...], weight_ref[...], preferred_element_type=jnp.float32)
    middle = tokens_ref[...].astype(jnp.float32) + RESIDUAL * branch
    middle_out[...] = middle
    recip = lax.rsqrt(jnp.mean(middle * middle, axis=1, keepdims=True) + EPSILON)
    normed = (middle * recip * gain_ref[...]).astype(jnp.bfloat16)
    normed_out[...] = normed
    logits = jnp.dot(normed, router_ref[...], preferred_element_type=jnp.float32)
    raised = jnp.where(chosen_ref[...] > 0.0, jnp.exp(logits), 0.0)
    gates_out[...] = raised / jnp.sum(raised, axis=1, keepdims=True)


def enter_middle(attended, weight_all, tokens, gain, router, chosen):
    length, width = tokens.shape
    rows = lambda columns: pl.BlockSpec((BLOCK, columns), lambda i: (i, 0))
    whole = lambda shape: pl.BlockSpec(
        shape, lambda i: (0,) * len(shape), pipeline_mode=pl.Buffered(1)
    )
    experts = router.shape[1]
    return pl.pallas_call(
        middle_kernel,
        out_shape=[
            jax.ShapeDtypeStruct((length, width), jnp.float32),
            jax.ShapeDtypeStruct((length, width), jnp.bfloat16),
            jax.ShapeDtypeStruct((length, experts), jnp.float32),
        ],
        grid=(length // BLOCK,),
        in_specs=[
            rows(attended.shape[1]),
            whole(weight_all.shape),
            rows(width),
            whole((1, width)),
            whole(router.shape),
            rows(experts),
        ],
        out_specs=[rows(width), rows(width), rows(experts)],
        scratch_shapes=[pltpu.VMEM((attended.shape[1], width), jnp.bfloat16)],
        compiler_params=pltpu.CompilerParams(
            dimension_semantics=("arbitrary",), vmem_limit_bytes=48 << 20
        ),
        cost_estimate=pl.CostEstimate(
            flops=2 * length * width * width, bytes_accessed=25 * 10**6, transcendentals=0
        ),
    )(attended, weight_all, tokens, gain.reshape(1, width), router, chosen)


def turn_kernel(
    n,
    part_ref,
    gates_part_ref,
    gates_ref,
    middle_ref,
    cotangent_ref,
    gain_ref,
    router_ref,
    grad_out,
    branch_out,
    logits_out,
    gain_out,
    summed_ref,
    gates_rows_ref,
    grad_gates_ref,
    *line,
):
    length = part_ref.shape[0]
    rows = length // STEPS

    def done(c):
        @pl.when(c == 0)
        def _():
            experts = gates_rows_ref.shape[0]
            empty = jnp.zeros((grad_gates_ref.shape[1] - experts, length), jnp.float32)
            grad_gates_ref[...] = jnp.transpose(
                jnp.concatenate([gates_rows_ref[...], empty], 0)
            )

        own = pl.ds(pl.multiple_of(c * rows, rows), rows)
        gates, grad_gates = gates_ref[own, :], grad_gates_ref[own, :]
        weighted = jnp.sum(gates * grad_gates, axis=1, keepdims=True)
        grad_logits = (gates * (grad_gates - weighted)).astype(jnp.bfloat16)
        logits_out[own, :] = grad_logits
        grad = summed_ref[own, :] + right_inner(grad_logits, router_ref[...])
        middle = middle_ref[own, :]
        recip = lax.rsqrt(jnp.mean(middle * middle, axis=1, keepdims=True) + EPSILON)
        unit = middle * recip
        gain_out[...] += jnp.sum(grad * unit, axis=0, keepdims=True)
        scaled = grad * gain_ref[...]
        back = recip * (scaled - unit * jnp.mean(scaled * unit, axis=1, keepdims=True))
        total = cotangent_ref[own, :].astype(jnp.float32) + back
        grad_out[own, :] = total
        branch_out[own, :] = (RESIDUAL * total).astype(jnp.bfloat16)

    begin, step, finish = line_stages(
        n, [part_ref, gates_part_ref], [summed_ref, gates_rows_ref], line, done, 1
    )
    begin()
    gain_out[...] = jnp.zeros_like(gain_out)
    lax.fori_loop(0, 2 * STEPS, step, 0)
    finish()


def turn_middle(n, part, gates_part, gates, middle, cotangent, gain, router, name):
    length, width = part.shape
    full = pl.BlockSpec(memory_space=pltpu.VMEM)
    f32 = jnp.float32
    return pl.pallas_call(
        functools.partial(turn_kernel, n),
        out_shape=[
            jax.ShapeDtypeStruct((length, width), f32),
            jax.ShapeDtypeStruct((length, width), jnp.bfloat16),
            jax.ShapeDtypeStruct(gates.shape, jnp.bfloat16),
            jax.ShapeDtypeStruct((1, width), f32),
        ],
        in_specs=[full] * 7,
        out_specs=[full] * 4,
        scratch_shapes=[
            pltpu.VMEM(part.shape, f32),
            pltpu.VMEM(gates_part.shape, f32),
            pltpu.VMEM(gates.shape, f32),
        ]
        + line_scratch([part, gates_part]),
        compiler_params=pltpu.CompilerParams(
            collective_id=name, has_side_effects=True, vmem_limit_bytes=58 << 20
        ),
        cost_estimate=pl.CostEstimate(
            flops=40 * length * width, bytes_accessed=60 * 10**6, transcendentals=0
        ),
    )(part, gates_part, gates, middle, cotangent, gain.reshape(1, width), router)


def last_kernel(count, summed_ref, tokens_ref, middle_ref, gain_ref, *refs):
    smalls, out_ref, small_outs = refs[:count], refs[count], refs[count + 1 :]
    hidden = tokens_ref[...].astype(jnp.float32)
    recip = lax.rsqrt(jnp.mean(hidden * hidden, axis=1, keepdims=True) + EPSILON)
    unit = hidden * recip
    scaled = summed_ref[...] * gain_ref[...]
    inner = jnp.mean(scaled * unit, axis=1, keepdims=True)
    out_ref[...] = middle_ref[...] + recip * (scaled - unit * inner)

    @pl.when(pl.program_id(0) == 0)
    def _():
        for small, out in zip(smalls, small_outs):
            out[...] = small[...]


def leave_first(summed, tokens, grad_middle, gain, smalls):
    length, width = tokens.shape
    rows = pl.BlockSpec((BLOCK // 2, width), lambda i: (i, 0))
    whole = lambda shape: pl.BlockSpec(shape, lambda i: (0, 0))
    f32 = jnp.float32
    return pl.pallas_call(
        functools.partial(last_kernel, len(smalls)),
        out_shape=[jax.ShapeDtypeStruct((length, width), f32)]
        + [jax.ShapeDtypeStruct(small.shape, f32) for small in smalls],
        grid=(2 * length // BLOCK,),
        in_specs=[rows, rows, rows, whole((1, width))] + [whole(small.shape) for small in smalls],
        out_specs=[rows] + [whole(small.shape) for small in smalls],
        compiler_params=pltpu.CompilerParams(vmem_limit_bytes=60 << 20),
        cost_estimate=pl.CostEstimate(
            flops=10 * length * width, bytes_accessed=14 * length * width, transcendentals=0
        ),
    )(summed, tokens, grad_middle, gain.reshape(1, width), *smalls)


SPAN = 768
ROWS = 256


def lane_halves(shape):
    return lax.broadcasted_iota(jnp.int32, shape, len(shape) - 1) // HEAD


def select_halves(tile, source, half):
    kept = jnp.where(lane_halves(tile.shape) == source, tile, 0.0)
    return kept if source == half else pltpu.roll(kept, HEAD, 1)


def spread_pairs(tile, target):
    for source in range(2):
        for half in range(2):
            target[2 * source + half] = select_halves(tile, source, half).astype(jnp.bfloat16)


def rope_tile(tile, cosine, sine_low, sine_high):
    return tile * cosine + pltpu.roll(tile, 128 - HEAD // 2, 1) * sine_low + pltpu.roll(
        tile, HEAD // 2, 1
    ) * sine_high


def rope_back_tile(tile, cosine, sine_low, sine_high):
    return (
        tile * cosine
        + pltpu.roll(tile * sine_low, HEAD // 2, 1)
        + pltpu.roll(tile * sine_high, 128 - HEAD // 2, 1)
    )


def window(block):
    first = block * ROWS
    return first, jnp.maximum(first + ROWS - SPAN, 0)


def attend_forward_kernel(
    heads,
    group,
    tokens_ref,
    gain_ref,
    query_w,
    key_w,
    value_w,
    cosine_ref,
    sine_low_ref,
    sine_high_ref,
    opening_ref,
    normed_out,
    query_out,
    key_out,
    value_out,
    attended_out,
    logsum_out,
    key_pairs,
    value_pairs,
    tiles_ref,
):
    tiles, length, unused = query_out.shape
    hidden = tokens_ref[...].astype(jnp.float32)
    recip = lax.rsqrt(jnp.mean(hidden * hidden, axis=1, keepdims=True) + EPSILON)
    normed_out[...] = (hidden * recip * gain_ref[...]).astype(jnp.bfloat16)
    cosine, sine_low, sine_high = cosine_ref[...], sine_low_ref[...], sine_high_ref[...]
    for tile in range(tiles):
        query = jnp.dot(
            normed_out[...],
            query_w[:, tile * 128 : (tile + 1) * 128],
            preferred_element_type=jnp.float32,
        )
        query_out[tile] = rope_tile(query, cosine, sine_low, sine_high).astype(jnp.bfloat16)
    key = rope_tile(
        jnp.dot(normed_out[...], key_w[...], preferred_element_type=jnp.float32),
        cosine,
        sine_low,
        sine_high,
    )
    value = jnp.dot(normed_out[...], value_w[...], preferred_element_type=jnp.float32)
    key_out[...] = key.astype(jnp.bfloat16)
    value_out[...] = value.astype(jnp.bfloat16)
    spread_pairs(key, key_pairs)
    spread_pairs(value, value_pairs)
    blocks = length // ROWS
    tiles_ref[...] = jnp.zeros_like(tiles_ref)

    def unit(step, carry):
        head, block = step // blocks, step % blocks
        tile, half = head // 2, head % 2
        pair = 2 * (head // group) + half
        first, low = window(block)
        rows = pl.ds(pl.multiple_of(first, ROWS), ROWS)
        span = pl.ds(pl.multiple_of(low, ROWS), SPAN)
        scores = right_inner(query_out[tile, rows, :], key_pairs[pair, span, :])
        columns = low + lax.broadcasted_iota(jnp.int32, (ROWS, SPAN), 1)
        own = first + lax.broadcasted_iota(jnp.int32, (ROWS, SPAN), 0)
        allowed = (columns >= opening_ref[rows, :]) & (columns <= own)
        raised = jnp.where(allowed, jnp.exp(ATTN_SCALE * scores), 0.0)
        total = jnp.sum(raised, axis=1, keepdims=True)
        product = jnp.dot(
            raised.astype(jnp.bfloat16), value_pairs[pair, span, :], preferred_element_type=jnp.float32
        )
        tiles_ref[tile, rows, :] += product / total
        wide = jnp.broadcast_to(jnp.log(total), (ROWS, 128))
        logsum_out[head, :, rows] = jnp.transpose(wide)[:1]
        return carry

    lax.fori_loop(0, heads * blocks, unit, 0)
    for tile in range(tiles):
        attended_out[:, tile * 128 : (tile + 1) * 128] = tiles_ref[tile].astype(jnp.bfloat16)


def attend_forward(tokens, gain, query_w, key_w, value_w, tables, opening, heads, group):
    length, width = tokens.shape
    wide = query_w.shape[1]
    tiles = wide // 128
    bf16, f32 = jnp.bfloat16, jnp.float32
    full = pl.BlockSpec(memory_space=pltpu.VMEM)
    return pl.pallas_call(
        functools.partial(attend_forward_kernel, heads, group),
        out_shape=[
            jax.ShapeDtypeStruct((length, width), bf16),
            jax.ShapeDtypeStruct((tiles, length, 128), bf16),
            jax.ShapeDtypeStruct((length, 128), bf16),
            jax.ShapeDtypeStruct((length, 128), bf16),
            jax.ShapeDtypeStruct((length, wide), bf16),
            jax.ShapeDtypeStruct((heads, 1, length), f32),
        ],
        in_specs=[full] * 9,
        out_specs=[full] * 6,
        scratch_shapes=[
            pltpu.VMEM((4, length, 128), bf16),
            pltpu.VMEM((4, length, 128), bf16),
            pltpu.VMEM((tiles, length, 128), f32),
        ],
        compiler_params=pltpu.CompilerParams(vmem_limit_bytes=48 << 20),
        cost_estimate=pl.CostEstimate(
            flops=8 * 10**9, bytes_accessed=12 * 10**6, transcendentals=5 * 10**6
        ),
    )(tokens, gain.reshape(1, width), query_w, key_w, value_w, *tables, opening.reshape(length, 1))


def attend_backward_kernel(
    n,
    heads,
    group,
    branch_ref,
    out_w,
    query_ref,
    key_ref,
    value_ref,
    attended_ref,
    logsum_ref,
    query_w,
    key_w,
    value_w,
    cosine_ref,
    sine_low_ref,
    sine_high_ref,
    opening_ref,
    tokens_ref,
    moe_ref,
    middle_ref,
    grads_out,
    normed_out,
    gain_out,
    output_ref,
    moe_sum,
    middle_rows,
    middle_sems,
    key_pairs,
    value_pairs,
    attend_grads,
    query_grads,
    key_grads,
    value_grads,
    delta_ref,
    *line,
):
    tiles, length, unused = query_ref.shape
    share = length // STEPS

    def share_rows(c):
        return pl.ds(pl.multiple_of(c * share, share), share)

    def fetch(c):
        slot = lax.rem(c, 2)
        return pltpu.make_async_copy(
            middle_ref.at[share_rows(c), :], middle_rows.at[slot], middle_sems.at[slot]
        )

    def done(c):
        fetch(c).wait()

        @pl.when(c + 1 < STEPS)
        def _():
            fetch(c + 1).start()

        total = middle_rows[lax.rem(c, 2)] + RESIDUAL * moe_sum[share_rows(c), :]
        output_ref[share_rows(c), :] = total.astype(jnp.bfloat16)

    line_start, line_step, line_end = line_stages(n, [moe_ref], [moe_sum], line, done)
    line_start()
    fetch(jnp.int32(0)).start()
    blocks = length // ROWS
    units = heads * blocks
    taken = 0

    def run_line(steps):
        nonlocal taken
        until = min(taken + steps, 2 * STEPS)
        lax.fori_loop(taken, until, line_step, 0)
        taken = until

    run_line(2)
    spread_pairs(key_ref[...].astype(jnp.float32), key_pairs)
    spread_pairs(value_ref[...].astype(jnp.float32), value_pairs)
    halves = (
        lax.broadcasted_iota(jnp.int32, (8, 128), 0) == lane_halves((8, 128))
    ).astype(jnp.float32)
    for tile in range(tiles):
        lanes = slice(tile * 128, (tile + 1) * 128)
        grad = right_inner(branch_ref[...], out_w[lanes, :]).astype(jnp.bfloat16)
        attend_grads[tile] = grad
        products = grad.astype(jnp.float32) * attended_ref[:, lanes].astype(jnp.float32)
        sums = lax.dot_general(
            halves,
            products,
            (((1,), (1,)), ((), ())),
            precision=lax.Precision.HIGHEST,
            preferred_element_type=jnp.float32,
        )
        delta_ref[2 * tile] = sums[0:1]
        delta_ref[2 * tile + 1] = sums[1:2]
        run_line(2)
    query_grads[...] = jnp.zeros_like(query_grads)
    key_grads[...] = jnp.zeros_like(key_grads)
    value_grads[...] = jnp.zeros_like(value_grads)
    before, each = taken, (2 * STEPS - 8 - taken) // units
    taken += units * each

    def unit(step, carry):
        lax.fori_loop(before + step * each, before + step * each + each, line_step, 0)
        head, block = step // blocks, step % blocks
        tile, half = head // 2, head % 2
        pair = 2 * (head // group) + half
        first, low = window(block)
        rows = pl.ds(pl.multiple_of(first, ROWS), ROWS)
        span = pl.ds(pl.multiple_of(low, ROWS), SPAN)
        keys = key_pairs[pair, span, :]
        query = query_ref[tile, rows, :]
        grad = attend_grads[tile, rows, :]
        scores = right_inner(keys, query)
        columns = low + lax.broadcasted_iota(jnp.int32, (SPAN, ROWS), 0)
        own = first + lax.broadcasted_iota(jnp.int32, (SPAN, ROWS), 1)
        allowed = (columns >= opening_ref[:, rows]) & (columns <= own)
        probs = jnp.where(
            allowed, jnp.exp(ATTN_SCALE * scores - logsum_ref[head, :, rows]), 0.0
        )
        grad_probs = right_inner(value_pairs[pair, span, :], grad)
        grad_scores = (probs * (grad_probs - delta_ref[head, :, rows])).astype(jnp.bfloat16)
        value_grads[pair, span, :] += jnp.dot(
            probs.astype(jnp.bfloat16), grad, preferred_element_type=jnp.float32
        )
        key_grads[pair, span, :] += jnp.dot(
            grad_scores, query, preferred_element_type=jnp.float32
        )
        query_grads[tile, rows, :] += left_inner(grad_scores, keys)
        return carry

    lax.fori_loop(0, units, unit, 0)
    cosine, sine_low, sine_high = cosine_ref[...], sine_low_ref[...], sine_high_ref[...]
    wide = tiles * 128
    for tile in range(tiles):
        grads_out[:, tile * 128 : (tile + 1) * 128] = rope_back_tile(
            ATTN_SCALE * query_grads[tile], cosine, sine_low, sine_high
        ).astype(jnp.bfloat16)
    totals = []
    for grads in (key_grads, value_grads):
        totals.append(
            sum(
                select_halves(grads[2 * source + half], half, source)
                for source in range(2)
                for half in range(2)
            )
        )
    grads_out[:, wide : wide + 128] = rope_back_tile(
        ATTN_SCALE * totals[0], cosine, sine_low, sine_high
    ).astype(jnp.bfloat16)
    grads_out[:, wide + 128 : wide + 256] = totals[1].astype(jnp.bfloat16)
    gain_sum = jnp.zeros((1, normed_out.shape[1]), jnp.float32)
    for block in range(blocks):
        rows = slice(block * ROWS, (block + 1) * ROWS)
        normed = (
            right_inner(grads_out[rows, :wide], query_w[...])
            + right_inner(grads_out[rows, wide : wide + 128], key_w[...])
            + right_inner(grads_out[rows, wide + 128 :], value_w[...])
        )
        normed_out[rows, :] = normed
        hidden = tokens_ref[rows, :].astype(jnp.float32)
        recip = lax.rsqrt(jnp.mean(hidden * hidden, axis=1, keepdims=True) + EPSILON)
        gain_sum += jnp.sum(normed * (hidden * recip), axis=0, keepdims=True)
        run_line(2)
    gain_out[...] = jnp.broadcast_to(gain_sum, gain_out.shape)
    run_line(2 * STEPS)
    line_end()


def attend_backward(
    n, branch, out_w, query, key, value, attended, logsum, query_w, key_w, value_w, tables, opening, tokens, moe, middle,
    heads, group, name,
):
    length, width = branch.shape
    tiles = query.shape[0]
    wide = tiles * 128
    bf16, f32 = jnp.bfloat16, jnp.float32
    full = pl.BlockSpec(memory_space=pltpu.VMEM)
    return pl.pallas_call(
        functools.partial(attend_backward_kernel, n, heads, group),
        out_shape=[
            jax.ShapeDtypeStruct((length, wide + 256), bf16),
            jax.ShapeDtypeStruct((length, width), f32),
            jax.ShapeDtypeStruct((8, width), f32),
            jax.ShapeDtypeStruct((length, width), bf16),
        ],
        in_specs=[full] * 16 + [pl.BlockSpec(memory_space=pl.ANY)],
        out_specs=[full] * 4,
        scratch_shapes=[
            pltpu.VMEM((length, width), f32),
            pltpu.VMEM((2, length // STEPS, width), f32),
            pltpu.SemaphoreType.DMA((2,)),
            pltpu.VMEM((4, length, 128), bf16),
            pltpu.VMEM((4, length, 128), bf16),
            pltpu.VMEM((tiles, length, 128), bf16),
            pltpu.VMEM((tiles, length, 128), f32),
            pltpu.VMEM((4, length, 128), f32),
            pltpu.VMEM((4, length, 128), f32),
            pltpu.VMEM((2 * tiles, 1, length), f32),
        ]
        + line_scratch([moe]),
        compiler_params=pltpu.CompilerParams(
            collective_id=name, has_side_effects=True, vmem_limit_bytes=63 << 20
        ),
        cost_estimate=pl.CostEstimate(
            flops=12 * 10**9, bytes_accessed=30 * 10**6, transcendentals=5 * 10**6
        ),
    )(
        branch, out_w, query, key, value, attended, logsum, query_w, key_w, value_w, *tables,
        opening.reshape(1, length), tokens, moe, middle,
    )


def finish_kernel(
    n,
    parts,
    local_ref,
    normed_ref,
    grads_ref,
    branch_ref,
    attended_ref,
    normed_two_ref,
    logits_ref,
    gain_ref,
    first_gain_ref,
    normed_out,
    query_out,
    key_out,
    value_out,
    branch_out,
    router_out,
    gain_out,
    first_gain_out,
    weights_ref,
    gains_ref,
    gain_send,
    gain_recv,
    *scratch,
):
    levels = parts.bit_length() - 1
    held = scratch[:levels]
    sends, recvs = scratch[levels : levels + 2]
    line_start, line_step, line_end = line_stages(n, [local_ref], [normed_out], scratch[levels + 2 :])
    me = lax.axis_index("dp")
    width = normed_ref.shape[1]
    own = width // parts
    wide, attended_wide = grads_ref.shape[1], attended_ref.shape[1]
    mine = lax.axis_index("tensor")
    line_start(
        [{"dp": jnp.bitwise_xor(me, 1 << level)} for level in range(levels)]
        + [{"tensor": lax.rem(mine + ahead, n)} for ahead in range(1, n)]
    )

    def run_line(first, last):
        lax.fori_loop(first, last, line_step, 0)

    gain_copies = [
        pltpu.make_async_remote_copy(
            src_ref=first_gain_ref,
            dst_ref=gains_ref.at[ahead],
            send_sem=gain_send.at[ahead],
            recv_sem=gain_recv.at[ahead],
            device_id={"tensor": lax.rem(mine + ahead, n)},
            device_id_type=MESH,
        )
        for ahead in range(1, n)
    ]
    for copy in gain_copies:
        copy.start()
    run_line(0, 2)
    first_gain = first_gain_ref[:1]
    for ahead, copy in enumerate(gain_copies, 1):
        copy.wait_recv()
        first_gain = first_gain + gains_ref[ahead, :1]
    pieces = 4
    block = width // pieces
    for piece in range(pieces):
        rows = slice(piece * block, (piece + 1) * block)
        weights_ref[rows, :wide] = left_inner(normed_ref[:, rows], grads_ref[...])
        weights_ref[rows, wide : wide + attended_wide] = left_inner(
            branch_ref[:, rows], attended_ref[...]
        )
        gain = jnp.transpose(jnp.broadcast_to(gain_ref[:, rows], (128, block)))
        own_gain = jnp.transpose(jnp.broadcast_to(first_gain[:, rows], (128, block)))
        lanes = lax.broadcasted_iota(jnp.int32, (block, 128), 1)
        weights_ref[rows, wide + attended_wide :] = jnp.where(
            lanes == 127,
            gain,
            jnp.where(
                lanes == 126, own_gain, left_inner(normed_two_ref[:, rows], logits_ref[...])
            ),
        )
        run_line(2 + 2 * piece, 4 + 2 * piece)
    done = 2 + 2 * pieces

    columns = weights_ref.shape[1]
    middle = columns // 256 * 128
    orders = (
        (slice(0, middle), list(range(levels))),
        (slice(middle, columns), [0] + list(range(levels - 1, 0, -1))),
    )

    def shard(number, lanes):
        return weights_ref.at[pl.ds(pl.multiple_of(number * own, own), own), lanes]

    def numbers(order, level, peer):
        fixed = sum(1 << bit for bit in order[: level + 1])
        base = jnp.bitwise_and(peer, fixed)
        free = order[level + 1 :]
        return [
            base + sum(((i >> place) & 1) << bit for place, bit in enumerate(free))
            for i in range(1 << len(free))
        ]

    def copies(level):
        made = []
        for side, (lanes, order) in enumerate(orders):
            peer = jnp.bitwise_xor(me, 1 << order[level])
            for i, number in enumerate(numbers(order, level, peer)):
                made.append(
                    pltpu.make_async_remote_copy(
                        src_ref=shard(number, lanes),
                        dst_ref=held[level].at[i, :, lanes],
                        send_sem=sends.at[side, level, i],
                        recv_sem=recvs.at[side, level, i],
                        device_id={"dp": peer},
                        device_id_type=MESH,
                    )
                )
        return made

    stops = [6] + [42] * (levels > 1) + [4, 0, 0]
    for level in range(levels):
        for copy in copies(level):
            copy.start()
        until = done + stops[level]
        run_line(done, until)
        done = until
        for copy in copies(level):
            copy.wait_recv()
        for lanes, order in orders:
            for i, number in enumerate(numbers(order, level, me)):
                target = shard(number, lanes)
                target[...] += held[level][i, :, lanes]
    everything = slice(0, columns)
    run_line(done, 2 * STEPS)
    kept = shard(me, everything)
    tail = jnp.transpose(kept[:, wide + attended_wide :])
    query_out[...] = kept[:, : query_out.shape[1]]
    key_out[...] = kept[:, wide - 256 : wide - 256 + key_out.shape[1]]
    value_out[...] = kept[:, wide - 128 : wide - 128 + value_out.shape[1]]
    branch_out[...] = kept[:, wide : wide + branch_out.shape[1]]
    router_out[...] = tail[: router_out.shape[0]]
    gain_out[...] = tail[127:]
    first_gain_out[...] = tail[126:127]
    for level in range(levels):
        for copy in copies(level):
            copy.wait_send()
    for copy in gain_copies:
        copy.wait_send()
    line_end()


def finish(
    n, parts, grad_local, normed_b, grads_wide, branch_b, attended, normed_two_b, grad_logits_b, gain_grad, first_gain_grad,
    wide_q, wide_k, experts, name,
):
    length, width = normed_b.shape
    columns = grads_wide.shape[1] + attended.shape[1] + 128
    full = pl.BlockSpec(memory_space=pltpu.VMEM)
    levels = parts.bit_length() - 1
    own = width // parts
    f32 = jnp.float32
    shapes = [(length, width), (own, wide_q), (own, wide_k), (own, wide_k), (own, wide_q)]
    shapes += [(experts, own), (1, own), (1, own)]
    return pl.pallas_call(
        functools.partial(finish_kernel, n, parts),
        out_shape=[jax.ShapeDtypeStruct(shape, f32) for shape in shapes],
        in_specs=[full] * 9,
        out_specs=[full] * 8,
        scratch_shapes=[
            pltpu.VMEM((width, columns), f32),
            pltpu.VMEM((n, 8, width), f32),
            pltpu.SemaphoreType.DMA((n,)),
            pltpu.SemaphoreType.DMA((n,)),
        ]
        + [pltpu.VMEM((parts >> (level + 1), own, columns), f32) for level in range(levels)]
        + [pltpu.SemaphoreType.DMA((2, levels, parts // 2))] * 2
        + line_scratch([grad_local]),
        compiler_params=pltpu.CompilerParams(
            collective_id=name, has_side_effects=True, vmem_limit_bytes=62 << 20
        ),
        cost_estimate=pl.CostEstimate(
            flops=2 * length * width * columns, bytes_accessed=50 * 10**6, transcendentals=0
        ),
    )(
        grad_local, normed_b, grads_wide, branch_b, attended, normed_two_b, grad_logits_b, gain_grad,
        first_gain_grad,
    )


def place_kernel(count, *refs):
    shards, (gate_out, up_out, down_out) = refs[:count], refs[-3:]
    gate, up, down = shards[-3:]
    gate_out[...] = gate[...]
    if count > 3:

        @pl.when(pl.program_id(0) == 0)
        def _():
            gate_out[...] = shards[0][...]

    up_out[...] = up[...]
    rows, hidden = down_out.shape[1], down.shape[2]
    for piece in range(down_out.shape[2] // hidden):
        down_out[0, :, piece * hidden : (piece + 1) * hidden] = down[
            0, piece * rows : (piece + 1) * rows, :
        ]


def place_shards(parts, first_shards, shards, experts, before):
    unused, rows, hidden = first_shards.shape
    shapes = [(experts, rows, hidden), (experts, rows, hidden)]
    shapes += [(experts, hidden // parts, rows * parts)]
    first = 0 if before is None else 1
    spec = lambda shape: pl.BlockSpec((1,) + shape[1:], lambda e: (first + e, 0, 0))
    one = lambda at: pl.BlockSpec((1, rows, hidden), lambda e: (at(e), 0, 0))
    if before is None:
        args = [first_shards] * 3
        in_specs = [one(lambda e: 0), one(lambda e: 1), one(lambda e: 2)]
        aliases = {}
    else:
        args = [first_shards] + [shards] * 3 + list(before)
        in_specs = [one(lambda e: 3), one(lambda e: jnp.maximum(3 * e - 1, 0))]
        in_specs += [one(lambda e: 3 * e), one(lambda e: 3 * e + 1)]
        in_specs += [pl.BlockSpec(memory_space=pl.ANY)] * 3
        aliases = {4: 0, 5: 1, 6: 2}
    return pl.pallas_call(
        functools.partial(place_kernel, 3 if before is None else 4),
        out_shape=[jax.ShapeDtypeStruct(shape, jnp.float32) for shape in shapes],
        grid=(1 if before is None else experts - 1,),
        in_specs=in_specs,
        out_specs=[spec(shape) for shape in shapes],
        input_output_aliases=aliases,
        compiler_params=pltpu.CompilerParams(vmem_limit_bytes=60 << 20),
        cost_estimate=pl.CostEstimate(
            flops=0, bytes_accessed=8 * 3 * rows * hidden * experts, transcendentals=0
        ),
    )(*args)


def on_device(
    ring,
    tokens,
    cotangent,
    segment_ids,
    routes,
    attn_gain,
    query_weight,
    key_weight,
    value_weight,
    out_weight,
    ffn_gain,
    router_weight,
    gate_weight,
    up_weight,
    down_weight,
):
    length = tokens.shape[0]
    width = tokens.shape[1]
    segment = segment_ids[0]
    heads_local = query_weight.shape[1] // HEAD
    kv_local = key_weight.shape[1] // HEAD
    group_size = heads_local // kv_local
    experts_all = router_weight.shape[1]
    experts_local = gate_weight.shape[0]
    parts = lax.axis_size("dp")
    opening = doc_openings(segment)
    tables = rope_tables(opening, HEAD)
    query_w, key_w, value_w = (pad_columns(w) for w in (query_weight, key_weight, value_weight))
    out_w = jnp.transpose(pad_columns(jnp.transpose(out_weight)))
    ways, out_rows = gather_out_weight(out_weight, parts)
    normed_b, queries, keys, values, attended, logsum = attend_forward(
        tokens, attn_gain, query_w, key_w, value_w, tables, opening, heads_local, group_size
    )
    all_ids = jnp.arange(experts_all, dtype=jnp.int32)
    chosen = jnp.sum((routes[:, :, None] == all_ids[None, None, :]).astype(jnp.int32), axis=1) > 0
    first_expert = lax.axis_index("tensor") * experts_local
    local_ids = first_expert + jnp.arange(experts_local, dtype=jnp.int32)
    picked = jnp.sum((routes[None, :, :] == local_ids[:, None, None]).astype(jnp.int32), axis=2)
    places_in = slot_places(picked)
    counts = jnp.sum(picked, axis=1)
    out_rows, attended = lax.optimization_barrier((out_rows, attended))
    out_all = lax.all_gather(out_rows, "dp") if ways > 1 else out_rows[None]
    attended_all = line_gather(attended, ring, 1)
    attended_all = attended_all.reshape(length, ring, attended.shape[1])
    attended_all = attended_all[:, :, : heads_local * HEAD].reshape(length, -1)
    router_w = pad_columns(router_weight)
    middle, normed_two_b, gate_probs = enter_middle(
        attended_all, out_all, tokens, ffn_gain, router_w, pad_columns(chosen.astype(jnp.float32))
    )
    gate_rows = jnp.transpose(lax.dynamic_slice_in_dim(gate_probs, first_expert, experts_local, 1))
    (grads_first, grads_next), sums = expert_stage(
        parts, 0, 2, (4, 2), counts, places_in, gate_rows, normed_two_b, cotangent,
        gate_weight, up_weight, down_weight, None,
    )
    shards_first = lax.psum_scatter(grads_first, "dp", scatter_dimension=1, tiled=True)
    (grads_last,), sums_last = expert_stage(
        parts, 2, experts_local - 2, (3 * experts_local - 4,), counts, places_in, gate_rows,
        normed_two_b, cotangent, gate_weight, up_weight, down_weight, (sums[0], sums[1], grads_next),
    )
    moe_part, grad_normed_part, unused = sums_last
    shards_first, grads_last, grad_normed_part = lax.optimization_barrier(
        (shards_first, grads_last, grad_normed_part)
    )
    shards_last = lax.psum_scatter(grads_last, "dp", scatter_dimension=1, tiled=True)
    grad_gates_local = jnp.concatenate([sums[2], sums_last[2]], 0).reshape(experts_local, length)
    grad_gates_part = lax.dynamic_update_slice_in_dim(
        jnp.zeros((experts_all, length), jnp.float32), grad_gates_local, first_expert, 0
    )
    grad_middle, grad_branch_b, grad_logits_b, grad_ffn_gain = turn_middle(
        ring, grad_normed_part, grad_gates_part, gate_probs, middle, cotangent, ffn_gain, router_w, 2
    )
    grads_wide, grad_normed_local, first_gain, output = attend_backward(
        ring, grad_branch_b, out_w, queries, keys, values, attended, logsum,
        query_w, key_w, value_w, tables, opening, tokens, moe_part, middle, heads_local, group_size, 3,
    )
    wide_q, wide_k = heads_local * HEAD, kv_local * HEAD
    grads_placed = place_shards(parts, shards_first, None, experts_local, None)
    grads_placed, grads_wide = lax.optimization_barrier((grads_placed, grads_wide))
    grad_normed, *small = finish(
        ring, parts, grad_normed_local, normed_b, grads_wide, grad_branch_b, attended, normed_two_b,
        grad_logits_b, grad_ffn_gain, first_gain, wide_q, wide_k, experts_all, 4,
    )
    grad_tokens, *small = leave_first(grad_normed, tokens, grad_middle, attn_gain, small)
    grad_query, grad_key, grad_value, grad_out, grad_router, grad_ffn_gain, grad_attn_gain = small
    shards_last, grad_tokens = lax.optimization_barrier((shards_last, grad_tokens))
    grad_gate, grad_up, grad_down = place_shards(
        parts, shards_first, shards_last, experts_local, grads_placed
    )
    return (
        output,
        grad_tokens,
        grad_attn_gain.reshape(-1),
        grad_query,
        grad_key,
        grad_value,
        jnp.transpose(grad_out),
        grad_ffn_gain.reshape(-1),
        jnp.transpose(grad_router),
        grad_gate,
        grad_up,
        grad_down,
    )


def solution(mesh):
    return jax.shard_map(
        functools.partial(on_device, mesh.shape["tensor"]),
        mesh=mesh,
        in_specs=(
            P("dp", None),
            P("dp", None),
            P("dp", None),
            P("dp", None),
            P(),
            P(None, "tensor"),
            P(None, "tensor"),
            P(None, "tensor"),
            P("tensor", None),
            P(),
            P(),
            P("tensor", None, None),
            P("tensor", None, None),
            P("tensor", None, None),
        ),
        out_specs=(
            P("dp", None),
            P("dp", None),
            P("dp"),
            P("dp", "tensor"),
            P("dp", "tensor"),
            P("dp", "tensor"),
            P("tensor", "dp"),
            P("dp"),
            P("dp", None),
            P("tensor", "dp", None),
            P("tensor", "dp", None),
            P("tensor", "dp", None),
        ),
        check_vma=False,
    )
```

```python
import functools

import jax
import jax.numpy as jnp
from jax import lax
from jax.experimental import pallas as pl
from jax.experimental.pallas import tpu as pltpu
from jax.sharding import PartitionSpec as P

MESH = pl.DeviceIdType.MESH

HEAD = 64
CAP = 384


EPSILON = 1e-06
RESIDUAL = 0.22
ATTN_SCALE = 0.015625
ROPE_BASE = 10000.0


def left_inner(first, second):
    return lax.dot_general(
        first, second, (((0,), (0,)), ((), ())), preferred_element_type=jnp.float32
    )


def right_inner(first, second):
    return lax.dot_general(
        first, second, (((1,), (1,)), ((), ())), preferred_element_type=jnp.float32
    )


def doc_openings(segment):
    return jnp.sum((segment[None, :] < segment[:, None]).astype(jnp.int32), axis=1)


def rope_tables(opening, head_size):
    halfway = head_size // 2
    spread = jnp.arange(halfway, dtype=jnp.float32) * (2.0 / head_size)
    inverse = jnp.power(ROPE_BASE, -spread)
    places = jnp.arange(opening.shape[0], dtype=jnp.int32)
    angles = (places - opening).astype(jnp.float32)[:, None] * inverse[None, :]
    cosine, sine = jnp.cos(angles), jnp.sin(angles)
    none = jnp.zeros_like(sine)
    return (
        jnp.concatenate([cosine] * 4, 1),
        jnp.concatenate([-sine, none] * 2, 1),
        jnp.concatenate([none, sine] * 2, 1),
    )


def pad_columns(weight):
    missing = -weight.shape[1] % 128
    return weight if missing == 0 else jnp.pad(weight, ((0, 0), (0, missing)))


def rms_forward(hidden, gain):
    recip = lax.rsqrt(jnp.mean(hidden * hidden, axis=-1, keepdims=True) + EPSILON)
    unit = hidden * recip
    return (unit * gain, unit, recip)


def rms_backward(gradient, unit, recip, gain):
    gain_grad = jnp.sum(gradient * unit, axis=0)
    scaled = gradient * gain
    return (recip * (scaled - unit * jnp.mean(scaled * unit, axis=-1, keepdims=True)), gain_grad)


def slot_places(picked):
    length = picked.shape[1]
    tokens = jnp.arange(length, dtype=jnp.int32)
    earlier = (tokens[:, None] < tokens[None, :]).astype(jnp.bfloat16)
    before = jnp.dot(picked.astype(jnp.bfloat16), earlier, preferred_element_type=jnp.float32)
    return jnp.where(picked > 0, before.astype(jnp.int32), -1)


STEPS = 32
LAG = 2


def line_stages(n, xs, outs, scratch, done=None, whole=0):
    count = len(xs)
    lows, highs = scratch[:count], scratch[count : 2 * count]
    low_recv, high_recv, total_recv, up_send, low_send, high_send = scratch[2 * count :]
    me = lax.axis_index("tensor")
    root = n // 2
    has_low, has_high = me > 0, me < n - 1

    def begin(others=()):
        barrier = pltpu.get_barrier_semaphore()
        for other in others:
            pl.semaphore_signal(barrier, inc=1, device_id=other, device_id_type=MESH)

        @pl.when(has_low)
        def _():
            pl.semaphore_signal(barrier, inc=1, device_id={"tensor": me - 1}, device_id_type=MESH)

        @pl.when(has_high)
        def _():
            pl.semaphore_signal(barrier, inc=1, device_id={"tensor": me + 1}, device_id_type=MESH)

        pl.semaphore_wait(
            barrier, len(others) + has_low.astype(jnp.int32) + has_high.astype(jnp.int32)
        )

    def piece(ref, c):
        rows = ref.shape[0] // STEPS
        return ref.at[pl.ds(pl.multiple_of(c * rows, rows), rows), :]

    cut = count - whole

    def copies(sources, targets, c, send, recv, to, uncut):
        return [
            pltpu.make_async_remote_copy(
                src_ref=source if uncut else piece(source, c),
                dst_ref=target if uncut else piece(target, c),
                send_sem=send.at[i, c],
                recv_sem=recv.at[i, c],
                device_id={"tensor": to},
                device_id_type=MESH,
            )
            for i, (source, target) in enumerate(zip(sources, targets))
            if (i >= cut) == uncut
        ]

    def each(sources, targets, c, send, recv, to, act):
        for copy in copies(sources, targets, c, send, recv, to, False):
            act(copy)
        if whole:

            @pl.when(c == 0)
            def _():
                for copy in copies(sources, targets, 0, send, recv, to, True):
                    act(copy)

    def start(sources, targets, c, send, recv, to):
        each(sources, targets, c, send, recv, to, lambda copy: copy.start())

    def arrived(targets, c, send, recv):
        each(targets, targets, c, send, recv, me, lambda copy: copy.wait_recv())

    def add(c, terms, targets):
        for i, target in enumerate(targets):
            if i < cut:
                piece(target, c)[...] = functools.reduce(
                    jnp.add, [piece(term[i], c)[...] for term in terms]
                )
            else:

                @pl.when(c == 0)
                def _():
                    target[...] = functools.reduce(jnp.add, [term[i][...] for term in terms])

    def reduce_step(c):
        for side, inner, held, recv, to in (
            (me < root, has_low, lows, low_recv, me + 1),
            (me > root, has_high, highs, high_recv, me - 1),
        ):

            @pl.when(side & inner)
            def _():
                arrived(held, c, up_send, recv)
                add(c, (held, xs), held)
                start(held, held, c, up_send, recv, to)

            @pl.when(side & jnp.logical_not(inner))
            def _():
                start(xs, held, c, up_send, recv, to)

        @pl.when(me == root)
        def _():
            arrived(lows, c, up_send, low_recv)
            if root < n - 1:
                arrived(highs, c, up_send, high_recv)
            add(c, (xs, lows, highs) if root < n - 1 else (xs, lows), outs)
            start(outs, outs, c, low_send, total_recv, me - 1)
            if root < n - 1:
                start(outs, outs, c, high_send, total_recv, me + 1)
            if done is not None:
                done(c)

    def total_step(c):
        @pl.when(me != root)
        def _():
            arrived(outs, c, low_send, total_recv)

        @pl.when((me < root) & has_low)
        def _():
            start(outs, outs, c, low_send, total_recv, me - 1)

        @pl.when((me > root) & has_high)
        def _():
            start(outs, outs, c, high_send, total_recv, me + 1)

        if done is not None:

            @pl.when(me != root)
            def _():
                done(c)

    lag = jnp.where(has_low & has_high, LAG, STEPS)

    def step(t, carry):
        @pl.when(t < STEPS)
        def _():
            reduce_step(t)

        @pl.when((t >= lag) & (t - lag < STEPS))
        def _():
            total_step(t - lag)

        return carry

    def finish():
        def drain(c, carry):
            for condition, send in (
                (me != root, up_send),
                ((me <= root) & has_low, low_send),
                ((me >= root) & has_high, high_send),
            ):

                @pl.when(condition)
                def _():
                    each(xs, lows, c, send, low_recv, me, lambda copy: copy.wait_send())

            return carry

        lax.fori_loop(0, STEPS, drain, 0)

    return begin, step, finish


def line_scratch(arrays):
    return [pltpu.VMEM(array.shape, jnp.float32) for array in arrays * 2] + [
        pltpu.SemaphoreType.DMA((len(arrays), STEPS))
    ] * 6


def expert_kernel(
    parts,
    first,
    numbers,
    chained,
    count_ref,
    place_ref,
    gate_ref,
    normed_ref,
    grad_ref,
    gate_w,
    up_w,
    down_w,
    *refs,
):
    if chained:
        moe_in, back_in = refs[:2]
        refs = refs[2:]
    grads_out, refs = refs[: len(numbers)], refs[len(numbers) :]
    moe_out, back_out, gates_out = refs[:3]
    rows_ref, grads_ref, active_ref, gate_in_ref, up_in_ref, weights_ref, sems, out_sems = refs[3:]
    expert = pl.program_id(0)
    filled = count_ref[first + expert]
    length, width = normed_ref.shape
    hidden_size = gate_w.shape[2]
    sizes = (128, 256, CAP)

    def by_size(run):
        low = None
        for rows in sizes:
            fits = filled <= rows if low is None else filled > low
            if low is not None and rows != sizes[-1]:
                fits = fits & (filled <= rows)
            pl.when(fits)(functools.partial(run, rows))
            low = rows

    if chained:
        copy_moe = pltpu.make_async_copy(moe_in, moe_out, sems.at[0])
        copy_back = pltpu.make_async_copy(back_in, back_out, sems.at[1])

        @pl.when(expert == 0)
        def _():
            copy_moe.start()
            copy_back.start()

    else:

        @pl.when(expert == 0)
        def _():
            moe_out[...] = jnp.zeros_like(moe_out)
            back_out[...] = jnp.zeros_like(back_out)

    def slots(rows):
        mask = lax.broadcasted_iota(jnp.int32, (rows, length), 0) == place_ref[0]
        return mask, jnp.where(mask, 1.0, 0.0).astype(jnp.bfloat16)

    def enter(rows):
        mask, picks = slots(rows)
        rows_in = jnp.dot(picks, normed_ref[...], preferred_element_type=jnp.float32).astype(jnp.bfloat16)
        grad_rows = (
            RESIDUAL * jnp.dot(picks, grad_ref[...], preferred_element_type=jnp.float32)
        ).astype(jnp.bfloat16)
        rows_ref[:rows] = rows_in
        grads_ref[:rows] = grad_rows
        gate = jnp.sum(jnp.where(mask, gate_ref[0], 0.0), axis=1, keepdims=True)
        gate_input = jnp.dot(rows_in, gate_w[0], preferred_element_type=jnp.float32)
        up_input = jnp.dot(rows_in, up_w[0], preferred_element_type=jnp.float32)
        grad_act = right_inner(grad_rows, down_w[0])
        sigmoid_val = jax.nn.sigmoid(gate_input)
        silu_out = gate_input * sigmoid_val
        hidden = silu_out * up_input
        active_ref[:rows] = (hidden * gate).astype(jnp.bfloat16)
        column = jnp.sum(grad_act * hidden, axis=1, keepdims=True)
        gates_out[0] = jnp.sum(jnp.where(mask, column, 0.0), axis=0, keepdims=True)
        grad_hidden = grad_act * gate
        gate_in_ref[:rows] = (
            grad_hidden * up_input * sigmoid_val * (1.0 + gate_input * (1.0 - sigmoid_val))
        ).astype(jnp.bfloat16)
        up_in_ref[:rows] = (grad_hidden * silu_out).astype(jnp.bfloat16)

    by_size(enter)
    if chained:

        @pl.when(expert == 0)
        def _():
            copy_moe.wait()
            copy_back.wait()

    def leave(rows):
        column = jnp.transpose(jnp.broadcast_to(place_ref[0], (128, length)))
        column = jnp.concatenate([column] * (rows // 128), 1)
        own = lax.broadcasted_iota(jnp.int32, (length, rows), 1)
        picks = jnp.where(own == column, 1.0, 0.0).astype(jnp.bfloat16)
        moe = jnp.dot(active_ref[:rows], down_w[0], preferred_element_type=jnp.float32)
        moe_out[...] += jnp.dot(
            picks, moe.astype(jnp.bfloat16), preferred_element_type=jnp.float32
        )
        back = right_inner(gate_in_ref[:rows], gate_w[0]) + right_inner(up_in_ref[:rows], up_w[0])
        back_out[...] += jnp.dot(
            picks, back.astype(jnp.bfloat16), preferred_element_type=jnp.float32
        )

    by_size(leave)

    def copies(target, number):
        return [
            pltpu.make_async_copy(weights_ref.at[kind], target.at[number, kind], out_sems.at[kind])
            for kind in range(3)
        ]

    @pl.when(expert > 0)
    def _():
        for copy in copies(grads_out[0], 0):
            copy.wait()

    def weigh(rows):
        grads = left_inner(
            rows_ref[:rows], jnp.concatenate([gate_in_ref[:rows], up_in_ref[:rows]], 1)
        )
        weights_ref[0] = grads[:, :hidden_size]
        weights_ref[1] = grads[:, hidden_size:]
        grad_down = left_inner(active_ref[:rows], grads_ref[:rows])
        own = hidden_size // parts
        blocks = width // hidden_size
        for part in range(parts):
            for piece in range(blocks):
                at = (part * blocks + piece) * own
                weights_ref[2, at : at + own, :] = grad_down[
                    part * own : (part + 1) * own, piece * hidden_size : (piece + 1) * hidden_size
                ]

    by_size(weigh)
    start = 0
    for target, number in zip(grads_out, numbers):

        @pl.when((expert >= start) & (expert < start + number))
        def _():
            for copy in copies(target, expert - start):
                copy.start()

        start += number

    @pl.when(expert == pl.num_programs(0) - 1)
    def _():
        for copy in copies(grads_out[0], 0):
            copy.wait()


def expert_stage(parts, first, numbers, counts, places, gate_rows, normed_b, grad_b, gate_w, up_w, down_w, sums):
    number = sum(numbers)
    length, width = normed_b.shape
    hidden = gate_w.shape[2]
    experts = places.shape[0]
    chained = sums is not None
    whole = lambda e, c: (0, 0)
    row_spec = pl.BlockSpec((1, 1, length), lambda e, c: (first + e, 0, 0))
    once = pl.Buffered(1)
    f32, bf16 = jnp.float32, jnp.bfloat16
    in_specs = [
        row_spec,
        row_spec,
        pl.BlockSpec((length, width), whole, pipeline_mode=once),
        pl.BlockSpec((length, width), whole, pipeline_mode=once),
        pl.BlockSpec((1, width, hidden), lambda e, c: (first + e, 0, 0)),
        pl.BlockSpec((1, width, hidden), lambda e, c: (first + e, 0, 0)),
        pl.BlockSpec((1, hidden, width), lambda e, c: (first + e, 0, 0)),
    ]
    args = [
        counts,
        places.reshape(experts, 1, length),
        gate_rows.reshape(experts, 1, length),
        normed_b,
        grad_b,
        gate_w,
        up_w,
        down_w,
    ]
    if chained:
        in_specs += [pl.BlockSpec(memory_space=pl.ANY)] * 2
        args += [sums[0], sums[1]]
    results = pl.pallas_call(
        functools.partial(expert_kernel, parts, first, numbers, chained),
        out_shape=[jax.ShapeDtypeStruct((some, 3, width, hidden), f32) for some in numbers]
        + [
            jax.ShapeDtypeStruct((length, width), f32),
            jax.ShapeDtypeStruct((length, width), f32),
            jax.ShapeDtypeStruct((number, 1, length), f32),
        ],
        grid_spec=pltpu.PrefetchScalarGridSpec(
            num_scalar_prefetch=1,
            grid=(number,),
            in_specs=in_specs,
            out_specs=[pl.BlockSpec(memory_space=pl.ANY)] * len(numbers)
            + [
                pl.BlockSpec((length, width), whole, pipeline_mode=once),
                pl.BlockSpec((length, width), whole, pipeline_mode=once),
                pl.BlockSpec((1, 1, length), lambda e, c: (e, 0, 0)),
            ],
            scratch_shapes=[
                pltpu.VMEM((CAP, width), bf16),
                pltpu.VMEM((CAP, width), bf16),
                pltpu.VMEM((CAP, hidden), bf16),
                pltpu.VMEM((CAP, hidden), bf16),
                pltpu.VMEM((CAP, hidden), bf16),
                pltpu.VMEM((3, width, hidden), f32),
                pltpu.SemaphoreType.DMA((2,)),
                pltpu.SemaphoreType.DMA((3,)),
            ],
        ),
        compiler_params=pltpu.CompilerParams(
            dimension_semantics=("arbitrary",), vmem_limit_bytes=63 << 20
        ),
        cost_estimate=pl.CostEstimate(
            flops=number * 8 * 10**9, bytes_accessed=number * 14 * 10**6, transcendentals=0
        ),
    )(*args)
    return results[: len(numbers)], results[len(numbers) :]


PIECES = 16


def line_gather_kernel(n, x_ref, out_ref, blocks_ref, recv, up_send, down_send):
    me = lax.axis_index("tensor")
    has_low, has_high = me > 0, me < n - 1
    barrier = pltpu.get_barrier_semaphore()

    @pl.when(has_low)
    def _():
        pl.semaphore_signal(barrier, inc=1, device_id={"tensor": me - 1}, device_id_type=MESH)

    @pl.when(has_high)
    def _():
        pl.semaphore_signal(barrier, inc=1, device_id={"tensor": me + 1}, device_id_type=MESH)

    blocks_ref[me] = x_ref[...].astype(jnp.float32)
    pl.semaphore_wait(barrier, has_low.astype(jnp.int32) + has_high.astype(jnp.int32))
    rows = x_ref.shape[0] // PIECES

    def copy(block, c, send, to):
        piece = blocks_ref.at[block, pl.ds(pl.multiple_of(c * rows, rows), rows), :]
        return pltpu.make_async_remote_copy(
            src_ref=piece,
            dst_ref=piece,
            send_sem=send.at[block, c],
            recv_sem=recv.at[block, c],
            device_id={"tensor": to},
            device_id_type=MESH,
        )

    for hop in range(n):
        low, high = me - hop, me + hop

        def step(c, carry):
            @pl.when(low >= 0)
            def _():
                if hop > 0:
                    copy(low, c, up_send, me).wait_recv()

                @pl.when(has_high)
                def _():
                    copy(low, c, up_send, me + 1).start()

            @pl.when(high < n)
            def _():
                if hop > 0:
                    copy(high, c, down_send, me).wait_recv()

                @pl.when(has_low)
                def _():
                    copy(high, c, down_send, me - 1).start()

            return carry

        lax.fori_loop(0, PIECES, step, 0)
    wide = x_ref.shape[1]
    for block in range(n):
        out_ref[:, block * wide : (block + 1) * wide] = blocks_ref[block].astype(jnp.bfloat16)
    for hop in range(n):
        low, high = me - hop, me + hop

        def drain(c, carry):
            @pl.when((low >= 0) & has_high)
            def _():
                copy(low, c, up_send, me).wait_send()

            @pl.when((high < n) & has_low)
            def _():
                copy(high, c, down_send, me).wait_send()

            return carry

        lax.fori_loop(0, PIECES, drain, 0)


def line_gather(x, n, name):
    length, wide = x.shape
    full = pl.BlockSpec(memory_space=pltpu.VMEM)
    return pl.pallas_call(
        functools.partial(line_gather_kernel, n),
        out_shape=jax.ShapeDtypeStruct((length, n * wide), jnp.bfloat16),
        in_specs=[full],
        out_specs=full,
        scratch_shapes=[pltpu.VMEM((n, length, wide), jnp.float32)]
        + [pltpu.SemaphoreType.DMA((n, PIECES))] * 3,
        compiler_params=pltpu.CompilerParams(
            collective_id=name, has_side_effects=True, vmem_limit_bytes=32 << 20
        ),
        cost_estimate=pl.CostEstimate(
            flops=0, bytes_accessed=16 * n * x.size, transcendentals=0
        ),
    )(x)


BLOCK = 256


def own_rows_kernel(parts, weight_ref, out_ref):
    rows = out_ref.shape[0]
    first = lax.axis_index("dp") * rows if parts > 1 else 0
    out_ref[...] = weight_ref[pl.ds(pl.multiple_of(first, 16), rows), :].astype(jnp.float32)


def gather_out_weight(out_weight, parts):
    rows, width = out_weight.shape
    ways = parts if rows % (16 * parts) == 0 else 1
    full = pl.BlockSpec(memory_space=pltpu.VMEM)
    own = pl.pallas_call(
        functools.partial(own_rows_kernel, ways),
        out_shape=jax.ShapeDtypeStruct((rows // ways, width), jnp.float32),
        in_specs=[full],
        out_specs=full,
    )(out_weight)
    gathered = lax.all_gather(own, ("dp", "tensor") if ways > 1 else "tensor")
    return gathered.reshape(ways, -1, rows // ways, width)


def middle_kernel(
    attended_ref, weight_all_ref, tokens_ref, gain_ref, router_ref, chosen_ref, middle_out, normed_out, gates_out, weight_ref
):
    ways, n, rows, unused = weight_all_ref.shape

    @pl.when(pl.program_id(0) == 0)
    def _():
        for way in range(ways):
            for block in range(n):
                at = (block * ways + way) * rows
                weight_ref[at : at + rows, :] = weight_all_ref[way, block].astype(jnp.bfloat16)

    branch = jnp.dot(attended_ref[...], weight_ref[...], preferred_element_type=jnp.float32)
    middle = tokens_ref[...].astype(jnp.float32) + RESIDUAL * branch
    middle_out[...] = middle
    recip = lax.rsqrt(jnp.mean(middle * middle, axis=1, keepdims=True) + EPSILON)
    normed = (middle * recip * gain_ref[...]).astype(jnp.bfloat16)
    normed_out[...] = normed
    logits = jnp.dot(normed, router_ref[...], preferred_element_type=jnp.float32)
    raised = jnp.where(chosen_ref[...] > 0.0, jnp.exp(logits), 0.0)
    gates_out[...] = raised / jnp.sum(raised, axis=1, keepdims=True)


def enter_middle(attended, weight_all, tokens, gain, router, chosen):
    length, width = tokens.shape
    rows = lambda columns: pl.BlockSpec((BLOCK, columns), lambda i: (i, 0))
    whole = lambda shape: pl.BlockSpec(
        shape, lambda i: (0,) * len(shape), pipeline_mode=pl.Buffered(1)
    )
    experts = router.shape[1]
    return pl.pallas_call(
        middle_kernel,
        out_shape=[
            jax.ShapeDtypeStruct((length, width), jnp.float32),
            jax.ShapeDtypeStruct((length, width), jnp.bfloat16),
            jax.ShapeDtypeStruct((length, experts), jnp.float32),
        ],
        grid=(length // BLOCK,),
        in_specs=[
            rows(attended.shape[1]),
            whole(weight_all.shape),
            rows(width),
            whole((1, width)),
            whole(router.shape),
            rows(experts),
        ],
        out_specs=[rows(width), rows(width), rows(experts)],
        scratch_shapes=[pltpu.VMEM((attended.shape[1], width), jnp.bfloat16)],
        compiler_params=pltpu.CompilerParams(
            dimension_semantics=("arbitrary",), vmem_limit_bytes=62 << 20
        ),
        cost_estimate=pl.CostEstimate(
            flops=2 * length * width * width, bytes_accessed=25 * 10**6, transcendentals=0
        ),
    )(attended, weight_all, tokens, gain.reshape(1, width), router, chosen)


def turn_kernel(
    n,
    part_ref,
    gates_part_ref,
    gates_ref,
    middle_ref,
    cotangent_ref,
    gain_ref,
    router_ref,
    grad_out,
    branch_out,
    logits_out,
    gain_out,
    summed_ref,
    gates_rows_ref,
    grad_gates_ref,
    *line,
):
    length = part_ref.shape[0]
    rows = length // STEPS

    def done(c):
        @pl.when(c == 0)
        def _():
            experts = gates_rows_ref.shape[0]
            empty = jnp.zeros((grad_gates_ref.shape[1] - experts, length), jnp.float32)
            grad_gates_ref[...] = jnp.transpose(
                jnp.concatenate([gates_rows_ref[...], empty], 0)
            )

        own = pl.ds(pl.multiple_of(c * rows, rows), rows)
        gates, grad_gates = gates_ref[own, :], grad_gates_ref[own, :]
        weighted = jnp.sum(gates * grad_gates, axis=1, keepdims=True)
        grad_logits = (gates * (grad_gates - weighted)).astype(jnp.bfloat16)
        logits_out[own, :] = grad_logits
        grad = summed_ref[own, :] + right_inner(grad_logits, router_ref[...])
        middle = middle_ref[own, :]
        recip = lax.rsqrt(jnp.mean(middle * middle, axis=1, keepdims=True) + EPSILON)
        unit = middle * recip
        gain_out[...] += jnp.sum(grad * unit, axis=0, keepdims=True)
        scaled = grad * gain_ref[...]
        back = recip * (scaled - unit * jnp.mean(scaled * unit, axis=1, keepdims=True))
        total = cotangent_ref[own, :].astype(jnp.float32) + back
        grad_out[own, :] = total
        branch_out[own, :] = (RESIDUAL * total).astype(jnp.bfloat16)

    begin, step, finish = line_stages(
        n, [part_ref, gates_part_ref], [summed_ref, gates_rows_ref], line, done, 1
    )
    begin()
    gain_out[...] = jnp.zeros_like(gain_out)
    lax.fori_loop(0, 2 * STEPS, step, 0)
    finish()


def turn_middle(n, part, gates_part, gates, middle, cotangent, gain, router, name):
    length, width = part.shape
    full = pl.BlockSpec(memory_space=pltpu.VMEM)
    f32 = jnp.float32
    return pl.pallas_call(
        functools.partial(turn_kernel, n),
        out_shape=[
            jax.ShapeDtypeStruct((length, width), f32),
            jax.ShapeDtypeStruct((length, width), jnp.bfloat16),
            jax.ShapeDtypeStruct(gates.shape, jnp.bfloat16),
            jax.ShapeDtypeStruct((1, width), f32),
        ],
        in_specs=[full] * 7,
        out_specs=[full] * 4,
        scratch_shapes=[
            pltpu.VMEM(part.shape, f32),
            pltpu.VMEM(gates_part.shape, f32),
            pltpu.VMEM(gates.shape, f32),
        ]
        + line_scratch([part, gates_part]),
        compiler_params=pltpu.CompilerParams(
            collective_id=name, has_side_effects=True, vmem_limit_bytes=58 << 20
        ),
        cost_estimate=pl.CostEstimate(
            flops=40 * length * width, bytes_accessed=60 * 10**6, transcendentals=0
        ),
    )(part, gates_part, gates, middle, cotangent, gain.reshape(1, width), router)


def last_kernel(count, summed_ref, tokens_ref, middle_ref, gain_ref, *refs):
    smalls, out_ref, small_outs = refs[:count], refs[count], refs[count + 1 :]
    hidden = tokens_ref[...].astype(jnp.float32)
    recip = lax.rsqrt(jnp.mean(hidden * hidden, axis=1, keepdims=True) + EPSILON)
    unit = hidden * recip
    scaled = summed_ref[...] * gain_ref[...]
    inner = jnp.mean(scaled * unit, axis=1, keepdims=True)
    out_ref[...] = middle_ref[...] + recip * (scaled - unit * inner)

    @pl.when(pl.program_id(0) == 0)
    def _():
        for small, out in zip(smalls, small_outs):
            out[...] = small[...]


def leave_first(summed, tokens, grad_middle, gain, smalls):
    length, width = tokens.shape
    rows = pl.BlockSpec((BLOCK // 2, width), lambda i: (i, 0))
    whole = lambda shape: pl.BlockSpec(shape, lambda i: (0, 0))
    f32 = jnp.float32
    return pl.pallas_call(
        functools.partial(last_kernel, len(smalls)),
        out_shape=[jax.ShapeDtypeStruct((length, width), f32)]
        + [jax.ShapeDtypeStruct(small.shape, f32) for small in smalls],
        grid=(2 * length // BLOCK,),
        in_specs=[rows, rows, rows, whole((1, width))] + [whole(small.shape) for small in smalls],
        out_specs=[rows] + [whole(small.shape) for small in smalls],
        compiler_params=pltpu.CompilerParams(vmem_limit_bytes=60 << 20),
        cost_estimate=pl.CostEstimate(
            flops=10 * length * width, bytes_accessed=14 * length * width, transcendentals=0
        ),
    )(summed, tokens, grad_middle, gain.reshape(1, width), *smalls)


SPAN = 768
ROWS = 256


def lane_halves(shape):
    return lax.broadcasted_iota(jnp.int32, shape, len(shape) - 1) // HEAD


def select_halves(tile, source, half):
    kept = jnp.where(lane_halves(tile.shape) == source, tile, 0.0)
    return kept if source == half else pltpu.roll(kept, HEAD, 1)


def spread_pairs(tile, target):
    for source in range(2):
        for half in range(2):
            target[2 * source + half] = select_halves(tile, source, half).astype(jnp.bfloat16)


def rope_tile(tile, cosine, sine_low, sine_high):
    return tile * cosine + pltpu.roll(tile, 128 - HEAD // 2, 1) * sine_low + pltpu.roll(
        tile, HEAD // 2, 1
    ) * sine_high


def rope_back_tile(tile, cosine, sine_low, sine_high):
    return (
        tile * cosine
        + pltpu.roll(tile * sine_low, HEAD // 2, 1)
        + pltpu.roll(tile * sine_high, 128 - HEAD // 2, 1)
    )


def window(block):
    first = block * ROWS
    return first, jnp.maximum(first + ROWS - SPAN, 0)


def attend_forward_kernel(
    heads,
    group,
    tokens_ref,
    gain_ref,
    query_w,
    key_w,
    value_w,
    cosine_ref,
    sine_low_ref,
    sine_high_ref,
    opening_ref,
    normed_out,
    query_out,
    key_out,
    value_out,
    attended_out,
    logsum_out,
    key_pairs,
    value_pairs,
    tiles_ref,
):
    tiles, length, unused = query_out.shape
    hidden = tokens_ref[...].astype(jnp.float32)
    recip = lax.rsqrt(jnp.mean(hidden * hidden, axis=1, keepdims=True) + EPSILON)
    normed_out[...] = (hidden * recip * gain_ref[...]).astype(jnp.bfloat16)
    cosine, sine_low, sine_high = cosine_ref[...], sine_low_ref[...], sine_high_ref[...]
    for tile in range(tiles):
        query = jnp.dot(
            normed_out[...],
            query_w[:, tile * 128 : (tile + 1) * 128],
            preferred_element_type=jnp.float32,
        )
        query_out[tile] = rope_tile(query, cosine, sine_low, sine_high).astype(jnp.bfloat16)
    key = rope_tile(
        jnp.dot(normed_out[...], key_w[...], preferred_element_type=jnp.float32),
        cosine,
        sine_low,
        sine_high,
    )
    value = jnp.dot(normed_out[...], value_w[...], preferred_element_type=jnp.float32)
    key_out[...] = key.astype(jnp.bfloat16)
    value_out[...] = value.astype(jnp.bfloat16)
    spread_pairs(key, key_pairs)
    spread_pairs(value, value_pairs)
    blocks = length // ROWS
    tiles_ref[...] = jnp.zeros_like(tiles_ref)

    def unit(step, carry):
        head, block = step // blocks, step % blocks
        tile, half = head // 2, head % 2
        pair = 2 * (head // group) + half
        first, low = window(block)
        rows = pl.ds(pl.multiple_of(first, ROWS), ROWS)
        span = pl.ds(pl.multiple_of(low, ROWS), SPAN)
        scores = right_inner(query_out[tile, rows, :], key_pairs[pair, span, :])
        columns = low + lax.broadcasted_iota(jnp.int32, (ROWS, SPAN), 1)
        own = first + lax.broadcasted_iota(jnp.int32, (ROWS, SPAN), 0)
        allowed = (columns >= opening_ref[rows, :]) & (columns <= own)
        raised = jnp.where(allowed, jnp.exp(ATTN_SCALE * scores), 0.0)
        total = jnp.sum(raised, axis=1, keepdims=True)
        product = jnp.dot(
            raised.astype(jnp.bfloat16), value_pairs[pair, span, :], preferred_element_type=jnp.float32
        )
        tiles_ref[tile, rows, :] += product / total
        wide = jnp.broadcast_to(jnp.log(total), (ROWS, 128))
        logsum_out[head, :, rows] = jnp.transpose(wide)[:1]
        return carry

    lax.fori_loop(0, heads * blocks, unit, 0)
    for tile in range(tiles):
        attended_out[:, tile * 128 : (tile + 1) * 128] = tiles_ref[tile].astype(jnp.bfloat16)


def attend_forward(tokens, gain, query_w, key_w, value_w, tables, opening, heads, group):
    length, width = tokens.shape
    wide = query_w.shape[1]
    tiles = wide // 128
    bf16, f32 = jnp.bfloat16, jnp.float32
    full = pl.BlockSpec(memory_space=pltpu.VMEM)
    return pl.pallas_call(
        functools.partial(attend_forward_kernel, heads, group),
        out_shape=[
            jax.ShapeDtypeStruct((length, width), bf16),
            jax.ShapeDtypeStruct((tiles, length, 128), bf16),
            jax.ShapeDtypeStruct((length, 128), bf16),
            jax.ShapeDtypeStruct((length, 128), bf16),
            jax.ShapeDtypeStruct((length, wide), bf16),
            jax.ShapeDtypeStruct((heads, 1, length), f32),
        ],
        in_specs=[full] * 9,
        out_specs=[full] * 6,
        scratch_shapes=[
            pltpu.VMEM((4, length, 128), bf16),
            pltpu.VMEM((4, length, 128), bf16),
            pltpu.VMEM((tiles, length, 128), f32),
        ],
        compiler_params=pltpu.CompilerParams(vmem_limit_bytes=62 << 20),
        cost_estimate=pl.CostEstimate(
            flops=8 * 10**9, bytes_accessed=12 * 10**6, transcendentals=5 * 10**6
        ),
    )(tokens, gain.reshape(1, width), query_w, key_w, value_w, *tables, opening.reshape(length, 1))


def attend_backward_kernel(
    n,
    heads,
    group,
    branch_ref,
    out_w,
    query_ref,
    key_ref,
    value_ref,
    attended_ref,
    logsum_ref,
    query_w,
    key_w,
    value_w,
    cosine_ref,
    sine_low_ref,
    sine_high_ref,
    opening_ref,
    tokens_ref,
    moe_ref,
    middle_ref,
    grads_out,
    normed_out,
    gain_out,
    output_ref,
    moe_sum,
    middle_rows,
    middle_sems,
    key_pairs,
    value_pairs,
    attend_grads,
    query_grads,
    key_grads,
    value_grads,
    delta_ref,
    *line,
):
    tiles, length, unused = query_ref.shape
    share = length // STEPS

    def share_rows(c):
        return pl.ds(pl.multiple_of(c * share, share), share)

    def fetch(c):
        slot = lax.rem(c, 2)
        return pltpu.make_async_copy(
            middle_ref.at[share_rows(c), :], middle_rows.at[slot], middle_sems.at[slot]
        )

    def done(c):
        fetch(c).wait()

        @pl.when(c + 1 < STEPS)
        def _():
            fetch(c + 1).start()

        total = middle_rows[lax.rem(c, 2)] + RESIDUAL * moe_sum[share_rows(c), :]
        output_ref[share_rows(c), :] = total.astype(jnp.bfloat16)

    line_start, line_step, line_end = line_stages(n, [moe_ref], [moe_sum], line, done)
    line_start()
    fetch(jnp.int32(0)).start()
    blocks = length // ROWS
    units = heads * blocks
    taken = 0

    def run_line(steps):
        nonlocal taken
        until = min(taken + steps, 2 * STEPS)
        lax.fori_loop(taken, until, line_step, 0)
        taken = until

    run_line(2)
    spread_pairs(key_ref[...].astype(jnp.float32), key_pairs)
    spread_pairs(value_ref[...].astype(jnp.float32), value_pairs)
    halves = (
        lax.broadcasted_iota(jnp.int32, (8, 128), 0) == lane_halves((8, 128))
    ).astype(jnp.float32)
    for tile in range(tiles):
        lanes = slice(tile * 128, (tile + 1) * 128)
        grad = right_inner(branch_ref[...], out_w[lanes, :]).astype(jnp.bfloat16)
        attend_grads[tile] = grad
        products = grad.astype(jnp.float32) * attended_ref[:, lanes].astype(jnp.float32)
        sums = lax.dot_general(
            halves,
            products,
            (((1,), (1,)), ((), ())),
            precision=lax.Precision.HIGHEST,
            preferred_element_type=jnp.float32,
        )
        delta_ref[2 * tile] = sums[0:1]
        delta_ref[2 * tile + 1] = sums[1:2]
        run_line(2)
    query_grads[...] = jnp.zeros_like(query_grads)
    key_grads[...] = jnp.zeros_like(key_grads)
    value_grads[...] = jnp.zeros_like(value_grads)
    before, each = taken, (2 * STEPS - 8 - taken) // units
    taken += units * each

    def unit(step, carry):
        lax.fori_loop(before + step * each, before + step * each + each, line_step, 0)
        head, block = step // blocks, step % blocks
        tile, half = head // 2, head % 2
        pair = 2 * (head // group) + half
        first, low = window(block)
        rows = pl.ds(pl.multiple_of(first, ROWS), ROWS)
        span = pl.ds(pl.multiple_of(low, ROWS), SPAN)
        keys = key_pairs[pair, span, :]
        query = query_ref[tile, rows, :]
        grad = attend_grads[tile, rows, :]
        scores = right_inner(keys, query)
        columns = low + lax.broadcasted_iota(jnp.int32, (SPAN, ROWS), 0)
        own = first + lax.broadcasted_iota(jnp.int32, (SPAN, ROWS), 1)
        allowed = (columns >= opening_ref[:, rows]) & (columns <= own)
        probs = jnp.where(
            allowed, jnp.exp(ATTN_SCALE * scores - logsum_ref[head, :, rows]), 0.0
        )
        grad_probs = right_inner(value_pairs[pair, span, :], grad)
        grad_scores = (probs * (grad_probs - delta_ref[head, :, rows])).astype(jnp.bfloat16)
        value_grads[pair, span, :] += jnp.dot(
            probs.astype(jnp.bfloat16), grad, preferred_element_type=jnp.float32
        )
        key_grads[pair, span, :] += jnp.dot(
            grad_scores, query, preferred_element_type=jnp.float32
        )
        query_grads[tile, rows, :] += left_inner(grad_scores, keys)
        return carry

    lax.fori_loop(0, units, unit, 0)
    cosine, sine_low, sine_high = cosine_ref[...], sine_low_ref[...], sine_high_ref[...]
    wide = tiles * 128
    for tile in range(tiles):
        grads_out[:, tile * 128 : (tile + 1) * 128] = rope_back_tile(
            ATTN_SCALE * query_grads[tile], cosine, sine_low, sine_high
        ).astype(jnp.bfloat16)
    totals = []
    for grads in (key_grads, value_grads):
        totals.append(
            sum(
                select_halves(grads[2 * source + half], half, source)
                for source in range(2)
                for half in range(2)
            )
        )
    grads_out[:, wide : wide + 128] = rope_back_tile(
        ATTN_SCALE * totals[0], cosine, sine_low, sine_high
    ).astype(jnp.bfloat16)
    grads_out[:, wide + 128 : wide + 256] = totals[1].astype(jnp.bfloat16)
    gain_sum = jnp.zeros((1, normed_out.shape[1]), jnp.float32)
    for block in range(blocks):
        rows = slice(block * ROWS, (block + 1) * ROWS)
        normed = (
            right_inner(grads_out[rows, :wide], query_w[...])
            + right_inner(grads_out[rows, wide : wide + 128], key_w[...])
            + right_inner(grads_out[rows, wide + 128 :], value_w[...])
        )
        normed_out[rows, :] = normed
        hidden = tokens_ref[rows, :].astype(jnp.float32)
        recip = lax.rsqrt(jnp.mean(hidden * hidden, axis=1, keepdims=True) + EPSILON)
        gain_sum += jnp.sum(normed * (hidden * recip), axis=0, keepdims=True)
        run_line(2)
    gain_out[...] = jnp.broadcast_to(gain_sum, gain_out.shape)
    run_line(2 * STEPS)
    line_end()


def attend_backward(
    n, branch, out_w, query, key, value, attended, logsum, query_w, key_w, value_w, tables, opening, tokens, moe, middle,
    heads, group, name,
):
    length, width = branch.shape
    tiles = query.shape[0]
    wide = tiles * 128
    bf16, f32 = jnp.bfloat16, jnp.float32
    full = pl.BlockSpec(memory_space=pltpu.VMEM)
    return pl.pallas_call(
        functools.partial(attend_backward_kernel, n, heads, group),
        out_shape=[
            jax.ShapeDtypeStruct((length, wide + 256), bf16),
            jax.ShapeDtypeStruct((length, width), f32),
            jax.ShapeDtypeStruct((8, width), f32),
            jax.ShapeDtypeStruct((length, width), bf16),
        ],
        in_specs=[full] * 16 + [pl.BlockSpec(memory_space=pl.ANY)],
        out_specs=[full] * 4,
        scratch_shapes=[
            pltpu.VMEM((length, width), f32),
            pltpu.VMEM((2, length // STEPS, width), f32),
            pltpu.SemaphoreType.DMA((2,)),
            pltpu.VMEM((4, length, 128), bf16),
            pltpu.VMEM((4, length, 128), bf16),
            pltpu.VMEM((tiles, length, 128), bf16),
            pltpu.VMEM((tiles, length, 128), f32),
            pltpu.VMEM((4, length, 128), f32),
            pltpu.VMEM((4, length, 128), f32),
            pltpu.VMEM((2 * tiles, 1, length), f32),
        ]
        + line_scratch([moe]),
        compiler_params=pltpu.CompilerParams(
            collective_id=name, has_side_effects=True, vmem_limit_bytes=63 << 20
        ),
        cost_estimate=pl.CostEstimate(
            flops=12 * 10**9, bytes_accessed=30 * 10**6, transcendentals=5 * 10**6
        ),
    )(
        branch, out_w, query, key, value, attended, logsum, query_w, key_w, value_w, *tables,
        opening.reshape(1, length), tokens, moe, middle,
    )


def finish_kernel(
    n,
    parts,
    local_ref,
    normed_ref,
    grads_ref,
    branch_ref,
    attended_ref,
    normed_two_ref,
    logits_ref,
    gain_ref,
    first_gain_ref,
    normed_out,
    query_out,
    key_out,
    value_out,
    branch_out,
    router_out,
    gain_out,
    first_gain_out,
    weights_ref,
    gains_ref,
    gain_send,
    gain_recv,
    *scratch,
):
    levels = parts.bit_length() - 1
    held = scratch[:levels]
    sends, recvs = scratch[levels : levels + 2]
    line_start, line_step, line_end = line_stages(n, [local_ref], [normed_out], scratch[levels + 2 :])
    me = lax.axis_index("dp")
    width = normed_ref.shape[1]
    own = width // parts
    wide, attended_wide = grads_ref.shape[1], attended_ref.shape[1]
    mine = lax.axis_index("tensor")
    line_start(
        [{"dp": jnp.bitwise_xor(me, 1 << level)} for level in range(levels)]
        + [{"tensor": lax.rem(mine + ahead, n)} for ahead in range(1, n)]
    )

    def run_line(first, last):
        lax.fori_loop(first, last, line_step, 0)

    gain_copies = [
        pltpu.make_async_remote_copy(
            src_ref=first_gain_ref,
            dst_ref=gains_ref.at[ahead],
            send_sem=gain_send.at[ahead],
            recv_sem=gain_recv.at[ahead],
            device_id={"tensor": lax.rem(mine + ahead, n)},
            device_id_type=MESH,
        )
        for ahead in range(1, n)
    ]
    for copy in gain_copies:
        copy.start()
    run_line(0, 2)
    first_gain = first_gain_ref[:1]
    for ahead, copy in enumerate(gain_copies, 1):
        copy.wait_recv()
        first_gain = first_gain + gains_ref[ahead, :1]
    pieces = 4
    block = width // pieces
    for piece in range(pieces):
        rows = slice(piece * block, (piece + 1) * block)
        weights_ref[rows, :wide] = left_inner(normed_ref[:, rows], grads_ref[...])
        weights_ref[rows, wide : wide + attended_wide] = left_inner(
            branch_ref[:, rows], attended_ref[...]
        )
        gain = jnp.transpose(jnp.broadcast_to(gain_ref[:, rows], (128, block)))
        own_gain = jnp.transpose(jnp.broadcast_to(first_gain[:, rows], (128, block)))
        lanes = lax.broadcasted_iota(jnp.int32, (block, 128), 1)
        weights_ref[rows, wide + attended_wide :] = jnp.where(
            lanes == 127,
            gain,
            jnp.where(
                lanes == 126, own_gain, left_inner(normed_two_ref[:, rows], logits_ref[...])
            ),
        )
        run_line(2 + 2 * piece, 4 + 2 * piece)
    done = 2 + 2 * pieces

    columns = weights_ref.shape[1]
    middle = columns // 256 * 128
    orders = (
        (slice(0, middle), list(range(levels))),
        (slice(middle, columns), [0] + list(range(levels - 1, 0, -1))),
    )

    def shard(number, lanes):
        return weights_ref.at[pl.ds(pl.multiple_of(number * own, own), own), lanes]

    def numbers(order, level, peer):
        fixed = sum(1 << bit for bit in order[: level + 1])
        base = jnp.bitwise_and(peer, fixed)
        free = order[level + 1 :]
        return [
            base + sum(((i >> place) & 1) << bit for place, bit in enumerate(free))
            for i in range(1 << len(free))
        ]

    def copies(level):
        made = []
        for side, (lanes, order) in enumerate(orders):
            peer = jnp.bitwise_xor(me, 1 << order[level])
            for i, number in enumerate(numbers(order, level, peer)):
                made.append(
                    pltpu.make_async_remote_copy(
                        src_ref=shard(number, lanes),
                        dst_ref=held[level].at[i, :, lanes],
                        send_sem=sends.at[side, level, i],
                        recv_sem=recvs.at[side, level, i],
                        device_id={"dp": peer},
                        device_id_type=MESH,
                    )
                )
        return made

    stops = [6] + [42] * (levels > 1) + [4, 0, 0]
    for level in range(levels):
        for copy in copies(level):
            copy.start()
        until = done + stops[level]
        run_line(done, until)
        done = until
        for copy in copies(level):
            copy.wait_recv()
        for lanes, order in orders:
            for i, number in enumerate(numbers(order, level, me)):
                target = shard(number, lanes)
                target[...] += held[level][i, :, lanes]
    everything = slice(0, columns)
    run_line(done, 2 * STEPS)
    kept = shard(me, everything)
    tail = jnp.transpose(kept[:, wide + attended_wide :])
    query_out[...] = kept[:, : query_out.shape[1]]
    key_out[...] = kept[:, wide - 256 : wide - 256 + key_out.shape[1]]
    value_out[...] = kept[:, wide - 128 : wide - 128 + value_out.shape[1]]
    branch_out[...] = kept[:, wide : wide + branch_out.shape[1]]
    router_out[...] = tail[: router_out.shape[0]]
    gain_out[...] = tail[127:]
    first_gain_out[...] = tail[126:127]
    for level in range(levels):
        for copy in copies(level):
            copy.wait_send()
    for copy in gain_copies:
        copy.wait_send()
    line_end()


def finish(
    n, parts, grad_local, normed_b, grads_wide, branch_b, attended, normed_two_b, grad_logits_b, gain_grad, first_gain_grad,
    wide_q, wide_k, experts, name,
):
    length, width = normed_b.shape
    columns = grads_wide.shape[1] + attended.shape[1] + 128
    full = pl.BlockSpec(memory_space=pltpu.VMEM)
    levels = parts.bit_length() - 1
    own = width // parts
    f32 = jnp.float32
    shapes = [(length, width), (own, wide_q), (own, wide_k), (own, wide_k), (own, wide_q)]
    shapes += [(experts, own), (1, own), (1, own)]
    return pl.pallas_call(
        functools.partial(finish_kernel, n, parts),
        out_shape=[jax.ShapeDtypeStruct(shape, f32) for shape in shapes],
        in_specs=[full] * 9,
        out_specs=[full] * 8,
        scratch_shapes=[
            pltpu.VMEM((width, columns), f32),
            pltpu.VMEM((n, 8, width), f32),
            pltpu.SemaphoreType.DMA((n,)),
            pltpu.SemaphoreType.DMA((n,)),
        ]
        + [pltpu.VMEM((parts >> (level + 1), own, columns), f32) for level in range(levels)]
        + [pltpu.SemaphoreType.DMA((2, levels, parts // 2))] * 2
        + line_scratch([grad_local]),
        compiler_params=pltpu.CompilerParams(
            collective_id=name, has_side_effects=True, vmem_limit_bytes=62 << 20
        ),
        cost_estimate=pl.CostEstimate(
            flops=2 * length * width * columns, bytes_accessed=50 * 10**6, transcendentals=0
        ),
    )(
        grad_local, normed_b, grads_wide, branch_b, attended, normed_two_b, grad_logits_b, gain_grad,
        first_gain_grad,
    )


def place_kernel(shards_ref, *refs):
    gate_out, up_out, down_out = refs[-3:]
    gate_out[0] = shards_ref[0, 0]
    up_out[0] = shards_ref[0, 1]
    rows, hidden = down_out.shape[1], shards_ref.shape[3]
    for piece in range(down_out.shape[2] // hidden):
        down_out[0, :, piece * hidden : (piece + 1) * hidden] = shards_ref[
            0, 2, piece * rows : (piece + 1) * rows, :
        ]


def place_shards(parts, shards, first, experts, before):
    number, unused, rows, hidden = shards.shape
    down_rows = hidden // parts
    width = rows * parts
    shapes = [(experts, rows, hidden), (experts, rows, hidden), (experts, down_rows, width)]
    spec = lambda shape: pl.BlockSpec((1,) + shape[1:], lambda e: (first + e, 0, 0))
    args, extra, aliases = [shards], [], {}
    if before is not None:
        args += list(before)
        extra = [pl.BlockSpec(memory_space=pl.ANY)] * 3
        aliases = {1: 0, 2: 1, 3: 2}
    return pl.pallas_call(
        place_kernel,
        out_shape=[jax.ShapeDtypeStruct(shape, jnp.float32) for shape in shapes],
        grid=(number,),
        in_specs=[pl.BlockSpec((1, 3, rows, hidden), lambda e: (e, 0, 0, 0))] + extra,
        out_specs=[spec(shape) for shape in shapes],
        input_output_aliases=aliases,
        compiler_params=pltpu.CompilerParams(vmem_limit_bytes=60 << 20),
        cost_estimate=pl.CostEstimate(
            flops=0, bytes_accessed=8 * shards.size, transcendentals=0
        ),
    )(*args)


def on_device(
    ring,
    tokens,
    cotangent,
    segment_ids,
    routes,
    attn_gain,
    query_weight,
    key_weight,
    value_weight,
    out_weight,
    ffn_gain,
    router_weight,
    gate_weight,
    up_weight,
    down_weight,
):
    length = tokens.shape[0]
    width = tokens.shape[1]
    segment = segment_ids[0]
    heads_local = query_weight.shape[1] // HEAD
    kv_local = key_weight.shape[1] // HEAD
    group_size = heads_local // kv_local
    experts_all = router_weight.shape[1]
    experts_local = gate_weight.shape[0]
    parts = lax.axis_size("dp")
    opening = doc_openings(segment)
    tables = rope_tables(opening, HEAD)
    query_w, key_w, value_w = (pad_columns(w) for w in (query_weight, key_weight, value_weight))
    out_w = jnp.transpose(pad_columns(jnp.transpose(out_weight)))
    out_all = gather_out_weight(out_weight, parts)
    normed_b, queries, keys, values, attended, logsum = attend_forward(
        tokens, attn_gain, query_w, key_w, value_w, tables, opening, heads_local, group_size
    )
    all_ids = jnp.arange(experts_all, dtype=jnp.int32)
    chosen = jnp.sum((routes[:, :, None] == all_ids[None, None, :]).astype(jnp.int32), axis=1) > 0
    first_expert = lax.axis_index("tensor") * experts_local
    local_ids = first_expert + jnp.arange(experts_local, dtype=jnp.int32)
    picked = jnp.sum((routes[None, :, :] == local_ids[:, None, None]).astype(jnp.int32), axis=2)
    places_in = slot_places(picked)
    counts = jnp.sum(picked, axis=1)
    attended_all = line_gather(attended, ring, 1)
    attended_all = attended_all.reshape(length, ring, attended.shape[1])
    attended_all = attended_all[:, :, : heads_local * HEAD].reshape(length, -1)
    router_w = pad_columns(router_weight)
    middle, normed_two_b, gate_probs = enter_middle(
        attended_all, out_all, tokens, ffn_gain, router_w, pad_columns(chosen.astype(jnp.float32))
    )
    gate_rows = jnp.transpose(lax.dynamic_slice_in_dim(gate_probs, first_expert, experts_local, 1))
    numbers = (max(1, experts_local // 10),)
    numbers += (experts_local - numbers[0],)
    (grads_first,), sums = expert_stage(
        parts, 0, numbers[:1], counts, places_in, gate_rows, normed_two_b, cotangent,
        gate_weight, up_weight, down_weight, None,
    )
    shards_first = lax.psum_scatter(grads_first, "dp", scatter_dimension=2, tiled=True)
    (grads_last,), sums_last = expert_stage(
        parts, numbers[0], numbers[1:], counts, places_in, gate_rows, normed_two_b, cotangent,
        gate_weight, up_weight, down_weight, sums,
    )
    moe_part, grad_normed_part, unused = sums_last
    shards_first, grads_last, grad_normed_part = lax.optimization_barrier(
        (shards_first, grads_last, grad_normed_part)
    )
    shards_last = lax.psum_scatter(grads_last, "dp", scatter_dimension=2, tiled=True)
    grad_gates_local = jnp.concatenate([sums[2], sums_last[2]], 0).reshape(experts_local, length)
    grad_gates_part = lax.dynamic_update_slice_in_dim(
        jnp.zeros((experts_all, length), jnp.float32), grad_gates_local, first_expert, 0
    )
    grad_middle, grad_branch_b, grad_logits_b, grad_ffn_gain = turn_middle(
        ring, grad_normed_part, grad_gates_part, gate_probs, middle, cotangent, ffn_gain, router_w, 2
    )
    grads_wide, grad_normed_local, first_gain, output = attend_backward(
        ring, grad_branch_b, out_w, queries, keys, values, attended, logsum,
        query_w, key_w, value_w, tables, opening, tokens, moe_part, middle, heads_local, group_size, 3,
    )
    wide_q, wide_k = heads_local * HEAD, kv_local * HEAD
    grads_placed = place_shards(parts, shards_first, 0, experts_local, None)
    grads_placed, grads_wide = lax.optimization_barrier((grads_placed, grads_wide))
    grad_normed, *small = finish(
        ring, parts, grad_normed_local, normed_b, grads_wide, grad_branch_b, attended, normed_two_b,
        grad_logits_b, grad_ffn_gain, first_gain, wide_q, wide_k, experts_all, 4,
    )
    grad_tokens, *small = leave_first(grad_normed, tokens, grad_middle, attn_gain, small)
    grad_query, grad_key, grad_value, grad_out, grad_router, grad_ffn_gain, grad_attn_gain = small
    shards_last, grad_tokens = lax.optimization_barrier((shards_last, grad_tokens))
    grad_gate, grad_up, grad_down = place_shards(
        parts, shards_last, numbers[0], experts_local, grads_placed
    )
    return (
        output,
        grad_tokens,
        grad_attn_gain.reshape(-1),
        grad_query,
        grad_key,
        grad_value,
        jnp.transpose(grad_out),
        grad_ffn_gain.reshape(-1),
        jnp.transpose(grad_router),
        grad_gate,
        grad_up,
        grad_down,
    )


def solution(mesh):
    return jax.shard_map(
        functools.partial(on_device, mesh.shape["tensor"]),
        mesh=mesh,
        in_specs=(
            P("dp", None),
            P("dp", None),
            P("dp", None),
            P("dp", None),
            P(),
            P(None, "tensor"),
            P(None, "tensor"),
            P(None, "tensor"),
            P("tensor", None),
            P(),
            P(),
            P("tensor", None, None),
            P("tensor", None, None),
            P("tensor", None, None),
        ),
        out_specs=(
            P("dp", None),
            P("dp", None),
            P("dp"),
            P("dp", "tensor"),
            P("dp", "tensor"),
            P("dp", "tensor"),
            P("tensor", "dp"),
            P("dp"),
            P("dp", None),
            P("tensor", "dp", None),
            P("tensor", "dp", None),
            P("tensor", "dp", None),
        ),
        check_vma=False,
    )
```

```python
import functools

import jax
import jax.numpy as jnp
from jax import lax
from jax.experimental import pallas as pl
from jax.experimental.pallas import tpu as pltpu
from jax.sharding import PartitionSpec as P

MESH = pl.DeviceIdType.MESH

HEAD = 64
CAP = 384


EPSILON = 1e-06
RESIDUAL = 0.22
ATTN_SCALE = 0.015625
ROPE_BASE = 10000.0


def left_inner(first, second):
    return lax.dot_general(
        first, second, (((0,), (0,)), ((), ())), preferred_element_type=jnp.float32
    )


def right_inner(first, second):
    return lax.dot_general(
        first, second, (((1,), (1,)), ((), ())), preferred_element_type=jnp.float32
    )


def doc_openings(segment):
    return jnp.sum((segment[None, :] < segment[:, None]).astype(jnp.int32), axis=1)


def rope_tables(opening, head_size):
    halfway = head_size // 2
    spread = jnp.arange(halfway, dtype=jnp.float32) * (2.0 / head_size)
    inverse = jnp.power(ROPE_BASE, -spread)
    places = jnp.arange(opening.shape[0], dtype=jnp.int32)
    angles = (places - opening).astype(jnp.float32)[:, None] * inverse[None, :]
    cosine, sine = jnp.cos(angles), jnp.sin(angles)
    none = jnp.zeros_like(sine)
    return (
        jnp.concatenate([cosine] * 4, 1),
        jnp.concatenate([-sine, none] * 2, 1),
        jnp.concatenate([none, sine] * 2, 1),
    )


def pad_columns(weight):
    missing = -weight.shape[1] % 128
    return weight if missing == 0 else jnp.pad(weight, ((0, 0), (0, missing)))


def rms_forward(hidden, gain):
    recip = lax.rsqrt(jnp.mean(hidden * hidden, axis=-1, keepdims=True) + EPSILON)
    unit = hidden * recip
    return (unit * gain, unit, recip)


def rms_backward(gradient, unit, recip, gain):
    gain_grad = jnp.sum(gradient * unit, axis=0)
    scaled = gradient * gain
    return (recip * (scaled - unit * jnp.mean(scaled * unit, axis=-1, keepdims=True)), gain_grad)


def slot_places(picked):
    length = picked.shape[1]
    tokens = jnp.arange(length, dtype=jnp.int32)
    earlier = (tokens[:, None] < tokens[None, :]).astype(jnp.bfloat16)
    before = jnp.dot(picked.astype(jnp.bfloat16), earlier, preferred_element_type=jnp.float32)
    return jnp.where(picked > 0, before.astype(jnp.int32), -1)


STEPS = 32
LAG = 2


def line_stages(n, xs, outs, scratch, done=None, whole=0):
    count = len(xs)
    lows, highs = scratch[:count], scratch[count : 2 * count]
    low_recv, high_recv, total_recv, up_send, low_send, high_send = scratch[2 * count :]
    me = lax.axis_index("tensor")
    root = n // 2
    has_low, has_high = me > 0, me < n - 1

    def begin(others=()):
        barrier = pltpu.get_barrier_semaphore()
        for other in others:
            pl.semaphore_signal(barrier, inc=1, device_id=other, device_id_type=MESH)

        @pl.when(has_low)
        def _():
            pl.semaphore_signal(barrier, inc=1, device_id={"tensor": me - 1}, device_id_type=MESH)

        @pl.when(has_high)
        def _():
            pl.semaphore_signal(barrier, inc=1, device_id={"tensor": me + 1}, device_id_type=MESH)

        pl.semaphore_wait(
            barrier, len(others) + has_low.astype(jnp.int32) + has_high.astype(jnp.int32)
        )

    def piece(ref, c):
        rows = ref.shape[0] // STEPS
        return ref.at[pl.ds(pl.multiple_of(c * rows, rows), rows), :]

    cut = count - whole

    def copies(sources, targets, c, send, recv, to, uncut):
        return [
            pltpu.make_async_remote_copy(
                src_ref=source if uncut else piece(source, c),
                dst_ref=target if uncut else piece(target, c),
                send_sem=send.at[i, c],
                recv_sem=recv.at[i, c],
                device_id={"tensor": to},
                device_id_type=MESH,
            )
            for i, (source, target) in enumerate(zip(sources, targets))
            if (i >= cut) == uncut
        ]

    def each(sources, targets, c, send, recv, to, act):
        for copy in copies(sources, targets, c, send, recv, to, False):
            act(copy)
        if whole:

            @pl.when(c == 0)
            def _():
                for copy in copies(sources, targets, 0, send, recv, to, True):
                    act(copy)

    def start(sources, targets, c, send, recv, to):
        each(sources, targets, c, send, recv, to, lambda copy: copy.start())

    def arrived(targets, c, send, recv):
        each(targets, targets, c, send, recv, me, lambda copy: copy.wait_recv())

    def add(c, terms, targets):
        for i, target in enumerate(targets):
            if i < cut:
                piece(target, c)[...] = functools.reduce(
                    jnp.add, [piece(term[i], c)[...] for term in terms]
                )
            else:

                @pl.when(c == 0)
                def _():
                    target[...] = functools.reduce(jnp.add, [term[i][...] for term in terms])

    def reduce_step(c):
        for side, inner, held, recv, to in (
            (me < root, has_low, lows, low_recv, me + 1),
            (me > root, has_high, highs, high_recv, me - 1),
        ):

            @pl.when(side & inner)
            def _():
                arrived(held, c, up_send, recv)
                add(c, (held, xs), held)
                start(held, held, c, up_send, recv, to)

            @pl.when(side & jnp.logical_not(inner))
            def _():
                start(xs, held, c, up_send, recv, to)

        @pl.when(me == root)
        def _():
            arrived(lows, c, up_send, low_recv)
            if root < n - 1:
                arrived(highs, c, up_send, high_recv)
            add(c, (xs, lows, highs) if root < n - 1 else (xs, lows), outs)
            start(outs, outs, c, low_send, total_recv, me - 1)
            if root < n - 1:
                start(outs, outs, c, high_send, total_recv, me + 1)
            if done is not None:
                done(c)

    def total_step(c):
        @pl.when(me != root)
        def _():
            arrived(outs, c, low_send, total_recv)

        @pl.when((me < root) & has_low)
        def _():
            start(outs, outs, c, low_send, total_recv, me - 1)

        @pl.when((me > root) & has_high)
        def _():
            start(outs, outs, c, high_send, total_recv, me + 1)

        if done is not None:

            @pl.when(me != root)
            def _():
                done(c)

    lag = jnp.where(has_low & has_high, LAG, STEPS)

    def step(t, carry):
        @pl.when(t < STEPS)
        def _():
            reduce_step(t)

        @pl.when((t >= lag) & (t - lag < STEPS))
        def _():
            total_step(t - lag)

        return carry

    def finish():
        def drain(c, carry):
            for condition, send in (
                (me != root, up_send),
                ((me <= root) & has_low, low_send),
                ((me >= root) & has_high, high_send),
            ):

                @pl.when(condition)
                def _():
                    each(xs, lows, c, send, low_recv, me, lambda copy: copy.wait_send())

            return carry

        lax.fori_loop(0, STEPS, drain, 0)

    return begin, step, finish


def line_scratch(arrays):
    return [pltpu.VMEM(array.shape, jnp.float32) for array in arrays * 2] + [
        pltpu.SemaphoreType.DMA((len(arrays), STEPS))
    ] * 6


def expert_kernel(
    parts,
    first,
    numbers,
    chained,
    count_ref,
    place_ref,
    gate_ref,
    normed_ref,
    grad_ref,
    gate_w,
    up_w,
    down_w,
    *refs,
):
    if chained:
        moe_in, back_in = refs[:2]
        refs = refs[2:]
    grads_out, refs = refs[: len(numbers)], refs[len(numbers) :]
    moe_out, back_out, gates_out = refs[:3]
    rows_ref, grads_ref, active_ref, gate_in_ref, up_in_ref, weights_ref, sems, out_sems = refs[3:]
    expert = pl.program_id(0)
    filled = count_ref[first + expert]
    length, width = normed_ref.shape
    hidden_size = gate_w.shape[2]
    sizes = (128, 256, CAP)

    def by_size(run):
        low = None
        for rows in sizes:
            fits = filled <= rows if low is None else filled > low
            if low is not None and rows != sizes[-1]:
                fits = fits & (filled <= rows)
            pl.when(fits)(functools.partial(run, rows))
            low = rows

    if chained:
        copy_moe = pltpu.make_async_copy(moe_in, moe_out, sems.at[0])
        copy_back = pltpu.make_async_copy(back_in, back_out, sems.at[1])

        @pl.when(expert == 0)
        def _():
            copy_moe.start()
            copy_back.start()

    else:

        @pl.when(expert == 0)
        def _():
            moe_out[...] = jnp.zeros_like(moe_out)
            back_out[...] = jnp.zeros_like(back_out)

    def slots(rows):
        mask = lax.broadcasted_iota(jnp.int32, (rows, length), 0) == place_ref[0]
        return mask, jnp.where(mask, 1.0, 0.0).astype(jnp.bfloat16)

    def enter(rows):
        mask, picks = slots(rows)
        rows_in = jnp.dot(picks, normed_ref[...], preferred_element_type=jnp.float32).astype(jnp.bfloat16)
        grad_rows = (
            RESIDUAL * jnp.dot(picks, grad_ref[...], preferred_element_type=jnp.float32)
        ).astype(jnp.bfloat16)
        rows_ref[:rows] = rows_in
        grads_ref[:rows] = grad_rows
        gate = jnp.sum(jnp.where(mask, gate_ref[0], 0.0), axis=1, keepdims=True)
        gate_input = jnp.dot(rows_in, gate_w[0], preferred_element_type=jnp.float32)
        up_input = jnp.dot(rows_in, up_w[0], preferred_element_type=jnp.float32)
        grad_act = right_inner(grad_rows, down_w[0])
        sigmoid_val = jax.nn.sigmoid(gate_input)
        silu_out = gate_input * sigmoid_val
        hidden = silu_out * up_input
        active_ref[:rows] = (hidden * gate).astype(jnp.bfloat16)
        column = jnp.sum(grad_act * hidden, axis=1, keepdims=True)
        gates_out[0] = jnp.sum(jnp.where(mask, column, 0.0), axis=0, keepdims=True)
        grad_hidden = grad_act * gate
        gate_in_ref[:rows] = (
            grad_hidden * up_input * sigmoid_val * (1.0 + gate_input * (1.0 - sigmoid_val))
        ).astype(jnp.bfloat16)
        up_in_ref[:rows] = (grad_hidden * silu_out).astype(jnp.bfloat16)

    by_size(enter)
    if chained:

        @pl.when(expert == 0)
        def _():
            copy_moe.wait()
            copy_back.wait()

    def leave(rows):
        column = jnp.transpose(jnp.broadcast_to(place_ref[0], (128, length)))
        column = jnp.concatenate([column] * (rows // 128), 1)
        own = lax.broadcasted_iota(jnp.int32, (length, rows), 1)
        picks = jnp.where(own == column, 1.0, 0.0).astype(jnp.bfloat16)
        moe = jnp.dot(active_ref[:rows], down_w[0], preferred_element_type=jnp.float32)
        moe_out[...] += jnp.dot(
            picks, moe.astype(jnp.bfloat16), preferred_element_type=jnp.float32
        )
        back = right_inner(gate_in_ref[:rows], gate_w[0]) + right_inner(up_in_ref[:rows], up_w[0])
        back_out[...] += jnp.dot(
            picks, back.astype(jnp.bfloat16), preferred_element_type=jnp.float32
        )

    by_size(leave)

    def copies(target, number):
        rows = width // 4
        return [
            pltpu.make_async_copy(
                weights_ref.at[kind, pl.ds(piece * rows, rows), :],
                target.at[number, kind, pl.ds(piece * rows, rows), :],
                out_sems.at[kind, piece],
            )
            for kind in range(3)
            for piece in range(4)
        ]

    @pl.when(expert > 0)
    def _():
        for copy in copies(grads_out[0], 0):
            copy.wait()

    def weigh(rows):
        grads = left_inner(
            rows_ref[:rows], jnp.concatenate([gate_in_ref[:rows], up_in_ref[:rows]], 1)
        )
        weights_ref[0] = grads[:, :hidden_size]
        weights_ref[1] = grads[:, hidden_size:]
        grad_down = left_inner(active_ref[:rows], grads_ref[:rows])
        own = hidden_size // parts
        blocks = width // hidden_size
        for part in range(parts):
            for piece in range(blocks):
                at = (part * blocks + piece) * own
                weights_ref[2, at : at + own, :] = grad_down[
                    part * own : (part + 1) * own, piece * hidden_size : (piece + 1) * hidden_size
                ]

    by_size(weigh)
    start = 0
    for target, number in zip(grads_out, numbers):

        @pl.when((expert >= start) & (expert < start + number))
        def _():
            for copy in copies(target, expert - start):
                copy.start()

        start += number

    @pl.when(expert == pl.num_programs(0) - 1)
    def _():
        for copy in copies(grads_out[0], 0):
            copy.wait()


def expert_stage(parts, first, numbers, counts, places, gate_rows, normed_b, grad_b, gate_w, up_w, down_w, sums):
    number = sum(numbers)
    length, width = normed_b.shape
    hidden = gate_w.shape[2]
    experts = places.shape[0]
    chained = sums is not None
    whole = lambda e, c: (0, 0)
    row_spec = pl.BlockSpec((1, 1, length), lambda e, c: (first + e, 0, 0))
    once = pl.Buffered(1)
    f32, bf16 = jnp.float32, jnp.bfloat16
    in_specs = [
        row_spec,
        row_spec,
        pl.BlockSpec((length, width), whole, pipeline_mode=once),
        pl.BlockSpec((length, width), whole, pipeline_mode=once),
        pl.BlockSpec((1, width, hidden), lambda e, c: (first + e, 0, 0)),
        pl.BlockSpec((1, width, hidden), lambda e, c: (first + e, 0, 0)),
        pl.BlockSpec((1, hidden, width), lambda e, c: (first + e, 0, 0)),
    ]
    args = [
        counts,
        places.reshape(experts, 1, length),
        gate_rows.reshape(experts, 1, length),
        normed_b,
        grad_b,
        gate_w,
        up_w,
        down_w,
    ]
    if chained:
        in_specs += [pl.BlockSpec(memory_space=pl.ANY)] * 2
        args += [sums[0], sums[1]]
    results = pl.pallas_call(
        functools.partial(expert_kernel, parts, first, numbers, chained),
        out_shape=[jax.ShapeDtypeStruct((some, 3, width, hidden), f32) for some in numbers]
        + [
            jax.ShapeDtypeStruct((length, width), f32),
            jax.ShapeDtypeStruct((length, width), f32),
            jax.ShapeDtypeStruct((number, 1, length), f32),
        ],
        grid_spec=pltpu.PrefetchScalarGridSpec(
            num_scalar_prefetch=1,
            grid=(number,),
            in_specs=in_specs,
            out_specs=[pl.BlockSpec(memory_space=pl.ANY)] * len(numbers)
            + [
                pl.BlockSpec((length, width), whole, pipeline_mode=once),
                pl.BlockSpec((length, width), whole, pipeline_mode=once),
                pl.BlockSpec((1, 1, length), lambda e, c: (e, 0, 0)),
            ],
            scratch_shapes=[
                pltpu.VMEM((CAP, width), bf16),
                pltpu.VMEM((CAP, width), bf16),
                pltpu.VMEM((CAP, hidden), bf16),
                pltpu.VMEM((CAP, hidden), bf16),
                pltpu.VMEM((CAP, hidden), bf16),
                pltpu.VMEM((3, width, hidden), f32),
                pltpu.SemaphoreType.DMA((2,)),
                pltpu.SemaphoreType.DMA((3, 4)),
            ],
        ),
        compiler_params=pltpu.CompilerParams(
            dimension_semantics=("arbitrary",), vmem_limit_bytes=63 << 20
        ),
        cost_estimate=pl.CostEstimate(
            flops=number * 8 * 10**9, bytes_accessed=number * 14 * 10**6, transcendentals=0
        ),
    )(*args)
    return results[: len(numbers)], results[len(numbers) :]


PIECES = 16


def line_gather_kernel(n, x_ref, out_ref, blocks_ref, recv, up_send, down_send):
    me = lax.axis_index("tensor")
    has_low, has_high = me > 0, me < n - 1
    barrier = pltpu.get_barrier_semaphore()

    @pl.when(has_low)
    def _():
        pl.semaphore_signal(barrier, inc=1, device_id={"tensor": me - 1}, device_id_type=MESH)

    @pl.when(has_high)
    def _():
        pl.semaphore_signal(barrier, inc=1, device_id={"tensor": me + 1}, device_id_type=MESH)

    blocks_ref[me] = x_ref[...].astype(jnp.float32)
    pl.semaphore_wait(barrier, has_low.astype(jnp.int32) + has_high.astype(jnp.int32))
    rows = x_ref.shape[0] // PIECES

    def copy(block, c, send, to):
        piece = blocks_ref.at[block, pl.ds(pl.multiple_of(c * rows, rows), rows), :]
        return pltpu.make_async_remote_copy(
            src_ref=piece,
            dst_ref=piece,
            send_sem=send.at[block, c],
            recv_sem=recv.at[block, c],
            device_id={"tensor": to},
            device_id_type=MESH,
        )

    for hop in range(n):
        low, high = me - hop, me + hop

        def step(c, carry):
            @pl.when(low >= 0)
            def _():
                if hop > 0:
                    copy(low, c, up_send, me).wait_recv()

                @pl.when(has_high)
                def _():
                    copy(low, c, up_send, me + 1).start()

            @pl.when(high < n)
            def _():
                if hop > 0:
                    copy(high, c, down_send, me).wait_recv()

                @pl.when(has_low)
                def _():
                    copy(high, c, down_send, me - 1).start()

            return carry

        lax.fori_loop(0, PIECES, step, 0)
    wide = x_ref.shape[1]
    for block in range(n):
        out_ref[:, block * wide : (block + 1) * wide] = blocks_ref[block].astype(jnp.bfloat16)
    for hop in range(n):
        low, high = me - hop, me + hop

        def drain(c, carry):
            @pl.when((low >= 0) & has_high)
            def _():
                copy(low, c, up_send, me).wait_send()

            @pl.when((high < n) & has_low)
            def _():
                copy(high, c, down_send, me).wait_send()

            return carry

        lax.fori_loop(0, PIECES, drain, 0)


def line_gather(x, n, name):
    length, wide = x.shape
    full = pl.BlockSpec(memory_space=pltpu.VMEM)
    return pl.pallas_call(
        functools.partial(line_gather_kernel, n),
        out_shape=jax.ShapeDtypeStruct((length, n * wide), jnp.bfloat16),
        in_specs=[full],
        out_specs=full,
        scratch_shapes=[pltpu.VMEM((n, length, wide), jnp.float32)]
        + [pltpu.SemaphoreType.DMA((n, PIECES))] * 3,
        compiler_params=pltpu.CompilerParams(
            collective_id=name, has_side_effects=True, vmem_limit_bytes=32 << 20
        ),
        cost_estimate=pl.CostEstimate(
            flops=0, bytes_accessed=16 * n * x.size, transcendentals=0
        ),
    )(x)


BLOCK = 256


def own_rows_kernel(parts, weight_ref, out_ref):
    rows = out_ref.shape[0]
    first = lax.axis_index("dp") * rows if parts > 1 else 0
    out_ref[...] = weight_ref[pl.ds(pl.multiple_of(first, 16), rows), :].astype(jnp.float32)


def gather_out_weight(out_weight, parts):
    rows, width = out_weight.shape
    ways = parts if rows % (16 * parts) == 0 else 1
    full = pl.BlockSpec(memory_space=pltpu.VMEM)
    own = pl.pallas_call(
        functools.partial(own_rows_kernel, ways),
        out_shape=jax.ShapeDtypeStruct((rows // ways, width), jnp.float32),
        in_specs=[full],
        out_specs=full,
    )(out_weight)
    return ways, lax.all_gather(own, "tensor")


def middle_kernel(
    attended_ref, weight_all_ref, tokens_ref, gain_ref, router_ref, chosen_ref, middle_out, normed_out, gates_out, weight_ref
):
    ways, n, rows, unused = weight_all_ref.shape

    @pl.when(pl.program_id(0) == 0)
    def _():
        for way in range(ways):
            for block in range(n):
                at = (block * ways + way) * rows
                weight_ref[at : at + rows, :] = weight_all_ref[way, block].astype(jnp.bfloat16)

    branch = jnp.dot(attended_ref[...], weight_ref[...], preferred_element_type=jnp.float32)
    middle = tokens_ref[...].astype(jnp.float32) + RESIDUAL * branch
    middle_out[...] = middle
    recip = lax.rsqrt(jnp.mean(middle * middle, axis=1, keepdims=True) + EPSILON)
    normed = (middle * recip * gain_ref[...]).astype(jnp.bfloat16)
    normed_out[...] = normed
    logits = jnp.dot(normed, router_ref[...], preferred_element_type=jnp.float32)
    raised = jnp.where(chosen_ref[...] > 0.0, jnp.exp(logits), 0.0)
    gates_out[...] = raised / jnp.sum(raised, axis=1, keepdims=True)


def enter_middle(attended, weight_all, tokens, gain, router, chosen):
    length, width = tokens.shape
    rows = lambda columns: pl.BlockSpec((BLOCK, columns), lambda i: (i, 0))
    whole = lambda shape: pl.BlockSpec(
        shape, lambda i: (0,) * len(shape), pipeline_mode=pl.Buffered(1)
    )
    experts = router.shape[1]
    return pl.pallas_call(
        middle_kernel,
        out_shape=[
            jax.ShapeDtypeStruct((length, width), jnp.float32),
            jax.ShapeDtypeStruct((length, width), jnp.bfloat16),
            jax.ShapeDtypeStruct((length, experts), jnp.float32),
        ],
        grid=(length // BLOCK,),
        in_specs=[
            rows(attended.shape[1]),
            whole(weight_all.shape),
            rows(width),
            whole((1, width)),
            whole(router.shape),
            rows(experts),
        ],
        out_specs=[rows(width), rows(width), rows(experts)],
        scratch_shapes=[pltpu.VMEM((attended.shape[1], width), jnp.bfloat16)],
        compiler_params=pltpu.CompilerParams(
            dimension_semantics=("arbitrary",), vmem_limit_bytes=48 << 20
        ),
        cost_estimate=pl.CostEstimate(
            flops=2 * length * width * width, bytes_accessed=25 * 10**6, transcendentals=0
        ),
    )(attended, weight_all, tokens, gain.reshape(1, width), router, chosen)


def turn_kernel(
    n,
    part_ref,
    gates_part_ref,
    gates_ref,
    middle_ref,
    cotangent_ref,
    gain_ref,
    router_ref,
    grad_out,
    branch_out,
    logits_out,
    gain_out,
    summed_ref,
    gates_rows_ref,
    grad_gates_ref,
    *line,
):
    length = part_ref.shape[0]
    rows = length // STEPS

    def done(c):
        @pl.when(c == 0)
        def _():
            experts = gates_rows_ref.shape[0]
            empty = jnp.zeros((grad_gates_ref.shape[1] - experts, length), jnp.float32)
            grad_gates_ref[...] = jnp.transpose(
                jnp.concatenate([gates_rows_ref[...], empty], 0)
            )

        own = pl.ds(pl.multiple_of(c * rows, rows), rows)
        gates, grad_gates = gates_ref[own, :], grad_gates_ref[own, :]
        weighted = jnp.sum(gates * grad_gates, axis=1, keepdims=True)
        grad_logits = (gates * (grad_gates - weighted)).astype(jnp.bfloat16)
        logits_out[own, :] = grad_logits
        grad = summed_ref[own, :] + right_inner(grad_logits, router_ref[...])
        middle = middle_ref[own, :]
        recip = lax.rsqrt(jnp.mean(middle * middle, axis=1, keepdims=True) + EPSILON)
        unit = middle * recip
        gain_out[...] += jnp.sum(grad * unit, axis=0, keepdims=True)
        scaled = grad * gain_ref[...]
        back = recip * (scaled - unit * jnp.mean(scaled * unit, axis=1, keepdims=True))
        total = cotangent_ref[own, :].astype(jnp.float32) + back
        grad_out[own, :] = total
        branch_out[own, :] = (RESIDUAL * total).astype(jnp.bfloat16)

    begin, step, finish = line_stages(
        n, [part_ref, gates_part_ref], [summed_ref, gates_rows_ref], line, done, 1
    )
    begin()
    gain_out[...] = jnp.zeros_like(gain_out)
    lax.fori_loop(0, 2 * STEPS, step, 0)
    finish()


def turn_middle(n, part, gates_part, gates, middle, cotangent, gain, router, name):
    length, width = part.shape
    full = pl.BlockSpec(memory_space=pltpu.VMEM)
    f32 = jnp.float32
    return pl.pallas_call(
        functools.partial(turn_kernel, n),
        out_shape=[
            jax.ShapeDtypeStruct((length, width), f32),
            jax.ShapeDtypeStruct((length, width), jnp.bfloat16),
            jax.ShapeDtypeStruct(gates.shape, jnp.bfloat16),
            jax.ShapeDtypeStruct((1, width), f32),
        ],
        in_specs=[full] * 7,
        out_specs=[full] * 4,
        scratch_shapes=[
            pltpu.VMEM(part.shape, f32),
            pltpu.VMEM(gates_part.shape, f32),
            pltpu.VMEM(gates.shape, f32),
        ]
        + line_scratch([part, gates_part]),
        compiler_params=pltpu.CompilerParams(
            collective_id=name, has_side_effects=True, vmem_limit_bytes=58 << 20
        ),
        cost_estimate=pl.CostEstimate(
            flops=40 * length * width, bytes_accessed=60 * 10**6, transcendentals=0
        ),
    )(part, gates_part, gates, middle, cotangent, gain.reshape(1, width), router)


def last_kernel(count, summed_ref, tokens_ref, middle_ref, gain_ref, *refs):
    smalls, out_ref, small_outs = refs[:count], refs[count], refs[count + 1 :]
    hidden = tokens_ref[...].astype(jnp.float32)
    recip = lax.rsqrt(jnp.mean(hidden * hidden, axis=1, keepdims=True) + EPSILON)
    unit = hidden * recip
    scaled = summed_ref[...] * gain_ref[...]
    inner = jnp.mean(scaled * unit, axis=1, keepdims=True)
    out_ref[...] = middle_ref[...] + recip * (scaled - unit * inner)

    @pl.when(pl.program_id(0) == 0)
    def _():
        for small, out in zip(smalls, small_outs):
            out[...] = small[...]


def leave_first(summed, tokens, grad_middle, gain, smalls):
    length, width = tokens.shape
    rows = pl.BlockSpec((BLOCK // 2, width), lambda i: (i, 0))
    whole = lambda shape: pl.BlockSpec(shape, lambda i: (0, 0))
    f32 = jnp.float32
    return pl.pallas_call(
        functools.partial(last_kernel, len(smalls)),
        out_shape=[jax.ShapeDtypeStruct((length, width), f32)]
        + [jax.ShapeDtypeStruct(small.shape, f32) for small in smalls],
        grid=(2 * length // BLOCK,),
        in_specs=[rows, rows, rows, whole((1, width))] + [whole(small.shape) for small in smalls],
        out_specs=[rows] + [whole(small.shape) for small in smalls],
        compiler_params=pltpu.CompilerParams(vmem_limit_bytes=60 << 20),
        cost_estimate=pl.CostEstimate(
            flops=10 * length * width, bytes_accessed=14 * length * width, transcendentals=0
        ),
    )(summed, tokens, grad_middle, gain.reshape(1, width), *smalls)


SPAN = 768
ROWS = 256


def lane_halves(shape):
    return lax.broadcasted_iota(jnp.int32, shape, len(shape) - 1) // HEAD


def select_halves(tile, source, half):
    kept = jnp.where(lane_halves(tile.shape) == source, tile, 0.0)
    return kept if source == half else pltpu.roll(kept, HEAD, 1)


def spread_pairs(tile, target):
    for source in range(2):
        for half in range(2):
            target[2 * source + half] = select_halves(tile, source, half).astype(jnp.bfloat16)


def rope_tile(tile, cosine, sine_low, sine_high):
    return tile * cosine + pltpu.roll(tile, 128 - HEAD // 2, 1) * sine_low + pltpu.roll(
        tile, HEAD // 2, 1
    ) * sine_high


def rope_back_tile(tile, cosine, sine_low, sine_high):
    return (
        tile * cosine
        + pltpu.roll(tile * sine_low, HEAD // 2, 1)
        + pltpu.roll(tile * sine_high, 128 - HEAD // 2, 1)
    )


def window(block):
    first = block * ROWS
    return first, jnp.maximum(first + ROWS - SPAN, 0)


def attend_forward_kernel(
    heads,
    group,
    tokens_ref,
    gain_ref,
    query_w,
    key_w,
    value_w,
    cosine_ref,
    sine_low_ref,
    sine_high_ref,
    opening_ref,
    normed_out,
    query_out,
    key_out,
    value_out,
    attended_out,
    logsum_out,
    key_pairs,
    value_pairs,
    tiles_ref,
):
    tiles, length, unused = query_out.shape
    hidden = tokens_ref[...].astype(jnp.float32)
    recip = lax.rsqrt(jnp.mean(hidden * hidden, axis=1, keepdims=True) + EPSILON)
    normed_out[...] = (hidden * recip * gain_ref[...]).astype(jnp.bfloat16)
    cosine, sine_low, sine_high = cosine_ref[...], sine_low_ref[...], sine_high_ref[...]
    for tile in range(tiles):
        query = jnp.dot(
            normed_out[...],
            query_w[:, tile * 128 : (tile + 1) * 128],
            preferred_element_type=jnp.float32,
        )
        query_out[tile] = rope_tile(query, cosine, sine_low, sine_high).astype(jnp.bfloat16)
    key = rope_tile(
        jnp.dot(normed_out[...], key_w[...], preferred_element_type=jnp.float32),
        cosine,
        sine_low,
        sine_high,
    )
    value = jnp.dot(normed_out[...], value_w[...], preferred_element_type=jnp.float32)
    key_out[...] = key.astype(jnp.bfloat16)
    value_out[...] = value.astype(jnp.bfloat16)
    spread_pairs(key, key_pairs)
    spread_pairs(value, value_pairs)
    blocks = length // ROWS
    tiles_ref[...] = jnp.zeros_like(tiles_ref)

    def unit(step, carry):
        head, block = step // blocks, step % blocks
        tile, half = head // 2, head % 2
        pair = 2 * (head // group) + half
        first, low = window(block)
        rows = pl.ds(pl.multiple_of(first, ROWS), ROWS)
        span = pl.ds(pl.multiple_of(low, ROWS), SPAN)
        scores = right_inner(query_out[tile, rows, :], key_pairs[pair, span, :])
        columns = low + lax.broadcasted_iota(jnp.int32, (ROWS, SPAN), 1)
        own = first + lax.broadcasted_iota(jnp.int32, (ROWS, SPAN), 0)
        allowed = (columns >= opening_ref[rows, :]) & (columns <= own)
        raised = jnp.where(allowed, jnp.exp(ATTN_SCALE * scores), 0.0)
        total = jnp.sum(raised, axis=1, keepdims=True)
        product = jnp.dot(
            raised.astype(jnp.bfloat16), value_pairs[pair, span, :], preferred_element_type=jnp.float32
        )
        tiles_ref[tile, rows, :] += product / total
        wide = jnp.broadcast_to(jnp.log(total), (ROWS, 128))
        logsum_out[head, :, rows] = jnp.transpose(wide)[:1]
        return carry

    lax.fori_loop(0, heads * blocks, unit, 0)
    for tile in range(tiles):
        attended_out[:, tile * 128 : (tile + 1) * 128] = tiles_ref[tile].astype(jnp.bfloat16)


def attend_forward(tokens, gain, query_w, key_w, value_w, tables, opening, heads, group):
    length, width = tokens.shape
    wide = query_w.shape[1]
    tiles = wide // 128
    bf16, f32 = jnp.bfloat16, jnp.float32
    full = pl.BlockSpec(memory_space=pltpu.VMEM)
    return pl.pallas_call(
        functools.partial(attend_forward_kernel, heads, group),
        out_shape=[
            jax.ShapeDtypeStruct((length, width), bf16),
            jax.ShapeDtypeStruct((tiles, length, 128), bf16),
            jax.ShapeDtypeStruct((length, 128), bf16),
            jax.ShapeDtypeStruct((length, 128), bf16),
            jax.ShapeDtypeStruct((length, wide), bf16),
            jax.ShapeDtypeStruct((heads, 1, length), f32),
        ],
        in_specs=[full] * 9,
        out_specs=[full] * 6,
        scratch_shapes=[
            pltpu.VMEM((4, length, 128), bf16),
            pltpu.VMEM((4, length, 128), bf16),
            pltpu.VMEM((tiles, length, 128), f32),
        ],
        compiler_params=pltpu.CompilerParams(vmem_limit_bytes=48 << 20),
        cost_estimate=pl.CostEstimate(
            flops=8 * 10**9, bytes_accessed=12 * 10**6, transcendentals=5 * 10**6
        ),
    )(tokens, gain.reshape(1, width), query_w, key_w, value_w, *tables, opening.reshape(length, 1))


def attend_backward_kernel(
    n,
    heads,
    group,
    branch_ref,
    out_w,
    query_ref,
    key_ref,
    value_ref,
    attended_ref,
    logsum_ref,
    query_w,
    key_w,
    value_w,
    cosine_ref,
    sine_low_ref,
    sine_high_ref,
    opening_ref,
    tokens_ref,
    moe_ref,
    middle_ref,
    grads_out,
    normed_out,
    gain_out,
    output_ref,
    moe_sum,
    middle_rows,
    middle_sems,
    key_pairs,
    value_pairs,
    attend_grads,
    query_grads,
    key_grads,
    value_grads,
    delta_ref,
    *line,
):
    tiles, length, unused = query_ref.shape
    share = length // STEPS

    def share_rows(c):
        return pl.ds(pl.multiple_of(c * share, share), share)

    def fetch(c):
        slot = lax.rem(c, 2)
        return pltpu.make_async_copy(
            middle_ref.at[share_rows(c), :], middle_rows.at[slot], middle_sems.at[slot]
        )

    def done(c):
        fetch(c).wait()

        @pl.when(c + 1 < STEPS)
        def _():
            fetch(c + 1).start()

        total = middle_rows[lax.rem(c, 2)] + RESIDUAL * moe_sum[share_rows(c), :]
        output_ref[share_rows(c), :] = total.astype(jnp.bfloat16)

    line_start, line_step, line_end = line_stages(n, [moe_ref], [moe_sum], line, done)
    line_start()
    fetch(jnp.int32(0)).start()
    blocks = length // ROWS
    units = heads * blocks
    taken = 0

    def run_line(steps):
        nonlocal taken
        until = min(taken + steps, 2 * STEPS)
        lax.fori_loop(taken, until, line_step, 0)
        taken = until

    run_line(2)
    spread_pairs(key_ref[...].astype(jnp.float32), key_pairs)
    spread_pairs(value_ref[...].astype(jnp.float32), value_pairs)
    halves = (
        lax.broadcasted_iota(jnp.int32, (8, 128), 0) == lane_halves((8, 128))
    ).astype(jnp.float32)
    for tile in range(tiles):
        lanes = slice(tile * 128, (tile + 1) * 128)
        grad = right_inner(branch_ref[...], out_w[lanes, :]).astype(jnp.bfloat16)
        attend_grads[tile] = grad
        products = grad.astype(jnp.float32) * attended_ref[:, lanes].astype(jnp.float32)
        sums = lax.dot_general(
            halves,
            products,
            (((1,), (1,)), ((), ())),
            precision=lax.Precision.HIGHEST,
            preferred_element_type=jnp.float32,
        )
        delta_ref[2 * tile] = sums[0:1]
        delta_ref[2 * tile + 1] = sums[1:2]
        run_line(2)
    query_grads[...] = jnp.zeros_like(query_grads)
    key_grads[...] = jnp.zeros_like(key_grads)
    value_grads[...] = jnp.zeros_like(value_grads)
    before, each = taken, (2 * STEPS - 8 - taken) // units
    taken += units * each

    def unit(step, carry):
        lax.fori_loop(before + step * each, before + step * each + each, line_step, 0)
        head, block = step // blocks, step % blocks
        tile, half = head // 2, head % 2
        pair = 2 * (head // group) + half
        first, low = window(block)
        rows = pl.ds(pl.multiple_of(first, ROWS), ROWS)
        span = pl.ds(pl.multiple_of(low, ROWS), SPAN)
        keys = key_pairs[pair, span, :]
        query = query_ref[tile, rows, :]
        grad = attend_grads[tile, rows, :]
        scores = right_inner(keys, query)
        columns = low + lax.broadcasted_iota(jnp.int32, (SPAN, ROWS), 0)
        own = first + lax.broadcasted_iota(jnp.int32, (SPAN, ROWS), 1)
        allowed = (columns >= opening_ref[:, rows]) & (columns <= own)
        probs = jnp.where(
            allowed, jnp.exp(ATTN_SCALE * scores - logsum_ref[head, :, rows]), 0.0
        )
        grad_probs = right_inner(value_pairs[pair, span, :], grad)
        grad_scores = (probs * (grad_probs - delta_ref[head, :, rows])).astype(jnp.bfloat16)
        value_grads[pair, span, :] += jnp.dot(
            probs.astype(jnp.bfloat16), grad, preferred_element_type=jnp.float32
        )
        key_grads[pair, span, :] += jnp.dot(
            grad_scores, query, preferred_element_type=jnp.float32
        )
        query_grads[tile, rows, :] += left_inner(grad_scores, keys)
        return carry

    lax.fori_loop(0, units, unit, 0)
    cosine, sine_low, sine_high = cosine_ref[...], sine_low_ref[...], sine_high_ref[...]
    wide = tiles * 128
    for tile in range(tiles):
        grads_out[:, tile * 128 : (tile + 1) * 128] = rope_back_tile(
            ATTN_SCALE * query_grads[tile], cosine, sine_low, sine_high
        ).astype(jnp.bfloat16)
    totals = []
    for grads in (key_grads, value_grads):
        totals.append(
            sum(
                select_halves(grads[2 * source + half], half, source)
                for source in range(2)
                for half in range(2)
            )
        )
    grads_out[:, wide : wide + 128] = rope_back_tile(
        ATTN_SCALE * totals[0], cosine, sine_low, sine_high
    ).astype(jnp.bfloat16)
    grads_out[:, wide + 128 : wide + 256] = totals[1].astype(jnp.bfloat16)
    gain_sum = jnp.zeros((1, normed_out.shape[1]), jnp.float32)
    for block in range(blocks):
        rows = slice(block * ROWS, (block + 1) * ROWS)
        normed = (
            right_inner(grads_out[rows, :wide], query_w[...])
            + right_inner(grads_out[rows, wide : wide + 128], key_w[...])
            + right_inner(grads_out[rows, wide + 128 :], value_w[...])
        )
        normed_out[rows, :] = normed
        hidden = tokens_ref[rows, :].astype(jnp.float32)
        recip = lax.rsqrt(jnp.mean(hidden * hidden, axis=1, keepdims=True) + EPSILON)
        gain_sum += jnp.sum(normed * (hidden * recip), axis=0, keepdims=True)
        run_line(2)
    gain_out[...] = jnp.broadcast_to(gain_sum, gain_out.shape)
    run_line(2 * STEPS)
    line_end()


def attend_backward(
    n, branch, out_w, query, key, value, attended, logsum, query_w, key_w, value_w, tables, opening, tokens, moe, middle,
    heads, group, name,
):
    length, width = branch.shape
    tiles = query.shape[0]
    wide = tiles * 128
    bf16, f32 = jnp.bfloat16, jnp.float32
    full = pl.BlockSpec(memory_space=pltpu.VMEM)
    return pl.pallas_call(
        functools.partial(attend_backward_kernel, n, heads, group),
        out_shape=[
            jax.ShapeDtypeStruct((length, wide + 256), bf16),
            jax.ShapeDtypeStruct((length, width), f32),
            jax.ShapeDtypeStruct((8, width), f32),
            jax.ShapeDtypeStruct((length, width), bf16),
        ],
        in_specs=[full] * 16 + [pl.BlockSpec(memory_space=pl.ANY)],
        out_specs=[full] * 4,
        scratch_shapes=[
            pltpu.VMEM((length, width), f32),
            pltpu.VMEM((2, length // STEPS, width), f32),
            pltpu.SemaphoreType.DMA((2,)),
            pltpu.VMEM((4, length, 128), bf16),
            pltpu.VMEM((4, length, 128), bf16),
            pltpu.VMEM((tiles, length, 128), bf16),
            pltpu.VMEM((tiles, length, 128), f32),
            pltpu.VMEM((4, length, 128), f32),
            pltpu.VMEM((4, length, 128), f32),
            pltpu.VMEM((2 * tiles, 1, length), f32),
        ]
        + line_scratch([moe]),
        compiler_params=pltpu.CompilerParams(
            collective_id=name, has_side_effects=True, vmem_limit_bytes=63 << 20
        ),
        cost_estimate=pl.CostEstimate(
            flops=12 * 10**9, bytes_accessed=30 * 10**6, transcendentals=5 * 10**6
        ),
    )(
        branch, out_w, query, key, value, attended, logsum, query_w, key_w, value_w, *tables,
        opening.reshape(1, length), tokens, moe, middle,
    )


def finish_kernel(
    n,
    parts,
    local_ref,
    normed_ref,
    grads_ref,
    branch_ref,
    attended_ref,
    normed_two_ref,
    logits_ref,
    gain_ref,
    first_gain_ref,
    normed_out,
    query_out,
    key_out,
    value_out,
    branch_out,
    router_out,
    gain_out,
    first_gain_out,
    weights_ref,
    gains_ref,
    gain_send,
    gain_recv,
    *scratch,
):
    levels = parts.bit_length() - 1
    held = scratch[:levels]
    sends, recvs = scratch[levels : levels + 2]
    line_start, line_step, line_end = line_stages(n, [local_ref], [normed_out], scratch[levels + 2 :])
    me = lax.axis_index("dp")
    width = normed_ref.shape[1]
    own = width // parts
    wide, attended_wide = grads_ref.shape[1], attended_ref.shape[1]
    mine = lax.axis_index("tensor")
    line_start(
        [{"dp": jnp.bitwise_xor(me, 1 << level)} for level in range(levels)]
        + [{"tensor": lax.rem(mine + ahead, n)} for ahead in range(1, n)]
    )

    def run_line(first, last):
        lax.fori_loop(first, last, line_step, 0)

    gain_copies = [
        pltpu.make_async_remote_copy(
            src_ref=first_gain_ref,
            dst_ref=gains_ref.at[ahead],
            send_sem=gain_send.at[ahead],
            recv_sem=gain_recv.at[ahead],
            device_id={"tensor": lax.rem(mine + ahead, n)},
            device_id_type=MESH,
        )
        for ahead in range(1, n)
    ]
    for copy in gain_copies:
        copy.start()
    run_line(0, 2)
    first_gain = first_gain_ref[:1]
    for ahead, copy in enumerate(gain_copies, 1):
        copy.wait_recv()
        first_gain = first_gain + gains_ref[ahead, :1]
    pieces = 4
    block = width // pieces
    for piece in range(pieces):
        rows = slice(piece * block, (piece + 1) * block)
        weights_ref[rows, :wide] = left_inner(normed_ref[:, rows], grads_ref[...])
        weights_ref[rows, wide : wide + attended_wide] = left_inner(
            branch_ref[:, rows], attended_ref[...]
        )
        gain = jnp.transpose(jnp.broadcast_to(gain_ref[:, rows], (128, block)))
        own_gain = jnp.transpose(jnp.broadcast_to(first_gain[:, rows], (128, block)))
        lanes = lax.broadcasted_iota(jnp.int32, (block, 128), 1)
        weights_ref[rows, wide + attended_wide :] = jnp.where(
            lanes == 127,
            gain,
            jnp.where(
                lanes == 126, own_gain, left_inner(normed_two_ref[:, rows], logits_ref[...])
            ),
        )
        run_line(2 + 2 * piece, 4 + 2 * piece)
    done = 2 + 2 * pieces

    columns = weights_ref.shape[1]
    middle = columns // 256 * 128
    orders = (
        (slice(0, middle), list(range(levels))),
        (slice(middle, columns), [0] + list(range(levels - 1, 0, -1))),
    )

    def shard(number, lanes):
        return weights_ref.at[pl.ds(pl.multiple_of(number * own, own), own), lanes]

    def numbers(order, level, peer):
        fixed = sum(1 << bit for bit in order[: level + 1])
        base = jnp.bitwise_and(peer, fixed)
        free = order[level + 1 :]
        return [
            base + sum(((i >> place) & 1) << bit for place, bit in enumerate(free))
            for i in range(1 << len(free))
        ]

    def copies(level):
        made = []
        for side, (lanes, order) in enumerate(orders):
            peer = jnp.bitwise_xor(me, 1 << order[level])
            for i, number in enumerate(numbers(order, level, peer)):
                made.append(
                    pltpu.make_async_remote_copy(
                        src_ref=shard(number, lanes),
                        dst_ref=held[level].at[i, :, lanes],
                        send_sem=sends.at[side, level, i],
                        recv_sem=recvs.at[side, level, i],
                        device_id={"dp": peer},
                        device_id_type=MESH,
                    )
                )
        return made

    stops = [6] + [42] * (levels > 1) + [4, 0, 0]
    for level in range(levels):
        for copy in copies(level):
            copy.start()
        until = done + stops[level]
        run_line(done, until)
        done = until
        for copy in copies(level):
            copy.wait_recv()
        for lanes, order in orders:
            for i, number in enumerate(numbers(order, level, me)):
                target = shard(number, lanes)
                target[...] += held[level][i, :, lanes]
    everything = slice(0, columns)
    run_line(done, 2 * STEPS)
    kept = shard(me, everything)
    tail = jnp.transpose(kept[:, wide + attended_wide :])
    query_out[...] = kept[:, : query_out.shape[1]]
    key_out[...] = kept[:, wide - 256 : wide - 256 + key_out.shape[1]]
    value_out[...] = kept[:, wide - 128 : wide - 128 + value_out.shape[1]]
    branch_out[...] = kept[:, wide : wide + branch_out.shape[1]]
    router_out[...] = tail[: router_out.shape[0]]
    gain_out[...] = tail[127:]
    first_gain_out[...] = tail[126:127]
    for level in range(levels):
        for copy in copies(level):
            copy.wait_send()
    for copy in gain_copies:
        copy.wait_send()
    line_end()


def finish(
    n, parts, grad_local, normed_b, grads_wide, branch_b, attended, normed_two_b, grad_logits_b, gain_grad, first_gain_grad,
    wide_q, wide_k, experts, name,
):
    length, width = normed_b.shape
    columns = grads_wide.shape[1] + attended.shape[1] + 128
    full = pl.BlockSpec(memory_space=pltpu.VMEM)
    levels = parts.bit_length() - 1
    own = width // parts
    f32 = jnp.float32
    shapes = [(length, width), (own, wide_q), (own, wide_k), (own, wide_k), (own, wide_q)]
    shapes += [(experts, own), (1, own), (1, own)]
    return pl.pallas_call(
        functools.partial(finish_kernel, n, parts),
        out_shape=[jax.ShapeDtypeStruct(shape, f32) for shape in shapes],
        in_specs=[full] * 9,
        out_specs=[full] * 8,
        scratch_shapes=[
            pltpu.VMEM((width, columns), f32),
            pltpu.VMEM((n, 8, width), f32),
            pltpu.SemaphoreType.DMA((n,)),
            pltpu.SemaphoreType.DMA((n,)),
        ]
        + [pltpu.VMEM((parts >> (level + 1), own, columns), f32) for level in range(levels)]
        + [pltpu.SemaphoreType.DMA((2, levels, parts // 2))] * 2
        + line_scratch([grad_local]),
        compiler_params=pltpu.CompilerParams(
            collective_id=name, has_side_effects=True, vmem_limit_bytes=62 << 20
        ),
        cost_estimate=pl.CostEstimate(
            flops=2 * length * width * columns, bytes_accessed=50 * 10**6, transcendentals=0
        ),
    )(
        grad_local, normed_b, grads_wide, branch_b, attended, normed_two_b, grad_logits_b, gain_grad,
        first_gain_grad,
    )


def place_kernel(shards_ref, *refs):
    gate_out, up_out, down_out = refs[-3:]
    gate_out[0] = shards_ref[0, 0]
    up_out[0] = shards_ref[0, 1]
    rows, hidden = down_out.shape[1], shards_ref.shape[3]
    for piece in range(down_out.shape[2] // hidden):
        down_out[0, :, piece * hidden : (piece + 1) * hidden] = shards_ref[
            0, 2, piece * rows : (piece + 1) * rows, :
        ]


def place_shards(parts, shards, first, experts, before):
    number, unused, rows, hidden = shards.shape
    down_rows = hidden // parts
    width = rows * parts
    shapes = [(experts, rows, hidden), (experts, rows, hidden), (experts, down_rows, width)]
    spec = lambda shape: pl.BlockSpec((1,) + shape[1:], lambda e: (first + e, 0, 0))
    args, extra, aliases = [shards], [], {}
    if before is not None:
        args += list(before)
        extra = [pl.BlockSpec(memory_space=pl.ANY)] * 3
        aliases = {1: 0, 2: 1, 3: 2}
    return pl.pallas_call(
        place_kernel,
        out_shape=[jax.ShapeDtypeStruct(shape, jnp.float32) for shape in shapes],
        grid=(number,),
        in_specs=[pl.BlockSpec((1, 3, rows, hidden), lambda e: (e, 0, 0, 0))] + extra,
        out_specs=[spec(shape) for shape in shapes],
        input_output_aliases=aliases,
        compiler_params=pltpu.CompilerParams(vmem_limit_bytes=60 << 20),
        cost_estimate=pl.CostEstimate(
            flops=0, bytes_accessed=8 * shards.size, transcendentals=0
        ),
    )(*args)


def on_device(
    ring,
    tokens,
    cotangent,
    segment_ids,
    routes,
    attn_gain,
    query_weight,
    key_weight,
    value_weight,
    out_weight,
    ffn_gain,
    router_weight,
    gate_weight,
    up_weight,
    down_weight,
):
    length = tokens.shape[0]
    width = tokens.shape[1]
    segment = segment_ids[0]
    heads_local = query_weight.shape[1] // HEAD
    kv_local = key_weight.shape[1] // HEAD
    group_size = heads_local // kv_local
    experts_all = router_weight.shape[1]
    experts_local = gate_weight.shape[0]
    parts = lax.axis_size("dp")
    opening = doc_openings(segment)
    tables = rope_tables(opening, HEAD)
    query_w, key_w, value_w = (pad_columns(w) for w in (query_weight, key_weight, value_weight))
    out_w = jnp.transpose(pad_columns(jnp.transpose(out_weight)))
    ways, out_rows = gather_out_weight(out_weight, parts)
    normed_b, queries, keys, values, attended, logsum = attend_forward(
        tokens, attn_gain, query_w, key_w, value_w, tables, opening, heads_local, group_size
    )
    all_ids = jnp.arange(experts_all, dtype=jnp.int32)
    chosen = jnp.sum((routes[:, :, None] == all_ids[None, None, :]).astype(jnp.int32), axis=1) > 0
    first_expert = lax.axis_index("tensor") * experts_local
    local_ids = first_expert + jnp.arange(experts_local, dtype=jnp.int32)
    picked = jnp.sum((routes[None, :, :] == local_ids[:, None, None]).astype(jnp.int32), axis=2)
    places_in = slot_places(picked)
    counts = jnp.sum(picked, axis=1)
    out_rows, attended = lax.optimization_barrier((out_rows, attended))
    out_all = lax.all_gather(out_rows, "dp") if ways > 1 else out_rows[None]
    attended_all = line_gather(attended, ring, 1)
    attended_all = attended_all.reshape(length, ring, attended.shape[1])
    attended_all = attended_all[:, :, : heads_local * HEAD].reshape(length, -1)
    router_w = pad_columns(router_weight)
    middle, normed_two_b, gate_probs = enter_middle(
        attended_all, out_all, tokens, ffn_gain, router_w, pad_columns(chosen.astype(jnp.float32))
    )
    gate_rows = jnp.transpose(lax.dynamic_slice_in_dim(gate_probs, first_expert, experts_local, 1))
    numbers = (max(1, experts_local // 10),)
    numbers += (experts_local - numbers[0],)
    (grads_first,), sums = expert_stage(
        parts, 0, numbers[:1], counts, places_in, gate_rows, normed_two_b, cotangent,
        gate_weight, up_weight, down_weight, None,
    )
    shards_first = lax.psum_scatter(grads_first, "dp", scatter_dimension=2, tiled=True)
    (grads_last,), sums_last = expert_stage(
        parts, numbers[0], numbers[1:], counts, places_in, gate_rows, normed_two_b, cotangent,
        gate_weight, up_weight, down_weight, sums,
    )
    moe_part, grad_normed_part, unused = sums_last
    shards_first, grads_last, grad_normed_part = lax.optimization_barrier(
        (shards_first, grads_last, grad_normed_part)
    )
    shards_last = lax.psum_scatter(grads_last, "dp", scatter_dimension=2, tiled=True)
    grad_gates_local = jnp.concatenate([sums[2], sums_last[2]], 0).reshape(experts_local, length)
    grad_gates_part = lax.dynamic_update_slice_in_dim(
        jnp.zeros((experts_all, length), jnp.float32), grad_gates_local, first_expert, 0
    )
    grad_middle, grad_branch_b, grad_logits_b, grad_ffn_gain = turn_middle(
        ring, grad_normed_part, grad_gates_part, gate_probs, middle, cotangent, ffn_gain, router_w, 2
    )
    grads_wide, grad_normed_local, first_gain, output = attend_backward(
        ring, grad_branch_b, out_w, queries, keys, values, attended, logsum,
        query_w, key_w, value_w, tables, opening, tokens, moe_part, middle, heads_local, group_size, 3,
    )
    wide_q, wide_k = heads_local * HEAD, kv_local * HEAD
    grads_placed = place_shards(parts, shards_first, 0, experts_local, None)
    grads_placed, grads_wide = lax.optimization_barrier((grads_placed, grads_wide))
    grad_normed, *small = finish(
        ring, parts, grad_normed_local, normed_b, grads_wide, grad_branch_b, attended, normed_two_b,
        grad_logits_b, grad_ffn_gain, first_gain, wide_q, wide_k, experts_all, 4,
    )
    grad_tokens, *small = leave_first(grad_normed, tokens, grad_middle, attn_gain, small)
    grad_query, grad_key, grad_value, grad_out, grad_router, grad_ffn_gain, grad_attn_gain = small
    shards_last, grad_tokens = lax.optimization_barrier((shards_last, grad_tokens))
    grad_gate, grad_up, grad_down = place_shards(
        parts, shards_last, numbers[0], experts_local, grads_placed
    )
    return (
        output,
        grad_tokens,
        grad_attn_gain.reshape(-1),
        grad_query,
        grad_key,
        grad_value,
        jnp.transpose(grad_out),
        grad_ffn_gain.reshape(-1),
        jnp.transpose(grad_router),
        grad_gate,
        grad_up,
        grad_down,
    )


def solution(mesh):
    return jax.shard_map(
        functools.partial(on_device, mesh.shape["tensor"]),
        mesh=mesh,
        in_specs=(
            P("dp", None),
            P("dp", None),
            P("dp", None),
            P("dp", None),
            P(),
            P(None, "tensor"),
            P(None, "tensor"),
            P(None, "tensor"),
            P("tensor", None),
            P(),
            P(),
            P("tensor", None, None),
            P("tensor", None, None),
            P("tensor", None, None),
        ),
        out_specs=(
            P("dp", None),
            P("dp", None),
            P("dp"),
            P("dp", "tensor"),
            P("dp", "tensor"),
            P("dp", "tensor"),
            P("tensor", "dp"),
            P("dp"),
            P("dp", None),
            P("tensor", "dp", None),
            P("tensor", "dp", None),
            P("tensor", "dp", None),
        ),
        check_vma=False,
    )
```

```python
import functools

import jax
import jax.numpy as jnp
from jax import lax
from jax.experimental import pallas as pl
from jax.experimental.pallas import tpu as pltpu
from jax.sharding import PartitionSpec as P

MESH = pl.DeviceIdType.MESH

HEAD = 64
CAP = 384


EPSILON = 1e-06
RESIDUAL = 0.22
ATTN_SCALE = 0.015625
ROPE_BASE = 10000.0


def left_inner(first, second):
    return lax.dot_general(
        first, second, (((0,), (0,)), ((), ())), preferred_element_type=jnp.float32
    )


def right_inner(first, second):
    return lax.dot_general(
        first, second, (((1,), (1,)), ((), ())), preferred_element_type=jnp.float32
    )


def doc_openings(segment):
    return jnp.sum((segment[None, :] < segment[:, None]).astype(jnp.int32), axis=1)


def rope_tables(opening, head_size):
    halfway = head_size // 2
    spread = jnp.arange(halfway, dtype=jnp.float32) * (2.0 / head_size)
    inverse = jnp.power(ROPE_BASE, -spread)
    places = jnp.arange(opening.shape[0], dtype=jnp.int32)
    angles = (places - opening).astype(jnp.float32)[:, None] * inverse[None, :]
    cosine, sine = jnp.cos(angles), jnp.sin(angles)
    none = jnp.zeros_like(sine)
    return (
        jnp.concatenate([cosine] * 4, 1),
        jnp.concatenate([-sine, none] * 2, 1),
        jnp.concatenate([none, sine] * 2, 1),
    )


def pad_columns(weight):
    missing = -weight.shape[1] % 128
    return weight if missing == 0 else jnp.pad(weight, ((0, 0), (0, missing)))


def rms_forward(hidden, gain):
    recip = lax.rsqrt(jnp.mean(hidden * hidden, axis=-1, keepdims=True) + EPSILON)
    unit = hidden * recip
    return (unit * gain, unit, recip)


def rms_backward(gradient, unit, recip, gain):
    gain_grad = jnp.sum(gradient * unit, axis=0)
    scaled = gradient * gain
    return (recip * (scaled - unit * jnp.mean(scaled * unit, axis=-1, keepdims=True)), gain_grad)


def slot_places(picked):
    length = picked.shape[1]
    tokens = jnp.arange(length, dtype=jnp.int32)
    earlier = (tokens[:, None] < tokens[None, :]).astype(jnp.bfloat16)
    before = jnp.dot(picked.astype(jnp.bfloat16), earlier, preferred_element_type=jnp.float32)
    return jnp.where(picked > 0, before.astype(jnp.int32), -1)


STEPS = 32
LAG = 2


def line_stages(n, xs, outs, scratch, done=None, whole=0):
    count = len(xs)
    lows, highs = scratch[:count], scratch[count : 2 * count]
    low_recv, high_recv, total_recv, up_send, low_send, high_send = scratch[2 * count :]
    me = lax.axis_index("tensor")
    root = n // 2
    has_low, has_high = me > 0, me < n - 1

    def begin(others=()):
        barrier = pltpu.get_barrier_semaphore()
        for other in others:
            pl.semaphore_signal(barrier, inc=1, device_id=other, device_id_type=MESH)

        @pl.when(has_low)
        def _():
            pl.semaphore_signal(barrier, inc=1, device_id={"tensor": me - 1}, device_id_type=MESH)

        @pl.when(has_high)
        def _():
            pl.semaphore_signal(barrier, inc=1, device_id={"tensor": me + 1}, device_id_type=MESH)

        pl.semaphore_wait(
            barrier, len(others) + has_low.astype(jnp.int32) + has_high.astype(jnp.int32)
        )

    def piece(ref, c):
        rows = ref.shape[0] // STEPS
        return ref.at[pl.ds(pl.multiple_of(c * rows, rows), rows), :]

    cut = count - whole

    def copies(sources, targets, c, send, recv, to, uncut):
        return [
            pltpu.make_async_remote_copy(
                src_ref=source if uncut else piece(source, c),
                dst_ref=target if uncut else piece(target, c),
                send_sem=send.at[i, c],
                recv_sem=recv.at[i, c],
                device_id={"tensor": to},
                device_id_type=MESH,
            )
            for i, (source, target) in enumerate(zip(sources, targets))
            if (i >= cut) == uncut
        ]

    def each(sources, targets, c, send, recv, to, act):
        for copy in copies(sources, targets, c, send, recv, to, False):
            act(copy)
        if whole:

            @pl.when(c == 0)
            def _():
                for copy in copies(sources, targets, 0, send, recv, to, True):
                    act(copy)

    def start(sources, targets, c, send, recv, to):
        each(sources, targets, c, send, recv, to, lambda copy: copy.start())

    def arrived(targets, c, send, recv):
        each(targets, targets, c, send, recv, me, lambda copy: copy.wait_recv())

    def add(c, terms, targets):
        for i, target in enumerate(targets):
            if i < cut:
                piece(target, c)[...] = functools.reduce(
                    jnp.add, [piece(term[i], c)[...] for term in terms]
                )
            else:

                @pl.when(c == 0)
                def _():
                    target[...] = functools.reduce(jnp.add, [term[i][...] for term in terms])

    def reduce_step(c):
        for side, inner, held, recv, to in (
            (me < root, has_low, lows, low_recv, me + 1),
            (me > root, has_high, highs, high_recv, me - 1),
        ):

            @pl.when(side & inner)
            def _():
                arrived(held, c, up_send, recv)
                add(c, (held, xs), held)
                start(held, held, c, up_send, recv, to)

            @pl.when(side & jnp.logical_not(inner))
            def _():
                start(xs, held, c, up_send, recv, to)

        @pl.when(me == root)
        def _():
            arrived(lows, c, up_send, low_recv)
            if root < n - 1:
                arrived(highs, c, up_send, high_recv)
            add(c, (xs, lows, highs) if root < n - 1 else (xs, lows), outs)
            start(outs, outs, c, low_send, total_recv, me - 1)
            if root < n - 1:
                start(outs, outs, c, high_send, total_recv, me + 1)
            if done is not None:
                done(c)

    def total_step(c):
        @pl.when(me != root)
        def _():
            arrived(outs, c, low_send, total_recv)

        @pl.when((me < root) & has_low)
        def _():
            start(outs, outs, c, low_send, total_recv, me - 1)

        @pl.when((me > root) & has_high)
        def _():
            start(outs, outs, c, high_send, total_recv, me + 1)

        if done is not None:

            @pl.when(me != root)
            def _():
                done(c)

    lag = jnp.where(has_low & has_high, LAG, STEPS)

    def step(t, carry):
        @pl.when(t < STEPS)
        def _():
            reduce_step(t)

        @pl.when((t >= lag) & (t - lag < STEPS))
        def _():
            total_step(t - lag)

        return carry

    def finish():
        def drain(c, carry):
            for condition, send in (
                (me != root, up_send),
                ((me <= root) & has_low, low_send),
                ((me >= root) & has_high, high_send),
            ):

                @pl.when(condition)
                def _():
                    each(xs, lows, c, send, low_recv, me, lambda copy: copy.wait_send())

            return carry

        lax.fori_loop(0, STEPS, drain, 0)

    return begin, step, finish


def line_scratch(arrays):
    return [pltpu.VMEM(array.shape, jnp.float32) for array in arrays * 2] + [
        pltpu.SemaphoreType.DMA((len(arrays), STEPS))
    ] * 6


def expert_kernel(
    parts,
    first,
    numbers,
    chained,
    count_ref,
    place_ref,
    gate_ref,
    normed_ref,
    grad_ref,
    gate_w,
    up_w,
    down_w,
    *refs,
):
    if chained:
        moe_in, back_in = refs[:2]
        refs = refs[2:]
    grads_out, refs = refs[: len(numbers)], refs[len(numbers) :]
    moe_final, back_final, gates_out = refs[:3]
    moe_out, back_out, rows_ref, grads_ref, active_ref, gate_in_ref, up_in_ref, weights_ref = refs[3:11]
    sems, out_sems = refs[11:]
    expert = pl.program_id(0)
    filled = count_ref[first + expert]
    length, width = normed_ref.shape
    hidden_size = gate_w.shape[2]
    sizes = (128, 256, CAP)

    def by_size(run):
        low = None
        for rows in sizes:
            fits = filled <= rows if low is None else filled > low
            if low is not None and rows != sizes[-1]:
                fits = fits & (filled <= rows)
            pl.when(fits)(functools.partial(run, rows))
            low = rows

    def sum_copies(sources, targets):
        rows = length // 4
        return [
            pltpu.make_async_copy(
                source.at[pl.ds(piece * rows, rows), :],
                target.at[pl.ds(piece * rows, rows), :],
                sems.at[i, piece],
            )
            for i, (source, target) in enumerate(zip(sources, targets))
            for piece in range(4)
        ]

    if chained:
        entering = sum_copies((moe_in, back_in), (moe_out, back_out))

        @pl.when(expert == 0)
        def _():
            for copy in entering:
                copy.start()

    else:

        @pl.when(expert == 0)
        def _():
            moe_out[...] = jnp.zeros_like(moe_out)
            back_out[...] = jnp.zeros_like(back_out)

    def slots(rows):
        mask = lax.broadcasted_iota(jnp.int32, (rows, length), 0) == place_ref[0]
        return mask, jnp.where(mask, 1.0, 0.0).astype(jnp.bfloat16)

    def enter(rows):
        mask, picks = slots(rows)
        rows_in = jnp.dot(picks, normed_ref[...], preferred_element_type=jnp.float32).astype(jnp.bfloat16)
        grad_rows = (
            RESIDUAL * jnp.dot(picks, grad_ref[...], preferred_element_type=jnp.float32)
        ).astype(jnp.bfloat16)
        rows_ref[:rows] = rows_in
        grads_ref[:rows] = grad_rows
        gate = jnp.sum(jnp.where(mask, gate_ref[0], 0.0), axis=1, keepdims=True)
        gate_input = jnp.dot(rows_in, gate_w[0], preferred_element_type=jnp.float32)
        up_input = jnp.dot(rows_in, up_w[0], preferred_element_type=jnp.float32)
        grad_act = right_inner(grad_rows, down_w[0])
        sigmoid_val = jax.nn.sigmoid(gate_input)
        silu_out = gate_input * sigmoid_val
        hidden = silu_out * up_input
        active_ref[:rows] = (hidden * gate).astype(jnp.bfloat16)
        column = jnp.sum(grad_act * hidden, axis=1, keepdims=True)
        gates_out[0] = jnp.sum(jnp.where(mask, column, 0.0), axis=0, keepdims=True)
        grad_hidden = grad_act * gate
        gate_in_ref[:rows] = (
            grad_hidden * up_input * sigmoid_val * (1.0 + gate_input * (1.0 - sigmoid_val))
        ).astype(jnp.bfloat16)
        up_in_ref[:rows] = (grad_hidden * silu_out).astype(jnp.bfloat16)

    by_size(enter)
    if chained:

        @pl.when(expert == 0)
        def _():
            for copy in entering:
                copy.wait()

    def leave(rows):
        column = jnp.transpose(jnp.broadcast_to(place_ref[0], (128, length)))
        column = jnp.concatenate([column] * (rows // 128), 1)
        own = lax.broadcasted_iota(jnp.int32, (length, rows), 1)
        picks = jnp.where(own == column, 1.0, 0.0).astype(jnp.bfloat16)
        moe = jnp.dot(active_ref[:rows], down_w[0], preferred_element_type=jnp.float32)
        moe_out[...] += jnp.dot(
            picks, moe.astype(jnp.bfloat16), preferred_element_type=jnp.float32
        )
        back = right_inner(gate_in_ref[:rows], gate_w[0]) + right_inner(up_in_ref[:rows], up_w[0])
        back_out[...] += jnp.dot(
            picks, back.astype(jnp.bfloat16), preferred_element_type=jnp.float32
        )

    by_size(leave)
    leaving = sum_copies((moe_out, back_out), (moe_final, back_final))
    last = expert == pl.num_programs(0) - 1

    @pl.when(last)
    def _():
        for copy in leaving:
            copy.start()

    def copies(target, number):
        rows = width // 8
        return [
            pltpu.make_async_copy(
                weights_ref.at[kind, pl.ds(piece * rows, rows), :],
                target.at[number, kind, pl.ds(piece * rows, rows), :],
                out_sems.at[kind, piece],
            )
            for kind in range(3)
            for piece in range(8)
        ]

    @pl.when(expert > 0)
    def _():
        for copy in copies(grads_out[0], 0):
            copy.wait()

    def weigh(rows):
        grads = left_inner(
            rows_ref[:rows], jnp.concatenate([gate_in_ref[:rows], up_in_ref[:rows]], 1)
        )
        weights_ref[0] = grads[:, :hidden_size]
        weights_ref[1] = grads[:, hidden_size:]
        grad_down = left_inner(active_ref[:rows], grads_ref[:rows])
        own = hidden_size // parts
        blocks = width // hidden_size
        for part in range(parts):
            for piece in range(blocks):
                at = (part * blocks + piece) * own
                weights_ref[2, at : at + own, :] = grad_down[
                    part * own : (part + 1) * own, piece * hidden_size : (piece + 1) * hidden_size
                ]

    by_size(weigh)
    start = 0
    for target, number in zip(grads_out, numbers):

        @pl.when((expert >= start) & (expert < start + number))
        def _():
            for copy in copies(target, expert - start):
                copy.start()

        start += number

    @pl.when(last)
    def _():
        for copy in copies(grads_out[0], 0) + leaving:
            copy.wait()


def expert_stage(parts, first, numbers, counts, places, gate_rows, normed_b, grad_b, gate_w, up_w, down_w, sums):
    number = sum(numbers)
    length, width = normed_b.shape
    hidden = gate_w.shape[2]
    experts = places.shape[0]
    chained = sums is not None
    whole = lambda e, c: (0, 0)
    row_spec = pl.BlockSpec((1, 1, length), lambda e, c: (first + e, 0, 0))
    once = pl.Buffered(1)
    f32, bf16 = jnp.float32, jnp.bfloat16
    in_specs = [
        row_spec,
        row_spec,
        pl.BlockSpec((length, width), whole, pipeline_mode=once),
        pl.BlockSpec((length, width), whole, pipeline_mode=once),
        pl.BlockSpec((1, width, hidden), lambda e, c: (first + e, 0, 0)),
        pl.BlockSpec((1, width, hidden), lambda e, c: (first + e, 0, 0)),
        pl.BlockSpec((1, hidden, width), lambda e, c: (first + e, 0, 0)),
    ]
    args = [
        counts,
        places.reshape(experts, 1, length),
        gate_rows.reshape(experts, 1, length),
        normed_b,
        grad_b,
        gate_w,
        up_w,
        down_w,
    ]
    if chained:
        in_specs += [pl.BlockSpec(memory_space=pl.ANY)] * 2
        args += [sums[0], sums[1]]
    results = pl.pallas_call(
        functools.partial(expert_kernel, parts, first, numbers, chained),
        out_shape=[jax.ShapeDtypeStruct((some, 3, width, hidden), f32) for some in numbers]
        + [
            jax.ShapeDtypeStruct((length, width), f32),
            jax.ShapeDtypeStruct((length, width), f32),
            jax.ShapeDtypeStruct((number, 1, length), f32),
        ],
        grid_spec=pltpu.PrefetchScalarGridSpec(
            num_scalar_prefetch=1,
            grid=(number,),
            in_specs=in_specs,
            out_specs=[pl.BlockSpec(memory_space=pl.ANY)] * len(numbers)
            + [
                pl.BlockSpec(memory_space=pl.ANY),
                pl.BlockSpec(memory_space=pl.ANY),
                pl.BlockSpec((1, 1, length), lambda e, c: (e, 0, 0)),
            ],
            scratch_shapes=[
                pltpu.VMEM((length, width), f32),
                pltpu.VMEM((length, width), f32),
                pltpu.VMEM((CAP, width), bf16),
                pltpu.VMEM((CAP, width), bf16),
                pltpu.VMEM((CAP, hidden), bf16),
                pltpu.VMEM((CAP, hidden), bf16),
                pltpu.VMEM((CAP, hidden), bf16),
                pltpu.VMEM((3, width, hidden), f32),
                pltpu.SemaphoreType.DMA((2, 4)),
                pltpu.SemaphoreType.DMA((3, 8)),
            ],
        ),
        compiler_params=pltpu.CompilerParams(
            dimension_semantics=("arbitrary",), vmem_limit_bytes=63 << 20
        ),
        cost_estimate=pl.CostEstimate(
            flops=number * 8 * 10**9, bytes_accessed=number * 14 * 10**6, transcendentals=0
        ),
    )(*args)
    return results[: len(numbers)], results[len(numbers) :]


PIECES = 16


def line_gather_kernel(n, x_ref, out_ref, blocks_ref, recv, up_send, down_send):
    me = lax.axis_index("tensor")
    has_low, has_high = me > 0, me < n - 1
    barrier = pltpu.get_barrier_semaphore()

    @pl.when(has_low)
    def _():
        pl.semaphore_signal(barrier, inc=1, device_id={"tensor": me - 1}, device_id_type=MESH)

    @pl.when(has_high)
    def _():
        pl.semaphore_signal(barrier, inc=1, device_id={"tensor": me + 1}, device_id_type=MESH)

    blocks_ref[me] = x_ref[...].astype(jnp.float32)
    pl.semaphore_wait(barrier, has_low.astype(jnp.int32) + has_high.astype(jnp.int32))
    rows = x_ref.shape[0] // PIECES

    def copy(block, c, send, to):
        piece = blocks_ref.at[block, pl.ds(pl.multiple_of(c * rows, rows), rows), :]
        return pltpu.make_async_remote_copy(
            src_ref=piece,
            dst_ref=piece,
            send_sem=send.at[block, c],
            recv_sem=recv.at[block, c],
            device_id={"tensor": to},
            device_id_type=MESH,
        )

    for hop in range(n):
        low, high = me - hop, me + hop

        def step(c, carry):
            @pl.when(low >= 0)
            def _():
                if hop > 0:
                    copy(low, c, up_send, me).wait_recv()

                @pl.when(has_high)
                def _():
                    copy(low, c, up_send, me + 1).start()

            @pl.when(high < n)
            def _():
                if hop > 0:
                    copy(high, c, down_send, me).wait_recv()

                @pl.when(has_low)
                def _():
                    copy(high, c, down_send, me - 1).start()

            return carry

        lax.fori_loop(0, PIECES, step, 0)
    wide = x_ref.shape[1]
    for block in range(n):
        out_ref[:, block * wide : (block + 1) * wide] = blocks_ref[block].astype(jnp.bfloat16)
    for hop in range(n):
        low, high = me - hop, me + hop

        def drain(c, carry):
            @pl.when((low >= 0) & has_high)
            def _():
                copy(low, c, up_send, me).wait_send()

            @pl.when((high < n) & has_low)
            def _():
                copy(high, c, down_send, me).wait_send()

            return carry

        lax.fori_loop(0, PIECES, drain, 0)


def line_gather(x, n, name):
    length, wide = x.shape
    full = pl.BlockSpec(memory_space=pltpu.VMEM)
    return pl.pallas_call(
        functools.partial(line_gather_kernel, n),
        out_shape=jax.ShapeDtypeStruct((length, n * wide), jnp.bfloat16),
        in_specs=[full],
        out_specs=full,
        scratch_shapes=[pltpu.VMEM((n, length, wide), jnp.float32)]
        + [pltpu.SemaphoreType.DMA((n, PIECES))] * 3,
        compiler_params=pltpu.CompilerParams(
            collective_id=name, has_side_effects=True, vmem_limit_bytes=32 << 20
        ),
        cost_estimate=pl.CostEstimate(
            flops=0, bytes_accessed=16 * n * x.size, transcendentals=0
        ),
    )(x)


BLOCK = 256


def own_rows_kernel(parts, weight_ref, out_ref):
    rows = out_ref.shape[0]
    first = lax.axis_index("dp") * rows if parts > 1 else 0
    out_ref[...] = weight_ref[pl.ds(pl.multiple_of(first, 16), rows), :].astype(jnp.float32)


def gather_out_weight(out_weight, parts):
    rows, width = out_weight.shape
    ways = parts if rows % (16 * parts) == 0 else 1
    full = pl.BlockSpec(memory_space=pltpu.VMEM)
    own = pl.pallas_call(
        functools.partial(own_rows_kernel, ways),
        out_shape=jax.ShapeDtypeStruct((rows // ways, width), jnp.float32),
        in_specs=[full],
        out_specs=full,
    )(out_weight)
    return ways, lax.all_gather(own, "tensor")


def middle_kernel(
    attended_ref, weight_all_ref, tokens_ref, gain_ref, router_ref, chosen_ref, middle_out, normed_out, gates_out, weight_ref
):
    ways, n, rows, unused = weight_all_ref.shape

    @pl.when(pl.program_id(0) == 0)
    def _():
        for way in range(ways):
            for block in range(n):
                at = (block * ways + way) * rows
                weight_ref[at : at + rows, :] = weight_all_ref[way, block].astype(jnp.bfloat16)

    branch = jnp.dot(attended_ref[...], weight_ref[...], preferred_element_type=jnp.float32)
    middle = tokens_ref[...].astype(jnp.float32) + RESIDUAL * branch
    middle_out[...] = middle
    recip = lax.rsqrt(jnp.mean(middle * middle, axis=1, keepdims=True) + EPSILON)
    normed = (middle * recip * gain_ref[...]).astype(jnp.bfloat16)
    normed_out[...] = normed
    logits = jnp.dot(normed, router_ref[...], preferred_element_type=jnp.float32)
    raised = jnp.where(chosen_ref[...] > 0.0, jnp.exp(logits), 0.0)
    gates_out[...] = raised / jnp.sum(raised, axis=1, keepdims=True)


def enter_middle(attended, weight_all, tokens, gain, router, chosen):
    length, width = tokens.shape
    rows = lambda columns: pl.BlockSpec((BLOCK, columns), lambda i: (i, 0))
    whole = lambda shape: pl.BlockSpec(
        shape, lambda i: (0,) * len(shape), pipeline_mode=pl.Buffered(1)
    )
    experts = router.shape[1]
    return pl.pallas_call(
        middle_kernel,
        out_shape=[
            jax.ShapeDtypeStruct((length, width), jnp.float32),
            jax.ShapeDtypeStruct((length, width), jnp.bfloat16),
            jax.ShapeDtypeStruct((length, experts), jnp.float32),
        ],
        grid=(length // BLOCK,),
        in_specs=[
            rows(attended.shape[1]),
            whole(weight_all.shape),
            rows(width),
            whole((1, width)),
            whole(router.shape),
            rows(experts),
        ],
        out_specs=[rows(width), rows(width), rows(experts)],
        scratch_shapes=[pltpu.VMEM((attended.shape[1], width), jnp.bfloat16)],
        compiler_params=pltpu.CompilerParams(
            dimension_semantics=("arbitrary",), vmem_limit_bytes=48 << 20
        ),
        cost_estimate=pl.CostEstimate(
            flops=2 * length * width * width, bytes_accessed=25 * 10**6, transcendentals=0
        ),
    )(attended, weight_all, tokens, gain.reshape(1, width), router, chosen)


def turn_kernel(
    n,
    part_ref,
    gates_part_ref,
    gates_ref,
    middle_ref,
    cotangent_ref,
    gain_ref,
    router_ref,
    grad_out,
    branch_out,
    logits_out,
    gain_out,
    summed_ref,
    gates_rows_ref,
    grad_gates_ref,
    *line,
):
    length = part_ref.shape[0]
    rows = length // STEPS

    def done(c):
        @pl.when(c == 0)
        def _():
            experts = gates_rows_ref.shape[0]
            empty = jnp.zeros((grad_gates_ref.shape[1] - experts, length), jnp.float32)
            grad_gates_ref[...] = jnp.transpose(
                jnp.concatenate([gates_rows_ref[...], empty], 0)
            )

        own = pl.ds(pl.multiple_of(c * rows, rows), rows)
        gates, grad_gates = gates_ref[own, :], grad_gates_ref[own, :]
        weighted = jnp.sum(gates * grad_gates, axis=1, keepdims=True)
        grad_logits = (gates * (grad_gates - weighted)).astype(jnp.bfloat16)
        logits_out[own, :] = grad_logits
        grad = summed_ref[own, :] + right_inner(grad_logits, router_ref[...])
        middle = middle_ref[own, :]
        recip = lax.rsqrt(jnp.mean(middle * middle, axis=1, keepdims=True) + EPSILON)
        unit = middle * recip
        gain_out[...] += jnp.sum(grad * unit, axis=0, keepdims=True)
        scaled = grad * gain_ref[...]
        back = recip * (scaled - unit * jnp.mean(scaled * unit, axis=1, keepdims=True))
        total = cotangent_ref[own, :].astype(jnp.float32) + back
        grad_out[own, :] = total
        branch_out[own, :] = (RESIDUAL * total).astype(jnp.bfloat16)

    begin, step, finish = line_stages(
        n, [part_ref, gates_part_ref], [summed_ref, gates_rows_ref], line, done, 1
    )
    begin()
    gain_out[...] = jnp.zeros_like(gain_out)
    lax.fori_loop(0, 2 * STEPS, step, 0)
    finish()


def turn_middle(n, part, gates_part, gates, middle, cotangent, gain, router, name):
    length, width = part.shape
    full = pl.BlockSpec(memory_space=pltpu.VMEM)
    f32 = jnp.float32
    return pl.pallas_call(
        functools.partial(turn_kernel, n),
        out_shape=[
            jax.ShapeDtypeStruct((length, width), f32),
            jax.ShapeDtypeStruct((length, width), jnp.bfloat16),
            jax.ShapeDtypeStruct(gates.shape, jnp.bfloat16),
            jax.ShapeDtypeStruct((1, width), f32),
        ],
        in_specs=[full] * 7,
        out_specs=[full] * 4,
        scratch_shapes=[
            pltpu.VMEM(part.shape, f32),
            pltpu.VMEM(gates_part.shape, f32),
            pltpu.VMEM(gates.shape, f32),
        ]
        + line_scratch([part, gates_part]),
        compiler_params=pltpu.CompilerParams(
            collective_id=name, has_side_effects=True, vmem_limit_bytes=58 << 20
        ),
        cost_estimate=pl.CostEstimate(
            flops=40 * length * width, bytes_accessed=60 * 10**6, transcendentals=0
        ),
    )(part, gates_part, gates, middle, cotangent, gain.reshape(1, width), router)


def last_kernel(count, summed_ref, tokens_ref, middle_ref, gain_ref, *refs):
    smalls, out_ref, small_outs = refs[:count], refs[count], refs[count + 1 :]
    hidden = tokens_ref[...].astype(jnp.float32)
    recip = lax.rsqrt(jnp.mean(hidden * hidden, axis=1, keepdims=True) + EPSILON)
    unit = hidden * recip
    scaled = summed_ref[...] * gain_ref[...]
    inner = jnp.mean(scaled * unit, axis=1, keepdims=True)
    out_ref[...] = middle_ref[...] + recip * (scaled - unit * inner)

    @pl.when(pl.program_id(0) == 0)
    def _():
        for small, out in zip(smalls, small_outs):
            out[...] = small[...]


def leave_first(summed, tokens, grad_middle, gain, smalls):
    length, width = tokens.shape
    rows = pl.BlockSpec((BLOCK, width), lambda i: (i, 0))
    whole = lambda shape: pl.BlockSpec(shape, lambda i: (0, 0))
    f32 = jnp.float32
    return pl.pallas_call(
        functools.partial(last_kernel, len(smalls)),
        out_shape=[jax.ShapeDtypeStruct((length, width), f32)]
        + [jax.ShapeDtypeStruct(small.shape, f32) for small in smalls],
        grid=(length // BLOCK,),
        in_specs=[rows, rows, rows, whole((1, width))] + [whole(small.shape) for small in smalls],
        out_specs=[rows] + [whole(small.shape) for small in smalls],
        compiler_params=pltpu.CompilerParams(vmem_limit_bytes=60 << 20),
        cost_estimate=pl.CostEstimate(
            flops=10 * length * width, bytes_accessed=14 * length * width, transcendentals=0
        ),
    )(summed, tokens, grad_middle, gain.reshape(1, width), *smalls)


SPAN = 768
ROWS = 256


def lane_halves(shape):
    return lax.broadcasted_iota(jnp.int32, shape, len(shape) - 1) // HEAD


def select_halves(tile, source, half):
    kept = jnp.where(lane_halves(tile.shape) == source, tile, 0.0)
    return kept if source == half else pltpu.roll(kept, HEAD, 1)


def spread_pairs(tile, target):
    for source in range(2):
        for half in range(2):
            target[2 * source + half] = select_halves(tile, source, half).astype(jnp.bfloat16)


def rope_tile(tile, cosine, sine_low, sine_high):
    return tile * cosine + pltpu.roll(tile, 128 - HEAD // 2, 1) * sine_low + pltpu.roll(
        tile, HEAD // 2, 1
    ) * sine_high


def rope_back_tile(tile, cosine, sine_low, sine_high):
    return (
        tile * cosine
        + pltpu.roll(tile * sine_low, HEAD // 2, 1)
        + pltpu.roll(tile * sine_high, 128 - HEAD // 2, 1)
    )


def window(block):
    first = block * ROWS
    return first, jnp.maximum(first + ROWS - SPAN, 0)


def attend_forward_kernel(
    heads,
    group,
    tokens_ref,
    gain_ref,
    query_w,
    key_w,
    value_w,
    cosine_ref,
    sine_low_ref,
    sine_high_ref,
    opening_ref,
    normed_out,
    query_out,
    key_out,
    value_out,
    attended_out,
    logsum_out,
    key_pairs,
    value_pairs,
    tiles_ref,
):
    tiles, length, unused = query_out.shape
    hidden = tokens_ref[...].astype(jnp.float32)
    recip = lax.rsqrt(jnp.mean(hidden * hidden, axis=1, keepdims=True) + EPSILON)
    normed_out[...] = (hidden * recip * gain_ref[...]).astype(jnp.bfloat16)
    cosine, sine_low, sine_high = cosine_ref[...], sine_low_ref[...], sine_high_ref[...]
    for tile in range(tiles):
        query = jnp.dot(
            normed_out[...],
            query_w[:, tile * 128 : (tile + 1) * 128],
            preferred_element_type=jnp.float32,
        )
        query_out[tile] = rope_tile(query, cosine, sine_low, sine_high).astype(jnp.bfloat16)
    key = rope_tile(
        jnp.dot(normed_out[...], key_w[...], preferred_element_type=jnp.float32),
        cosine,
        sine_low,
        sine_high,
    )
    value = jnp.dot(normed_out[...], value_w[...], preferred_element_type=jnp.float32)
    key_out[...] = key.astype(jnp.bfloat16)
    value_out[...] = value.astype(jnp.bfloat16)
    spread_pairs(key, key_pairs)
    spread_pairs(value, value_pairs)
    blocks = length // ROWS
    tiles_ref[...] = jnp.zeros_like(tiles_ref)

    def unit(step, carry):
        head, block = step // blocks, step % blocks
        tile, half = head // 2, head % 2
        pair = 2 * (head // group) + half
        first, low = window(block)
        rows = pl.ds(pl.multiple_of(first, ROWS), ROWS)
        span = pl.ds(pl.multiple_of(low, ROWS), SPAN)
        scores = right_inner(query_out[tile, rows, :], key_pairs[pair, span, :])
        columns = low + lax.broadcasted_iota(jnp.int32, (ROWS, SPAN), 1)
        own = first + lax.broadcasted_iota(jnp.int32, (ROWS, SPAN), 0)
        allowed = (columns >= opening_ref[rows, :]) & (columns <= own)
        raised = jnp.where(allowed, jnp.exp(ATTN_SCALE * scores), 0.0)
        total = jnp.sum(raised, axis=1, keepdims=True)
        product = jnp.dot(
            raised.astype(jnp.bfloat16), value_pairs[pair, span, :], preferred_element_type=jnp.float32
        )
        tiles_ref[tile, rows, :] += product / total
        wide = jnp.broadcast_to(jnp.log(total), (ROWS, 128))
        logsum_out[head, :, rows] = jnp.transpose(wide)[:1]
        return carry

    lax.fori_loop(0, heads * blocks, unit, 0)
    for tile in range(tiles):
        attended_out[:, tile * 128 : (tile + 1) * 128] = tiles_ref[tile].astype(jnp.bfloat16)


def attend_forward(tokens, gain, query_w, key_w, value_w, tables, opening, heads, group):
    length, width = tokens.shape
    wide = query_w.shape[1]
    tiles = wide // 128
    bf16, f32 = jnp.bfloat16, jnp.float32
    full = pl.BlockSpec(memory_space=pltpu.VMEM)
    return pl.pallas_call(
        functools.partial(attend_forward_kernel, heads, group),
        out_shape=[
            jax.ShapeDtypeStruct((length, width), bf16),
            jax.ShapeDtypeStruct((tiles, length, 128), bf16),
            jax.ShapeDtypeStruct((length, 128), bf16),
            jax.ShapeDtypeStruct((length, 128), bf16),
            jax.ShapeDtypeStruct((length, wide), bf16),
            jax.ShapeDtypeStruct((heads, 1, length), f32),
        ],
        in_specs=[full] * 9,
        out_specs=[full] * 6,
        scratch_shapes=[
            pltpu.VMEM((4, length, 128), bf16),
            pltpu.VMEM((4, length, 128), bf16),
            pltpu.VMEM((tiles, length, 128), f32),
        ],
        compiler_params=pltpu.CompilerParams(vmem_limit_bytes=48 << 20),
        cost_estimate=pl.CostEstimate(
            flops=8 * 10**9, bytes_accessed=12 * 10**6, transcendentals=5 * 10**6
        ),
    )(tokens, gain.reshape(1, width), query_w, key_w, value_w, *tables, opening.reshape(length, 1))


def attend_backward_kernel(
    n,
    heads,
    group,
    branch_ref,
    out_w,
    query_ref,
    key_ref,
    value_ref,
    attended_ref,
    logsum_ref,
    query_w,
    key_w,
    value_w,
    cosine_ref,
    sine_low_ref,
    sine_high_ref,
    opening_ref,
    tokens_ref,
    moe_ref,
    middle_ref,
    grads_out,
    normed_out,
    gain_out,
    output_ref,
    moe_sum,
    middle_rows,
    middle_sems,
    key_pairs,
    value_pairs,
    attend_grads,
    query_grads,
    key_grads,
    value_grads,
    delta_ref,
    *line,
):
    tiles, length, unused = query_ref.shape
    share = length // STEPS

    def share_rows(c):
        return pl.ds(pl.multiple_of(c * share, share), share)

    def fetch(c):
        slot = lax.rem(c, 2)
        return pltpu.make_async_copy(
            middle_ref.at[share_rows(c), :], middle_rows.at[slot], middle_sems.at[slot]
        )

    def done(c):
        fetch(c).wait()

        @pl.when(c + 1 < STEPS)
        def _():
            fetch(c + 1).start()

        total = middle_rows[lax.rem(c, 2)] + RESIDUAL * moe_sum[share_rows(c), :]
        output_ref[share_rows(c), :] = total.astype(jnp.bfloat16)

    line_start, line_step, line_end = line_stages(n, [moe_ref], [moe_sum], line, done)
    line_start()
    fetch(jnp.int32(0)).start()
    blocks = length // ROWS
    units = heads * blocks
    taken = 0

    def run_line(steps):
        nonlocal taken
        until = min(taken + steps, 2 * STEPS)
        lax.fori_loop(taken, until, line_step, 0)
        taken = until

    run_line(2)
    spread_pairs(key_ref[...].astype(jnp.float32), key_pairs)
    spread_pairs(value_ref[...].astype(jnp.float32), value_pairs)
    halves = (
        lax.broadcasted_iota(jnp.int32, (8, 128), 0) == lane_halves((8, 128))
    ).astype(jnp.float32)
    for tile in range(tiles):
        lanes = slice(tile * 128, (tile + 1) * 128)
        grad = right_inner(branch_ref[...], out_w[lanes, :]).astype(jnp.bfloat16)
        attend_grads[tile] = grad
        products = grad.astype(jnp.float32) * attended_ref[:, lanes].astype(jnp.float32)
        sums = lax.dot_general(
            halves,
            products,
            (((1,), (1,)), ((), ())),
            precision=lax.Precision.HIGHEST,
            preferred_element_type=jnp.float32,
        )
        delta_ref[2 * tile] = sums[0:1]
        delta_ref[2 * tile + 1] = sums[1:2]
        run_line(2)
    query_grads[...] = jnp.zeros_like(query_grads)
    key_grads[...] = jnp.zeros_like(key_grads)
    value_grads[...] = jnp.zeros_like(value_grads)
    before, each = taken, (2 * STEPS - 8 - taken) // units
    taken += units * each

    def unit(step, carry):
        lax.fori_loop(before + step * each, before + step * each + each, line_step, 0)
        head, block = step // blocks, step % blocks
        tile, half = head // 2, head % 2
        pair = 2 * (head // group) + half
        first, low = window(block)
        rows = pl.ds(pl.multiple_of(first, ROWS), ROWS)
        span = pl.ds(pl.multiple_of(low, ROWS), SPAN)
        keys = key_pairs[pair, span, :]
        query = query_ref[tile, rows, :]
        grad = attend_grads[tile, rows, :]
        scores = right_inner(keys, query)
        columns = low + lax.broadcasted_iota(jnp.int32, (SPAN, ROWS), 0)
        own = first + lax.broadcasted_iota(jnp.int32, (SPAN, ROWS), 1)
        allowed = (columns >= opening_ref[:, rows]) & (columns <= own)
        probs = jnp.where(
            allowed, jnp.exp(ATTN_SCALE * scores - logsum_ref[head, :, rows]), 0.0
        )
        grad_probs = right_inner(value_pairs[pair, span, :], grad)
        grad_scores = (probs * (grad_probs - delta_ref[head, :, rows])).astype(jnp.bfloat16)
        value_grads[pair, span, :] += jnp.dot(
            probs.astype(jnp.bfloat16), grad, preferred_element_type=jnp.float32
        )
        key_grads[pair, span, :] += jnp.dot(
            grad_scores, query, preferred_element_type=jnp.float32
        )
        query_grads[tile, rows, :] += left_inner(grad_scores, keys)
        return carry

    lax.fori_loop(0, units, unit, 0)
    cosine, sine_low, sine_high = cosine_ref[...], sine_low_ref[...], sine_high_ref[...]
    wide = tiles * 128
    for tile in range(tiles):
        grads_out[:, tile * 128 : (tile + 1) * 128] = rope_back_tile(
            ATTN_SCALE * query_grads[tile], cosine, sine_low, sine_high
        ).astype(jnp.bfloat16)
    totals = []
    for grads in (key_grads, value_grads):
        totals.append(
            sum(
                select_halves(grads[2 * source + half], half, source)
                for source in range(2)
                for half in range(2)
            )
        )
    grads_out[:, wide : wide + 128] = rope_back_tile(
        ATTN_SCALE * totals[0], cosine, sine_low, sine_high
    ).astype(jnp.bfloat16)
    grads_out[:, wide + 128 : wide + 256] = totals[1].astype(jnp.bfloat16)
    gain_sum = jnp.zeros((1, normed_out.shape[1]), jnp.float32)
    for block in range(blocks):
        rows = slice(block * ROWS, (block + 1) * ROWS)
        normed = (
            right_inner(grads_out[rows, :wide], query_w[...])
            + right_inner(grads_out[rows, wide : wide + 128], key_w[...])
            + right_inner(grads_out[rows, wide + 128 :], value_w[...])
        )
        normed_out[rows, :] = normed
        hidden = tokens_ref[rows, :].astype(jnp.float32)
        recip = lax.rsqrt(jnp.mean(hidden * hidden, axis=1, keepdims=True) + EPSILON)
        gain_sum += jnp.sum(normed * (hidden * recip), axis=0, keepdims=True)
        run_line(2)
    gain_out[...] = jnp.broadcast_to(gain_sum, gain_out.shape)
    run_line(2 * STEPS)
    line_end()


def attend_backward(
    n, branch, out_w, query, key, value, attended, logsum, query_w, key_w, value_w, tables, opening, tokens, moe, middle,
    heads, group, name,
):
    length, width = branch.shape
    tiles = query.shape[0]
    wide = tiles * 128
    bf16, f32 = jnp.bfloat16, jnp.float32
    full = pl.BlockSpec(memory_space=pltpu.VMEM)
    return pl.pallas_call(
        functools.partial(attend_backward_kernel, n, heads, group),
        out_shape=[
            jax.ShapeDtypeStruct((length, wide + 256), bf16),
            jax.ShapeDtypeStruct((length, width), f32),
            jax.ShapeDtypeStruct((8, width), f32),
            jax.ShapeDtypeStruct((length, width), bf16),
        ],
        in_specs=[full] * 16 + [pl.BlockSpec(memory_space=pl.ANY)],
        out_specs=[full] * 4,
        scratch_shapes=[
            pltpu.VMEM((length, width), f32),
            pltpu.VMEM((2, length // STEPS, width), f32),
            pltpu.SemaphoreType.DMA((2,)),
            pltpu.VMEM((4, length, 128), bf16),
            pltpu.VMEM((4, length, 128), bf16),
            pltpu.VMEM((tiles, length, 128), bf16),
            pltpu.VMEM((tiles, length, 128), f32),
            pltpu.VMEM((4, length, 128), f32),
            pltpu.VMEM((4, length, 128), f32),
            pltpu.VMEM((2 * tiles, 1, length), f32),
        ]
        + line_scratch([moe]),
        compiler_params=pltpu.CompilerParams(
            collective_id=name, has_side_effects=True, vmem_limit_bytes=63 << 20
        ),
        cost_estimate=pl.CostEstimate(
            flops=12 * 10**9, bytes_accessed=30 * 10**6, transcendentals=5 * 10**6
        ),
    )(
        branch, out_w, query, key, value, attended, logsum, query_w, key_w, value_w, *tables,
        opening.reshape(1, length), tokens, moe, middle,
    )


def finish_kernel(
    n,
    parts,
    local_ref,
    normed_ref,
    grads_ref,
    branch_ref,
    attended_ref,
    normed_two_ref,
    logits_ref,
    gain_ref,
    first_gain_ref,
    normed_out,
    query_out,
    key_out,
    value_out,
    branch_out,
    router_out,
    gain_out,
    first_gain_out,
    weights_ref,
    gains_ref,
    gain_send,
    gain_recv,
    *scratch,
):
    levels = parts.bit_length() - 1
    held = scratch[:levels]
    sends, recvs = scratch[levels : levels + 2]
    line_start, line_step, line_end = line_stages(n, [local_ref], [normed_out], scratch[levels + 2 :])
    me = lax.axis_index("dp")
    width = normed_ref.shape[1]
    own = width // parts
    wide, attended_wide = grads_ref.shape[1], attended_ref.shape[1]
    mine = lax.axis_index("tensor")
    line_start(
        [{"dp": jnp.bitwise_xor(me, 1 << level)} for level in range(levels)]
        + [{"tensor": lax.rem(mine + ahead, n)} for ahead in range(1, n)]
    )

    def run_line(first, last):
        lax.fori_loop(first, last, line_step, 0)

    gain_copies = [
        pltpu.make_async_remote_copy(
            src_ref=first_gain_ref,
            dst_ref=gains_ref.at[ahead],
            send_sem=gain_send.at[ahead],
            recv_sem=gain_recv.at[ahead],
            device_id={"tensor": lax.rem(mine + ahead, n)},
            device_id_type=MESH,
        )
        for ahead in range(1, n)
    ]
    for copy in gain_copies:
        copy.start()
    run_line(0, 2)
    first_gain = first_gain_ref[:1]
    for ahead, copy in enumerate(gain_copies, 1):
        copy.wait_recv()
        first_gain = first_gain + gains_ref[ahead, :1]
    pieces = 4
    block = width // pieces
    for piece in range(pieces):
        rows = slice(piece * block, (piece + 1) * block)
        weights_ref[rows, :wide] = left_inner(normed_ref[:, rows], grads_ref[...])
        weights_ref[rows, wide : wide + attended_wide] = left_inner(
            branch_ref[:, rows], attended_ref[...]
        )
        gain = jnp.transpose(jnp.broadcast_to(gain_ref[:, rows], (128, block)))
        own_gain = jnp.transpose(jnp.broadcast_to(first_gain[:, rows], (128, block)))
        lanes = lax.broadcasted_iota(jnp.int32, (block, 128), 1)
        weights_ref[rows, wide + attended_wide :] = jnp.where(
            lanes == 127,
            gain,
            jnp.where(
                lanes == 126, own_gain, left_inner(normed_two_ref[:, rows], logits_ref[...])
            ),
        )
        run_line(2 + 2 * piece, 4 + 2 * piece)
    done = 2 + 2 * pieces

    columns = weights_ref.shape[1]
    middle = columns // 256 * 128
    orders = (
        (slice(0, middle), list(range(levels))),
        (slice(middle, columns), [0] + list(range(levels - 1, 0, -1))),
    )

    def shard(number, lanes):
        return weights_ref.at[pl.ds(pl.multiple_of(number * own, own), own), lanes]

    def numbers(order, level, peer):
        fixed = sum(1 << bit for bit in order[: level + 1])
        base = jnp.bitwise_and(peer, fixed)
        free = order[level + 1 :]
        return [
            base + sum(((i >> place) & 1) << bit for place, bit in enumerate(free))
            for i in range(1 << len(free))
        ]

    def copies(level):
        made = []
        for side, (lanes, order) in enumerate(orders):
            peer = jnp.bitwise_xor(me, 1 << order[level])
            for i, number in enumerate(numbers(order, level, peer)):
                made.append(
                    pltpu.make_async_remote_copy(
                        src_ref=shard(number, lanes),
                        dst_ref=held[level].at[i, :, lanes],
                        send_sem=sends.at[side, level, i],
                        recv_sem=recvs.at[side, level, i],
                        device_id={"dp": peer},
                        device_id_type=MESH,
                    )
                )
        return made

    stops = [6] + [42] * (levels > 1) + [4, 0, 0]
    for level in range(levels):
        for copy in copies(level):
            copy.start()
        until = done + stops[level]
        run_line(done, until)
        done = until
        for copy in copies(level):
            copy.wait_recv()
        for lanes, order in orders:
            for i, number in enumerate(numbers(order, level, me)):
                target = shard(number, lanes)
                target[...] += held[level][i, :, lanes]
    everything = slice(0, columns)
    run_line(done, 2 * STEPS)
    kept = shard(me, everything)
    tail = jnp.transpose(kept[:, wide + attended_wide :])
    query_out[...] = kept[:, : query_out.shape[1]]
    key_out[...] = kept[:, wide - 256 : wide - 256 + key_out.shape[1]]
    value_out[...] = kept[:, wide - 128 : wide - 128 + value_out.shape[1]]
    branch_out[...] = kept[:, wide : wide + branch_out.shape[1]]
    router_out[...] = tail[: router_out.shape[0]]
    gain_out[...] = tail[127:]
    first_gain_out[...] = tail[126:127]
    for level in range(levels):
        for copy in copies(level):
            copy.wait_send()
    for copy in gain_copies:
        copy.wait_send()
    line_end()


def finish(
    n, parts, grad_local, normed_b, grads_wide, branch_b, attended, normed_two_b, grad_logits_b, gain_grad, first_gain_grad,
    wide_q, wide_k, experts, name,
):
    length, width = normed_b.shape
    columns = grads_wide.shape[1] + attended.shape[1] + 128
    full = pl.BlockSpec(memory_space=pltpu.VMEM)
    levels = parts.bit_length() - 1
    own = width // parts
    f32 = jnp.float32
    shapes = [(length, width), (own, wide_q), (own, wide_k), (own, wide_k), (own, wide_q)]
    shapes += [(experts, own), (1, own), (1, own)]
    return pl.pallas_call(
        functools.partial(finish_kernel, n, parts),
        out_shape=[jax.ShapeDtypeStruct(shape, f32) for shape in shapes],
        in_specs=[full] * 9,
        out_specs=[full] * 8,
        scratch_shapes=[
            pltpu.VMEM((width, columns), f32),
            pltpu.VMEM((n, 8, width), f32),
            pltpu.SemaphoreType.DMA((n,)),
            pltpu.SemaphoreType.DMA((n,)),
        ]
        + [pltpu.VMEM((parts >> (level + 1), own, columns), f32) for level in range(levels)]
        + [pltpu.SemaphoreType.DMA((2, levels, parts // 2))] * 2
        + line_scratch([grad_local]),
        compiler_params=pltpu.CompilerParams(
            collective_id=name, has_side_effects=True, vmem_limit_bytes=62 << 20
        ),
        cost_estimate=pl.CostEstimate(
            flops=2 * length * width * columns, bytes_accessed=50 * 10**6, transcendentals=0
        ),
    )(
        grad_local, normed_b, grads_wide, branch_b, attended, normed_two_b, grad_logits_b, gain_grad,
        first_gain_grad,
    )


def place_kernel(gate_ref, up_ref, down_ref, *refs):
    gate_out, up_out, down_out = refs[-3:]
    gate_out[0] = gate_ref[0, 0]
    up_out[0] = up_ref[0, 0]
    rows, hidden = down_out.shape[1], down_ref.shape[3]
    for piece in range(down_out.shape[2] // hidden):
        down_out[0, :, piece * hidden : (piece + 1) * hidden] = down_ref[
            0, 0, piece * rows : (piece + 1) * rows, :
        ]


def place_shards(parts, shards, first, experts, before):
    number, unused, rows, hidden = shards.shape
    down_rows = hidden // parts
    width = rows * parts
    shapes = [(experts, rows, hidden), (experts, rows, hidden), (experts, down_rows, width)]
    spec = lambda shape: pl.BlockSpec((1,) + shape[1:], lambda e: (first + e, 0, 0))
    one = lambda kind: pl.BlockSpec((1, 1, rows, hidden), lambda e: (e, kind, 0, 0))
    args, extra, aliases = [shards] * 3, [], {}
    if before is not None:
        args += list(before)
        extra = [pl.BlockSpec(memory_space=pl.ANY)] * 3
        aliases = {3: 0, 4: 1, 5: 2}
    return pl.pallas_call(
        place_kernel,
        out_shape=[jax.ShapeDtypeStruct(shape, jnp.float32) for shape in shapes],
        grid=(number,),
        in_specs=[one(kind) for kind in range(3)] + extra,
        out_specs=[spec(shape) for shape in shapes],
        input_output_aliases=aliases,
        compiler_params=pltpu.CompilerParams(vmem_limit_bytes=60 << 20),
        cost_estimate=pl.CostEstimate(
            flops=0, bytes_accessed=8 * shards.size, transcendentals=0
        ),
    )(*args)


def on_device(
    ring,
    tokens,
    cotangent,
    segment_ids,
    routes,
    attn_gain,
    query_weight,
    key_weight,
    value_weight,
    out_weight,
    ffn_gain,
    router_weight,
    gate_weight,
    up_weight,
    down_weight,
):
    length = tokens.shape[0]
    width = tokens.shape[1]
    segment = segment_ids[0]
    heads_local = query_weight.shape[1] // HEAD
    kv_local = key_weight.shape[1] // HEAD
    group_size = heads_local // kv_local
    experts_all = router_weight.shape[1]
    experts_local = gate_weight.shape[0]
    parts = lax.axis_size("dp")
    opening = doc_openings(segment)
    tables = rope_tables(opening, HEAD)
    query_w, key_w, value_w = (pad_columns(w) for w in (query_weight, key_weight, value_weight))
    out_w = jnp.transpose(pad_columns(jnp.transpose(out_weight)))
    ways, out_rows = gather_out_weight(out_weight, parts)
    normed_b, queries, keys, values, attended, logsum = attend_forward(
        tokens, attn_gain, query_w, key_w, value_w, tables, opening, heads_local, group_size
    )
    all_ids = jnp.arange(experts_all, dtype=jnp.int32)
    chosen = jnp.sum((routes[:, :, None] == all_ids[None, None, :]).astype(jnp.int32), axis=1) > 0
    first_expert = lax.axis_index("tensor") * experts_local
    local_ids = first_expert + jnp.arange(experts_local, dtype=jnp.int32)
    picked = jnp.sum((routes[None, :, :] == local_ids[:, None, None]).astype(jnp.int32), axis=2)
    places_in = slot_places(picked)
    counts = jnp.sum(picked, axis=1)
    out_rows, attended = lax.optimization_barrier((out_rows, attended))
    out_all = lax.all_gather(out_rows, "dp") if ways > 1 else out_rows[None]
    attended_all = line_gather(attended, ring, 1)
    attended_all = attended_all.reshape(length, ring, attended.shape[1])
    attended_all = attended_all[:, :, : heads_local * HEAD].reshape(length, -1)
    router_w = pad_columns(router_weight)
    middle, normed_two_b, gate_probs = enter_middle(
        attended_all, out_all, tokens, ffn_gain, router_w, pad_columns(chosen.astype(jnp.float32))
    )
    gate_rows = jnp.transpose(lax.dynamic_slice_in_dim(gate_probs, first_expert, experts_local, 1))
    numbers = (max(1, experts_local // 10),)
    numbers += (experts_local - numbers[0],)
    (grads_first,), sums = expert_stage(
        parts, 0, numbers[:1], counts, places_in, gate_rows, normed_two_b, cotangent,
        gate_weight, up_weight, down_weight, None,
    )
    shards_first = lax.psum_scatter(grads_first, "dp", scatter_dimension=2, tiled=True)
    (grads_last,), sums_last = expert_stage(
        parts, numbers[0], numbers[1:], counts, places_in, gate_rows, normed_two_b, cotangent,
        gate_weight, up_weight, down_weight, sums,
    )
    moe_part, grad_normed_part, unused = sums_last
    shards_first, grads_last, grad_normed_part = lax.optimization_barrier(
        (shards_first, grads_last, grad_normed_part)
    )
    shards_last = lax.psum_scatter(grads_last, "dp", scatter_dimension=2, tiled=True)
    grad_gates_local = jnp.concatenate([sums[2], sums_last[2]], 0).reshape(experts_local, length)
    grad_gates_part = lax.dynamic_update_slice_in_dim(
        jnp.zeros((experts_all, length), jnp.float32), grad_gates_local, first_expert, 0
    )
    grad_middle, grad_branch_b, grad_logits_b, grad_ffn_gain = turn_middle(
        ring, grad_normed_part, grad_gates_part, gate_probs, middle, cotangent, ffn_gain, router_w, 2
    )
    grads_wide, grad_normed_local, first_gain, output = attend_backward(
        ring, grad_branch_b, out_w, queries, keys, values, attended, logsum,
        query_w, key_w, value_w, tables, opening, tokens, moe_part, middle, heads_local, group_size, 3,
    )
    wide_q, wide_k = heads_local * HEAD, kv_local * HEAD
    grads_placed = place_shards(parts, shards_first, 0, experts_local, None)
    grads_placed, grads_wide = lax.optimization_barrier((grads_placed, grads_wide))
    grad_normed, *small = finish(
        ring, parts, grad_normed_local, normed_b, grads_wide, grad_branch_b, attended, normed_two_b,
        grad_logits_b, grad_ffn_gain, first_gain, wide_q, wide_k, experts_all, 4,
    )
    grad_tokens, *small = leave_first(grad_normed, tokens, grad_middle, attn_gain, small)
    grad_query, grad_key, grad_value, grad_out, grad_router, grad_ffn_gain, grad_attn_gain = small
    shards_last, grad_tokens = lax.optimization_barrier((shards_last, grad_tokens))
    grad_gate, grad_up, grad_down = place_shards(
        parts, shards_last, numbers[0], experts_local, grads_placed
    )
    return (
        output,
        grad_tokens,
        grad_attn_gain.reshape(-1),
        grad_query,
        grad_key,
        grad_value,
        jnp.transpose(grad_out),
        grad_ffn_gain.reshape(-1),
        jnp.transpose(grad_router),
        grad_gate,
        grad_up,
        grad_down,
    )


def solution(mesh):
    return jax.shard_map(
        functools.partial(on_device, mesh.shape["tensor"]),
        mesh=mesh,
        in_specs=(
            P("dp", None),
            P("dp", None),
            P("dp", None),
            P("dp", None),
            P(),
            P(None, "tensor"),
            P(None, "tensor"),
            P(None, "tensor"),
            P("tensor", None),
            P(),
            P(),
            P("tensor", None, None),
            P("tensor", None, None),
            P("tensor", None, None),
        ),
        out_specs=(
            P("dp", None),
            P("dp", None),
            P("dp"),
            P("dp", "tensor"),
            P("dp", "tensor"),
            P("dp", "tensor"),
            P("tensor", "dp"),
            P("dp"),
            P("dp", None),
            P("tensor", "dp", None),
            P("tensor", "dp", None),
            P("tensor", "dp", None),
        ),
        check_vma=False,
    )
```

```python
import functools

import jax
import jax.numpy as jnp
from jax import lax
from jax.experimental import pallas as pl
from jax.experimental.pallas import tpu as pltpu
from jax.sharding import PartitionSpec as P

MESH = pl.DeviceIdType.MESH

HEAD = 64
CAP = 384


EPSILON = 1e-06
RESIDUAL = 0.22
ATTN_SCALE = 0.015625
ROPE_BASE = 10000.0


def left_inner(first, second):
    return lax.dot_general(
        first, second, (((0,), (0,)), ((), ())), preferred_element_type=jnp.float32
    )


def right_inner(first, second):
    return lax.dot_general(
        first, second, (((1,), (1,)), ((), ())), preferred_element_type=jnp.float32
    )


def doc_openings(segment):
    return jnp.sum((segment[None, :] < segment[:, None]).astype(jnp.int32), axis=1)


def rope_tables(opening, head_size):
    halfway = head_size // 2
    spread = jnp.arange(halfway, dtype=jnp.float32) * (2.0 / head_size)
    inverse = jnp.power(ROPE_BASE, -spread)
    places = jnp.arange(opening.shape[0], dtype=jnp.int32)
    angles = (places - opening).astype(jnp.float32)[:, None] * inverse[None, :]
    cosine, sine = jnp.cos(angles), jnp.sin(angles)
    none = jnp.zeros_like(sine)
    return (
        jnp.concatenate([cosine] * 4, 1),
        jnp.concatenate([-sine, none] * 2, 1),
        jnp.concatenate([none, sine] * 2, 1),
    )


def pad_columns(weight):
    missing = -weight.shape[1] % 128
    return weight if missing == 0 else jnp.pad(weight, ((0, 0), (0, missing)))


def rms_forward(hidden, gain):
    recip = lax.rsqrt(jnp.mean(hidden * hidden, axis=-1, keepdims=True) + EPSILON)
    unit = hidden * recip
    return (unit * gain, unit, recip)


def rms_backward(gradient, unit, recip, gain):
    gain_grad = jnp.sum(gradient * unit, axis=0)
    scaled = gradient * gain
    return (recip * (scaled - unit * jnp.mean(scaled * unit, axis=-1, keepdims=True)), gain_grad)


def slot_places(picked):
    length = picked.shape[1]
    tokens = jnp.arange(length, dtype=jnp.int32)
    earlier = (tokens[:, None] < tokens[None, :]).astype(jnp.bfloat16)
    before = jnp.dot(picked.astype(jnp.bfloat16), earlier, preferred_element_type=jnp.float32)
    return jnp.where(picked > 0, before.astype(jnp.int32), -1)


STEPS = 32
LAG = 2


def line_stages(n, xs, outs, scratch, done=None, whole=0):
    count = len(xs)
    lows, highs = scratch[:count], scratch[count : 2 * count]
    low_recv, high_recv, total_recv, up_send, low_send, high_send = scratch[2 * count :]
    me = lax.axis_index("tensor")
    root = n // 2
    has_low, has_high = me > 0, me < n - 1

    def begin(others=()):
        barrier = pltpu.get_barrier_semaphore()
        for other in others:
            pl.semaphore_signal(barrier, inc=1, device_id=other, device_id_type=MESH)

        @pl.when(has_low)
        def _():
            pl.semaphore_signal(barrier, inc=1, device_id={"tensor": me - 1}, device_id_type=MESH)

        @pl.when(has_high)
        def _():
            pl.semaphore_signal(barrier, inc=1, device_id={"tensor": me + 1}, device_id_type=MESH)

        pl.semaphore_wait(
            barrier, len(others) + has_low.astype(jnp.int32) + has_high.astype(jnp.int32)
        )

    def piece(ref, c):
        rows = ref.shape[0] // STEPS
        return ref.at[pl.ds(pl.multiple_of(c * rows, rows), rows), :]

    cut = count - whole

    def copies(sources, targets, c, send, recv, to, uncut):
        return [
            pltpu.make_async_remote_copy(
                src_ref=source if uncut else piece(source, c),
                dst_ref=target if uncut else piece(target, c),
                send_sem=send.at[i, c],
                recv_sem=recv.at[i, c],
                device_id={"tensor": to},
                device_id_type=MESH,
            )
            for i, (source, target) in enumerate(zip(sources, targets))
            if (i >= cut) == uncut
        ]

    def each(sources, targets, c, send, recv, to, act):
        for copy in copies(sources, targets, c, send, recv, to, False):
            act(copy)
        if whole:

            @pl.when(c == 0)
            def _():
                for copy in copies(sources, targets, 0, send, recv, to, True):
                    act(copy)

    def start(sources, targets, c, send, recv, to):
        each(sources, targets, c, send, recv, to, lambda copy: copy.start())

    def arrived(targets, c, send, recv):
        each(targets, targets, c, send, recv, me, lambda copy: copy.wait_recv())

    def add(c, terms, targets):
        for i, target in enumerate(targets):
            if i < cut:
                piece(target, c)[...] = functools.reduce(
                    jnp.add, [piece(term[i], c)[...] for term in terms]
                )
            else:

                @pl.when(c == 0)
                def _():
                    target[...] = functools.reduce(jnp.add, [term[i][...] for term in terms])

    def reduce_step(c):
        for side, inner, held, recv, to in (
            (me < root, has_low, lows, low_recv, me + 1),
            (me > root, has_high, highs, high_recv, me - 1),
        ):

            @pl.when(side & inner)
            def _():
                arrived(held, c, up_send, recv)
                add(c, (held, xs), held)
                start(held, held, c, up_send, recv, to)

            @pl.when(side & jnp.logical_not(inner))
            def _():
                start(xs, held, c, up_send, recv, to)

        @pl.when(me == root)
        def _():
            arrived(lows, c, up_send, low_recv)
            if root < n - 1:
                arrived(highs, c, up_send, high_recv)
            add(c, (xs, lows, highs) if root < n - 1 else (xs, lows), outs)
            start(outs, outs, c, low_send, total_recv, me - 1)
            if root < n - 1:
                start(outs, outs, c, high_send, total_recv, me + 1)
            if done is not None:
                done(c)

    def total_step(c):
        @pl.when(me != root)
        def _():
            arrived(outs, c, low_send, total_recv)

        @pl.when((me < root) & has_low)
        def _():
            start(outs, outs, c, low_send, total_recv, me - 1)

        @pl.when((me > root) & has_high)
        def _():
            start(outs, outs, c, high_send, total_recv, me + 1)

        if done is not None:

            @pl.when(me != root)
            def _():
                done(c)

    lag = jnp.where(has_low & has_high, LAG, STEPS)

    def step(t, carry):
        @pl.when(t < STEPS)
        def _():
            reduce_step(t)

        @pl.when((t >= lag) & (t - lag < STEPS))
        def _():
            total_step(t - lag)

        return carry

    def finish():
        def drain(c, carry):
            for condition, send in (
                (me != root, up_send),
                ((me <= root) & has_low, low_send),
                ((me >= root) & has_high, high_send),
            ):

                @pl.when(condition)
                def _():
                    each(xs, lows, c, send, low_recv, me, lambda copy: copy.wait_send())

            return carry

        lax.fori_loop(0, STEPS, drain, 0)

    return begin, step, finish


def line_scratch(arrays):
    return [pltpu.VMEM(array.shape, jnp.float32) for array in arrays * 2] + [
        pltpu.SemaphoreType.DMA((len(arrays), STEPS))
    ] * 6


def expert_kernel(
    parts,
    first,
    numbers,
    chained,
    count_ref,
    place_ref,
    gate_ref,
    normed_ref,
    grad_ref,
    gate_w,
    up_w,
    down_w,
    *refs,
):
    if chained:
        moe_in, back_in = refs[:2]
        refs = refs[2:]
    grads_out, refs = refs[: len(numbers)], refs[len(numbers) :]
    moe_final, back_final, gates_out = refs[:3]
    moe_out, back_out, rows_ref, grads_ref, active_ref, gate_in_ref, up_in_ref, weights_ref = refs[3:11]
    sems, out_sems = refs[11:]
    expert = pl.program_id(0)
    filled = count_ref[first + expert]
    length, width = normed_ref.shape
    hidden_size = gate_w.shape[2]
    sizes = (128, 256, CAP)

    def by_size(run):
        low = None
        for rows in sizes:
            fits = filled <= rows if low is None else filled > low
            if low is not None and rows != sizes[-1]:
                fits = fits & (filled <= rows)
            pl.when(fits)(functools.partial(run, rows))
            low = rows

    def sum_copies(sources, targets):
        rows = length // 4
        return [
            pltpu.make_async_copy(
                source.at[pl.ds(piece * rows, rows), :],
                target.at[pl.ds(piece * rows, rows), :],
                sems.at[i, piece],
            )
            for i, (source, target) in enumerate(zip(sources, targets))
            for piece in range(4)
        ]

    if chained:
        entering = sum_copies((moe_in, back_in), (moe_out, back_out))

        @pl.when(expert == 0)
        def _():
            for copy in entering:
                copy.start()

    else:

        @pl.when(expert == 0)
        def _():
            moe_out[...] = jnp.zeros_like(moe_out)
            back_out[...] = jnp.zeros_like(back_out)

    def slots(rows):
        mask = lax.broadcasted_iota(jnp.int32, (rows, length), 0) == place_ref[0]
        return mask, jnp.where(mask, 1.0, 0.0).astype(jnp.bfloat16)

    def enter(rows):
        mask, picks = slots(rows)
        rows_in = jnp.dot(picks, normed_ref[...], preferred_element_type=jnp.float32).astype(jnp.bfloat16)
        grad_rows = (
            RESIDUAL * jnp.dot(picks, grad_ref[...], preferred_element_type=jnp.float32)
        ).astype(jnp.bfloat16)
        rows_ref[:rows] = rows_in
        grads_ref[:rows] = grad_rows
        gate = jnp.sum(jnp.where(mask, gate_ref[0], 0.0), axis=1, keepdims=True)
        gate_input = jnp.dot(rows_in, gate_w[0], preferred_element_type=jnp.float32)
        up_input = jnp.dot(rows_in, up_w[0], preferred_element_type=jnp.float32)
        grad_act = right_inner(grad_rows, down_w[0])
        sigmoid_val = jax.nn.sigmoid(gate_input)
        silu_out = gate_input * sigmoid_val
        hidden = silu_out * up_input
        active_ref[:rows] = (hidden * gate).astype(jnp.bfloat16)
        column = jnp.sum(grad_act * hidden, axis=1, keepdims=True)
        gates_out[0] = jnp.sum(jnp.where(mask, column, 0.0), axis=0, keepdims=True)
        grad_hidden = grad_act * gate
        gate_in_ref[:rows] = (
            grad_hidden * up_input * sigmoid_val * (1.0 + gate_input * (1.0 - sigmoid_val))
        ).astype(jnp.bfloat16)
        up_in_ref[:rows] = (grad_hidden * silu_out).astype(jnp.bfloat16)

    by_size(enter)
    if chained:

        @pl.when(expert == 0)
        def _():
            for copy in entering:
                copy.wait()

    def leave(rows):
        column = jnp.transpose(jnp.broadcast_to(place_ref[0], (128, length)))
        column = jnp.concatenate([column] * (rows // 128), 1)
        own = lax.broadcasted_iota(jnp.int32, (length, rows), 1)
        picks = jnp.where(own == column, 1.0, 0.0).astype(jnp.bfloat16)
        moe = jnp.dot(active_ref[:rows], down_w[0], preferred_element_type=jnp.float32)
        moe_out[...] += jnp.dot(
            picks, moe.astype(jnp.bfloat16), preferred_element_type=jnp.float32
        )
        back = right_inner(gate_in_ref[:rows], gate_w[0]) + right_inner(up_in_ref[:rows], up_w[0])
        back_out[...] += jnp.dot(
            picks, back.astype(jnp.bfloat16), preferred_element_type=jnp.float32
        )

    by_size(leave)
    leaving = sum_copies((moe_out, back_out), (moe_final, back_final))
    last = expert == pl.num_programs(0) - 1

    @pl.when(last)
    def _():
        for copy in leaving:
            copy.start()

    def copies(target, number):
        rows = width // 4
        return [
            pltpu.make_async_copy(
                weights_ref.at[kind, pl.ds(piece * rows, rows), :],
                target.at[number, kind, pl.ds(piece * rows, rows), :],
                out_sems.at[kind, piece],
            )
            for kind in range(3)
            for piece in range(4)
        ]

    @pl.when(expert > 0)
    def _():
        for copy in copies(grads_out[0], 0):
            copy.wait()

    def weigh(rows):
        grads = left_inner(
            rows_ref[:rows], jnp.concatenate([gate_in_ref[:rows], up_in_ref[:rows]], 1)
        )
        weights_ref[0] = grads[:, :hidden_size]
        weights_ref[1] = grads[:, hidden_size:]
        grad_down = left_inner(active_ref[:rows], grads_ref[:rows])
        own = hidden_size // parts
        blocks = width // hidden_size
        for part in range(parts):
            for piece in range(blocks):
                at = (part * blocks + piece) * own
                weights_ref[2, at : at + own, :] = grad_down[
                    part * own : (part + 1) * own, piece * hidden_size : (piece + 1) * hidden_size
                ]

    by_size(weigh)
    start = 0
    for target, number in zip(grads_out, numbers):

        @pl.when((expert >= start) & (expert < start + number))
        def _():
            for copy in copies(target, expert - start):
                copy.start()

        start += number

    @pl.when(last)
    def _():
        for copy in copies(grads_out[0], 0) + leaving:
            copy.wait()


def expert_stage(parts, first, numbers, counts, places, gate_rows, normed_b, grad_b, gate_w, up_w, down_w, sums):
    number = sum(numbers)
    length, width = normed_b.shape
    hidden = gate_w.shape[2]
    experts = places.shape[0]
    chained = sums is not None
    whole = lambda e, c: (0, 0)
    row_spec = pl.BlockSpec((1, 1, length), lambda e, c: (first + e, 0, 0))
    once = pl.Buffered(1)
    f32, bf16 = jnp.float32, jnp.bfloat16
    in_specs = [
        row_spec,
        row_spec,
        pl.BlockSpec((length, width), whole, pipeline_mode=once),
        pl.BlockSpec((length, width), whole, pipeline_mode=once),
        pl.BlockSpec((1, width, hidden), lambda e, c: (first + e, 0, 0)),
        pl.BlockSpec((1, width, hidden), lambda e, c: (first + e, 0, 0)),
        pl.BlockSpec((1, hidden, width), lambda e, c: (first + e, 0, 0)),
    ]
    args = [
        counts,
        places.reshape(experts, 1, length),
        gate_rows.reshape(experts, 1, length),
        normed_b,
        grad_b,
        gate_w,
        up_w,
        down_w,
    ]
    if chained:
        in_specs += [pl.BlockSpec(memory_space=pl.ANY)] * 2
        args += [sums[0], sums[1]]
    results = pl.pallas_call(
        functools.partial(expert_kernel, parts, first, numbers, chained),
        out_shape=[jax.ShapeDtypeStruct((some, 3, width, hidden), f32) for some in numbers]
        + [
            jax.ShapeDtypeStruct((length, width), f32),
            jax.ShapeDtypeStruct((length, width), f32),
            jax.ShapeDtypeStruct((number, 1, length), f32),
        ],
        grid_spec=pltpu.PrefetchScalarGridSpec(
            num_scalar_prefetch=1,
            grid=(number,),
            in_specs=in_specs,
            out_specs=[pl.BlockSpec(memory_space=pl.ANY)] * len(numbers)
            + [
                pl.BlockSpec(memory_space=pl.ANY),
                pl.BlockSpec(memory_space=pl.ANY),
                pl.BlockSpec((1, 1, length), lambda e, c: (e, 0, 0)),
            ],
            scratch_shapes=[
                pltpu.VMEM((length, width), f32),
                pltpu.VMEM((length, width), f32),
                pltpu.VMEM((CAP, width), bf16),
                pltpu.VMEM((CAP, width), bf16),
                pltpu.VMEM((CAP, hidden), bf16),
                pltpu.VMEM((CAP, hidden), bf16),
                pltpu.VMEM((CAP, hidden), bf16),
                pltpu.VMEM((3, width, hidden), f32),
                pltpu.SemaphoreType.DMA((2, 4)),
                pltpu.SemaphoreType.DMA((3, 4)),
            ],
        ),
        compiler_params=pltpu.CompilerParams(
            dimension_semantics=("arbitrary",), vmem_limit_bytes=63 << 20
        ),
        cost_estimate=pl.CostEstimate(
            flops=number * 8 * 10**9, bytes_accessed=number * 14 * 10**6, transcendentals=0
        ),
    )(*args)
    return results[: len(numbers)], results[len(numbers) :]


PIECES = 16


def line_gather_kernel(n, x_ref, out_ref, blocks_ref, recv, up_send, down_send):
    me = lax.axis_index("tensor")
    has_low, has_high = me > 0, me < n - 1
    barrier = pltpu.get_barrier_semaphore()

    @pl.when(has_low)
    def _():
        pl.semaphore_signal(barrier, inc=1, device_id={"tensor": me - 1}, device_id_type=MESH)

    @pl.when(has_high)
    def _():
        pl.semaphore_signal(barrier, inc=1, device_id={"tensor": me + 1}, device_id_type=MESH)

    blocks_ref[me] = x_ref[...].astype(jnp.float32)
    pl.semaphore_wait(barrier, has_low.astype(jnp.int32) + has_high.astype(jnp.int32))
    rows = x_ref.shape[0] // PIECES

    def copy(block, c, send, to):
        piece = blocks_ref.at[block, pl.ds(pl.multiple_of(c * rows, rows), rows), :]
        return pltpu.make_async_remote_copy(
            src_ref=piece,
            dst_ref=piece,
            send_sem=send.at[block, c],
            recv_sem=recv.at[block, c],
            device_id={"tensor": to},
            device_id_type=MESH,
        )

    for hop in range(n):
        low, high = me - hop, me + hop

        def step(c, carry):
            @pl.when(low >= 0)
            def _():
                if hop > 0:
                    copy(low, c, up_send, me).wait_recv()

                @pl.when(has_high)
                def _():
                    copy(low, c, up_send, me + 1).start()

            @pl.when(high < n)
            def _():
                if hop > 0:
                    copy(high, c, down_send, me).wait_recv()

                @pl.when(has_low)
                def _():
                    copy(high, c, down_send, me - 1).start()

            return carry

        lax.fori_loop(0, PIECES, step, 0)
    wide = x_ref.shape[1]
    for block in range(n):
        out_ref[:, block * wide : (block + 1) * wide] = blocks_ref[block].astype(jnp.bfloat16)
    for hop in range(n):
        low, high = me - hop, me + hop

        def drain(c, carry):
            @pl.when((low >= 0) & has_high)
            def _():
                copy(low, c, up_send, me).wait_send()

            @pl.when((high < n) & has_low)
            def _():
                copy(high, c, down_send, me).wait_send()

            return carry

        lax.fori_loop(0, PIECES, drain, 0)


def line_gather(x, n, name):
    length, wide = x.shape
    full = pl.BlockSpec(memory_space=pltpu.VMEM)
    return pl.pallas_call(
        functools.partial(line_gather_kernel, n),
        out_shape=jax.ShapeDtypeStruct((length, n * wide), jnp.bfloat16),
        in_specs=[full],
        out_specs=full,
        scratch_shapes=[pltpu.VMEM((n, length, wide), jnp.float32)]
        + [pltpu.SemaphoreType.DMA((n, PIECES))] * 3,
        compiler_params=pltpu.CompilerParams(
            collective_id=name, has_side_effects=True, vmem_limit_bytes=32 << 20
        ),
        cost_estimate=pl.CostEstimate(
            flops=0, bytes_accessed=16 * n * x.size, transcendentals=0
        ),
    )(x)


BLOCK = 256


def own_rows_kernel(parts, weight_ref, out_ref):
    rows = out_ref.shape[0]
    first = lax.axis_index("dp") * rows if parts > 1 else 0
    out_ref[...] = weight_ref[pl.ds(pl.multiple_of(first, 16), rows), :].astype(jnp.float32)


def gather_out_weight(out_weight, parts):
    rows, width = out_weight.shape
    ways = parts if rows % (16 * parts) == 0 else 1
    full = pl.BlockSpec(memory_space=pltpu.VMEM)
    own = pl.pallas_call(
        functools.partial(own_rows_kernel, ways),
        out_shape=jax.ShapeDtypeStruct((rows // ways, width), jnp.float32),
        in_specs=[full],
        out_specs=full,
    )(out_weight)
    return ways, lax.all_gather(own, "tensor")


def middle_kernel(
    attended_ref, weight_all_ref, tokens_ref, gain_ref, router_ref, chosen_ref, middle_out, normed_out, gates_out, weight_ref
):
    ways, n, rows, unused = weight_all_ref.shape

    @pl.when(pl.program_id(0) == 0)
    def _():
        for way in range(ways):
            for block in range(n):
                at = (block * ways + way) * rows
                weight_ref[at : at + rows, :] = weight_all_ref[way, block].astype(jnp.bfloat16)

    branch = jnp.dot(attended_ref[...], weight_ref[...], preferred_element_type=jnp.float32)
    middle = tokens_ref[...].astype(jnp.float32) + RESIDUAL * branch
    middle_out[...] = middle
    recip = lax.rsqrt(jnp.mean(middle * middle, axis=1, keepdims=True) + EPSILON)
    normed = (middle * recip * gain_ref[...]).astype(jnp.bfloat16)
    normed_out[...] = normed
    logits = jnp.dot(normed, router_ref[...], preferred_element_type=jnp.float32)
    raised = jnp.where(chosen_ref[...] > 0.0, jnp.exp(logits), 0.0)
    gates_out[...] = raised / jnp.sum(raised, axis=1, keepdims=True)


def enter_middle(attended, weight_all, tokens, gain, router, chosen):
    length, width = tokens.shape
    rows = lambda columns: pl.BlockSpec((BLOCK, columns), lambda i: (i, 0))
    whole = lambda shape: pl.BlockSpec(
        shape, lambda i: (0,) * len(shape), pipeline_mode=pl.Buffered(1)
    )
    experts = router.shape[1]
    return pl.pallas_call(
        middle_kernel,
        out_shape=[
            jax.ShapeDtypeStruct((length, width), jnp.float32),
            jax.ShapeDtypeStruct((length, width), jnp.bfloat16),
            jax.ShapeDtypeStruct((length, experts), jnp.float32),
        ],
        grid=(length // BLOCK,),
        in_specs=[
            rows(attended.shape[1]),
            whole(weight_all.shape),
            rows(width),
            whole((1, width)),
            whole(router.shape),
            rows(experts),
        ],
        out_specs=[rows(width), rows(width), rows(experts)],
        scratch_shapes=[pltpu.VMEM((attended.shape[1], width), jnp.bfloat16)],
        compiler_params=pltpu.CompilerParams(
            dimension_semantics=("arbitrary",), vmem_limit_bytes=48 << 20
        ),
        cost_estimate=pl.CostEstimate(
            flops=2 * length * width * width, bytes_accessed=25 * 10**6, transcendentals=0
        ),
    )(attended, weight_all, tokens, gain.reshape(1, width), router, chosen)


def turn_kernel(
    n,
    part_ref,
    gates_part_ref,
    gates_ref,
    middle_ref,
    cotangent_ref,
    gain_ref,
    router_ref,
    grad_out,
    branch_out,
    logits_out,
    gain_out,
    summed_ref,
    gates_rows_ref,
    grad_gates_ref,
    *line,
):
    length = part_ref.shape[0]
    rows = length // STEPS

    def done(c):
        @pl.when(c == 0)
        def _():
            experts = gates_rows_ref.shape[0]
            empty = jnp.zeros((grad_gates_ref.shape[1] - experts, length), jnp.float32)
            grad_gates_ref[...] = jnp.transpose(
                jnp.concatenate([gates_rows_ref[...], empty], 0)
            )

        own = pl.ds(pl.multiple_of(c * rows, rows), rows)
        gates, grad_gates = gates_ref[own, :], grad_gates_ref[own, :]
        weighted = jnp.sum(gates * grad_gates, axis=1, keepdims=True)
        grad_logits = (gates * (grad_gates - weighted)).astype(jnp.bfloat16)
        logits_out[own, :] = grad_logits
        grad = summed_ref[own, :] + right_inner(grad_logits, router_ref[...])
        middle = middle_ref[own, :]
        recip = lax.rsqrt(jnp.mean(middle * middle, axis=1, keepdims=True) + EPSILON)
        unit = middle * recip
        gain_out[...] += jnp.sum(grad * unit, axis=0, keepdims=True)
        scaled = grad * gain_ref[...]
        back = recip * (scaled - unit * jnp.mean(scaled * unit, axis=1, keepdims=True))
        total = cotangent_ref[own, :].astype(jnp.float32) + back
        grad_out[own, :] = total
        branch_out[own, :] = (RESIDUAL * total).astype(jnp.bfloat16)

    begin, step, finish = line_stages(
        n, [part_ref, gates_part_ref], [summed_ref, gates_rows_ref], line, done, 1
    )
    begin()
    gain_out[...] = jnp.zeros_like(gain_out)
    lax.fori_loop(0, 2 * STEPS, step, 0)
    finish()


def turn_middle(n, part, gates_part, gates, middle, cotangent, gain, router, name):
    length, width = part.shape
    full = pl.BlockSpec(memory_space=pltpu.VMEM)
    f32 = jnp.float32
    return pl.pallas_call(
        functools.partial(turn_kernel, n),
        out_shape=[
            jax.ShapeDtypeStruct((length, width), f32),
            jax.ShapeDtypeStruct((length, width), jnp.bfloat16),
            jax.ShapeDtypeStruct(gates.shape, jnp.bfloat16),
            jax.ShapeDtypeStruct((1, width), f32),
        ],
        in_specs=[full] * 7,
        out_specs=[full] * 4,
        scratch_shapes=[
            pltpu.VMEM(part.shape, f32),
            pltpu.VMEM(gates_part.shape, f32),
            pltpu.VMEM(gates.shape, f32),
        ]
        + line_scratch([part, gates_part]),
        compiler_params=pltpu.CompilerParams(
            collective_id=name, has_side_effects=True, vmem_limit_bytes=58 << 20
        ),
        cost_estimate=pl.CostEstimate(
            flops=40 * length * width, bytes_accessed=60 * 10**6, transcendentals=0
        ),
    )(part, gates_part, gates, middle, cotangent, gain.reshape(1, width), router)


def last_kernel(count, summed_ref, tokens_ref, middle_ref, gain_ref, *refs):
    smalls, out_ref, small_outs = refs[:count], refs[count], refs[count + 1 :]
    hidden = tokens_ref[...].astype(jnp.float32)
    recip = lax.rsqrt(jnp.mean(hidden * hidden, axis=1, keepdims=True) + EPSILON)
    unit = hidden * recip
    scaled = summed_ref[...] * gain_ref[...]
    inner = jnp.mean(scaled * unit, axis=1, keepdims=True)
    out_ref[...] = middle_ref[...] + recip * (scaled - unit * inner)

    @pl.when(pl.program_id(0) == 0)
    def _():
        for small, out in zip(smalls, small_outs):
            out[...] = small[...]


def leave_first(summed, tokens, grad_middle, gain, smalls):
    length, width = tokens.shape
    rows = pl.BlockSpec((BLOCK, width), lambda i: (i, 0))
    whole = lambda shape: pl.BlockSpec(shape, lambda i: (0, 0))
    f32 = jnp.float32
    return pl.pallas_call(
        functools.partial(last_kernel, len(smalls)),
        out_shape=[jax.ShapeDtypeStruct((length, width), f32)]
        + [jax.ShapeDtypeStruct(small.shape, f32) for small in smalls],
        grid=(length // BLOCK,),
        in_specs=[rows, rows, rows, whole((1, width))] + [whole(small.shape) for small in smalls],
        out_specs=[rows] + [whole(small.shape) for small in smalls],
        compiler_params=pltpu.CompilerParams(vmem_limit_bytes=60 << 20),
        cost_estimate=pl.CostEstimate(
            flops=10 * length * width, bytes_accessed=14 * length * width, transcendentals=0
        ),
    )(summed, tokens, grad_middle, gain.reshape(1, width), *smalls)


SPAN = 768
ROWS = 256


def lane_halves(shape):
    return lax.broadcasted_iota(jnp.int32, shape, len(shape) - 1) // HEAD


def select_halves(tile, source, half):
    kept = jnp.where(lane_halves(tile.shape) == source, tile, 0.0)
    return kept if source == half else pltpu.roll(kept, HEAD, 1)


def spread_pairs(tile, target):
    for source in range(2):
        for half in range(2):
            target[2 * source + half] = select_halves(tile, source, half).astype(jnp.bfloat16)


def rope_tile(tile, cosine, sine_low, sine_high):
    return tile * cosine + pltpu.roll(tile, 128 - HEAD // 2, 1) * sine_low + pltpu.roll(
        tile, HEAD // 2, 1
    ) * sine_high


def rope_back_tile(tile, cosine, sine_low, sine_high):
    return (
        tile * cosine
        + pltpu.roll(tile * sine_low, HEAD // 2, 1)
        + pltpu.roll(tile * sine_high, 128 - HEAD // 2, 1)
    )


def window(block):
    first = block * ROWS
    return first, jnp.maximum(first + ROWS - SPAN, 0)


def attend_forward_kernel(
    heads,
    group,
    tokens_ref,
    gain_ref,
    query_w,
    key_w,
    value_w,
    cosine_ref,
    sine_low_ref,
    sine_high_ref,
    opening_ref,
    normed_out,
    query_out,
    key_out,
    value_out,
    attended_out,
    logsum_out,
    key_pairs,
    value_pairs,
    tiles_ref,
):
    tiles, length, unused = query_out.shape
    hidden = tokens_ref[...].astype(jnp.float32)
    recip = lax.rsqrt(jnp.mean(hidden * hidden, axis=1, keepdims=True) + EPSILON)
    normed_out[...] = (hidden * recip * gain_ref[...]).astype(jnp.bfloat16)
    cosine, sine_low, sine_high = cosine_ref[...], sine_low_ref[...], sine_high_ref[...]
    for tile in range(tiles):
        query = jnp.dot(
            normed_out[...],
            query_w[:, tile * 128 : (tile + 1) * 128],
            preferred_element_type=jnp.float32,
        )
        query_out[tile] = rope_tile(query, cosine, sine_low, sine_high).astype(jnp.bfloat16)
    key = rope_tile(
        jnp.dot(normed_out[...], key_w[...], preferred_element_type=jnp.float32),
        cosine,
        sine_low,
        sine_high,
    )
    value = jnp.dot(normed_out[...], value_w[...], preferred_element_type=jnp.float32)
    key_out[...] = key.astype(jnp.bfloat16)
    value_out[...] = value.astype(jnp.bfloat16)
    spread_pairs(key, key_pairs)
    spread_pairs(value, value_pairs)
    blocks = length // ROWS
    tiles_ref[...] = jnp.zeros_like(tiles_ref)

    for block in range(blocks):
        first = block * ROWS
        low = max(first + ROWS - SPAN, 0)
        rows, span = slice(first, first + ROWS), slice(low, first + ROWS)
        shape = (ROWS, first + ROWS - low)
        columns = low + lax.broadcasted_iota(jnp.int32, shape, 1)
        own = first + lax.broadcasted_iota(jnp.int32, shape, 0)

        def unit(head, carry):
            tile, half = head // 2, head % 2
            pair = 2 * (head // group) + half
            scores = right_inner(query_out[tile, rows, :], key_pairs[pair, span, :])
            allowed = (columns >= opening_ref[rows, :]) & (columns <= own)
            raised = jnp.where(allowed, jnp.exp(ATTN_SCALE * scores), 0.0)
            total = jnp.sum(raised, axis=1, keepdims=True)
            product = jnp.dot(
                raised.astype(jnp.bfloat16),
                value_pairs[pair, span, :],
                preferred_element_type=jnp.float32,
            )
            tiles_ref[tile, rows, :] += product / total
            wide = jnp.broadcast_to(jnp.log(total), (ROWS, 128))
            logsum_out[head, :, rows] = jnp.transpose(wide)[:1]
            return carry

        lax.fori_loop(0, heads, unit, 0)
    for tile in range(tiles):
        attended_out[:, tile * 128 : (tile + 1) * 128] = tiles_ref[tile].astype(jnp.bfloat16)


def attend_forward(tokens, gain, query_w, key_w, value_w, tables, opening, heads, group):
    length, width = tokens.shape
    wide = query_w.shape[1]
    tiles = wide // 128
    bf16, f32 = jnp.bfloat16, jnp.float32
    full = pl.BlockSpec(memory_space=pltpu.VMEM)
    return pl.pallas_call(
        functools.partial(attend_forward_kernel, heads, group),
        out_shape=[
            jax.ShapeDtypeStruct((length, width), bf16),
            jax.ShapeDtypeStruct((tiles, length, 128), bf16),
            jax.ShapeDtypeStruct((length, 128), bf16),
            jax.ShapeDtypeStruct((length, 128), bf16),
            jax.ShapeDtypeStruct((length, wide), bf16),
            jax.ShapeDtypeStruct((heads, 1, length), f32),
        ],
        in_specs=[full] * 9,
        out_specs=[full] * 6,
        scratch_shapes=[
            pltpu.VMEM((4, length, 128), bf16),
            pltpu.VMEM((4, length, 128), bf16),
            pltpu.VMEM((tiles, length, 128), f32),
        ],
        compiler_params=pltpu.CompilerParams(vmem_limit_bytes=48 << 20),
        cost_estimate=pl.CostEstimate(
            flops=8 * 10**9, bytes_accessed=12 * 10**6, transcendentals=5 * 10**6
        ),
    )(tokens, gain.reshape(1, width), query_w, key_w, value_w, *tables, opening.reshape(length, 1))


def attend_backward_kernel(
    n,
    heads,
    group,
    branch_ref,
    out_w,
    query_ref,
    key_ref,
    value_ref,
    attended_ref,
    logsum_ref,
    query_w,
    key_w,
    value_w,
    cosine_ref,
    sine_low_ref,
    sine_high_ref,
    opening_ref,
    tokens_ref,
    moe_ref,
    middle_ref,
    grads_out,
    normed_out,
    gain_out,
    output_ref,
    moe_sum,
    middle_rows,
    middle_sems,
    key_pairs,
    value_pairs,
    attend_grads,
    query_grads,
    key_grads,
    value_grads,
    delta_ref,
    *line,
):
    tiles, length, unused = query_ref.shape
    share = length // STEPS

    def share_rows(c):
        return pl.ds(pl.multiple_of(c * share, share), share)

    def fetch(c):
        slot = lax.rem(c, 2)
        return pltpu.make_async_copy(
            middle_ref.at[share_rows(c), :], middle_rows.at[slot], middle_sems.at[slot]
        )

    def done(c):
        fetch(c).wait()

        @pl.when(c + 1 < STEPS)
        def _():
            fetch(c + 1).start()

        total = middle_rows[lax.rem(c, 2)] + RESIDUAL * moe_sum[share_rows(c), :]
        output_ref[share_rows(c), :] = total.astype(jnp.bfloat16)

    line_start, line_step, line_end = line_stages(n, [moe_ref], [moe_sum], line, done)
    line_start()
    fetch(jnp.int32(0)).start()
    blocks = length // ROWS
    units = heads * blocks
    taken = 0

    def run_line(steps):
        nonlocal taken
        until = min(taken + steps, 2 * STEPS)
        lax.fori_loop(taken, until, line_step, 0)
        taken = until

    run_line(2)
    spread_pairs(key_ref[...].astype(jnp.float32), key_pairs)
    spread_pairs(value_ref[...].astype(jnp.float32), value_pairs)
    halves = (
        lax.broadcasted_iota(jnp.int32, (8, 128), 0) == lane_halves((8, 128))
    ).astype(jnp.float32)
    for tile in range(tiles):
        lanes = slice(tile * 128, (tile + 1) * 128)
        grad = right_inner(branch_ref[...], out_w[lanes, :]).astype(jnp.bfloat16)
        attend_grads[tile] = grad
        products = grad.astype(jnp.float32) * attended_ref[:, lanes].astype(jnp.float32)
        sums = lax.dot_general(
            halves,
            products,
            (((1,), (1,)), ((), ())),
            precision=lax.Precision.HIGHEST,
            preferred_element_type=jnp.float32,
        )
        delta_ref[2 * tile] = sums[0:1]
        delta_ref[2 * tile + 1] = sums[1:2]
        run_line(2)
    query_grads[...] = jnp.zeros_like(query_grads)
    key_grads[...] = jnp.zeros_like(key_grads)
    value_grads[...] = jnp.zeros_like(value_grads)
    before, each = taken, (2 * STEPS - 8 - taken) // units
    taken += units * each

    def unit(step, carry):
        lax.fori_loop(before + step * each, before + step * each + each, line_step, 0)
        head, block = step // blocks, step % blocks
        tile, half = head // 2, head % 2
        pair = 2 * (head // group) + half
        first, low = window(block)
        rows = pl.ds(pl.multiple_of(first, ROWS), ROWS)
        span = pl.ds(pl.multiple_of(low, ROWS), SPAN)
        keys = key_pairs[pair, span, :]
        query = query_ref[tile, rows, :]
        grad = attend_grads[tile, rows, :]
        scores = right_inner(keys, query)
        columns = low + lax.broadcasted_iota(jnp.int32, (SPAN, ROWS), 0)
        own = first + lax.broadcasted_iota(jnp.int32, (SPAN, ROWS), 1)
        allowed = (columns >= opening_ref[:, rows]) & (columns <= own)
        probs = jnp.where(
            allowed, jnp.exp(ATTN_SCALE * scores - logsum_ref[head, :, rows]), 0.0
        )
        grad_probs = right_inner(value_pairs[pair, span, :], grad)
        grad_scores = (probs * (grad_probs - delta_ref[head, :, rows])).astype(jnp.bfloat16)
        value_grads[pair, span, :] += jnp.dot(
            probs.astype(jnp.bfloat16), grad, preferred_element_type=jnp.float32
        )
        key_grads[pair, span, :] += jnp.dot(
            grad_scores, query, preferred_element_type=jnp.float32
        )
        query_grads[tile, rows, :] += left_inner(grad_scores, keys)
        return carry

    lax.fori_loop(0, units, unit, 0)
    cosine, sine_low, sine_high = cosine_ref[...], sine_low_ref[...], sine_high_ref[...]
    wide = tiles * 128
    for tile in range(tiles):
        grads_out[:, tile * 128 : (tile + 1) * 128] = rope_back_tile(
            ATTN_SCALE * query_grads[tile], cosine, sine_low, sine_high
        ).astype(jnp.bfloat16)
    totals = []
    for grads in (key_grads, value_grads):
        totals.append(
            sum(
                select_halves(grads[2 * source + half], half, source)
                for source in range(2)
                for half in range(2)
            )
        )
    grads_out[:, wide : wide + 128] = rope_back_tile(
        ATTN_SCALE * totals[0], cosine, sine_low, sine_high
    ).astype(jnp.bfloat16)
    grads_out[:, wide + 128 : wide + 256] = totals[1].astype(jnp.bfloat16)
    gain_sum = jnp.zeros((1, normed_out.shape[1]), jnp.float32)
    for block in range(blocks):
        rows = slice(block * ROWS, (block + 1) * ROWS)
        normed = (
            right_inner(grads_out[rows, :wide], query_w[...])
            + right_inner(grads_out[rows, wide : wide + 128], key_w[...])
            + right_inner(grads_out[rows, wide + 128 :], value_w[...])
        )
        normed_out[rows, :] = normed
        hidden = tokens_ref[rows, :].astype(jnp.float32)
        recip = lax.rsqrt(jnp.mean(hidden * hidden, axis=1, keepdims=True) + EPSILON)
        gain_sum += jnp.sum(normed * (hidden * recip), axis=0, keepdims=True)
        run_line(2)
    gain_out[...] = jnp.broadcast_to(gain_sum, gain_out.shape)
    run_line(2 * STEPS)
    line_end()


def attend_backward(
    n, branch, out_w, query, key, value, attended, logsum, query_w, key_w, value_w, tables, opening, tokens, moe, middle,
    heads, group, name,
):
    length, width = branch.shape
    tiles = query.shape[0]
    wide = tiles * 128
    bf16, f32 = jnp.bfloat16, jnp.float32
    full = pl.BlockSpec(memory_space=pltpu.VMEM)
    return pl.pallas_call(
        functools.partial(attend_backward_kernel, n, heads, group),
        out_shape=[
            jax.ShapeDtypeStruct((length, wide + 256), bf16),
            jax.ShapeDtypeStruct((length, width), f32),
            jax.ShapeDtypeStruct((8, width), f32),
            jax.ShapeDtypeStruct((length, width), bf16),
        ],
        in_specs=[full] * 16 + [pl.BlockSpec(memory_space=pl.ANY)],
        out_specs=[full] * 4,
        scratch_shapes=[
            pltpu.VMEM((length, width), f32),
            pltpu.VMEM((2, length // STEPS, width), f32),
            pltpu.SemaphoreType.DMA((2,)),
            pltpu.VMEM((4, length, 128), bf16),
            pltpu.VMEM((4, length, 128), bf16),
            pltpu.VMEM((tiles, length, 128), bf16),
            pltpu.VMEM((tiles, length, 128), f32),
            pltpu.VMEM((4, length, 128), f32),
            pltpu.VMEM((4, length, 128), f32),
            pltpu.VMEM((2 * tiles, 1, length), f32),
        ]
        + line_scratch([moe]),
        compiler_params=pltpu.CompilerParams(
            collective_id=name, has_side_effects=True, vmem_limit_bytes=63 << 20
        ),
        cost_estimate=pl.CostEstimate(
            flops=12 * 10**9, bytes_accessed=30 * 10**6, transcendentals=5 * 10**6
        ),
    )(
        branch, out_w, query, key, value, attended, logsum, query_w, key_w, value_w, *tables,
        opening.reshape(1, length), tokens, moe, middle,
    )


def finish_kernel(
    n,
    parts,
    local_ref,
    normed_ref,
    grads_ref,
    branch_ref,
    attended_ref,
    normed_two_ref,
    logits_ref,
    gain_ref,
    first_gain_ref,
    normed_out,
    query_out,
    key_out,
    value_out,
    branch_out,
    router_out,
    gain_out,
    first_gain_out,
    weights_ref,
    gains_ref,
    gain_send,
    gain_recv,
    *scratch,
):
    levels = parts.bit_length() - 1
    held = scratch[:levels]
    sends, recvs = scratch[levels : levels + 2]
    line_start, line_step, line_end = line_stages(n, [local_ref], [normed_out], scratch[levels + 2 :])
    me = lax.axis_index("dp")
    width = normed_ref.shape[1]
    own = width // parts
    wide, attended_wide = grads_ref.shape[1], attended_ref.shape[1]
    mine = lax.axis_index("tensor")
    line_start(
        [{"dp": jnp.bitwise_xor(me, 1 << level)} for level in range(levels)]
        + [{"tensor": lax.rem(mine + ahead, n)} for ahead in range(1, n)]
    )

    def run_line(first, last):
        lax.fori_loop(first, last, line_step, 0)

    gain_copies = [
        pltpu.make_async_remote_copy(
            src_ref=first_gain_ref,
            dst_ref=gains_ref.at[ahead],
            send_sem=gain_send.at[ahead],
            recv_sem=gain_recv.at[ahead],
            device_id={"tensor": lax.rem(mine + ahead, n)},
            device_id_type=MESH,
        )
        for ahead in range(1, n)
    ]
    for copy in gain_copies:
        copy.start()
    run_line(0, 2)
    first_gain = first_gain_ref[:1]
    for ahead, copy in enumerate(gain_copies, 1):
        copy.wait_recv()
        first_gain = first_gain + gains_ref[ahead, :1]
    pieces = 4
    block = width // pieces
    for piece in range(pieces):
        rows = slice(piece * block, (piece + 1) * block)
        weights_ref[rows, :wide] = left_inner(normed_ref[:, rows], grads_ref[...])
        weights_ref[rows, wide : wide + attended_wide] = left_inner(
            branch_ref[:, rows], attended_ref[...]
        )
        gain = jnp.transpose(jnp.broadcast_to(gain_ref[:, rows], (128, block)))
        own_gain = jnp.transpose(jnp.broadcast_to(first_gain[:, rows], (128, block)))
        lanes = lax.broadcasted_iota(jnp.int32, (block, 128), 1)
        weights_ref[rows, wide + attended_wide :] = jnp.where(
            lanes == 127,
            gain,
            jnp.where(
                lanes == 126, own_gain, left_inner(normed_two_ref[:, rows], logits_ref[...])
            ),
        )
        run_line(2 + 2 * piece, 4 + 2 * piece)
    done = 2 + 2 * pieces

    columns = weights_ref.shape[1]
    middle = columns // 256 * 128
    orders = (
        (slice(0, middle), list(range(levels))),
        (slice(middle, columns), [0] + list(range(levels - 1, 0, -1))),
    )

    def shard(number, lanes):
        return weights_ref.at[pl.ds(pl.multiple_of(number * own, own), own), lanes]

    def numbers(order, level, peer):
        fixed = sum(1 << bit for bit in order[: level + 1])
        base = jnp.bitwise_and(peer, fixed)
        free = order[level + 1 :]
        return [
            base + sum(((i >> place) & 1) << bit for place, bit in enumerate(free))
            for i in range(1 << len(free))
        ]

    def copies(level):
        made = []
        for side, (lanes, order) in enumerate(orders):
            peer = jnp.bitwise_xor(me, 1 << order[level])
            for i, number in enumerate(numbers(order, level, peer)):
                made.append(
                    pltpu.make_async_remote_copy(
                        src_ref=shard(number, lanes),
                        dst_ref=held[level].at[i, :, lanes],
                        send_sem=sends.at[side, level, i],
                        recv_sem=recvs.at[side, level, i],
                        device_id={"dp": peer},
                        device_id_type=MESH,
                    )
                )
        return made

    stops = [6] + [42] * (levels > 1) + [4, 0, 0]
    for level in range(levels):
        for copy in copies(level):
            copy.start()
        until = done + stops[level]
        run_line(done, until)
        done = until
        for copy in copies(level):
            copy.wait_recv()
        for lanes, order in orders:
            for i, number in enumerate(numbers(order, level, me)):
                target = shard(number, lanes)
                target[...] += held[level][i, :, lanes]
    everything = slice(0, columns)
    run_line(done, 2 * STEPS)
    kept = shard(me, everything)
    tail = jnp.transpose(kept[:, wide + attended_wide :])
    query_out[...] = kept[:, : query_out.shape[1]]
    key_out[...] = kept[:, wide - 256 : wide - 256 + key_out.shape[1]]
    value_out[...] = kept[:, wide - 128 : wide - 128 + value_out.shape[1]]
    branch_out[...] = kept[:, wide : wide + branch_out.shape[1]]
    router_out[...] = tail[: router_out.shape[0]]
    gain_out[...] = tail[127:]
    first_gain_out[...] = tail[126:127]
    for level in range(levels):
        for copy in copies(level):
            copy.wait_send()
    for copy in gain_copies:
        copy.wait_send()
    line_end()


def finish(
    n, parts, grad_local, normed_b, grads_wide, branch_b, attended, normed_two_b, grad_logits_b, gain_grad, first_gain_grad,
    wide_q, wide_k, experts, name,
):
    length, width = normed_b.shape
    columns = grads_wide.shape[1] + attended.shape[1] + 128
    full = pl.BlockSpec(memory_space=pltpu.VMEM)
    levels = parts.bit_length() - 1
    own = width // parts
    f32 = jnp.float32
    shapes = [(length, width), (own, wide_q), (own, wide_k), (own, wide_k), (own, wide_q)]
    shapes += [(experts, own), (1, own), (1, own)]
    return pl.pallas_call(
        functools.partial(finish_kernel, n, parts),
        out_shape=[jax.ShapeDtypeStruct(shape, f32) for shape in shapes],
        in_specs=[full] * 9,
        out_specs=[full] * 8,
        scratch_shapes=[
            pltpu.VMEM((width, columns), f32),
            pltpu.VMEM((n, 8, width), f32),
            pltpu.SemaphoreType.DMA((n,)),
            pltpu.SemaphoreType.DMA((n,)),
        ]
        + [pltpu.VMEM((parts >> (level + 1), own, columns), f32) for level in range(levels)]
        + [pltpu.SemaphoreType.DMA((2, levels, parts // 2))] * 2
        + line_scratch([grad_local]),
        compiler_params=pltpu.CompilerParams(
            collective_id=name, has_side_effects=True, vmem_limit_bytes=62 << 20
        ),
        cost_estimate=pl.CostEstimate(
            flops=2 * length * width * columns, bytes_accessed=50 * 10**6, transcendentals=0
        ),
    )(
        grad_local, normed_b, grads_wide, branch_b, attended, normed_two_b, grad_logits_b, gain_grad,
        first_gain_grad,
    )


def place_kernel(gate_ref, up_ref, down_ref, *refs):
    gate_out, up_out, down_out = refs[-3:]
    gate_out[0] = gate_ref[0, 0]
    up_out[0] = up_ref[0, 0]
    rows, hidden = down_out.shape[1], down_ref.shape[3]
    for piece in range(down_out.shape[2] // hidden):
        down_out[0, :, piece * hidden : (piece + 1) * hidden] = down_ref[
            0, 0, piece * rows : (piece + 1) * rows, :
        ]


def place_shards(parts, shards, first, experts, before):
    number, unused, rows, hidden = shards.shape
    down_rows = hidden // parts
    width = rows * parts
    shapes = [(experts, rows, hidden), (experts, rows, hidden), (experts, down_rows, width)]
    spec = lambda shape: pl.BlockSpec((1,) + shape[1:], lambda e: (first + e, 0, 0))
    one = lambda kind: pl.BlockSpec((1, 1, rows, hidden), lambda e: (e, kind, 0, 0))
    args, extra, aliases = [shards] * 3, [], {}
    if before is not None:
        args += list(before)
        extra = [pl.BlockSpec(memory_space=pl.ANY)] * 3
        aliases = {3: 0, 4: 1, 5: 2}
    return pl.pallas_call(
        place_kernel,
        out_shape=[jax.ShapeDtypeStruct(shape, jnp.float32) for shape in shapes],
        grid=(number,),
        in_specs=[one(kind) for kind in range(3)] + extra,
        out_specs=[spec(shape) for shape in shapes],
        input_output_aliases=aliases,
        compiler_params=pltpu.CompilerParams(vmem_limit_bytes=60 << 20),
        cost_estimate=pl.CostEstimate(
            flops=0, bytes_accessed=8 * shards.size, transcendentals=0
        ),
    )(*args)


def on_device(
    ring,
    tokens,
    cotangent,
    segment_ids,
    routes,
    attn_gain,
    query_weight,
    key_weight,
    value_weight,
    out_weight,
    ffn_gain,
    router_weight,
    gate_weight,
    up_weight,
    down_weight,
):
    length = tokens.shape[0]
    width = tokens.shape[1]
    segment = segment_ids[0]
    heads_local = query_weight.shape[1] // HEAD
    kv_local = key_weight.shape[1] // HEAD
    group_size = heads_local // kv_local
    experts_all = router_weight.shape[1]
    experts_local = gate_weight.shape[0]
    parts = lax.axis_size("dp")
    opening = doc_openings(segment)
    tables = rope_tables(opening, HEAD)
    query_w, key_w, value_w = (pad_columns(w) for w in (query_weight, key_weight, value_weight))
    out_w = jnp.transpose(pad_columns(jnp.transpose(out_weight)))
    ways, out_rows = gather_out_weight(out_weight, parts)
    normed_b, queries, keys, values, attended, logsum = attend_forward(
        tokens, attn_gain, query_w, key_w, value_w, tables, opening, heads_local, group_size
    )
    all_ids = jnp.arange(experts_all, dtype=jnp.int32)
    chosen = jnp.sum((routes[:, :, None] == all_ids[None, None, :]).astype(jnp.int32), axis=1) > 0
    first_expert = lax.axis_index("tensor") * experts_local
    local_ids = first_expert + jnp.arange(experts_local, dtype=jnp.int32)
    picked = jnp.sum((routes[None, :, :] == local_ids[:, None, None]).astype(jnp.int32), axis=2)
    places_in = slot_places(picked)
    counts = jnp.sum(picked, axis=1)
    out_rows, attended = lax.optimization_barrier((out_rows, attended))
    out_all = lax.all_gather(out_rows, "dp") if ways > 1 else out_rows[None]
    attended_all = line_gather(attended, ring, 1)
    attended_all = attended_all.reshape(length, ring, attended.shape[1])
    attended_all = attended_all[:, :, : heads_local * HEAD].reshape(length, -1)
    router_w = pad_columns(router_weight)
    middle, normed_two_b, gate_probs = enter_middle(
        attended_all, out_all, tokens, ffn_gain, router_w, pad_columns(chosen.astype(jnp.float32))
    )
    gate_rows = jnp.transpose(lax.dynamic_slice_in_dim(gate_probs, first_expert, experts_local, 1))
    numbers = (max(1, experts_local // 10),)
    numbers += (experts_local - numbers[0],)
    (grads_first,), sums = expert_stage(
        parts, 0, numbers[:1], counts, places_in, gate_rows, normed_two_b, cotangent,
        gate_weight, up_weight, down_weight, None,
    )
    shards_first = lax.psum_scatter(grads_first, "dp", scatter_dimension=2, tiled=True)
    (grads_last,), sums_last = expert_stage(
        parts, numbers[0], numbers[1:], counts, places_in, gate_rows, normed_two_b, cotangent,
        gate_weight, up_weight, down_weight, sums,
    )
    moe_part, grad_normed_part, unused = sums_last
    shards_first, grads_last, grad_normed_part = lax.optimization_barrier(
        (shards_first, grads_last, grad_normed_part)
    )
    shards_last = lax.psum_scatter(grads_last, "dp", scatter_dimension=2, tiled=True)
    grad_gates_local = jnp.concatenate([sums[2], sums_last[2]], 0).reshape(experts_local, length)
    grad_gates_part = lax.dynamic_update_slice_in_dim(
        jnp.zeros((experts_all, length), jnp.float32), grad_gates_local, first_expert, 0
    )
    grad_middle, grad_branch_b, grad_logits_b, grad_ffn_gain = turn_middle(
        ring, grad_normed_part, grad_gates_part, gate_probs, middle, cotangent, ffn_gain, router_w, 2
    )
    grads_wide, grad_normed_local, first_gain, output = attend_backward(
        ring, grad_branch_b, out_w, queries, keys, values, attended, logsum,
        query_w, key_w, value_w, tables, opening, tokens, moe_part, middle, heads_local, group_size, 3,
    )
    wide_q, wide_k = heads_local * HEAD, kv_local * HEAD
    grads_placed = place_shards(parts, shards_first, 0, experts_local, None)
    grads_placed, grads_wide = lax.optimization_barrier((grads_placed, grads_wide))
    grad_normed, *small = finish(
        ring, parts, grad_normed_local, normed_b, grads_wide, grad_branch_b, attended, normed_two_b,
        grad_logits_b, grad_ffn_gain, first_gain, wide_q, wide_k, experts_all, 4,
    )
    grad_tokens, *small = leave_first(grad_normed, tokens, grad_middle, attn_gain, small)
    grad_query, grad_key, grad_value, grad_out, grad_router, grad_ffn_gain, grad_attn_gain = small
    shards_last, grad_tokens = lax.optimization_barrier((shards_last, grad_tokens))
    grad_gate, grad_up, grad_down = place_shards(
        parts, shards_last, numbers[0], experts_local, grads_placed
    )
    return (
        output,
        grad_tokens,
        grad_attn_gain.reshape(-1),
        grad_query,
        grad_key,
        grad_value,
        jnp.transpose(grad_out),
        grad_ffn_gain.reshape(-1),
        jnp.transpose(grad_router),
        grad_gate,
        grad_up,
        grad_down,
    )


def solution(mesh):
    return jax.shard_map(
        functools.partial(on_device, mesh.shape["tensor"]),
        mesh=mesh,
        in_specs=(
            P("dp", None),
            P("dp", None),
            P("dp", None),
            P("dp", None),
            P(),
            P(None, "tensor"),
            P(None, "tensor"),
            P(None, "tensor"),
            P("tensor", None),
            P(),
            P(),
            P("tensor", None, None),
            P("tensor", None, None),
            P("tensor", None, None),
        ),
        out_specs=(
            P("dp", None),
            P("dp", None),
            P("dp"),
            P("dp", "tensor"),
            P("dp", "tensor"),
            P("dp", "tensor"),
            P("tensor", "dp"),
            P("dp"),
            P("dp", None),
            P("tensor", "dp", None),
            P("tensor", "dp", None),
            P("tensor", "dp", None),
        ),
        check_vma=False,
    )
```

```python
import functools

import jax
import jax.numpy as jnp
from jax import lax
from jax.experimental import pallas as pl
from jax.experimental.pallas import tpu as pltpu
from jax.sharding import PartitionSpec as P

MESH = pl.DeviceIdType.MESH

HEAD = 64
CAP = 384


EPSILON = 1e-06
RESIDUAL = 0.22
ATTN_SCALE = 0.015625
ROPE_BASE = 10000.0


def left_inner(first, second):
    return lax.dot_general(
        first, second, (((0,), (0,)), ((), ())), preferred_element_type=jnp.float32
    )


def right_inner(first, second):
    return lax.dot_general(
        first, second, (((1,), (1,)), ((), ())), preferred_element_type=jnp.float32
    )


def doc_openings(segment):
    return jnp.sum((segment[None, :] < segment[:, None]).astype(jnp.int32), axis=1)


def rope_tables(opening, head_size):
    halfway = head_size // 2
    spread = jnp.arange(halfway, dtype=jnp.float32) * (2.0 / head_size)
    inverse = jnp.power(ROPE_BASE, -spread)
    places = jnp.arange(opening.shape[0], dtype=jnp.int32)
    angles = (places - opening).astype(jnp.float32)[:, None] * inverse[None, :]
    cosine, sine = jnp.cos(angles), jnp.sin(angles)
    none = jnp.zeros_like(sine)
    return (
        jnp.concatenate([cosine] * 4, 1),
        jnp.concatenate([-sine, none] * 2, 1),
        jnp.concatenate([none, sine] * 2, 1),
    )


def pad_columns(weight):
    missing = -weight.shape[1] % 128
    return weight if missing == 0 else jnp.pad(weight, ((0, 0), (0, missing)))


def rms_forward(hidden, gain):
    recip = lax.rsqrt(jnp.mean(hidden * hidden, axis=-1, keepdims=True) + EPSILON)
    unit = hidden * recip
    return (unit * gain, unit, recip)


def rms_backward(gradient, unit, recip, gain):
    gain_grad = jnp.sum(gradient * unit, axis=0)
    scaled = gradient * gain
    return (recip * (scaled - unit * jnp.mean(scaled * unit, axis=-1, keepdims=True)), gain_grad)


def slot_places(picked):
    length = picked.shape[1]
    tokens = jnp.arange(length, dtype=jnp.int32)
    earlier = (tokens[:, None] < tokens[None, :]).astype(jnp.bfloat16)
    before = jnp.dot(picked.astype(jnp.bfloat16), earlier, preferred_element_type=jnp.float32)
    return jnp.where(picked > 0, before.astype(jnp.int32), -1)


STEPS = 32
LAG = 2


def line_stages(n, xs, outs, scratch, done=None, whole=0):
    count = len(xs)
    lows, highs = scratch[:count], scratch[count : 2 * count]
    low_recv, high_recv, total_recv, up_send, low_send, high_send = scratch[2 * count :]
    me = lax.axis_index("tensor")
    root = n // 2
    has_low, has_high = me > 0, me < n - 1

    def begin(others=()):
        barrier = pltpu.get_barrier_semaphore()
        for other in others:
            pl.semaphore_signal(barrier, inc=1, device_id=other, device_id_type=MESH)

        @pl.when(has_low)
        def _():
            pl.semaphore_signal(barrier, inc=1, device_id={"tensor": me - 1}, device_id_type=MESH)

        @pl.when(has_high)
        def _():
            pl.semaphore_signal(barrier, inc=1, device_id={"tensor": me + 1}, device_id_type=MESH)

        pl.semaphore_wait(
            barrier, len(others) + has_low.astype(jnp.int32) + has_high.astype(jnp.int32)
        )

    def piece(ref, c):
        rows = ref.shape[0] // STEPS
        return ref.at[pl.ds(pl.multiple_of(c * rows, rows), rows), :]

    cut = count - whole

    def copies(sources, targets, c, send, recv, to, uncut):
        return [
            pltpu.make_async_remote_copy(
                src_ref=source if uncut else piece(source, c),
                dst_ref=target if uncut else piece(target, c),
                send_sem=send.at[i, c],
                recv_sem=recv.at[i, c],
                device_id={"tensor": to},
                device_id_type=MESH,
            )
            for i, (source, target) in enumerate(zip(sources, targets))
            if (i >= cut) == uncut
        ]

    def each(sources, targets, c, send, recv, to, act):
        for copy in copies(sources, targets, c, send, recv, to, False):
            act(copy)
        if whole:

            @pl.when(c == 0)
            def _():
                for copy in copies(sources, targets, 0, send, recv, to, True):
                    act(copy)

    def start(sources, targets, c, send, recv, to):
        each(sources, targets, c, send, recv, to, lambda copy: copy.start())

    def arrived(targets, c, send, recv):
        each(targets, targets, c, send, recv, me, lambda copy: copy.wait_recv())

    def add(c, terms, targets):
        for i, target in enumerate(targets):
            if i < cut:
                piece(target, c)[...] = functools.reduce(
                    jnp.add, [piece(term[i], c)[...] for term in terms]
                )
            else:

                @pl.when(c == 0)
                def _():
                    target[...] = functools.reduce(jnp.add, [term[i][...] for term in terms])

    def reduce_step(c):
        for side, inner, held, recv, to in (
            (me < root, has_low, lows, low_recv, me + 1),
            (me > root, has_high, highs, high_recv, me - 1),
        ):

            @pl.when(side & inner)
            def _():
                arrived(held, c, up_send, recv)
                add(c, (held, xs), held)
                start(held, held, c, up_send, recv, to)

            @pl.when(side & jnp.logical_not(inner))
            def _():
                start(xs, held, c, up_send, recv, to)

        @pl.when(me == root)
        def _():
            arrived(lows, c, up_send, low_recv)
            if root < n - 1:
                arrived(highs, c, up_send, high_recv)
            add(c, (xs, lows, highs) if root < n - 1 else (xs, lows), outs)
            start(outs, outs, c, low_send, total_recv, me - 1)
            if root < n - 1:
                start(outs, outs, c, high_send, total_recv, me + 1)
            if done is not None:
                done(c)

    def total_step(c):
        @pl.when(me != root)
        def _():
            arrived(outs, c, low_send, total_recv)

        @pl.when((me < root) & has_low)
        def _():
            start(outs, outs, c, low_send, total_recv, me - 1)

        @pl.when((me > root) & has_high)
        def _():
            start(outs, outs, c, high_send, total_recv, me + 1)

        if done is not None:

            @pl.when(me != root)
            def _():
                done(c)

    lag = jnp.where(has_low & has_high, LAG, STEPS)

    def step(t, carry):
        @pl.when(t < STEPS)
        def _():
            reduce_step(t)

        @pl.when((t >= lag) & (t - lag < STEPS))
        def _():
            total_step(t - lag)

        return carry

    def finish():
        def drain(c, carry):
            for condition, send in (
                (me != root, up_send),
                ((me <= root) & has_low, low_send),
                ((me >= root) & has_high, high_send),
            ):

                @pl.when(condition)
                def _():
                    each(xs, lows, c, send, low_recv, me, lambda copy: copy.wait_send())

            return carry

        lax.fori_loop(0, STEPS, drain, 0)

    return begin, step, finish


def line_scratch(arrays):
    return [pltpu.VMEM(array.shape, jnp.float32) for array in arrays * 2] + [
        pltpu.SemaphoreType.DMA((len(arrays), STEPS))
    ] * 6


def expert_kernel(
    parts,
    first,
    numbers,
    chained,
    count_ref,
    place_ref,
    gate_ref,
    normed_ref,
    grad_ref,
    gate_w,
    up_w,
    down_w,
    *refs,
):
    if chained:
        moe_in, back_in = refs[:2]
        refs = refs[2:]
    grads_out, refs = refs[: len(numbers)], refs[len(numbers) :]
    moe_final, back_final, gates_out = refs[:3]
    moe_out, back_out, rows_ref, grads_ref, active_ref, gate_in_ref, up_in_ref, weights_ref = refs[3:11]
    sems, out_sems = refs[11:]
    expert = pl.program_id(0)
    filled = count_ref[first + expert]
    length, width = normed_ref.shape
    hidden_size = gate_w.shape[2]
    sizes = (128, 256, CAP)

    def by_size(run):
        low = None
        for rows in sizes:
            fits = filled <= rows if low is None else filled > low
            if low is not None and rows != sizes[-1]:
                fits = fits & (filled <= rows)
            pl.when(fits)(functools.partial(run, rows))
            low = rows

    def sum_copies(sources, targets):
        rows = length // 4
        return [
            pltpu.make_async_copy(
                source.at[pl.ds(piece * rows, rows), :],
                target.at[pl.ds(piece * rows, rows), :],
                sems.at[i, piece],
            )
            for i, (source, target) in enumerate(zip(sources, targets))
            for piece in range(4)
        ]

    if chained:
        entering = sum_copies((moe_in, back_in), (moe_out, back_out))

        @pl.when(expert == 0)
        def _():
            for copy in entering:
                copy.start()

    else:

        @pl.when(expert == 0)
        def _():
            moe_out[...] = jnp.zeros_like(moe_out)
            back_out[...] = jnp.zeros_like(back_out)

    def slots(rows):
        mask = lax.broadcasted_iota(jnp.int32, (rows, length), 0) == place_ref[0]
        return mask, jnp.where(mask, 1.0, 0.0).astype(jnp.bfloat16)

    def enter(rows):
        mask, picks = slots(rows)
        rows_in = jnp.dot(picks, normed_ref[...], preferred_element_type=jnp.float32).astype(jnp.bfloat16)
        grad_rows = (
            RESIDUAL * jnp.dot(picks, grad_ref[...], preferred_element_type=jnp.float32)
        ).astype(jnp.bfloat16)
        rows_ref[:rows] = rows_in
        grads_ref[:rows] = grad_rows
        gate = jnp.sum(jnp.where(mask, gate_ref[0], 0.0), axis=1, keepdims=True)
        gate_input = jnp.dot(rows_in, gate_w[0], preferred_element_type=jnp.float32)
        up_input = jnp.dot(rows_in, up_w[0], preferred_element_type=jnp.float32)
        grad_act = right_inner(grad_rows, down_w[0])
        sigmoid_val = jax.nn.sigmoid(gate_input)
        silu_out = gate_input * sigmoid_val
        hidden = silu_out * up_input
        active_ref[:rows] = (hidden * gate).astype(jnp.bfloat16)
        column = jnp.sum(grad_act * hidden, axis=1, keepdims=True)
        gates_out[0] = jnp.sum(jnp.where(mask, column, 0.0), axis=0, keepdims=True)
        grad_hidden = grad_act * gate
        gate_in_ref[:rows] = (
            grad_hidden * up_input * sigmoid_val * (1.0 + gate_input * (1.0 - sigmoid_val))
        ).astype(jnp.bfloat16)
        up_in_ref[:rows] = (grad_hidden * silu_out).astype(jnp.bfloat16)

    by_size(enter)
    if chained:

        @pl.when(expert == 0)
        def _():
            for copy in entering:
                copy.wait()

    def leave(rows):
        column = jnp.transpose(jnp.broadcast_to(place_ref[0], (128, length)))
        column = jnp.concatenate([column] * (rows // 128), 1)
        own = lax.broadcasted_iota(jnp.int32, (length, rows), 1)
        picks = jnp.where(own == column, 1.0, 0.0).astype(jnp.bfloat16)
        moe = jnp.dot(active_ref[:rows], down_w[0], preferred_element_type=jnp.float32)
        moe_out[...] += jnp.dot(
            picks, moe.astype(jnp.bfloat16), preferred_element_type=jnp.float32
        )
        back = right_inner(gate_in_ref[:rows], gate_w[0]) + right_inner(up_in_ref[:rows], up_w[0])
        back_out[...] += jnp.dot(
            picks, back.astype(jnp.bfloat16), preferred_element_type=jnp.float32
        )

    by_size(leave)
    leaving = sum_copies((moe_out, back_out), (moe_final, back_final))
    last = expert == pl.num_programs(0) - 1

    @pl.when(last)
    def _():
        for copy in leaving:
            copy.start()

    def copies(target, number):
        rows = width // 4
        return [
            pltpu.make_async_copy(
                weights_ref.at[kind, pl.ds(piece * rows, rows), :],
                target.at[number, kind, pl.ds(piece * rows, rows), :],
                out_sems.at[kind, piece],
            )
            for kind in range(3)
            for piece in range(4)
        ]

    @pl.when(expert > 0)
    def _():
        for copy in copies(grads_out[0], 0):
            copy.wait()

    def weigh(rows):
        grads = left_inner(
            rows_ref[:rows], jnp.concatenate([gate_in_ref[:rows], up_in_ref[:rows]], 1)
        )
        weights_ref[0] = grads[:, :hidden_size]
        weights_ref[1] = grads[:, hidden_size:]
        grad_down = left_inner(active_ref[:rows], grads_ref[:rows])
        own = hidden_size // parts
        blocks = width // hidden_size
        for part in range(parts):
            for piece in range(blocks):
                at = (part * blocks + piece) * own
                weights_ref[2, at : at + own, :] = grad_down[
                    part * own : (part + 1) * own, piece * hidden_size : (piece + 1) * hidden_size
                ]

    by_size(weigh)
    start = 0
    for target, number in zip(grads_out, numbers):

        @pl.when((expert >= start) & (expert < start + number))
        def _():
            for copy in copies(target, expert - start):
                copy.start()

        start += number

    @pl.when(last)
    def _():
        for copy in copies(grads_out[0], 0) + leaving:
            copy.wait()


def expert_stage(parts, first, numbers, counts, places, gate_rows, normed_b, grad_b, gate_w, up_w, down_w, sums):
    number = sum(numbers)
    length, width = normed_b.shape
    hidden = gate_w.shape[2]
    experts = places.shape[0]
    chained = sums is not None
    whole = lambda e, c: (0, 0)
    row_spec = pl.BlockSpec((1, 1, length), lambda e, c: (first + e, 0, 0))
    once = pl.Buffered(1)
    f32, bf16 = jnp.float32, jnp.bfloat16
    in_specs = [
        row_spec,
        row_spec,
        pl.BlockSpec((length, width), whole, pipeline_mode=once),
        pl.BlockSpec((length, width), whole, pipeline_mode=once),
        pl.BlockSpec((1, width, hidden), lambda e, c: (first + e, 0, 0)),
        pl.BlockSpec((1, width, hidden), lambda e, c: (first + e, 0, 0)),
        pl.BlockSpec((1, hidden, width), lambda e, c: (first + e, 0, 0)),
    ]
    args = [
        counts,
        places.reshape(experts, 1, length),
        gate_rows.reshape(experts, 1, length),
        normed_b,
        grad_b,
        gate_w,
        up_w,
        down_w,
    ]
    if chained:
        in_specs += [pl.BlockSpec(memory_space=pl.ANY)] * 2
        args += [sums[0], sums[1]]
    results = pl.pallas_call(
        functools.partial(expert_kernel, parts, first, numbers, chained),
        out_shape=[jax.ShapeDtypeStruct((some, 3, width, hidden), f32) for some in numbers]
        + [
            jax.ShapeDtypeStruct((length, width), f32),
            jax.ShapeDtypeStruct((length, width), f32),
            jax.ShapeDtypeStruct((number, 1, length), f32),
        ],
        grid_spec=pltpu.PrefetchScalarGridSpec(
            num_scalar_prefetch=1,
            grid=(number,),
            in_specs=in_specs,
            out_specs=[pl.BlockSpec(memory_space=pl.ANY)] * len(numbers)
            + [
                pl.BlockSpec(memory_space=pl.ANY),
                pl.BlockSpec(memory_space=pl.ANY),
                pl.BlockSpec((1, 1, length), lambda e, c: (e, 0, 0)),
            ],
            scratch_shapes=[
                pltpu.VMEM((length, width), f32),
                pltpu.VMEM((length, width), f32),
                pltpu.VMEM((CAP, width), bf16),
                pltpu.VMEM((CAP, width), bf16),
                pltpu.VMEM((CAP, hidden), bf16),
                pltpu.VMEM((CAP, hidden), bf16),
                pltpu.VMEM((CAP, hidden), bf16),
                pltpu.VMEM((3, width, hidden), f32),
                pltpu.SemaphoreType.DMA((2, 4)),
                pltpu.SemaphoreType.DMA((3, 4)),
            ],
        ),
        compiler_params=pltpu.CompilerParams(
            dimension_semantics=("arbitrary",), vmem_limit_bytes=63 << 20
        ),
        cost_estimate=pl.CostEstimate(
            flops=number * 8 * 10**9, bytes_accessed=number * 14 * 10**6, transcendentals=0
        ),
    )(*args)
    return results[: len(numbers)], results[len(numbers) :]


PIECES = 16


def line_gather_kernel(n, x_ref, out_ref, blocks_ref, recv, up_send, down_send):
    me = lax.axis_index("tensor")
    has_low, has_high = me > 0, me < n - 1
    barrier = pltpu.get_barrier_semaphore()

    @pl.when(has_low)
    def _():
        pl.semaphore_signal(barrier, inc=1, device_id={"tensor": me - 1}, device_id_type=MESH)

    @pl.when(has_high)
    def _():
        pl.semaphore_signal(barrier, inc=1, device_id={"tensor": me + 1}, device_id_type=MESH)

    blocks_ref[me] = x_ref[...].astype(jnp.float32)
    pl.semaphore_wait(barrier, has_low.astype(jnp.int32) + has_high.astype(jnp.int32))
    rows = x_ref.shape[0] // PIECES

    def copy(block, c, send, to):
        piece = blocks_ref.at[block, pl.ds(pl.multiple_of(c * rows, rows), rows), :]
        return pltpu.make_async_remote_copy(
            src_ref=piece,
            dst_ref=piece,
            send_sem=send.at[block, c],
            recv_sem=recv.at[block, c],
            device_id={"tensor": to},
            device_id_type=MESH,
        )

    for hop in range(n):
        low, high = me - hop, me + hop

        def step(c, carry):
            @pl.when(low >= 0)
            def _():
                if hop > 0:
                    copy(low, c, up_send, me).wait_recv()

                @pl.when(has_high)
                def _():
                    copy(low, c, up_send, me + 1).start()

            @pl.when(high < n)
            def _():
                if hop > 0:
                    copy(high, c, down_send, me).wait_recv()

                @pl.when(has_low)
                def _():
                    copy(high, c, down_send, me - 1).start()

            return carry

        lax.fori_loop(0, PIECES, step, 0)
    wide = x_ref.shape[1]
    for block in range(n):
        out_ref[:, block * wide : (block + 1) * wide] = blocks_ref[block].astype(jnp.bfloat16)
    for hop in range(n):
        low, high = me - hop, me + hop

        def drain(c, carry):
            @pl.when((low >= 0) & has_high)
            def _():
                copy(low, c, up_send, me).wait_send()

            @pl.when((high < n) & has_low)
            def _():
                copy(high, c, down_send, me).wait_send()

            return carry

        lax.fori_loop(0, PIECES, drain, 0)


def line_gather(x, n, name):
    length, wide = x.shape
    full = pl.BlockSpec(memory_space=pltpu.VMEM)
    return pl.pallas_call(
        functools.partial(line_gather_kernel, n),
        out_shape=jax.ShapeDtypeStruct((length, n * wide), jnp.bfloat16),
        in_specs=[full],
        out_specs=full,
        scratch_shapes=[pltpu.VMEM((n, length, wide), jnp.float32)]
        + [pltpu.SemaphoreType.DMA((n, PIECES))] * 3,
        compiler_params=pltpu.CompilerParams(
            collective_id=name, has_side_effects=True, vmem_limit_bytes=32 << 20
        ),
        cost_estimate=pl.CostEstimate(
            flops=0, bytes_accessed=16 * n * x.size, transcendentals=0
        ),
    )(x)


BLOCK = 256


def own_rows_kernel(parts, weight_ref, out_ref):
    rows = out_ref.shape[0]
    first = lax.axis_index("dp") * rows if parts > 1 else 0
    out_ref[...] = weight_ref[pl.ds(pl.multiple_of(first, 16), rows), :].astype(jnp.float32)


def gather_out_weight(out_weight, parts):
    rows, width = out_weight.shape
    ways = parts if rows % (16 * parts) == 0 else 1
    full = pl.BlockSpec(memory_space=pltpu.VMEM)
    own = pl.pallas_call(
        functools.partial(own_rows_kernel, ways),
        out_shape=jax.ShapeDtypeStruct((rows // ways, width), jnp.float32),
        in_specs=[full],
        out_specs=full,
    )(out_weight)
    return ways, lax.all_gather(own, "tensor")


def middle_kernel(
    attended_ref, weight_all_ref, tokens_ref, gain_ref, router_ref, chosen_ref, middle_out, normed_out, gates_out, weight_ref
):
    ways, n, rows, unused = weight_all_ref.shape

    @pl.when(pl.program_id(0) == 0)
    def _():
        for way in range(ways):
            for block in range(n):
                at = (block * ways + way) * rows
                weight_ref[at : at + rows, :] = weight_all_ref[way, block].astype(jnp.bfloat16)

    branch = jnp.dot(attended_ref[...], weight_ref[...], preferred_element_type=jnp.float32)
    middle = tokens_ref[...].astype(jnp.float32) + RESIDUAL * branch
    middle_out[...] = middle
    recip = lax.rsqrt(jnp.mean(middle * middle, axis=1, keepdims=True) + EPSILON)
    normed = (middle * recip * gain_ref[...]).astype(jnp.bfloat16)
    normed_out[...] = normed
    logits = jnp.dot(normed, router_ref[...], preferred_element_type=jnp.float32)
    raised = jnp.where(chosen_ref[...] > 0.0, jnp.exp(logits), 0.0)
    gates_out[...] = raised / jnp.sum(raised, axis=1, keepdims=True)


def enter_middle(attended, weight_all, tokens, gain, router, chosen):
    length, width = tokens.shape
    rows = lambda columns: pl.BlockSpec((BLOCK, columns), lambda i: (i, 0))
    whole = lambda shape: pl.BlockSpec(
        shape, lambda i: (0,) * len(shape), pipeline_mode=pl.Buffered(1)
    )
    experts = router.shape[1]
    return pl.pallas_call(
        middle_kernel,
        out_shape=[
            jax.ShapeDtypeStruct((length, width), jnp.float32),
            jax.ShapeDtypeStruct((length, width), jnp.bfloat16),
            jax.ShapeDtypeStruct((length, experts), jnp.float32),
        ],
        grid=(length // BLOCK,),
        in_specs=[
            rows(attended.shape[1]),
            whole(weight_all.shape),
            rows(width),
            whole((1, width)),
            whole(router.shape),
            rows(experts),
        ],
        out_specs=[rows(width), rows(width), rows(experts)],
        scratch_shapes=[pltpu.VMEM((attended.shape[1], width), jnp.bfloat16)],
        compiler_params=pltpu.CompilerParams(
            dimension_semantics=("arbitrary",), vmem_limit_bytes=48 << 20
        ),
        cost_estimate=pl.CostEstimate(
            flops=2 * length * width * width, bytes_accessed=25 * 10**6, transcendentals=0
        ),
    )(attended, weight_all, tokens, gain.reshape(1, width), router, chosen)


def turn_kernel(
    n,
    part_ref,
    gates_part_ref,
    gates_ref,
    middle_ref,
    cotangent_ref,
    gain_ref,
    router_ref,
    grad_out,
    branch_out,
    logits_out,
    gain_out,
    summed_ref,
    gates_rows_ref,
    grad_gates_ref,
    *line,
):
    length = part_ref.shape[0]
    rows = length // STEPS

    def done(c):
        @pl.when(c == 0)
        def _():
            experts = gates_rows_ref.shape[0]
            empty = jnp.zeros((grad_gates_ref.shape[1] - experts, length), jnp.float32)
            grad_gates_ref[...] = jnp.transpose(
                jnp.concatenate([gates_rows_ref[...], empty], 0)
            )

        own = pl.ds(pl.multiple_of(c * rows, rows), rows)
        gates, grad_gates = gates_ref[own, :], grad_gates_ref[own, :]
        weighted = jnp.sum(gates * grad_gates, axis=1, keepdims=True)
        grad_logits = (gates * (grad_gates - weighted)).astype(jnp.bfloat16)
        logits_out[own, :] = grad_logits
        grad = summed_ref[own, :] + right_inner(grad_logits, router_ref[...])
        middle = middle_ref[own, :]
        recip = lax.rsqrt(jnp.mean(middle * middle, axis=1, keepdims=True) + EPSILON)
        unit = middle * recip
        gain_out[...] += jnp.sum(grad * unit, axis=0, keepdims=True)
        scaled = grad * gain_ref[...]
        back = recip * (scaled - unit * jnp.mean(scaled * unit, axis=1, keepdims=True))
        total = cotangent_ref[own, :].astype(jnp.float32) + back
        grad_out[own, :] = total
        branch_out[own, :] = (RESIDUAL * total).astype(jnp.bfloat16)

    begin, step, finish = line_stages(
        n, [part_ref, gates_part_ref], [summed_ref, gates_rows_ref], line, done, 1
    )
    begin()
    gain_out[...] = jnp.zeros_like(gain_out)
    lax.fori_loop(0, 2 * STEPS, step, 0)
    finish()


def turn_middle(n, part, gates_part, gates, middle, cotangent, gain, router, name):
    length, width = part.shape
    full = pl.BlockSpec(memory_space=pltpu.VMEM)
    f32 = jnp.float32
    return pl.pallas_call(
        functools.partial(turn_kernel, n),
        out_shape=[
            jax.ShapeDtypeStruct((length, width), f32),
            jax.ShapeDtypeStruct((length, width), jnp.bfloat16),
            jax.ShapeDtypeStruct(gates.shape, jnp.bfloat16),
            jax.ShapeDtypeStruct((1, width), f32),
        ],
        in_specs=[full] * 7,
        out_specs=[full] * 4,
        scratch_shapes=[
            pltpu.VMEM(part.shape, f32),
            pltpu.VMEM(gates_part.shape, f32),
            pltpu.VMEM(gates.shape, f32),
        ]
        + line_scratch([part, gates_part]),
        compiler_params=pltpu.CompilerParams(
            collective_id=name, has_side_effects=True, vmem_limit_bytes=58 << 20
        ),
        cost_estimate=pl.CostEstimate(
            flops=40 * length * width, bytes_accessed=60 * 10**6, transcendentals=0
        ),
    )(part, gates_part, gates, middle, cotangent, gain.reshape(1, width), router)


def last_kernel(count, summed_ref, tokens_ref, middle_ref, gain_ref, *refs):
    smalls, out_ref, small_outs = refs[:count], refs[count], refs[count + 1 :]
    hidden = tokens_ref[...].astype(jnp.float32)
    recip = lax.rsqrt(jnp.mean(hidden * hidden, axis=1, keepdims=True) + EPSILON)
    unit = hidden * recip
    scaled = summed_ref[...] * gain_ref[...]
    inner = jnp.mean(scaled * unit, axis=1, keepdims=True)
    out_ref[...] = middle_ref[...] + recip * (scaled - unit * inner)

    @pl.when(pl.program_id(0) == 0)
    def _():
        for small, out in zip(smalls, small_outs):
            out[...] = small[...]


def leave_first(summed, tokens, grad_middle, gain, smalls):
    length, width = tokens.shape
    rows = pl.BlockSpec((BLOCK, width), lambda i: (i, 0))
    whole = lambda shape: pl.BlockSpec(shape, lambda i: (0, 0))
    f32 = jnp.float32
    return pl.pallas_call(
        functools.partial(last_kernel, len(smalls)),
        out_shape=[jax.ShapeDtypeStruct((length, width), f32)]
        + [jax.ShapeDtypeStruct(small.shape, f32) for small in smalls],
        grid=(length // BLOCK,),
        in_specs=[rows, rows, rows, whole((1, width))] + [whole(small.shape) for small in smalls],
        out_specs=[rows] + [whole(small.shape) for small in smalls],
        compiler_params=pltpu.CompilerParams(vmem_limit_bytes=60 << 20),
        cost_estimate=pl.CostEstimate(
            flops=10 * length * width, bytes_accessed=14 * length * width, transcendentals=0
        ),
    )(summed, tokens, grad_middle, gain.reshape(1, width), *smalls)


SPAN = 768
ROWS = 256


def lane_halves(shape):
    return lax.broadcasted_iota(jnp.int32, shape, len(shape) - 1) // HEAD


def select_halves(tile, source, half):
    kept = jnp.where(lane_halves(tile.shape) == source, tile, 0.0)
    return kept if source == half else pltpu.roll(kept, HEAD, 1)


def spread_pairs(tile, target):
    for source in range(2):
        for half in range(2):
            target[2 * source + half] = select_halves(tile, source, half).astype(jnp.bfloat16)


def rope_tile(tile, cosine, sine_low, sine_high):
    return tile * cosine + pltpu.roll(tile, 128 - HEAD // 2, 1) * sine_low + pltpu.roll(
        tile, HEAD // 2, 1
    ) * sine_high


def rope_back_tile(tile, cosine, sine_low, sine_high):
    return (
        tile * cosine
        + pltpu.roll(tile * sine_low, HEAD // 2, 1)
        + pltpu.roll(tile * sine_high, 128 - HEAD // 2, 1)
    )


def window(block):
    first = block * ROWS
    return first, jnp.maximum(first + ROWS - SPAN, 0)


def attend_forward_kernel(
    heads,
    group,
    tokens_ref,
    gain_ref,
    query_w,
    key_w,
    value_w,
    cosine_ref,
    sine_low_ref,
    sine_high_ref,
    opening_ref,
    normed_out,
    query_out,
    key_out,
    value_out,
    attended_out,
    logsum_out,
    key_pairs,
    value_pairs,
    tiles_ref,
):
    tiles, length, unused = query_out.shape
    hidden = tokens_ref[...].astype(jnp.float32)
    recip = lax.rsqrt(jnp.mean(hidden * hidden, axis=1, keepdims=True) + EPSILON)
    normed_out[...] = (hidden * recip * gain_ref[...]).astype(jnp.bfloat16)
    cosine, sine_low, sine_high = cosine_ref[...], sine_low_ref[...], sine_high_ref[...]
    for tile in range(tiles):
        query = jnp.dot(
            normed_out[...],
            query_w[:, tile * 128 : (tile + 1) * 128],
            preferred_element_type=jnp.float32,
        )
        query_out[tile] = rope_tile(query, cosine, sine_low, sine_high).astype(jnp.bfloat16)
    key = rope_tile(
        jnp.dot(normed_out[...], key_w[...], preferred_element_type=jnp.float32),
        cosine,
        sine_low,
        sine_high,
    )
    value = jnp.dot(normed_out[...], value_w[...], preferred_element_type=jnp.float32)
    key_out[...] = key.astype(jnp.bfloat16)
    value_out[...] = value.astype(jnp.bfloat16)
    spread_pairs(key, key_pairs)
    spread_pairs(value, value_pairs)
    blocks = length // ROWS
    tiles_ref[...] = jnp.zeros_like(tiles_ref)

    for block in range(blocks):
        first = block * ROWS
        low = max(first + ROWS - SPAN, 0)
        rows, span = slice(first, first + ROWS), slice(low, first + ROWS)
        shape = (ROWS, first + ROWS - low)
        columns = low + lax.broadcasted_iota(jnp.int32, shape, 1)
        own = first + lax.broadcasted_iota(jnp.int32, shape, 0)

        def unit(head, carry):
            tile, half = head // 2, head % 2
            pair = 2 * (head // group) + half
            scores = right_inner(query_out[tile, rows, :], key_pairs[pair, span, :])
            allowed = (columns >= opening_ref[rows, :]) & (columns <= own)
            raised = jnp.where(allowed, jnp.exp(ATTN_SCALE * scores), 0.0)
            total = jnp.sum(raised, axis=1, keepdims=True)
            product = jnp.dot(
                raised.astype(jnp.bfloat16),
                value_pairs[pair, span, :],
                preferred_element_type=jnp.float32,
            )
            tiles_ref[tile, rows, :] += product / total
            wide = jnp.broadcast_to(jnp.log(total), (ROWS, 128))
            logsum_out[head, :, rows] = jnp.transpose(wide)[:1]
            return carry

        lax.fori_loop(0, heads, unit, 0)
    for tile in range(tiles):
        attended_out[:, tile * 128 : (tile + 1) * 128] = tiles_ref[tile].astype(jnp.bfloat16)


def attend_forward(tokens, gain, query_w, key_w, value_w, tables, opening, heads, group):
    length, width = tokens.shape
    wide = query_w.shape[1]
    tiles = wide // 128
    bf16, f32 = jnp.bfloat16, jnp.float32
    full = pl.BlockSpec(memory_space=pltpu.VMEM)
    return pl.pallas_call(
        functools.partial(attend_forward_kernel, heads, group),
        out_shape=[
            jax.ShapeDtypeStruct((length, width), bf16),
            jax.ShapeDtypeStruct((tiles, length, 128), bf16),
            jax.ShapeDtypeStruct((length, 128), bf16),
            jax.ShapeDtypeStruct((length, 128), bf16),
            jax.ShapeDtypeStruct((length, wide), bf16),
            jax.ShapeDtypeStruct((heads, 1, length), f32),
        ],
        in_specs=[full] * 9,
        out_specs=[full] * 6,
        scratch_shapes=[
            pltpu.VMEM((4, length, 128), bf16),
            pltpu.VMEM((4, length, 128), bf16),
            pltpu.VMEM((tiles, length, 128), f32),
        ],
        compiler_params=pltpu.CompilerParams(vmem_limit_bytes=48 << 20),
        cost_estimate=pl.CostEstimate(
            flops=8 * 10**9, bytes_accessed=12 * 10**6, transcendentals=5 * 10**6
        ),
    )(tokens, gain.reshape(1, width), query_w, key_w, value_w, *tables, opening.reshape(length, 1))


def attend_backward_kernel(
    n,
    heads,
    group,
    branch_ref,
    out_w,
    query_ref,
    key_ref,
    value_ref,
    attended_ref,
    logsum_ref,
    query_w,
    key_w,
    value_w,
    cosine_ref,
    sine_low_ref,
    sine_high_ref,
    opening_ref,
    tokens_ref,
    moe_ref,
    middle_ref,
    grads_out,
    normed_out,
    gain_out,
    output_ref,
    moe_sum,
    middle_rows,
    middle_sems,
    key_pairs,
    value_pairs,
    attend_grads,
    query_grads,
    key_grads,
    value_grads,
    delta_ref,
    *line,
):
    tiles, length, unused = query_ref.shape
    share = length // STEPS

    def share_rows(c):
        return pl.ds(pl.multiple_of(c * share, share), share)

    def fetch(c):
        slot = lax.rem(c, 2)
        return pltpu.make_async_copy(
            middle_ref.at[share_rows(c), :], middle_rows.at[slot], middle_sems.at[slot]
        )

    def done(c):
        fetch(c).wait()

        @pl.when(c + 1 < STEPS)
        def _():
            fetch(c + 1).start()

        total = middle_rows[lax.rem(c, 2)] + RESIDUAL * moe_sum[share_rows(c), :]
        output_ref[share_rows(c), :] = total.astype(jnp.bfloat16)

    line_start, line_step, line_end = line_stages(n, [moe_ref], [moe_sum], line, done)
    line_start()
    fetch(jnp.int32(0)).start()
    blocks = length // ROWS
    units = heads * blocks
    taken = 0

    def run_line(steps):
        nonlocal taken
        until = min(taken + steps, 2 * STEPS)
        lax.fori_loop(taken, until, line_step, 0)
        taken = until

    run_line(2)
    spread_pairs(key_ref[...].astype(jnp.float32), key_pairs)
    spread_pairs(value_ref[...].astype(jnp.float32), value_pairs)
    halves = (
        lax.broadcasted_iota(jnp.int32, (8, 128), 0) == lane_halves((8, 128))
    ).astype(jnp.float32)
    for tile in range(tiles):
        lanes = slice(tile * 128, (tile + 1) * 128)
        grad = right_inner(branch_ref[...], out_w[lanes, :]).astype(jnp.bfloat16)
        attend_grads[tile] = grad
        products = grad.astype(jnp.float32) * attended_ref[:, lanes].astype(jnp.float32)
        sums = lax.dot_general(
            halves,
            products,
            (((1,), (1,)), ((), ())),
            precision=lax.Precision.HIGHEST,
            preferred_element_type=jnp.float32,
        )
        delta_ref[2 * tile] = sums[0:1]
        delta_ref[2 * tile + 1] = sums[1:2]
        run_line(2)
    query_grads[...] = jnp.zeros_like(query_grads)
    key_grads[...] = jnp.zeros_like(key_grads)
    value_grads[...] = jnp.zeros_like(value_grads)
    before, each = taken, (2 * STEPS - 8 - taken) // units
    taken += units * each

    def unit(step, carry):
        lax.fori_loop(before + step * each, before + step * each + each, line_step, 0)
        head, block = step // blocks, step % blocks
        tile, half = head // 2, head % 2
        pair = 2 * (head // group) + half
        first, low = window(block)
        rows = pl.ds(pl.multiple_of(first, ROWS), ROWS)
        span = pl.ds(pl.multiple_of(low, ROWS), SPAN)
        keys = key_pairs[pair, span, :]
        query = query_ref[tile, rows, :]
        grad = attend_grads[tile, rows, :]
        scores = right_inner(keys, query)
        columns = low + lax.broadcasted_iota(jnp.int32, (SPAN, ROWS), 0)
        own = first + lax.broadcasted_iota(jnp.int32, (SPAN, ROWS), 1)
        allowed = (columns >= opening_ref[:, rows]) & (columns <= own)
        probs = jnp.where(
            allowed, jnp.exp(ATTN_SCALE * scores - logsum_ref[head, :, rows]), 0.0
        )
        grad_probs = right_inner(value_pairs[pair, span, :], grad)
        grad_scores = (probs * (grad_probs - delta_ref[head, :, rows])).astype(jnp.bfloat16)
        value_grads[pair, span, :] += jnp.dot(
            probs.astype(jnp.bfloat16), grad, preferred_element_type=jnp.float32
        )
        key_grads[pair, span, :] += jnp.dot(
            grad_scores, query, preferred_element_type=jnp.float32
        )
        query_grads[tile, rows, :] += left_inner(grad_scores, keys)
        return carry

    lax.fori_loop(0, units, unit, 0)
    cosine, sine_low, sine_high = cosine_ref[...], sine_low_ref[...], sine_high_ref[...]
    wide = tiles * 128
    for tile in range(tiles):
        grads_out[:, tile * 128 : (tile + 1) * 128] = rope_back_tile(
            ATTN_SCALE * query_grads[tile], cosine, sine_low, sine_high
        ).astype(jnp.bfloat16)
    totals = []
    for grads in (key_grads, value_grads):
        totals.append(
            sum(
                select_halves(grads[2 * source + half], half, source)
                for source in range(2)
                for half in range(2)
            )
        )
    grads_out[:, wide : wide + 128] = rope_back_tile(
        ATTN_SCALE * totals[0], cosine, sine_low, sine_high
    ).astype(jnp.bfloat16)
    grads_out[:, wide + 128 : wide + 256] = totals[1].astype(jnp.bfloat16)
    gain_sum = jnp.zeros((1, normed_out.shape[1]), jnp.float32)
    for block in range(blocks):
        rows = slice(block * ROWS, (block + 1) * ROWS)
        normed = (
            right_inner(grads_out[rows, :wide], query_w[...])
            + right_inner(grads_out[rows, wide : wide + 128], key_w[...])
            + right_inner(grads_out[rows, wide + 128 :], value_w[...])
        )
        normed_out[rows, :] = normed
        hidden = tokens_ref[rows, :].astype(jnp.float32)
        recip = lax.rsqrt(jnp.mean(hidden * hidden, axis=1, keepdims=True) + EPSILON)
        gain_sum += jnp.sum(normed * (hidden * recip), axis=0, keepdims=True)
        run_line(2)
    gain_out[...] = jnp.broadcast_to(gain_sum, gain_out.shape)
    run_line(2 * STEPS)
    line_end()


def attend_backward(
    n, branch, out_w, query, key, value, attended, logsum, query_w, key_w, value_w, tables, opening, tokens, moe, middle,
    heads, group, name,
):
    length, width = branch.shape
    tiles = query.shape[0]
    wide = tiles * 128
    bf16, f32 = jnp.bfloat16, jnp.float32
    full = pl.BlockSpec(memory_space=pltpu.VMEM)
    return pl.pallas_call(
        functools.partial(attend_backward_kernel, n, heads, group),
        out_shape=[
            jax.ShapeDtypeStruct((length, wide + 256), bf16),
            jax.ShapeDtypeStruct((length, width), f32),
            jax.ShapeDtypeStruct((8, width), f32),
            jax.ShapeDtypeStruct((length, width), bf16),
        ],
        in_specs=[full] * 16 + [pl.BlockSpec(memory_space=pl.ANY)],
        out_specs=[full] * 4,
        scratch_shapes=[
            pltpu.VMEM((length, width), f32),
            pltpu.VMEM((2, length // STEPS, width), f32),
            pltpu.SemaphoreType.DMA((2,)),
            pltpu.VMEM((4, length, 128), bf16),
            pltpu.VMEM((4, length, 128), bf16),
            pltpu.VMEM((tiles, length, 128), bf16),
            pltpu.VMEM((tiles, length, 128), f32),
            pltpu.VMEM((4, length, 128), f32),
            pltpu.VMEM((4, length, 128), f32),
            pltpu.VMEM((2 * tiles, 1, length), f32),
        ]
        + line_scratch([moe]),
        compiler_params=pltpu.CompilerParams(
            collective_id=name, has_side_effects=True, vmem_limit_bytes=63 << 20
        ),
        cost_estimate=pl.CostEstimate(
            flops=12 * 10**9, bytes_accessed=30 * 10**6, transcendentals=5 * 10**6
        ),
    )(
        branch, out_w, query, key, value, attended, logsum, query_w, key_w, value_w, *tables,
        opening.reshape(1, length), tokens, moe, middle,
    )


def finish_kernel(
    n,
    parts,
    local_ref,
    normed_ref,
    grads_ref,
    branch_ref,
    attended_ref,
    normed_two_ref,
    logits_ref,
    gain_ref,
    first_gain_ref,
    normed_out,
    query_out,
    key_out,
    value_out,
    branch_out,
    router_out,
    gain_out,
    first_gain_out,
    weights_ref,
    gains_ref,
    gain_send,
    gain_recv,
    *scratch,
):
    levels = parts.bit_length() - 1
    held = scratch[:levels]
    sends, recvs = scratch[levels : levels + 2]
    line_start, line_step, line_end = line_stages(n, [local_ref], [normed_out], scratch[levels + 2 :])
    me = lax.axis_index("dp")
    width = normed_ref.shape[1]
    own = width // parts
    wide, attended_wide = grads_ref.shape[1], attended_ref.shape[1]
    mine = lax.axis_index("tensor")
    line_start(
        [{"dp": jnp.bitwise_xor(me, 1 << level)} for level in range(levels)]
        + [{"tensor": lax.rem(mine + ahead, n)} for ahead in range(1, n)]
    )

    def run_line(first, last):
        lax.fori_loop(first, last, line_step, 0)

    gain_copies = [
        pltpu.make_async_remote_copy(
            src_ref=first_gain_ref,
            dst_ref=gains_ref.at[ahead],
            send_sem=gain_send.at[ahead],
            recv_sem=gain_recv.at[ahead],
            device_id={"tensor": lax.rem(mine + ahead, n)},
            device_id_type=MESH,
        )
        for ahead in range(1, n)
    ]
    for copy in gain_copies:
        copy.start()
    run_line(0, 2)
    first_gain = first_gain_ref[:1]
    for ahead, copy in enumerate(gain_copies, 1):
        copy.wait_recv()
        first_gain = first_gain + gains_ref[ahead, :1]
    pieces = 4
    block = width // pieces
    for piece in range(pieces):
        rows = slice(piece * block, (piece + 1) * block)
        weights_ref[rows, :wide] = left_inner(normed_ref[:, rows], grads_ref[...])
        weights_ref[rows, wide : wide + attended_wide] = left_inner(
            branch_ref[:, rows], attended_ref[...]
        )
        gain = jnp.transpose(jnp.broadcast_to(gain_ref[:, rows], (128, block)))
        own_gain = jnp.transpose(jnp.broadcast_to(first_gain[:, rows], (128, block)))
        lanes = lax.broadcasted_iota(jnp.int32, (block, 128), 1)
        weights_ref[rows, wide + attended_wide :] = jnp.where(
            lanes == 127,
            gain,
            jnp.where(
                lanes == 126, own_gain, left_inner(normed_two_ref[:, rows], logits_ref[...])
            ),
        )
        run_line(2 + 2 * piece, 4 + 2 * piece)
    done = 2 + 2 * pieces

    columns = weights_ref.shape[1]
    middle = columns // 256 * 128
    orders = (
        (slice(0, middle), list(range(levels))),
        (slice(middle, columns), [0] + list(range(levels - 1, 0, -1))),
    )

    def shard(number, lanes):
        return weights_ref.at[pl.ds(pl.multiple_of(number * own, own), own), lanes]

    def numbers(order, level, peer):
        fixed = sum(1 << bit for bit in order[: level + 1])
        base = jnp.bitwise_and(peer, fixed)
        free = order[level + 1 :]
        return [
            base + sum(((i >> place) & 1) << bit for place, bit in enumerate(free))
            for i in range(1 << len(free))
        ]

    def copies(level):
        made = []
        for side, (lanes, order) in enumerate(orders):
            peer = jnp.bitwise_xor(me, 1 << order[level])
            for i, number in enumerate(numbers(order, level, peer)):
                made.append(
                    pltpu.make_async_remote_copy(
                        src_ref=shard(number, lanes),
                        dst_ref=held[level].at[i, :, lanes],
                        send_sem=sends.at[side, level, i],
                        recv_sem=recvs.at[side, level, i],
                        device_id={"dp": peer},
                        device_id_type=MESH,
                    )
                )
        return made

    stops = [6] + [42] * (levels > 1) + [4, 0, 0]
    for level in range(levels):
        for copy in copies(level):
            copy.start()
        until = done + stops[level]
        run_line(done, until)
        done = until
        for copy in copies(level):
            copy.wait_recv()
        for lanes, order in orders:
            for i, number in enumerate(numbers(order, level, me)):
                target = shard(number, lanes)
                target[...] += held[level][i, :, lanes]
    everything = slice(0, columns)
    run_line(done, 2 * STEPS)
    kept = shard(me, everything)
    tail = jnp.transpose(kept[:, wide + attended_wide :])
    query_out[...] = kept[:, : query_out.shape[1]]
    key_out[...] = kept[:, wide - 256 : wide - 256 + key_out.shape[1]]
    value_out[...] = kept[:, wide - 128 : wide - 128 + value_out.shape[1]]
    branch_out[...] = kept[:, wide : wide + branch_out.shape[1]]
    router_out[...] = tail[: router_out.shape[0]]
    gain_out[...] = tail[127:]
    first_gain_out[...] = tail[126:127]
    for level in range(levels):
        for copy in copies(level):
            copy.wait_send()
    for copy in gain_copies:
        copy.wait_send()
    line_end()


def finish(
    n, parts, grad_local, normed_b, grads_wide, branch_b, attended, normed_two_b, grad_logits_b, gain_grad, first_gain_grad,
    wide_q, wide_k, experts, name,
):
    length, width = normed_b.shape
    columns = grads_wide.shape[1] + attended.shape[1] + 128
    full = pl.BlockSpec(memory_space=pltpu.VMEM)
    levels = parts.bit_length() - 1
    own = width // parts
    f32 = jnp.float32
    shapes = [(length, width), (own, wide_q), (own, wide_k), (own, wide_k), (own, wide_q)]
    shapes += [(experts, own), (1, own), (1, own)]
    return pl.pallas_call(
        functools.partial(finish_kernel, n, parts),
        out_shape=[jax.ShapeDtypeStruct(shape, f32) for shape in shapes],
        in_specs=[full] * 9,
        out_specs=[full] * 8,
        scratch_shapes=[
            pltpu.VMEM((width, columns), f32),
            pltpu.VMEM((n, 8, width), f32),
            pltpu.SemaphoreType.DMA((n,)),
            pltpu.SemaphoreType.DMA((n,)),
        ]
        + [pltpu.VMEM((parts >> (level + 1), own, columns), f32) for level in range(levels)]
        + [pltpu.SemaphoreType.DMA((2, levels, parts // 2))] * 2
        + line_scratch([grad_local]),
        compiler_params=pltpu.CompilerParams(
            collective_id=name, has_side_effects=True, vmem_limit_bytes=62 << 20
        ),
        cost_estimate=pl.CostEstimate(
            flops=2 * length * width * columns, bytes_accessed=50 * 10**6, transcendentals=0
        ),
    )(
        grad_local, normed_b, grads_wide, branch_b, attended, normed_two_b, grad_logits_b, gain_grad,
        first_gain_grad,
    )


def place_kernel(gate_ref, up_ref, down_ref, *refs):
    gate_out, up_out, down_out = refs[-3:]
    gate_out[0] = gate_ref[0, 0]
    up_out[0] = up_ref[0, 0]
    rows, hidden = down_out.shape[1], down_ref.shape[3]
    for piece in range(down_out.shape[2] // hidden):
        down_out[0, :, piece * hidden : (piece + 1) * hidden] = down_ref[
            0, 0, piece * rows : (piece + 1) * rows, :
        ]


def place_shards(parts, shards, first, experts, before):
    number, unused, rows, hidden = shards.shape
    down_rows = hidden // parts
    width = rows * parts
    shapes = [(experts, rows, hidden), (experts, rows, hidden), (experts, down_rows, width)]
    spec = lambda shape: pl.BlockSpec((1,) + shape[1:], lambda e: (first + e, 0, 0))
    one = lambda kind: pl.BlockSpec((1, 1, rows, hidden), lambda e: (e, kind, 0, 0))
    args, extra, aliases = [shards] * 3, [], {}
    if before is not None:
        args += list(before)
        extra = [pl.BlockSpec(memory_space=pl.ANY)] * 3
        aliases = {3: 0, 4: 1, 5: 2}
    return pl.pallas_call(
        place_kernel,
        out_shape=[jax.ShapeDtypeStruct(shape, jnp.float32) for shape in shapes],
        grid=(number,),
        in_specs=[one(kind) for kind in range(3)] + extra,
        out_specs=[spec(shape) for shape in shapes],
        input_output_aliases=aliases,
        compiler_params=pltpu.CompilerParams(vmem_limit_bytes=60 << 20),
        cost_estimate=pl.CostEstimate(
            flops=0, bytes_accessed=8 * shards.size, transcendentals=0
        ),
    )(*args)


def on_device(
    ring,
    tokens,
    cotangent,
    segment_ids,
    routes,
    attn_gain,
    query_weight,
    key_weight,
    value_weight,
    out_weight,
    ffn_gain,
    router_weight,
    gate_weight,
    up_weight,
    down_weight,
):
    length = tokens.shape[0]
    width = tokens.shape[1]
    segment = segment_ids[0]
    heads_local = query_weight.shape[1] // HEAD
    kv_local = key_weight.shape[1] // HEAD
    group_size = heads_local // kv_local
    experts_all = router_weight.shape[1]
    experts_local = gate_weight.shape[0]
    parts = lax.axis_size("dp")
    opening = doc_openings(segment)
    tables = rope_tables(opening, HEAD)
    query_w, key_w, value_w = (pad_columns(w) for w in (query_weight, key_weight, value_weight))
    out_w = jnp.transpose(pad_columns(jnp.transpose(out_weight)))
    ways, out_rows = gather_out_weight(out_weight, parts)
    normed_b, queries, keys, values, attended, logsum = attend_forward(
        tokens, attn_gain, query_w, key_w, value_w, tables, opening, heads_local, group_size
    )
    all_ids = jnp.arange(experts_all, dtype=jnp.int32)
    chosen = jnp.sum((routes[:, :, None] == all_ids[None, None, :]).astype(jnp.int32), axis=1) > 0
    first_expert = lax.axis_index("tensor") * experts_local
    local_ids = first_expert + jnp.arange(experts_local, dtype=jnp.int32)
    picked = jnp.sum((routes[None, :, :] == local_ids[:, None, None]).astype(jnp.int32), axis=2)
    places_in = slot_places(picked)
    counts = jnp.sum(picked, axis=1)
    chosen = pad_columns(chosen.astype(jnp.float32))
    out_rows, attended, chosen, places_in, counts = lax.optimization_barrier(
        (out_rows, attended, chosen, places_in, counts)
    )
    out_all = lax.all_gather(out_rows, "dp") if ways > 1 else out_rows[None]
    attended_all = line_gather(attended, ring, 1)
    attended_all = attended_all.reshape(length, ring, attended.shape[1])
    attended_all = attended_all[:, :, : heads_local * HEAD].reshape(length, -1)
    router_w = pad_columns(router_weight)
    middle, normed_two_b, gate_probs = enter_middle(
        attended_all, out_all, tokens, ffn_gain, router_w, chosen
    )
    gate_rows = jnp.transpose(lax.dynamic_slice_in_dim(gate_probs, first_expert, experts_local, 1))
    numbers = (max(1, experts_local // 10),)
    numbers += (experts_local - numbers[0],)
    (grads_first,), sums = expert_stage(
        parts, 0, numbers[:1], counts, places_in, gate_rows, normed_two_b, cotangent,
        gate_weight, up_weight, down_weight, None,
    )
    shards_first = lax.psum_scatter(grads_first, "dp", scatter_dimension=2, tiled=True)
    (grads_last,), sums_last = expert_stage(
        parts, numbers[0], numbers[1:], counts, places_in, gate_rows, normed_two_b, cotangent,
        gate_weight, up_weight, down_weight, sums,
    )
    moe_part, grad_normed_part, unused = sums_last
    shards_first, grads_last, grad_normed_part = lax.optimization_barrier(
        (shards_first, grads_last, grad_normed_part)
    )
    shards_last = lax.psum_scatter(grads_last, "dp", scatter_dimension=2, tiled=True)
    grad_gates_local = jnp.concatenate([sums[2], sums_last[2]], 0).reshape(experts_local, length)
    grad_gates_part = lax.dynamic_update_slice_in_dim(
        jnp.zeros((experts_all, length), jnp.float32), grad_gates_local, first_expert, 0
    )
    grad_middle, grad_branch_b, grad_logits_b, grad_ffn_gain = turn_middle(
        ring, grad_normed_part, grad_gates_part, gate_probs, middle, cotangent, ffn_gain, router_w, 2
    )
    grads_wide, grad_normed_local, first_gain, output = attend_backward(
        ring, grad_branch_b, out_w, queries, keys, values, attended, logsum,
        query_w, key_w, value_w, tables, opening, tokens, moe_part, middle, heads_local, group_size, 3,
    )
    wide_q, wide_k = heads_local * HEAD, kv_local * HEAD
    grads_placed = place_shards(parts, shards_first, 0, experts_local, None)
    grads_placed, grads_wide = lax.optimization_barrier((grads_placed, grads_wide))
    grad_normed, *small = finish(
        ring, parts, grad_normed_local, normed_b, grads_wide, grad_branch_b, attended, normed_two_b,
        grad_logits_b, grad_ffn_gain, first_gain, wide_q, wide_k, experts_all, 4,
    )
    grad_tokens, *small = leave_first(grad_normed, tokens, grad_middle, attn_gain, small)
    grad_query, grad_key, grad_value, grad_out, grad_router, grad_ffn_gain, grad_attn_gain = small
    shards_last, grad_tokens = lax.optimization_barrier((shards_last, grad_tokens))
    grad_gate, grad_up, grad_down = place_shards(
        parts, shards_last, numbers[0], experts_local, grads_placed
    )
    return (
        output,
        grad_tokens,
        grad_attn_gain.reshape(-1),
        grad_query,
        grad_key,
        grad_value,
        jnp.transpose(grad_out),
        grad_ffn_gain.reshape(-1),
        jnp.transpose(grad_router),
        grad_gate,
        grad_up,
        grad_down,
    )


def solution(mesh):
    return jax.shard_map(
        functools.partial(on_device, mesh.shape["tensor"]),
        mesh=mesh,
        in_specs=(
            P("dp", None),
            P("dp", None),
            P("dp", None),
            P("dp", None),
            P(),
            P(None, "tensor"),
            P(None, "tensor"),
            P(None, "tensor"),
            P("tensor", None),
            P(),
            P(),
            P("tensor", None, None),
            P("tensor", None, None),
            P("tensor", None, None),
        ),
        out_specs=(
            P("dp", None),
            P("dp", None),
            P("dp"),
            P("dp", "tensor"),
            P("dp", "tensor"),
            P("dp", "tensor"),
            P("tensor", "dp"),
            P("dp"),
            P("dp", None),
            P("tensor", "dp", None),
            P("tensor", "dp", None),
            P("tensor", "dp", None),
        ),
        check_vma=False,
    )
```
